128 devices in a mesh: seq: 16 (over y, z_lo, core), vis: 8 (over z_hi, x).
Axes of the slice: x: 4, y: 4, z: 4 (z_hi: 2, z_lo: 2; z = z_hi * 2 + z_lo), core: 2. Of those that a mesh axis runs over, the one named last changes fastest.
Arguments:
- text: bfloat16 [4096, 8192], P('seq'), may hold values from -6 to 6
- frames: bfloat16 [4096, 8192], P(('seq', 'vis')), may hold values from -60 to 60
- tile_pos: int32 [4096], P(('seq', 'vis')), may hold values from 0 to 4095, as said below
- frame_count: int32 [128], P(('seq', 'vis')), may hold values from 2 to 32
- doc_ids: int32 [4096], replicated, may hold values from 0 to 3, never falling along the last dimension, each value on 1 to 2048 neighbouring positions
- norm_gain: float32 [8192], replicated, may hold values from 0.1 to 1.9
- w_query: bfloat16 [8192, 8192], P(None, 'vis'), may hold values from -4 to 4
- q_bias: float32 [8192], P('vis'), may hold values from -3 to 3
- w_key: bfloat16 [8192, 1024], P(None, 'vis'), may hold values from -4 to 4
- w_value: bfloat16 [8192, 1024], P(None, 'vis'), may hold values from -0.0625 to 0.0625
- v_bias: float32 [1024], P('vis'), may hold values from -3 to 3
Outputs:
- attended: bfloat16 [4096, 8192], P('seq', 'vis')
The draws below stay inside these ranges and needn't reach their ends.
Inputs may be any that keep to these rules, and one draw needn't show every extreme that they name: `tile_pos`: all entries together name every position of the window once. Of one device's 32 rows, at most 2 of those below its frame_count fall into one shard of 256 positions, and in every draw one shard receives exactly 2 usable rows from every device. Rows at or beyond the count are unused. `doc_ids`: never falling along the window.
All inputs are finite; a program needn't handle non-finite values.
Results may differ from the reference program's by a relative error of at most 0.0069.
Values may be sent and summed in bfloat16 or wider, within the bound.
A program may use at most 128 MiB of HBM per device.

```python
import math
import jax
import jax.numpy as jnp
import numpy as np
from jax import lax

D = 8192
HEADS = 64
KV_HEADS = 8
HEAD_DIM = 128
DOCS = 4
TOK_DEV = 256
QPG = 8
TOKENS = 4096
CAP = 2
F_DEV = 32
N_SEQ = 16
N_VIS = 8


def permute_rows(seeds, length):

    def permute_one(seed_key):
        return jax.random.permutation(seed_key, length)
    return jax.vmap(permute_one)(seeds)


def tile_layout(key):
    devices = N_SEQ * N_VIS
    slots = N_SEQ * CAP
    folded = jax.random.fold_in(key, 71)
    key_counts, key_owner, key_busy, key_quiet, key_windows, key_order = jax.random.split(folded, 6)
    counts = jax.random.randint(key_counts, (devices, N_SEQ), 0, CAP + 1)
    full_owner = jax.random.randint(key_owner, (), 0, N_SEQ)
    owner_ids = jnp.arange(N_SEQ)[None, :]
    device_ids = jnp.arange(devices)[:, None]
    busiest = jax.random.randint(key_busy, (), 0, devices)
    quietest = (busiest + 1 + jax.random.randint(key_quiet, (), 0, devices - 1)) % devices
    counts = jnp.where(owner_ids == full_owner, CAP, counts)
    counts = jnp.where(device_ids == busiest, CAP, counts)
    counts = jnp.where((device_ids == quietest) & (owner_ids != full_owner), 0, counts)
    windows = permute_rows(jax.random.split(key_windows, N_SEQ), devices)
    offsets = jnp.arange(CAP)[None, None, :]
    places = jnp.arange(N_SEQ)[None, :, None] * TOK_DEV + windows.T[:, :, None] * CAP + offsets
    usable = (offsets < counts[:, :, None]).reshape(devices, slots)
    shuffle = permute_rows(jax.random.split(key_order, devices), slots)
    sort_keys = jnp.where(usable, 0, slots) + shuffle
    order = jnp.argsort(sort_keys, axis=1)
    placed = jnp.take_along_axis(places.reshape(devices, slots), order, axis=1)
    return (placed.reshape(devices * slots).astype(jnp.int32), jnp.sum(counts, axis=1).astype(jnp.int32))


def draw_tile_pos(key, part):
    return tile_layout(key)[0]


def draw_frame_count(key, part):
    return tile_layout(key)[1]


def draw_frames(key, part):
    base = jax.random.normal(jax.random.fold_in(key, 5), (TOKENS, D), jnp.float32)
    return jnp.clip(base, -60.0, 60.0).astype(jnp.bfloat16)


def draw_w_key(key, part):
    matrix = jax.random.normal(jax.random.fold_in(key, 31), (D, KV_HEADS * HEAD_DIM), jnp.float32) / math.sqrt(D)
    return jnp.clip(matrix, -4.0, 4.0).astype(jnp.bfloat16)


def draw_w_query(key, part):
    matrix = jax.random.normal(jax.random.fold_in(key, 37), (D, HEADS * HEAD_DIM), jnp.float32) * (2.0 / math.sqrt(D))
    return jnp.clip(matrix, -4.0, 4.0).astype(jnp.bfloat16)


def steps_of(stream_key, shape, cuts, least, top_value):
    factor_of = 1.0
    for dim, parts in cuts:
        heights = jax.random.uniform(jax.random.fold_in(jax.random.fold_in(stream_key, 6), dim), (parts,), jnp.float32, least / len(cuts), top_value / len(cuts))
        factor_of = factor_of * jnp.repeat(jnp.exp(heights), shape[dim] // parts).reshape((-1,) + (1,) * (len(shape) - 1 - dim))
    return factor_of


def split_up(count, total, limit, slope):
    loads = [(1 << 20) // math.isqrt(rank ** slope) + 1 for rank in range(2, count + 1)]
    surplus, holding = total - limit - (count - 1), [1] * (count - 1)
    while surplus > 0:
        movable = [i for i in range(count - 1) if holding[i] < limit]
        mass, budget = sum([loads[i] for i in movable]), surplus
        for i in movable:
            addition = min(limit - holding[i], max(1, budget * loads[i] // mass), surplus)
            holding[i] = holding[i] + addition
            surplus = surplus - addition
    return np.array([limit] + holding)


def uneven(rng, count, total, limit, slope):
    if count == 2:
        one = jax.random.randint(rng, (), max(1, total - limit), min(limit, total - 1) + 1)
        return jnp.stack([one, total - one])
    tallies = jnp.asarray(split_up(count, total, limit, slope), jnp.int32)
    couples = (count - 1) // 2
    giver, sink = tallies[1:1 + 2 * couples:2], tallies[2:2 + 2 * couples:2]
    slack = jnp.minimum(giver - 1, limit - sink)
    moved = jax.random.randint(jax.random.fold_in(rng, 1), (couples,), 0, 1 << 20) % (slack + 1)
    tallies = tallies.at[1:1 + 2 * couples:2].set(giver - moved).at[2:2 + 2 * couples:2].set(sink + moved)
    return tallies[jax.random.permutation(jax.random.fold_in(rng, 2), count)]


def bell_draw(own_key, shape, deviation, reach, cuts=(), held_as=jnp.bfloat16):
    loudness = steps_of(own_key, shape, cuts, -0.22, 0.18) if cuts else 1.0
    values = jax.random.normal(own_key, shape, jnp.float32) * deviation * loudness
    return jnp.minimum(jnp.maximum(values, -reach), reach).astype(held_as)


def setup_inputs(seed: int = 0) -> dict:
    key_of = jax.random.split(jax.random.key(seed), 12)
    text = bell_draw(key_of[0], (TOKENS, D), 1.0, 6.0, ((0, 16),))
    frames = draw_frames(jax.random.fold_in(key_of[11], 71), 0)
    tile_pos = draw_tile_pos(jax.random.fold_in(key_of[11], 71), 0)
    frame_count = draw_frame_count(jax.random.fold_in(key_of[11], 71), 0)
    doc_ids = jnp.searchsorted(jnp.cumsum(uneven(key_of[4], DOCS, TOKENS, TOKENS // 2, 2)), jnp.arange(TOKENS), side="right").astype(jnp.int32)
    norm_gain = jnp.clip(1.0 + 0.18 * jax.random.normal(key_of[5], (D,), jnp.float32), 0.1, 1.9)
    w_query = draw_w_query(jax.random.fold_in(key_of[11], 71), 0)
    q_bias = bell_draw(key_of[7], (HEADS * HEAD_DIM,), 0.5, 3.0, ((0, 8),), jnp.float32)
    w_key = draw_w_key(jax.random.fold_in(key_of[11], 71), 0)
    w_value = bell_draw(key_of[9], (D, KV_HEADS * HEAD_DIM), D ** -0.5, 0.0625, ((1, 8),))
    v_bias = bell_draw(key_of[10], (KV_HEADS * HEAD_DIM,), 0.5, 3.0, ((0, 8),), jnp.float32)
    return {"text": text, "frames": frames, "tile_pos": tile_pos, "frame_count": frame_count, "doc_ids": doc_ids, "norm_gain": norm_gain, "w_query": w_query, "q_bias": q_bias, "w_key": w_key, "w_value": w_value, "v_bias": v_bias}


epsilon = 1e-06

def reference(text, frames, tile_pos, frame_count, doc_ids, norm_gain, w_query, q_bias, w_key, w_value, v_bias):
    usable = (jnp.arange(F_DEV, dtype=jnp.int32)[None, :] < frame_count[:, None]).reshape(TOKENS)
    target = jnp.where(usable, tile_pos, TOKENS).astype(jnp.int32)
    merged = text.at[target].set(frames, mode='drop')
    widened = merged.astype(jnp.float32)
    mean_square = lax.optimization_barrier(jnp.mean(widened * widened, axis=1, keepdims=True))
    normed = (widened * lax.rsqrt(mean_square + epsilon) * norm_gain).astype(jnp.bfloat16)
    queries = (jnp.dot(normed, w_query, preferred_element_type=jnp.float32) + q_bias).astype(jnp.bfloat16)
    key_rows = jnp.dot(normed, w_key, preferred_element_type=jnp.float32).astype(jnp.bfloat16)
    values = (jnp.dot(normed, w_value, preferred_element_type=jnp.float32) + v_bias).astype(jnp.bfloat16)
    query_groups = queries.reshape(TOKENS, KV_HEADS, QPG, HEAD_DIM).transpose(1, 0, 2, 3)
    key_groups = key_rows.reshape(TOKENS, KV_HEADS, HEAD_DIM).transpose(1, 0, 2)
    value_groups = values.reshape(TOKENS, KV_HEADS, HEAD_DIM).transpose(1, 0, 2)
    block_rows = min(512, TOKENS)
    positions = jnp.arange(TOKENS, dtype=jnp.int32)
    score_scale = HEAD_DIM ** (-0.5)

    def one_group(operands):
        query_group, key_group, value_group = operands
        key_wide = key_group.astype(jnp.float32)
        value_wide = value_group.astype(jnp.float32)

        def one_block(block_index):
            row_start = (block_index * block_rows).astype(jnp.int32)
            query_block = lax.dynamic_slice_in_dim(query_group, row_start, block_rows, 0).astype(jnp.float32)
            query_place = row_start + jnp.arange(block_rows, dtype=jnp.int32)
            query_docs = lax.dynamic_slice_in_dim(doc_ids, row_start, block_rows, 0)
            scores = jnp.einsum('qjd,kd->qjk', query_block, key_wide) * score_scale
            allowed = (positions[None, :] <= query_place[:, None]) & (doc_ids[None, :] == query_docs[:, None])
            allowed = allowed[:, None, :]
            row_peak = lax.optimization_barrier(jnp.max(jnp.where(allowed, scores, -jnp.inf), axis=2, keepdims=True))
            raised = jnp.where(allowed, jnp.exp(scores - row_peak), 0.0)
            row_total = lax.optimization_barrier(jnp.sum(raised, axis=2))
            weights = raised.astype(jnp.bfloat16)
            summed = jnp.einsum('qjk,kd->qjd', weights.astype(jnp.float32), value_wide)
            return (summed / row_total[:, :, None]).astype(jnp.bfloat16)
        outputs = lax.map(one_block, jnp.arange(TOKENS // block_rows, dtype=jnp.int32))
        return outputs.reshape(TOKENS, QPG, HEAD_DIM)
    result = lax.map(one_group, (query_groups, key_groups, value_groups))
    return result.transpose(1, 0, 2, 3).reshape(TOKENS, HEADS * HEAD_DIM)
```

```python
import jax
import jax.numpy as jnp
from jax import lax
from jax.sharding import PartitionSpec as P
from jax.experimental import pallas as pl
from jax.experimental.pallas import tpu as pltpu

HEAD_DIM = 128


epsilon = 1e-06
negative = -1e30


def frame_slots(frames, tile_pos, frame_count, shard_rows, owners, capacity):
    row_count = frames.shape[0]
    row_ids = jnp.arange(row_count, dtype=jnp.int32)
    usable = row_ids < frame_count[0]
    owner = jnp.where(usable, tile_pos // shard_rows, owners)
    hits = (owner[:, None] == jnp.arange(owners, dtype=jnp.int32)[None, :]).astype(jnp.int32)
    earlier = (row_ids[:, None] > row_ids[None, :]).astype(jnp.int32)
    before = jnp.dot(earlier, hits, preferred_element_type=jnp.int32)
    rank = jnp.sum(before * hits, axis=1)
    slot_index = owner * capacity + rank
    slot_ids = jnp.arange(owners * capacity, dtype=jnp.int32)
    match = usable[:, None] & (slot_index[:, None] == slot_ids[None, :])
    filled = jnp.any(match, axis=0)
    source = jnp.sum(jnp.where(match, row_ids[:, None], 0), axis=0)
    slot_rows = jnp.where(filled[:, None], frames[source], jnp.zeros((), frames.dtype))
    slot_place = jnp.where(filled, tile_pos[source], -1)
    return (
        slot_rows.reshape(owners, capacity, frames.shape[1]),
        slot_place.reshape(owners, capacity),
    )


def place_frames(text, incoming, incoming_place, first_row):
    local_place = incoming_place - first_row
    lookup = local_place[None, :] == jnp.arange(text.shape[0], dtype=jnp.int32)[:, None]
    covered = jnp.any(lookup, axis=1)
    source = jnp.sum(
        jnp.where(lookup, jnp.arange(local_place.shape[0], dtype=jnp.int32)[None, :], 0), axis=1
    )
    return jnp.where(covered[:, None], incoming[source], text)


def on_device(
    text, frames, tile_pos, frame_count, doc_ids, norm_gain, w_query, q_bias, w_key, w_value, v_bias
):
    seq_count = lax.axis_size("seq")
    vis_count = lax.axis_size("vis")
    shard_index = lax.axis_index("seq")
    shard_rows = text.shape[0]
    capacity = shard_rows // (seq_count * vis_count)
    first_row = shard_index * shard_rows
    slot_rows, slot_place = frame_slots(
        frames, tile_pos, frame_count, shard_rows, seq_count, capacity
    )
    wide_rows = jnp.broadcast_to(slot_rows[:, None], (seq_count, vis_count) + slot_rows.shape[1:])
    wide_rows = wide_rows.reshape(seq_count * vis_count, capacity, slot_rows.shape[2])
    wide_place = jnp.broadcast_to(slot_place[:, None], (seq_count, vis_count, capacity))
    wide_place = wide_place.reshape(seq_count * vis_count, capacity)
    incoming, incoming_place = (
        lax.all_to_all(wide_rows, ("seq", "vis"), split_axis=0, concat_axis=0, tiled=True),
        lax.all_to_all(wide_place, ("seq", "vis"), split_axis=0, concat_axis=0, tiled=True),
    )
    incoming = incoming.reshape(-1, incoming.shape[-1])
    incoming_place = incoming_place.reshape(-1)
    merged = place_frames(text, incoming, incoming_place, first_row)
    widened = merged.astype(jnp.float32)
    mean_square = jnp.mean(widened * widened, axis=1, keepdims=True)
    normed = (widened * lax.rsqrt(mean_square + epsilon) * norm_gain).astype(jnp.bfloat16)
    queries = (jnp.dot(normed, w_query, preferred_element_type=jnp.float32) + q_bias).astype(
        jnp.bfloat16
    )
    key_rows = jnp.dot(normed, w_key, preferred_element_type=jnp.float32).astype(jnp.bfloat16)
    value_rows = (jnp.dot(normed, w_value, preferred_element_type=jnp.float32) + v_bias).astype(
        jnp.bfloat16
    )
    keyval = jnp.concatenate([key_rows, value_rows], axis=1)
    kv_heads = w_key.shape[1] // HEAD_DIM
    per_group = w_query.shape[1] // HEAD_DIM // kv_heads
    own_docs = lax.dynamic_slice_in_dim(doc_ids, first_row, shard_rows)
    incoming_keys = lax.all_gather(keyval, "seq", axis=0, tiled=True)
    doc_start = jnp.sum((doc_ids < own_docs[0]).astype(jnp.int32))
    last_row = first_row + shard_rows - 1
    block_range = jnp.stack([doc_start // KEY_BLOCK, last_row // KEY_BLOCK, first_row]).astype(jnp.int32)
    return flash_attention(block_range, queries, incoming_keys, own_docs, doc_ids, kv_heads)


KEY_BLOCK = 512


def flash_kernel(
    range_ref, q_ref, k_ref, v_ref, qdoc_ref, kdoc_ref, out_ref, peak_ref, total_ref, acc_ref
):
    step = pl.program_id(0)
    block = range_ref[0] + step
    rows = q_ref.shape[0]
    heads = q_ref.shape[1] // HEAD_DIM

    @pl.when(step == 0)
    def _():
        peak_ref[...] = jnp.full(peak_ref.shape, negative, jnp.float32)
        total_ref[...] = jnp.zeros(total_ref.shape, jnp.float32)
        acc_ref[...] = jnp.zeros(acc_ref.shape, jnp.float32)

    @pl.when(block <= range_ref[1])
    def _():
        key_place = block * KEY_BLOCK + lax.broadcasted_iota(jnp.int32, (1, KEY_BLOCK), 1)
        query_place = range_ref[2] + lax.broadcasted_iota(jnp.int32, (rows, 1), 0)
        allowed = (key_place <= query_place) & (kdoc_ref[...] == qdoc_ref[...])
        keys = k_ref[...]
        vals = v_ref[...]
        for h in range(heads):
            cols = slice(h * HEAD_DIM, (h + 1) * HEAD_DIM)
            scores = lax.dot_general(
                q_ref[:, cols], keys, (((1,), (1,)), ((), ())),
                preferred_element_type=jnp.float32,
            ) * HEAD_DIM ** (-0.5)
            scores = jnp.where(allowed, scores, negative)
            old_peak = peak_ref[h]
            new_peak = jnp.maximum(old_peak, jnp.max(scores, axis=1, keepdims=True))
            raised = jnp.where(allowed, jnp.exp(scores - new_peak[:, :1]), 0.0)
            factor = jnp.exp(old_peak - new_peak)
            total_ref[h] = total_ref[h] * factor + jnp.sum(raised, axis=1, keepdims=True)
            peak_ref[h] = new_peak
            product = jnp.dot(raised.astype(jnp.bfloat16), vals, preferred_element_type=jnp.float32)
            acc_ref[:, cols] = acc_ref[:, cols] * factor[:, :1] + product

    @pl.when(step == pl.num_programs(0) - 1)
    def _():
        for h in range(heads):
            cols = slice(h * HEAD_DIM, (h + 1) * HEAD_DIM)
            out_ref[:, cols] = (acc_ref[:, cols] / total_ref[h][:, :1]).astype(out_ref.dtype)


def flash_attention(block_range, queries, keyval, own_docs, doc_ids, kv_heads):
    rows, width = queries.shape
    key_rows = keyval.shape[0]
    steps = key_rows // KEY_BLOCK
    heads = width // HEAD_DIM

    def key_block(j, r):
        return (jnp.minimum(r[0] + j, r[1]), 0)

    def value_block(j, r):
        return (jnp.minimum(r[0] + j, r[1]), 1)

    def doc_block(j, r):
        return (0, jnp.minimum(r[0] + j, r[1]))

    grid_spec = pltpu.PrefetchScalarGridSpec(
        num_scalar_prefetch=1,
        grid=(steps,),
        in_specs=[
            pl.BlockSpec((rows, width), lambda j, r: (0, 0)),
            pl.BlockSpec((KEY_BLOCK, HEAD_DIM), key_block),
            pl.BlockSpec((KEY_BLOCK, HEAD_DIM), value_block),
            pl.BlockSpec((rows, 1), lambda j, r: (0, 0)),
            pl.BlockSpec((1, KEY_BLOCK), doc_block),
        ],
        out_specs=pl.BlockSpec((rows, width), lambda j, r: (0, 0)),
        scratch_shapes=[
            pltpu.VMEM((heads, rows, 1), jnp.float32),
            pltpu.VMEM((heads, rows, 1), jnp.float32),
            pltpu.VMEM((rows, width), jnp.float32),
        ],
    )
    flops = 4 * rows * width * key_rows // 2
    return pl.pallas_call(
        flash_kernel,
        out_shape=jax.ShapeDtypeStruct((rows, width), jnp.bfloat16),
        grid_spec=grid_spec,
        compiler_params=pltpu.CompilerParams(dimension_semantics=("arbitrary",)),
        cost_estimate=pl.CostEstimate(
            flops=flops, transcendentals=rows * heads * key_rows // 2,
            bytes_accessed=2 * (2 * rows * width + key_rows * 2 * HEAD_DIM),
        ),
    )(block_range, queries, keyval, keyval, own_docs.reshape(rows, 1), doc_ids.reshape(1, -1))


def solution(mesh):
    in_specs = (
        P("seq", None),
        P(("seq", "vis"), None),
        P(("seq", "vis")),
        P(("seq", "vis")),
        P(),
        P(),
        P(None, "vis"),
        P("vis"),
        P(None, "vis"),
        P(None, "vis"),
        P("vis"),
    )
    out_specs = P("seq", "vis")
    return jax.shard_map(
        on_device, mesh=mesh, in_specs=in_specs, out_specs=out_specs, check_vma=False
    )
```

```python
import jax
import jax.numpy as jnp
from jax import lax
from jax.sharding import PartitionSpec as P
from jax.experimental import pallas as pl
from jax.experimental.pallas import tpu as pltpu

HEAD_DIM = 128


epsilon = 1e-06
negative = -1e30


def frame_slots(frames, tile_pos, frame_count, shard_rows, owners, capacity):
    row_count = frames.shape[0]
    row_ids = jnp.arange(row_count, dtype=jnp.int32)
    usable = row_ids < frame_count[0]
    owner = jnp.where(usable, tile_pos // shard_rows, owners)
    hits = (owner[:, None] == jnp.arange(owners, dtype=jnp.int32)[None, :]).astype(jnp.int32)
    earlier = (row_ids[:, None] > row_ids[None, :]).astype(jnp.int32)
    before = jnp.dot(earlier, hits, preferred_element_type=jnp.int32)
    rank = jnp.sum(before * hits, axis=1)
    slot_index = owner * capacity + rank
    slot_ids = jnp.arange(owners * capacity, dtype=jnp.int32)
    match = usable[:, None] & (slot_index[:, None] == slot_ids[None, :])
    filled = jnp.any(match, axis=0)
    local = tile_pos - owner * shard_rows
    slot_local = jnp.sum(jnp.where(match, local[:, None], 0), axis=0)
    slot_local = jnp.where(filled, slot_local, -1)
    slot_rows = jnp.dot(
        match.T.astype(frames.dtype), frames, preferred_element_type=jnp.float32
    ).astype(frames.dtype)
    place_col = jnp.broadcast_to(slot_local[:, None], (slot_local.shape[0], 128)).astype(frames.dtype)
    payload = jnp.concatenate([slot_rows, place_col], axis=1)
    return payload.reshape(owners, capacity, payload.shape[1])


def place_frames(text, incoming, incoming_place):
    lookup = incoming_place[None, :] == jnp.arange(text.shape[0], dtype=jnp.int32)[:, None]
    covered = jnp.any(lookup, axis=1)
    placed = jnp.dot(
        lookup.astype(incoming.dtype), incoming, preferred_element_type=jnp.float32
    ).astype(text.dtype)
    return jnp.where(covered[:, None], placed, text)


def on_device(
    text, frames, tile_pos, frame_count, doc_ids, norm_gain, w_query, q_bias, w_key, w_value, v_bias
):
    seq_count = lax.axis_size("seq")
    vis_count = lax.axis_size("vis")
    shard_index = lax.axis_index("seq")
    shard_rows = text.shape[0]
    capacity = shard_rows // (seq_count * vis_count)
    first_row = shard_index * shard_rows
    payload = frame_slots(frames, tile_pos, frame_count, shard_rows, seq_count, capacity)
    arrived = lax.all_to_all(payload, "seq", split_axis=0, concat_axis=0, tiled=True)
    gathered = lax.all_gather(arrived, "vis", axis=0, tiled=True)
    gathered = gathered.reshape(-1, gathered.shape[-1])
    width = text.shape[1]
    incoming_place = gathered[:, width].astype(jnp.int32)
    merged = place_frames(text, gathered[:, :width], incoming_place)
    widened = merged.astype(jnp.float32)
    mean_square = jnp.mean(widened * widened, axis=1, keepdims=True)
    normed = (widened * lax.rsqrt(mean_square + epsilon) * norm_gain).astype(jnp.bfloat16)
    queries = (jnp.dot(normed, w_query, preferred_element_type=jnp.float32) + q_bias).astype(
        jnp.bfloat16
    )
    key_rows = jnp.dot(normed, w_key, preferred_element_type=jnp.float32).astype(jnp.bfloat16)
    value_rows = (jnp.dot(normed, w_value, preferred_element_type=jnp.float32) + v_bias).astype(
        jnp.bfloat16
    )
    keyval = jnp.concatenate([key_rows, value_rows], axis=1)
    kv_heads = w_key.shape[1] // HEAD_DIM
    per_group = w_query.shape[1] // HEAD_DIM // kv_heads
    own_docs = lax.dynamic_slice_in_dim(doc_ids, first_row, shard_rows)
    incoming_keys = lax.all_gather(keyval, "seq", axis=0, tiled=True)
    doc_start = jnp.sum((doc_ids < own_docs[0]).astype(jnp.int32))
    last_row = first_row + shard_rows - 1
    block_range = jnp.stack([doc_start // KEY_BLOCK, last_row // KEY_BLOCK, first_row]).astype(jnp.int32)
    return flash_attention(block_range, queries, incoming_keys, own_docs, doc_ids, kv_heads)


KEY_BLOCK = 512


def flash_kernel(
    range_ref, q_ref, k_ref, v_ref, qdoc_ref, kdoc_ref, out_ref, peak_ref, total_ref, acc_ref
):
    step = pl.program_id(0)
    block = range_ref[0] + step
    rows = q_ref.shape[0]
    heads = q_ref.shape[1] // HEAD_DIM

    @pl.when(step == 0)
    def _():
        peak_ref[...] = jnp.full(peak_ref.shape, negative, jnp.float32)
        total_ref[...] = jnp.zeros(total_ref.shape, jnp.float32)
        acc_ref[...] = jnp.zeros(acc_ref.shape, jnp.float32)

    @pl.when(block <= range_ref[1])
    def _():
        key_place = block * KEY_BLOCK + lax.broadcasted_iota(jnp.int32, (1, KEY_BLOCK), 1)
        query_place = range_ref[2] + lax.broadcasted_iota(jnp.int32, (rows, 1), 0)
        allowed = (key_place <= query_place) & (kdoc_ref[...] == qdoc_ref[...])
        keys = k_ref[...]
        vals = v_ref[...]
        for h in range(heads):
            cols = slice(h * HEAD_DIM, (h + 1) * HEAD_DIM)
            scores = lax.dot_general(
                q_ref[:, cols], keys, (((1,), (1,)), ((), ())),
                preferred_element_type=jnp.float32,
            ) * HEAD_DIM ** (-0.5)
            scores = jnp.where(allowed, scores, negative)
            old_peak = peak_ref[h]
            new_peak = jnp.maximum(old_peak, jnp.max(scores, axis=1, keepdims=True))
            raised = jnp.where(allowed, jnp.exp(scores - new_peak[:, :1]), 0.0)
            factor = jnp.exp(old_peak - new_peak)
            total_ref[h] = total_ref[h] * factor + jnp.sum(raised, axis=1, keepdims=True)
            peak_ref[h] = new_peak
            product = jnp.dot(raised.astype(jnp.bfloat16), vals, preferred_element_type=jnp.float32)
            acc_ref[:, cols] = acc_ref[:, cols] * factor[:, :1] + product

    @pl.when(step == pl.num_programs(0) - 1)
    def _():
        for h in range(heads):
            cols = slice(h * HEAD_DIM, (h + 1) * HEAD_DIM)
            out_ref[:, cols] = (acc_ref[:, cols] / total_ref[h][:, :1]).astype(out_ref.dtype)


def flash_attention(block_range, queries, keyval, own_docs, doc_ids, kv_heads):
    rows, width = queries.shape
    key_rows = keyval.shape[0]
    steps = key_rows // KEY_BLOCK
    heads = width // HEAD_DIM

    def key_block(j, r):
        return (jnp.minimum(r[0] + j, r[1]), 0)

    def value_block(j, r):
        return (jnp.minimum(r[0] + j, r[1]), 1)

    def doc_block(j, r):
        return (0, jnp.minimum(r[0] + j, r[1]))

    grid_spec = pltpu.PrefetchScalarGridSpec(
        num_scalar_prefetch=1,
        grid=(steps,),
        in_specs=[
            pl.BlockSpec((rows, width), lambda j, r: (0, 0)),
            pl.BlockSpec((KEY_BLOCK, HEAD_DIM), key_block),
            pl.BlockSpec((KEY_BLOCK, HEAD_DIM), value_block),
            pl.BlockSpec((rows, 1), lambda j, r: (0, 0)),
            pl.BlockSpec((1, KEY_BLOCK), doc_block),
        ],
        out_specs=pl.BlockSpec((rows, width), lambda j, r: (0, 0)),
        scratch_shapes=[
            pltpu.VMEM((heads, rows, 1), jnp.float32),
            pltpu.VMEM((heads, rows, 1), jnp.float32),
            pltpu.VMEM((rows, width), jnp.float32),
        ],
    )
    flops = 4 * rows * width * key_rows // 2
    return pl.pallas_call(
        flash_kernel,
        out_shape=jax.ShapeDtypeStruct((rows, width), jnp.bfloat16),
        grid_spec=grid_spec,
        compiler_params=pltpu.CompilerParams(dimension_semantics=("arbitrary",)),
        cost_estimate=pl.CostEstimate(
            flops=flops, transcendentals=rows * heads * key_rows // 2,
            bytes_accessed=2 * (2 * rows * width + key_rows * 2 * HEAD_DIM),
        ),
    )(block_range, queries, keyval, keyval, own_docs.reshape(rows, 1), doc_ids.reshape(1, -1))


def solution(mesh):
    in_specs = (
        P("seq", None),
        P(("seq", "vis"), None),
        P(("seq", "vis")),
        P(("seq", "vis")),
        P(),
        P(),
        P(None, "vis"),
        P("vis"),
        P(None, "vis"),
        P(None, "vis"),
        P("vis"),
    )
    out_specs = P("seq", "vis")
    return jax.shard_map(
        on_device, mesh=mesh, in_specs=in_specs, out_specs=out_specs, check_vma=False
    )
```

```python
import jax
import jax.numpy as jnp
from jax import lax
from jax.sharding import PartitionSpec as P
from jax.experimental import pallas as pl
from jax.experimental.pallas import tpu as pltpu

HEAD_DIM = 128


epsilon = 1e-06
negative = -1e30


def frame_slots(frames, tile_pos, frame_count, shard_rows, owners, capacity):
    row_count = frames.shape[0]
    row_ids = jnp.arange(row_count, dtype=jnp.int32)
    usable = row_ids < frame_count[0]
    owner = jnp.where(usable, tile_pos // shard_rows, owners)
    hits = (owner[:, None] == jnp.arange(owners, dtype=jnp.int32)[None, :]).astype(jnp.int32)
    earlier = (row_ids[:, None] > row_ids[None, :]).astype(jnp.int32)
    before = jnp.dot(earlier, hits, preferred_element_type=jnp.int32)
    rank = jnp.sum(before * hits, axis=1)
    slot_index = owner * capacity + rank
    slot_ids = jnp.arange(owners * capacity, dtype=jnp.int32)
    match = usable[:, None] & (slot_index[:, None] == slot_ids[None, :])
    filled = jnp.any(match, axis=0)
    local = tile_pos - owner * shard_rows
    slot_local = jnp.sum(jnp.where(match, local[:, None], 0), axis=0)
    slot_local = jnp.where(filled, slot_local, -1)
    slot_rows = jnp.dot(
        match.T.astype(frames.dtype), frames, preferred_element_type=jnp.float32
    ).astype(frames.dtype)
    place_col = jnp.broadcast_to(slot_local[:, None], (slot_local.shape[0], 128)).astype(frames.dtype)
    payload = jnp.concatenate([slot_rows, place_col], axis=1)
    return payload.reshape(owners, capacity, payload.shape[1])


def place_frames(text, incoming, incoming_place):
    lookup = incoming_place[None, :] == jnp.arange(text.shape[0], dtype=jnp.int32)[:, None]
    covered = jnp.any(lookup, axis=1)
    placed = jnp.dot(
        lookup.astype(incoming.dtype), incoming, preferred_element_type=jnp.float32
    ).astype(text.dtype)
    return jnp.where(covered[:, None], placed, text)


def exchange_kernel(payload_ref, out_ref, send_a, recv_a, send_b, recv_b, local_sem):
    seq_count = lax.axis_size("seq")
    vis_count = lax.axis_size("vis")
    me_seq = lax.axis_index("seq")
    me_vis = lax.axis_index("vis")
    barrier = pltpu.get_barrier_semaphore()
    for k in range(1, seq_count):
        pl.semaphore_signal(
            barrier, inc=1, device_id=(lax.rem(me_seq + k, seq_count), me_vis),
            device_id_type=pl.DeviceIdType.MESH,
        )
    for k in range(1, vis_count):
        pl.semaphore_signal(
            barrier, inc=1, device_id=(me_seq, lax.rem(me_vis + k, vis_count)),
            device_id_type=pl.DeviceIdType.MESH,
        )
    pl.semaphore_wait(barrier, seq_count + vis_count - 2)
    base = me_vis * seq_count
    local = pltpu.make_async_copy(payload_ref.at[me_seq], out_ref.at[base + me_seq], local_sem.at[0])
    local.start()
    first = []
    for k in range(1, seq_count):
        target = lax.rem(me_seq + k, seq_count)
        copy = pltpu.make_async_remote_copy(
            src_ref=payload_ref.at[target],
            dst_ref=out_ref.at[base + me_seq],
            send_sem=send_a.at[k],
            recv_sem=recv_a.at[k],
            device_id=(target, me_vis),
            device_id_type=pl.DeviceIdType.MESH,
        )
        copy.start()
        first.append(copy)
    local.wait()
    for k in range(1, seq_count):
        source = lax.rem(me_seq + seq_count - k, seq_count)
        incoming = pltpu.make_async_remote_copy(
            src_ref=payload_ref.at[source],
            dst_ref=out_ref.at[base + source],
            send_sem=send_a.at[k],
            recv_sem=recv_a.at[k],
            device_id=(source, me_vis),
            device_id_type=pl.DeviceIdType.MESH,
        )
        incoming.wait_recv()
    for copy in first:
        copy.wait_send()
    block = out_ref.at[pl.ds(base, seq_count)]
    second = []
    for k in range(1, vis_count):
        target = lax.rem(me_vis + k, vis_count)
        copy = pltpu.make_async_remote_copy(
            src_ref=block,
            dst_ref=block,
            send_sem=send_b.at[k],
            recv_sem=recv_b.at[k],
            device_id=(me_seq, target),
            device_id_type=pl.DeviceIdType.MESH,
        )
        copy.start()
        second.append(copy)
    for k in range(1, vis_count):
        source = lax.rem(me_vis + vis_count - k, vis_count)
        landing = out_ref.at[pl.ds(source * seq_count, seq_count)]
        incoming = pltpu.make_async_remote_copy(
            src_ref=landing,
            dst_ref=landing,
            send_sem=send_b.at[k],
            recv_sem=recv_b.at[k],
            device_id=(me_seq, source),
            device_id_type=pl.DeviceIdType.MESH,
        )
        incoming.wait_recv()
    for copy in second:
        copy.wait_send()


def exchange_frames(payload, vis_count):
    owners, capacity, width = payload.shape
    return pl.pallas_call(
        exchange_kernel,
        out_shape=jax.ShapeDtypeStruct((vis_count * owners, capacity, width), payload.dtype),
        in_specs=[pl.BlockSpec(memory_space=pl.ANY)],
        out_specs=pl.BlockSpec(memory_space=pl.ANY),
        scratch_shapes=[
            pltpu.SemaphoreType.DMA((owners,)),
            pltpu.SemaphoreType.DMA((owners,)),
            pltpu.SemaphoreType.DMA((vis_count,)),
            pltpu.SemaphoreType.DMA((vis_count,)),
            pltpu.SemaphoreType.DMA((1,)),
        ],
        compiler_params=pltpu.CompilerParams(collective_id=1, has_side_effects=True),
    )(payload)


def on_device(
    text, frames, tile_pos, frame_count, doc_ids, norm_gain, w_query, q_bias, w_key, w_value, v_bias
):
    seq_count = lax.axis_size("seq")
    vis_count = lax.axis_size("vis")
    shard_index = lax.axis_index("seq")
    shard_rows = text.shape[0]
    capacity = shard_rows // (seq_count * vis_count)
    first_row = shard_index * shard_rows
    payload = frame_slots(frames, tile_pos, frame_count, shard_rows, seq_count, capacity)
    gathered = exchange_frames(payload, vis_count)
    gathered = gathered.reshape(-1, gathered.shape[-1])
    width = text.shape[1]
    incoming_place = gathered[:, width].astype(jnp.int32)
    merged = place_frames(text, gathered[:, :width], incoming_place)
    widened = merged.astype(jnp.float32)
    mean_square = jnp.mean(widened * widened, axis=1, keepdims=True)
    normed = (widened * lax.rsqrt(mean_square + epsilon) * norm_gain).astype(jnp.bfloat16)
    queries = (jnp.dot(normed, w_query, preferred_element_type=jnp.float32) + q_bias).astype(
        jnp.bfloat16
    )
    key_rows = jnp.dot(normed, w_key, preferred_element_type=jnp.float32).astype(jnp.bfloat16)
    value_rows = (jnp.dot(normed, w_value, preferred_element_type=jnp.float32) + v_bias).astype(
        jnp.bfloat16
    )
    keyval = jnp.concatenate([key_rows, value_rows], axis=1)
    kv_heads = w_key.shape[1] // HEAD_DIM
    per_group = w_query.shape[1] // HEAD_DIM // kv_heads
    own_docs = lax.dynamic_slice_in_dim(doc_ids, first_row, shard_rows)
    incoming_keys = lax.all_gather(keyval, "seq", axis=0, tiled=True)
    doc_start = jnp.sum((doc_ids < own_docs[0]).astype(jnp.int32))
    last_row = first_row + shard_rows - 1
    block_range = jnp.stack([doc_start // KEY_BLOCK, last_row // KEY_BLOCK, first_row]).astype(jnp.int32)
    return flash_attention(block_range, queries, incoming_keys, own_docs, doc_ids, kv_heads)


KEY_BLOCK = 512


def flash_kernel(
    range_ref, q_ref, k_ref, v_ref, qdoc_ref, kdoc_ref, out_ref, peak_ref, total_ref, acc_ref
):
    step = pl.program_id(0)
    block = range_ref[0] + step
    rows = q_ref.shape[0]
    heads = q_ref.shape[1] // HEAD_DIM

    @pl.when(step == 0)
    def _():
        peak_ref[...] = jnp.full(peak_ref.shape, negative, jnp.float32)
        total_ref[...] = jnp.zeros(total_ref.shape, jnp.float32)
        acc_ref[...] = jnp.zeros(acc_ref.shape, jnp.float32)

    @pl.when(block <= range_ref[1])
    def _():
        key_place = block * KEY_BLOCK + lax.broadcasted_iota(jnp.int32, (1, KEY_BLOCK), 1)
        query_place = range_ref[2] + lax.broadcasted_iota(jnp.int32, (rows, 1), 0)
        allowed = (key_place <= query_place) & (kdoc_ref[...] == qdoc_ref[...])
        keys = k_ref[...]
        vals = v_ref[...]
        for h in range(heads):
            cols = slice(h * HEAD_DIM, (h + 1) * HEAD_DIM)
            scores = lax.dot_general(
                q_ref[:, cols], keys, (((1,), (1,)), ((), ())),
                preferred_element_type=jnp.float32,
            ) * HEAD_DIM ** (-0.5)
            scores = jnp.where(allowed, scores, negative)
            old_peak = peak_ref[h]
            new_peak = jnp.maximum(old_peak, jnp.max(scores, axis=1, keepdims=True))
            raised = jnp.where(allowed, jnp.exp(scores - new_peak[:, :1]), 0.0)
            factor = jnp.exp(old_peak - new_peak)
            total_ref[h] = total_ref[h] * factor + jnp.sum(raised, axis=1, keepdims=True)
            peak_ref[h] = new_peak
            product = jnp.dot(raised.astype(jnp.bfloat16), vals, preferred_element_type=jnp.float32)
            acc_ref[:, cols] = acc_ref[:, cols] * factor[:, :1] + product

    @pl.when(step == pl.num_programs(0) - 1)
    def _():
        for h in range(heads):
            cols = slice(h * HEAD_DIM, (h + 1) * HEAD_DIM)
            out_ref[:, cols] = (acc_ref[:, cols] / total_ref[h][:, :1]).astype(out_ref.dtype)


def flash_attention(block_range, queries, keyval, own_docs, doc_ids, kv_heads):
    rows, width = queries.shape
    key_rows = keyval.shape[0]
    steps = key_rows // KEY_BLOCK
    heads = width // HEAD_DIM

    def key_block(j, r):
        return (jnp.minimum(r[0] + j, r[1]), 0)

    def value_block(j, r):
        return (jnp.minimum(r[0] + j, r[1]), 1)

    def doc_block(j, r):
        return (0, jnp.minimum(r[0] + j, r[1]))

    grid_spec = pltpu.PrefetchScalarGridSpec(
        num_scalar_prefetch=1,
        grid=(steps,),
        in_specs=[
            pl.BlockSpec((rows, width), lambda j, r: (0, 0)),
            pl.BlockSpec((KEY_BLOCK, HEAD_DIM), key_block),
            pl.BlockSpec((KEY_BLOCK, HEAD_DIM), value_block),
            pl.BlockSpec((rows, 1), lambda j, r: (0, 0)),
            pl.BlockSpec((1, KEY_BLOCK), doc_block),
        ],
        out_specs=pl.BlockSpec((rows, width), lambda j, r: (0, 0)),
        scratch_shapes=[
            pltpu.VMEM((heads, rows, 1), jnp.float32),
            pltpu.VMEM((heads, rows, 1), jnp.float32),
            pltpu.VMEM((rows, width), jnp.float32),
        ],
    )
    flops = 4 * rows * width * key_rows // 2
    return pl.pallas_call(
        flash_kernel,
        out_shape=jax.ShapeDtypeStruct((rows, width), jnp.bfloat16),
        grid_spec=grid_spec,
        compiler_params=pltpu.CompilerParams(dimension_semantics=("arbitrary",)),
        cost_estimate=pl.CostEstimate(
            flops=flops, transcendentals=rows * heads * key_rows // 2,
            bytes_accessed=2 * (2 * rows * width + key_rows * 2 * HEAD_DIM),
        ),
    )(block_range, queries, keyval, keyval, own_docs.reshape(rows, 1), doc_ids.reshape(1, -1))


def solution(mesh):
    in_specs = (
        P("seq", None),
        P(("seq", "vis"), None),
        P(("seq", "vis")),
        P(("seq", "vis")),
        P(),
        P(),
        P(None, "vis"),
        P("vis"),
        P(None, "vis"),
        P(None, "vis"),
        P("vis"),
    )
    out_specs = P("seq", "vis")
    return jax.shard_map(
        on_device, mesh=mesh, in_specs=in_specs, out_specs=out_specs, check_vma=False
    )
```

```python
import jax
import jax.numpy as jnp
from jax import lax
from jax.sharding import PartitionSpec as P
from jax.experimental import pallas as pl
from jax.experimental.pallas import tpu as pltpu

HEAD_DIM = 128


epsilon = 1e-06
negative = -1e30


def frame_slots(frames, tile_pos, frame_count, shard_rows, owners, capacity):
    row_count = frames.shape[0]
    row_ids = jnp.arange(row_count, dtype=jnp.int32)
    usable = row_ids < frame_count[0]
    owner = jnp.where(usable, tile_pos // shard_rows, owners)
    hits = (owner[:, None] == jnp.arange(owners, dtype=jnp.int32)[None, :]).astype(jnp.int32)
    earlier = (row_ids[:, None] > row_ids[None, :]).astype(jnp.int32)
    before = jnp.dot(earlier, hits, preferred_element_type=jnp.int32)
    rank = jnp.sum(before * hits, axis=1)
    slot_index = owner * capacity + rank
    slot_ids = jnp.arange(owners * capacity, dtype=jnp.int32)
    match = usable[:, None] & (slot_index[:, None] == slot_ids[None, :])
    filled = jnp.any(match, axis=0)
    local = tile_pos - owner * shard_rows
    slot_local = jnp.sum(jnp.where(match, local[:, None], 0), axis=0)
    slot_local = jnp.where(filled, slot_local, -1)
    slot_rows = jnp.dot(
        match.T.astype(frames.dtype), frames, preferred_element_type=jnp.float32
    ).astype(frames.dtype)
    place_col = jnp.broadcast_to(slot_local[:, None], (slot_local.shape[0], 128)).astype(frames.dtype)
    payload = jnp.concatenate([slot_rows, place_col], axis=1)
    return payload.reshape(owners, capacity, payload.shape[1])


def place_frames(text, incoming, incoming_place):
    lookup = incoming_place[None, :] == jnp.arange(text.shape[0], dtype=jnp.int32)[:, None]
    covered = jnp.any(lookup, axis=1)
    placed = jnp.dot(
        lookup.astype(incoming.dtype), incoming, preferred_element_type=jnp.float32
    ).astype(text.dtype)
    return jnp.where(covered[:, None], placed, text)


def exchange_kernel(payload_ref, out_ref, send_a, recv_a, send_b, recv_b, local_sem):
    seq_count = lax.axis_size("seq")
    vis_count = lax.axis_size("vis")
    ring = vis_count // 2
    me_seq = lax.axis_index("seq")
    me_vis = lax.axis_index("vis")
    ring_pos = lax.rem(me_vis, ring)
    ring_id = me_vis // ring

    def vis_of(ring_index, position):
        return ring_index * ring + lax.rem(position + ring, ring)

    right = vis_of(ring_id, ring_pos + 1)
    left = vis_of(ring_id, ring_pos - 1)
    partner = vis_of(1 - ring_id, ring_pos)
    barrier = pltpu.get_barrier_semaphore()
    for k in range(1, seq_count):
        pl.semaphore_signal(
            barrier, inc=1, device_id=(lax.rem(me_seq + k, seq_count), me_vis),
            device_id_type=pl.DeviceIdType.MESH,
        )
    for peer in (left, right, partner):
        pl.semaphore_signal(
            barrier, inc=1, device_id=(me_seq, peer), device_id_type=pl.DeviceIdType.MESH
        )
    pl.semaphore_wait(barrier, seq_count + 2)
    base = me_vis * seq_count
    local = pltpu.make_async_copy(payload_ref.at[me_seq], out_ref.at[base + me_seq], local_sem.at[0])
    local.start()
    first = []
    for k in range(1, seq_count):
        target = lax.rem(me_seq + k, seq_count)
        copy = pltpu.make_async_remote_copy(
            src_ref=payload_ref.at[target],
            dst_ref=out_ref.at[base + me_seq],
            send_sem=send_a.at[k],
            recv_sem=recv_a.at[k],
            device_id=(target, me_vis),
            device_id_type=pl.DeviceIdType.MESH,
        )
        copy.start()
        first.append(copy)
    local.wait()
    for k in range(1, seq_count):
        source = lax.rem(me_seq + seq_count - k, seq_count)
        incoming = pltpu.make_async_remote_copy(
            src_ref=payload_ref.at[source],
            dst_ref=out_ref.at[base + source],
            send_sem=send_a.at[k],
            recv_sem=recv_a.at[k],
            device_id=(source, me_vis),
            device_id_type=pl.DeviceIdType.MESH,
        )
        incoming.wait_recv()
    for copy in first:
        copy.wait_send()

    half = seq_count // 2

    def region(owner, part):
        if part == 0:
            return out_ref.at[pl.ds(owner * seq_count, seq_count)]
        start = owner * seq_count + (part - 1) * half
        return out_ref.at[pl.ds(start, half)]

    def link(owner, part, peer, index):
        piece = region(owner, part)
        return pltpu.make_async_remote_copy(
            src_ref=piece,
            dst_ref=piece,
            send_sem=send_b.at[index],
            recv_sem=recv_b.at[index],
            device_id=(me_seq, peer),
            device_id_type=pl.DeviceIdType.MESH,
        )

    far = vis_of(ring_id, ring_pos + 2)
    left_partner = vis_of(1 - ring_id, ring_pos - 1)
    right_partner = vis_of(1 - ring_id, ring_pos + 1)
    far_partner = vis_of(1 - ring_id, ring_pos + 2)
    sent = []

    def send(owner, part, peer, index):
        copy = link(owner, part, peer, index)
        copy.start()
        sent.append(copy)

    send(me_vis, 0, right, 1)
    send(me_vis, 0, left, 2)
    send(me_vis, 0, partner, 3)
    link(partner, 0, partner, 3).wait_recv()
    send(partner, 0, right, 4)
    send(partner, 0, left, 5)
    link(left, 0, left, 1).wait_recv()
    send(left, 1, right, 6)
    link(right, 0, right, 2).wait_recv()
    send(right, 2, left, 7)
    link(left_partner, 0, left, 4).wait_recv()
    send(left_partner, 1, right, 8)
    link(right_partner, 0, right, 5).wait_recv()
    send(right_partner, 2, left, 9)
    link(far, 1, left, 6).wait_recv()
    link(far, 2, right, 7).wait_recv()
    link(far_partner, 1, left, 8).wait_recv()
    link(far_partner, 2, right, 9).wait_recv()
    for copy in sent:
        copy.wait_send()


def exchange_frames(payload, vis_count):
    owners, capacity, width = payload.shape
    return pl.pallas_call(
        exchange_kernel,
        out_shape=jax.ShapeDtypeStruct((vis_count * owners, capacity, width), payload.dtype),
        in_specs=[pl.BlockSpec(memory_space=pl.ANY)],
        out_specs=pl.BlockSpec(memory_space=pl.ANY),
        scratch_shapes=[
            pltpu.SemaphoreType.DMA((owners,)),
            pltpu.SemaphoreType.DMA((owners,)),
            pltpu.SemaphoreType.DMA((10,)),
            pltpu.SemaphoreType.DMA((10,)),
            pltpu.SemaphoreType.DMA((1,)),
        ],
        compiler_params=pltpu.CompilerParams(collective_id=1, has_side_effects=True),
    )(payload)


def on_device(
    text, frames, tile_pos, frame_count, doc_ids, norm_gain, w_query, q_bias, w_key, w_value, v_bias
):
    seq_count = lax.axis_size("seq")
    vis_count = lax.axis_size("vis")
    shard_index = lax.axis_index("seq")
    shard_rows = text.shape[0]
    capacity = shard_rows // (seq_count * vis_count)
    first_row = shard_index * shard_rows
    payload = frame_slots(frames, tile_pos, frame_count, shard_rows, seq_count, capacity)
    gathered = exchange_frames(payload, vis_count)
    gathered = gathered.reshape(-1, gathered.shape[-1])
    width = text.shape[1]
    incoming_place = gathered[:, width].astype(jnp.int32)
    merged = place_frames(text, gathered[:, :width], incoming_place)
    widened = merged.astype(jnp.float32)
    mean_square = jnp.mean(widened * widened, axis=1, keepdims=True)
    normed = (widened * lax.rsqrt(mean_square + epsilon) * norm_gain).astype(jnp.bfloat16)
    queries = (jnp.dot(normed, w_query, preferred_element_type=jnp.float32) + q_bias).astype(
        jnp.bfloat16
    )
    key_rows = jnp.dot(normed, w_key, preferred_element_type=jnp.float32).astype(jnp.bfloat16)
    value_rows = (jnp.dot(normed, w_value, preferred_element_type=jnp.float32) + v_bias).astype(
        jnp.bfloat16
    )
    keyval = jnp.concatenate([key_rows, value_rows], axis=1)
    kv_heads = w_key.shape[1] // HEAD_DIM
    per_group = w_query.shape[1] // HEAD_DIM // kv_heads
    own_docs = lax.dynamic_slice_in_dim(doc_ids, first_row, shard_rows)
    incoming_keys = lax.all_gather(keyval, "seq", axis=0, tiled=True)
    doc_start = jnp.sum((doc_ids < own_docs[0]).astype(jnp.int32))
    last_row = first_row + shard_rows - 1
    block_range = jnp.stack([doc_start // KEY_BLOCK, last_row // KEY_BLOCK, first_row]).astype(jnp.int32)
    return flash_attention(block_range, queries, incoming_keys, own_docs, doc_ids, kv_heads)


KEY_BLOCK = 512


def flash_kernel(
    range_ref, q_ref, k_ref, v_ref, qdoc_ref, kdoc_ref, out_ref, peak_ref, total_ref, acc_ref
):
    step = pl.program_id(0)
    block = range_ref[0] + step
    rows = q_ref.shape[0]
    heads = q_ref.shape[1] // HEAD_DIM

    @pl.when(step == 0)
    def _():
        peak_ref[...] = jnp.full(peak_ref.shape, negative, jnp.float32)
        total_ref[...] = jnp.zeros(total_ref.shape, jnp.float32)
        acc_ref[...] = jnp.zeros(acc_ref.shape, jnp.float32)

    @pl.when(block <= range_ref[1])
    def _():
        key_place = block * KEY_BLOCK + lax.broadcasted_iota(jnp.int32, (1, KEY_BLOCK), 1)
        query_place = range_ref[2] + lax.broadcasted_iota(jnp.int32, (rows, 1), 0)
        allowed = (key_place <= query_place) & (kdoc_ref[...] == qdoc_ref[...])
        keys = k_ref[...]
        vals = v_ref[...]
        for h in range(heads):
            cols = slice(h * HEAD_DIM, (h + 1) * HEAD_DIM)
            scores = lax.dot_general(
                q_ref[:, cols], keys, (((1,), (1,)), ((), ())),
                preferred_element_type=jnp.float32,
            ) * HEAD_DIM ** (-0.5)
            scores = jnp.where(allowed, scores, negative)
            old_peak = peak_ref[h]
            new_peak = jnp.maximum(old_peak, jnp.max(scores, axis=1, keepdims=True))
            raised = jnp.where(allowed, jnp.exp(scores - new_peak[:, :1]), 0.0)
            factor = jnp.exp(old_peak - new_peak)
            total_ref[h] = total_ref[h] * factor + jnp.sum(raised, axis=1, keepdims=True)
            peak_ref[h] = new_peak
            product = jnp.dot(raised.astype(jnp.bfloat16), vals, preferred_element_type=jnp.float32)
            acc_ref[:, cols] = acc_ref[:, cols] * factor[:, :1] + product

    @pl.when(step == pl.num_programs(0) - 1)
    def _():
        for h in range(heads):
            cols = slice(h * HEAD_DIM, (h + 1) * HEAD_DIM)
            out_ref[:, cols] = (acc_ref[:, cols] / total_ref[h][:, :1]).astype(out_ref.dtype)


def flash_attention(block_range, queries, keyval, own_docs, doc_ids, kv_heads):
    rows, width = queries.shape
    key_rows = keyval.shape[0]
    steps = key_rows // KEY_BLOCK
    heads = width // HEAD_DIM

    def key_block(j, r):
        return (jnp.minimum(r[0] + j, r[1]), 0)

    def value_block(j, r):
        return (jnp.minimum(r[0] + j, r[1]), 1)

    def doc_block(j, r):
        return (0, jnp.minimum(r[0] + j, r[1]))

    grid_spec = pltpu.PrefetchScalarGridSpec(
        num_scalar_prefetch=1,
        grid=(steps,),
        in_specs=[
            pl.BlockSpec((rows, width), lambda j, r: (0, 0)),
            pl.BlockSpec((KEY_BLOCK, HEAD_DIM), key_block),
            pl.BlockSpec((KEY_BLOCK, HEAD_DIM), value_block),
            pl.BlockSpec((rows, 1), lambda j, r: (0, 0)),
            pl.BlockSpec((1, KEY_BLOCK), doc_block),
        ],
        out_specs=pl.BlockSpec((rows, width), lambda j, r: (0, 0)),
        scratch_shapes=[
            pltpu.VMEM((heads, rows, 1), jnp.float32),
            pltpu.VMEM((heads, rows, 1), jnp.float32),
            pltpu.VMEM((rows, width), jnp.float32),
        ],
    )
    flops = 4 * rows * width * key_rows // 2
    return pl.pallas_call(
        flash_kernel,
        out_shape=jax.ShapeDtypeStruct((rows, width), jnp.bfloat16),
        grid_spec=grid_spec,
        compiler_params=pltpu.CompilerParams(dimension_semantics=("arbitrary",)),
        cost_estimate=pl.CostEstimate(
            flops=flops, transcendentals=rows * heads * key_rows // 2,
            bytes_accessed=2 * (2 * rows * width + key_rows * 2 * HEAD_DIM),
        ),
    )(block_range, queries, keyval, keyval, own_docs.reshape(rows, 1), doc_ids.reshape(1, -1))


def solution(mesh):
    in_specs = (
        P("seq", None),
        P(("seq", "vis"), None),
        P(("seq", "vis")),
        P(("seq", "vis")),
        P(),
        P(),
        P(None, "vis"),
        P("vis"),
        P(None, "vis"),
        P(None, "vis"),
        P("vis"),
    )
    out_specs = P("seq", "vis")
    return jax.shard_map(
        on_device, mesh=mesh, in_specs=in_specs, out_specs=out_specs, check_vma=False
    )
```

```python
import jax
import jax.numpy as jnp
from jax import lax
from jax.sharding import PartitionSpec as P
from jax.experimental import pallas as pl
from jax.experimental.pallas import tpu as pltpu

HEAD_DIM = 128


epsilon = 1e-06
negative = -1e30


def frame_slots(frames, tile_pos, frame_count, shard_rows, owners, capacity):
    row_count = frames.shape[0]
    row_ids = jnp.arange(row_count, dtype=jnp.int32)
    usable = row_ids < frame_count[0]
    owner = jnp.where(usable, tile_pos // shard_rows, owners)
    hits = (owner[:, None] == jnp.arange(owners, dtype=jnp.int32)[None, :]).astype(jnp.int32)
    earlier = (row_ids[:, None] > row_ids[None, :]).astype(jnp.int32)
    before = jnp.dot(earlier, hits, preferred_element_type=jnp.int32)
    rank = jnp.sum(before * hits, axis=1)
    slot_index = owner * capacity + rank
    slot_ids = jnp.arange(owners * capacity, dtype=jnp.int32)
    match = usable[:, None] & (slot_index[:, None] == slot_ids[None, :])
    filled = jnp.any(match, axis=0)
    local = tile_pos - owner * shard_rows
    slot_local = jnp.sum(jnp.where(match, local[:, None], 0), axis=0)
    slot_local = jnp.where(filled, slot_local, -1)
    slot_rows = jnp.dot(
        match.T.astype(frames.dtype), frames, preferred_element_type=jnp.float32
    ).astype(frames.dtype)
    place_col = jnp.broadcast_to(slot_local[:, None], (slot_local.shape[0], 128)).astype(frames.dtype)
    payload = jnp.concatenate([slot_rows, place_col], axis=1)
    return payload.reshape(owners, capacity, payload.shape[1])


def place_frames(text, incoming, incoming_place, width):
    lookup = incoming_place[None] == jnp.arange(text.shape[0], dtype=jnp.int32)[:, None, None]
    covered = jnp.any(lookup, axis=(1, 2))
    placed = lax.dot_general(
        lookup.astype(incoming.dtype), incoming, (((1, 2), (0, 1)), ((), ())),
        preferred_element_type=jnp.float32,
    )[:, :width].astype(text.dtype)
    return jnp.where(covered[:, None], placed, text)


def exchange_kernel(payload_ref, out_ref, send_a, recv_a, send_b, recv_b, local_sem):
    seq_count = lax.axis_size("seq")
    vis_count = lax.axis_size("vis")
    ring = vis_count // 2
    me_seq = lax.axis_index("seq")
    me_vis = lax.axis_index("vis")
    ring_pos = lax.rem(me_vis, ring)
    ring_id = me_vis // ring

    def vis_of(ring_index, position):
        return ring_index * ring + lax.rem(position + ring, ring)

    right = vis_of(ring_id, ring_pos + 1)
    left = vis_of(ring_id, ring_pos - 1)
    partner = vis_of(1 - ring_id, ring_pos)
    barrier = pltpu.get_barrier_semaphore()
    for k in range(1, seq_count):
        pl.semaphore_signal(
            barrier, inc=1, device_id=(lax.rem(me_seq + k, seq_count), me_vis),
            device_id_type=pl.DeviceIdType.MESH,
        )
    for peer in (left, right, partner):
        pl.semaphore_signal(
            barrier, inc=1, device_id=(me_seq, peer), device_id_type=pl.DeviceIdType.MESH
        )
    pl.semaphore_wait(barrier, seq_count + 2)
    base = me_vis * seq_count
    local = pltpu.make_async_copy(payload_ref.at[me_seq], out_ref.at[base + me_seq], local_sem.at[0])
    local.start()
    first = []
    for k in range(1, seq_count):
        target = lax.rem(me_seq + k, seq_count)
        copy = pltpu.make_async_remote_copy(
            src_ref=payload_ref.at[target],
            dst_ref=out_ref.at[base + me_seq],
            send_sem=send_a.at[k],
            recv_sem=recv_a.at[k],
            device_id=(target, me_vis),
            device_id_type=pl.DeviceIdType.MESH,
        )
        copy.start()
        first.append(copy)
    local.wait()
    for k in range(1, seq_count):
        source = lax.rem(me_seq + seq_count - k, seq_count)
        incoming = pltpu.make_async_remote_copy(
            src_ref=payload_ref.at[source],
            dst_ref=out_ref.at[base + source],
            send_sem=send_a.at[k],
            recv_sem=recv_a.at[k],
            device_id=(source, me_vis),
            device_id_type=pl.DeviceIdType.MESH,
        )
        incoming.wait_recv()
    for copy in first:
        copy.wait_send()

    half = seq_count // 2

    def region(owner, part):
        if part == 0:
            return out_ref.at[pl.ds(owner * seq_count, seq_count)]
        start = owner * seq_count + (part - 1) * half
        return out_ref.at[pl.ds(start, half)]

    def link(owner, part, peer, index):
        piece = region(owner, part)
        return pltpu.make_async_remote_copy(
            src_ref=piece,
            dst_ref=piece,
            send_sem=send_b.at[index],
            recv_sem=recv_b.at[index],
            device_id=(me_seq, peer),
            device_id_type=pl.DeviceIdType.MESH,
        )

    far = vis_of(ring_id, ring_pos + 2)
    left_partner = vis_of(1 - ring_id, ring_pos - 1)
    right_partner = vis_of(1 - ring_id, ring_pos + 1)
    far_partner = vis_of(1 - ring_id, ring_pos + 2)
    sent = []

    def send(owner, part, peer, index):
        copy = link(owner, part, peer, index)
        copy.start()
        sent.append(copy)

    send(me_vis, 0, right, 1)
    send(me_vis, 0, left, 2)
    send(me_vis, 0, partner, 3)
    link(partner, 0, partner, 3).wait_recv()
    send(partner, 0, right, 4)
    send(partner, 0, left, 5)
    link(left, 0, left, 1).wait_recv()
    send(left, 1, right, 6)
    link(right, 0, right, 2).wait_recv()
    send(right, 2, left, 7)
    link(left_partner, 0, left, 4).wait_recv()
    send(left_partner, 1, right, 8)
    link(right_partner, 0, right, 5).wait_recv()
    send(right_partner, 2, left, 9)
    link(far, 1, left, 6).wait_recv()
    link(far, 2, right, 7).wait_recv()
    link(far_partner, 1, left, 8).wait_recv()
    link(far_partner, 2, right, 9).wait_recv()
    for copy in sent:
        copy.wait_send()


def exchange_frames(payload, vis_count):
    owners, capacity, width = payload.shape
    return pl.pallas_call(
        exchange_kernel,
        out_shape=jax.ShapeDtypeStruct((vis_count * owners, capacity, width), payload.dtype),
        in_specs=[pl.BlockSpec(memory_space=pl.ANY)],
        out_specs=pl.BlockSpec(memory_space=pl.ANY),
        scratch_shapes=[
            pltpu.SemaphoreType.DMA((owners,)),
            pltpu.SemaphoreType.DMA((owners,)),
            pltpu.SemaphoreType.DMA((10,)),
            pltpu.SemaphoreType.DMA((10,)),
            pltpu.SemaphoreType.DMA((1,)),
        ],
        compiler_params=pltpu.CompilerParams(collective_id=1, has_side_effects=True),
    )(payload)


def on_device(
    text, frames, tile_pos, frame_count, doc_ids, norm_gain, w_query, q_bias, w_key, w_value, v_bias
):
    seq_count = lax.axis_size("seq")
    vis_count = lax.axis_size("vis")
    shard_index = lax.axis_index("seq")
    shard_rows = text.shape[0]
    capacity = shard_rows // (seq_count * vis_count)
    first_row = shard_index * shard_rows
    payload = frame_slots(frames, tile_pos, frame_count, shard_rows, seq_count, capacity)
    gathered = exchange_frames(payload, vis_count)
    width = text.shape[1]
    incoming_place = gathered[:, :, width].astype(jnp.int32)
    merged = place_frames(text, gathered, incoming_place, width)
    widened = merged.astype(jnp.float32)
    mean_square = jnp.mean(widened * widened, axis=1, keepdims=True)
    normed = (widened * lax.rsqrt(mean_square + epsilon) * norm_gain).astype(jnp.bfloat16)
    queries = (jnp.dot(normed, w_query, preferred_element_type=jnp.float32) + q_bias).astype(
        jnp.bfloat16
    )
    key_rows = jnp.dot(normed, w_key, preferred_element_type=jnp.float32).astype(jnp.bfloat16)
    value_rows = (jnp.dot(normed, w_value, preferred_element_type=jnp.float32) + v_bias).astype(
        jnp.bfloat16
    )
    keyval = jnp.concatenate([key_rows, value_rows], axis=1)
    kv_heads = w_key.shape[1] // HEAD_DIM
    per_group = w_query.shape[1] // HEAD_DIM // kv_heads
    own_docs = lax.dynamic_slice_in_dim(doc_ids, first_row, shard_rows)
    incoming_keys = lax.all_gather(keyval, "seq", axis=0, tiled=True)
    doc_start = jnp.sum((doc_ids < own_docs[0]).astype(jnp.int32))
    last_row = first_row + shard_rows - 1
    block_range = jnp.stack([doc_start // KEY_BLOCK, last_row // KEY_BLOCK, first_row]).astype(jnp.int32)
    return flash_attention(block_range, queries, incoming_keys, own_docs, doc_ids, kv_heads)


KEY_BLOCK = 512


def flash_kernel(
    range_ref, q_ref, k_ref, v_ref, qdoc_ref, kdoc_ref, out_ref, peak_ref, total_ref, acc_ref
):
    step = pl.program_id(0)
    block = range_ref[0] + step
    rows = q_ref.shape[0]
    heads = q_ref.shape[1] // HEAD_DIM

    @pl.when(step == 0)
    def _():
        peak_ref[...] = jnp.full(peak_ref.shape, negative, jnp.float32)
        total_ref[...] = jnp.zeros(total_ref.shape, jnp.float32)
        acc_ref[...] = jnp.zeros(acc_ref.shape, jnp.float32)

    @pl.when(block <= range_ref[1])
    def _():
        key_place = block * KEY_BLOCK + lax.broadcasted_iota(jnp.int32, (1, KEY_BLOCK), 1)
        query_place = range_ref[2] + lax.broadcasted_iota(jnp.int32, (rows, 1), 0)
        allowed = (key_place <= query_place) & (kdoc_ref[...] == qdoc_ref[...])
        keys = k_ref[...]
        vals = v_ref[...]
        for h in range(heads):
            cols = slice(h * HEAD_DIM, (h + 1) * HEAD_DIM)
            scores = lax.dot_general(
                q_ref[:, cols], keys, (((1,), (1,)), ((), ())),
                preferred_element_type=jnp.float32,
            ) * HEAD_DIM ** (-0.5)
            scores = jnp.where(allowed, scores, negative)
            old_peak = peak_ref[h]
            new_peak = jnp.maximum(old_peak, jnp.max(scores, axis=1, keepdims=True))
            raised = jnp.where(allowed, jnp.exp(scores - new_peak[:, :1]), 0.0)
            factor = jnp.exp(old_peak - new_peak)
            total_ref[h] = total_ref[h] * factor + jnp.sum(raised, axis=1, keepdims=True)
            peak_ref[h] = new_peak
            product = jnp.dot(raised.astype(jnp.bfloat16), vals, preferred_element_type=jnp.float32)
            acc_ref[:, cols] = acc_ref[:, cols] * factor[:, :1] + product

    @pl.when(step == pl.num_programs(0) - 1)
    def _():
        for h in range(heads):
            cols = slice(h * HEAD_DIM, (h + 1) * HEAD_DIM)
            out_ref[:, cols] = (acc_ref[:, cols] / total_ref[h][:, :1]).astype(out_ref.dtype)


def flash_attention(block_range, queries, keyval, own_docs, doc_ids, kv_heads):
    rows, width = queries.shape
    key_rows = keyval.shape[0]
    steps = key_rows // KEY_BLOCK
    heads = width // HEAD_DIM

    def key_block(j, r):
        return (jnp.minimum(r[0] + j, r[1]), 0)

    def value_block(j, r):
        return (jnp.minimum(r[0] + j, r[1]), 1)

    def doc_block(j, r):
        return (0, jnp.minimum(r[0] + j, r[1]))

    grid_spec = pltpu.PrefetchScalarGridSpec(
        num_scalar_prefetch=1,
        grid=(steps,),
        in_specs=[
            pl.BlockSpec((rows, width), lambda j, r: (0, 0)),
            pl.BlockSpec((KEY_BLOCK, HEAD_DIM), key_block),
            pl.BlockSpec((KEY_BLOCK, HEAD_DIM), value_block),
            pl.BlockSpec((rows, 1), lambda j, r: (0, 0)),
            pl.BlockSpec((1, KEY_BLOCK), doc_block),
        ],
        out_specs=pl.BlockSpec((rows, width), lambda j, r: (0, 0)),
        scratch_shapes=[
            pltpu.VMEM((heads, rows, 1), jnp.float32),
            pltpu.VMEM((heads, rows, 1), jnp.float32),
            pltpu.VMEM((rows, width), jnp.float32),
        ],
    )
    flops = 4 * rows * width * key_rows // 2
    return pl.pallas_call(
        flash_kernel,
        out_shape=jax.ShapeDtypeStruct((rows, width), jnp.bfloat16),
        grid_spec=grid_spec,
        compiler_params=pltpu.CompilerParams(dimension_semantics=("arbitrary",)),
        cost_estimate=pl.CostEstimate(
            flops=flops, transcendentals=rows * heads * key_rows // 2,
            bytes_accessed=2 * (2 * rows * width + key_rows * 2 * HEAD_DIM),
        ),
    )(block_range, queries, keyval, keyval, own_docs.reshape(rows, 1), doc_ids.reshape(1, -1))


def solution(mesh):
    in_specs = (
        P("seq", None),
        P(("seq", "vis"), None),
        P(("seq", "vis")),
        P(("seq", "vis")),
        P(),
        P(),
        P(None, "vis"),
        P("vis"),
        P(None, "vis"),
        P(None, "vis"),
        P("vis"),
    )
    out_specs = P("seq", "vis")
    return jax.shard_map(
        on_device, mesh=mesh, in_specs=in_specs, out_specs=out_specs, check_vma=False
    )
```

```python
import jax
import jax.numpy as jnp
from jax import lax
from jax.sharding import PartitionSpec as P
from jax.experimental import pallas as pl
from jax.experimental.pallas import tpu as pltpu

HEAD_DIM = 128


epsilon = 1e-06
negative = -1e30


def frame_slots(frames, tile_pos, frame_count, shard_rows, owners, capacity):
    row_count = frames.shape[0]
    row_ids = jnp.arange(row_count, dtype=jnp.int32)
    usable = row_ids < frame_count[0]
    owner = jnp.where(usable, tile_pos // shard_rows, owners)
    hits = (owner[:, None] == jnp.arange(owners, dtype=jnp.int32)[None, :]).astype(jnp.int32)
    earlier = (row_ids[:, None] > row_ids[None, :]).astype(jnp.int32)
    before = jnp.dot(earlier, hits, preferred_element_type=jnp.int32)
    rank = jnp.sum(before * hits, axis=1)
    slot_index = owner * capacity + rank
    slot_ids = jnp.arange(owners * capacity, dtype=jnp.int32)
    match = usable[:, None] & (slot_index[:, None] == slot_ids[None, :])
    filled = jnp.any(match, axis=0)
    local = tile_pos - owner * shard_rows
    slot_local = jnp.sum(jnp.where(match, local[:, None], 0), axis=0)
    slot_local = jnp.where(filled, slot_local, -1)
    slot_rows = jnp.dot(
        match.T.astype(frames.dtype), frames, preferred_element_type=jnp.float32
    ).astype(frames.dtype)
    place_col = jnp.broadcast_to(slot_local[:, None], (slot_local.shape[0], 128)).astype(frames.dtype)
    payload = jnp.concatenate([slot_rows, place_col], axis=1)
    return payload.reshape(owners, capacity, payload.shape[1])


def place_frames(text, incoming, incoming_place, width):
    lookup = incoming_place[None] == jnp.arange(text.shape[0], dtype=jnp.int32)[:, None, None]
    covered = jnp.any(lookup, axis=(1, 2))
    placed = lax.dot_general(
        lookup.astype(incoming.dtype), incoming, (((1, 2), (0, 1)), ((), ())),
        preferred_element_type=jnp.float32,
    )[:, :width].astype(text.dtype)
    return jnp.where(covered[:, None], placed, text)


def exchange_kernel(payload_ref, out_ref, send_a, recv_a, send_b, recv_b, local_sem):
    seq_count = lax.axis_size("seq")
    vis_count = lax.axis_size("vis")
    ring = vis_count // 2
    me_seq = lax.axis_index("seq")
    me_vis = lax.axis_index("vis")
    ring_pos = lax.rem(me_vis, ring)
    ring_id = me_vis // ring

    def vis_of(ring_index, position):
        return ring_index * ring + lax.rem(position + ring, ring)

    right = vis_of(ring_id, ring_pos + 1)
    left = vis_of(ring_id, ring_pos - 1)
    partner = vis_of(1 - ring_id, ring_pos)
    barrier = pltpu.get_barrier_semaphore()
    for k in range(1, seq_count):
        pl.semaphore_signal(
            barrier, inc=1, device_id=(lax.rem(me_seq + k, seq_count), me_vis),
            device_id_type=pl.DeviceIdType.MESH,
        )
    for peer in (left, right, partner):
        pl.semaphore_signal(
            barrier, inc=1, device_id=(me_seq, peer), device_id_type=pl.DeviceIdType.MESH
        )
    pl.semaphore_wait(barrier, seq_count + 2)
    base = me_vis * seq_count
    local = pltpu.make_async_copy(payload_ref.at[me_seq], out_ref.at[base + me_seq], local_sem.at[0])
    local.start()
    first = []
    for k in range(1, seq_count):
        target = lax.rem(me_seq + k, seq_count)
        copy = pltpu.make_async_remote_copy(
            src_ref=payload_ref.at[target],
            dst_ref=out_ref.at[base + me_seq],
            send_sem=send_a.at[k],
            recv_sem=recv_a.at[k],
            device_id=(target, me_vis),
            device_id_type=pl.DeviceIdType.MESH,
        )
        copy.start()
        first.append(copy)
    local.wait()
    for k in range(1, seq_count):
        source = lax.rem(me_seq + seq_count - k, seq_count)
        incoming = pltpu.make_async_remote_copy(
            src_ref=payload_ref.at[source],
            dst_ref=out_ref.at[base + source],
            send_sem=send_a.at[k],
            recv_sem=recv_a.at[k],
            device_id=(source, me_vis),
            device_id_type=pl.DeviceIdType.MESH,
        )
        incoming.wait_recv()
    for copy in first:
        copy.wait_send()

    half = seq_count // 2

    def region(owner, part):
        if part == 0:
            return out_ref.at[pl.ds(owner * seq_count, seq_count)]
        start = owner * seq_count + (part - 1) * half
        return out_ref.at[pl.ds(start, half)]

    def link(owner, part, peer, index):
        piece = region(owner, part)
        return pltpu.make_async_remote_copy(
            src_ref=piece,
            dst_ref=piece,
            send_sem=send_b.at[index],
            recv_sem=recv_b.at[index],
            device_id=(me_seq, peer),
            device_id_type=pl.DeviceIdType.MESH,
        )

    far = vis_of(ring_id, ring_pos + 2)
    left_partner = vis_of(1 - ring_id, ring_pos - 1)
    right_partner = vis_of(1 - ring_id, ring_pos + 1)
    far_partner = vis_of(1 - ring_id, ring_pos + 2)
    sent = []

    def send(owner, part, peer, index):
        copy = link(owner, part, peer, index)
        copy.start()
        sent.append(copy)

    send(me_vis, 0, right, 1)
    send(me_vis, 0, left, 2)
    send(me_vis, 0, partner, 3)
    link(partner, 0, partner, 3).wait_recv()
    send(partner, 0, right, 4)
    send(partner, 0, left, 5)
    link(left, 0, left, 1).wait_recv()
    send(left, 1, right, 6)
    link(right, 0, right, 2).wait_recv()
    send(right, 2, left, 7)
    link(left_partner, 0, left, 4).wait_recv()
    send(left_partner, 1, right, 8)
    link(right_partner, 0, right, 5).wait_recv()
    send(right_partner, 2, left, 9)
    link(far, 1, left, 6).wait_recv()
    link(far, 2, right, 7).wait_recv()
    link(far_partner, 1, left, 8).wait_recv()
    link(far_partner, 2, right, 9).wait_recv()
    for copy in sent:
        copy.wait_send()


def exchange_frames(payload, vis_count):
    owners, capacity, width = payload.shape
    return pl.pallas_call(
        exchange_kernel,
        out_shape=jax.ShapeDtypeStruct((vis_count * owners, capacity, width), payload.dtype),
        in_specs=[pl.BlockSpec(memory_space=pl.ANY)],
        out_specs=pl.BlockSpec(memory_space=pl.ANY),
        scratch_shapes=[
            pltpu.SemaphoreType.DMA((owners,)),
            pltpu.SemaphoreType.DMA((owners,)),
            pltpu.SemaphoreType.DMA((10,)),
            pltpu.SemaphoreType.DMA((10,)),
            pltpu.SemaphoreType.DMA((1,)),
        ],
        compiler_params=pltpu.CompilerParams(collective_id=1, has_side_effects=True),
    )(payload)


def on_device(
    text, frames, tile_pos, frame_count, doc_ids, norm_gain, w_query, q_bias, w_key, w_value, v_bias
):
    seq_count = lax.axis_size("seq")
    vis_count = lax.axis_size("vis")
    shard_index = lax.axis_index("seq")
    shard_rows = text.shape[0]
    capacity = shard_rows // (seq_count * vis_count)
    first_row = shard_index * shard_rows
    payload = frame_slots(frames, tile_pos, frame_count, shard_rows, seq_count, capacity)
    gathered = exchange_frames(payload, vis_count)
    width = text.shape[1]
    incoming_place = gathered[:, :, width].astype(jnp.int32)
    merged = place_frames(text, gathered, incoming_place, width)
    widened = merged.astype(jnp.float32)
    mean_square = jnp.mean(widened * widened, axis=1, keepdims=True)
    normed = (widened * lax.rsqrt(mean_square + epsilon) * norm_gain).astype(jnp.bfloat16)
    normed = lax.optimization_barrier(normed)
    queries = (jnp.dot(normed, w_query, preferred_element_type=jnp.float32) + q_bias).astype(
        jnp.bfloat16
    )
    key_rows = jnp.dot(normed, w_key, preferred_element_type=jnp.float32).astype(jnp.bfloat16)
    value_rows = (jnp.dot(normed, w_value, preferred_element_type=jnp.float32) + v_bias).astype(
        jnp.bfloat16
    )
    keyval = jnp.concatenate([key_rows, value_rows], axis=1)
    kv_heads = w_key.shape[1] // HEAD_DIM
    per_group = w_query.shape[1] // HEAD_DIM // kv_heads
    own_docs = lax.dynamic_slice_in_dim(doc_ids, first_row, shard_rows)
    incoming_keys = lax.all_gather(keyval, "seq", axis=0, tiled=True)
    doc_start = jnp.sum((doc_ids < own_docs[0]).astype(jnp.int32))
    last_row = first_row + shard_rows - 1
    block_range = jnp.stack([doc_start // KEY_BLOCK, last_row // KEY_BLOCK, first_row]).astype(jnp.int32)
    return flash_attention(block_range, queries, incoming_keys, own_docs, doc_ids, kv_heads)


KEY_BLOCK = 512


def flash_kernel(
    range_ref, q_ref, k_ref, v_ref, qdoc_ref, kdoc_ref, out_ref, peak_ref, total_ref, acc_ref
):
    step = pl.program_id(0)
    block = range_ref[0] + step
    rows = q_ref.shape[0]
    heads = q_ref.shape[1] // HEAD_DIM

    @pl.when(step == 0)
    def _():
        peak_ref[...] = jnp.full(peak_ref.shape, negative, jnp.float32)
        total_ref[...] = jnp.zeros(total_ref.shape, jnp.float32)
        acc_ref[...] = jnp.zeros(acc_ref.shape, jnp.float32)

    @pl.when(block <= range_ref[1])
    def _():
        key_place = block * KEY_BLOCK + lax.broadcasted_iota(jnp.int32, (1, KEY_BLOCK), 1)
        query_place = range_ref[2] + lax.broadcasted_iota(jnp.int32, (rows, 1), 0)
        allowed = (key_place <= query_place) & (kdoc_ref[...] == qdoc_ref[...])
        keys = k_ref[...]
        vals = v_ref[...]
        for h in range(heads):
            cols = slice(h * HEAD_DIM, (h + 1) * HEAD_DIM)
            scores = lax.dot_general(
                q_ref[:, cols], keys, (((1,), (1,)), ((), ())),
                preferred_element_type=jnp.float32,
            ) * HEAD_DIM ** (-0.5)
            scores = jnp.where(allowed, scores, negative)
            old_peak = peak_ref[h]
            new_peak = jnp.maximum(old_peak, jnp.max(scores, axis=1, keepdims=True))
            raised = jnp.where(allowed, jnp.exp(scores - new_peak[:, :1]), 0.0)
            factor = jnp.exp(old_peak - new_peak)
            total_ref[h] = total_ref[h] * factor + jnp.sum(raised, axis=1, keepdims=True)
            peak_ref[h] = new_peak
            product = jnp.dot(raised.astype(jnp.bfloat16), vals, preferred_element_type=jnp.float32)
            acc_ref[:, cols] = acc_ref[:, cols] * factor[:, :1] + product

    @pl.when(step == pl.num_programs(0) - 1)
    def _():
        for h in range(heads):
            cols = slice(h * HEAD_DIM, (h + 1) * HEAD_DIM)
            out_ref[:, cols] = (acc_ref[:, cols] / total_ref[h][:, :1]).astype(out_ref.dtype)


def flash_attention(block_range, queries, keyval, own_docs, doc_ids, kv_heads):
    rows, width = queries.shape
    key_rows = keyval.shape[0]
    steps = key_rows // KEY_BLOCK
    heads = width // HEAD_DIM

    def key_block(j, r):
        return (jnp.minimum(r[0] + j, r[1]), 0)

    def value_block(j, r):
        return (jnp.minimum(r[0] + j, r[1]), 1)

    def doc_block(j, r):
        return (0, jnp.minimum(r[0] + j, r[1]))

    grid_spec = pltpu.PrefetchScalarGridSpec(
        num_scalar_prefetch=1,
        grid=(steps,),
        in_specs=[
            pl.BlockSpec((rows, width), lambda j, r: (0, 0)),
            pl.BlockSpec((KEY_BLOCK, HEAD_DIM), key_block),
            pl.BlockSpec((KEY_BLOCK, HEAD_DIM), value_block),
            pl.BlockSpec((rows, 1), lambda j, r: (0, 0)),
            pl.BlockSpec((1, KEY_BLOCK), doc_block),
        ],
        out_specs=pl.BlockSpec((rows, width), lambda j, r: (0, 0)),
        scratch_shapes=[
            pltpu.VMEM((heads, rows, 1), jnp.float32),
            pltpu.VMEM((heads, rows, 1), jnp.float32),
            pltpu.VMEM((rows, width), jnp.float32),
        ],
    )
    flops = 4 * rows * width * key_rows // 2
    return pl.pallas_call(
        flash_kernel,
        out_shape=jax.ShapeDtypeStruct((rows, width), jnp.bfloat16),
        grid_spec=grid_spec,
        compiler_params=pltpu.CompilerParams(dimension_semantics=("arbitrary",)),
        cost_estimate=pl.CostEstimate(
            flops=flops, transcendentals=rows * heads * key_rows // 2,
            bytes_accessed=2 * (2 * rows * width + key_rows * 2 * HEAD_DIM),
        ),
    )(block_range, queries, keyval, keyval, own_docs.reshape(rows, 1), doc_ids.reshape(1, -1))


def solution(mesh):
    in_specs = (
        P("seq", None),
        P(("seq", "vis"), None),
        P(("seq", "vis")),
        P(("seq", "vis")),
        P(),
        P(),
        P(None, "vis"),
        P("vis"),
        P(None, "vis"),
        P(None, "vis"),
        P("vis"),
    )
    out_specs = P("seq", "vis")
    return jax.shard_map(
        on_device, mesh=mesh, in_specs=in_specs, out_specs=out_specs, check_vma=False
    )
```

```python
import jax
import jax.numpy as jnp
from jax import lax
from jax.sharding import PartitionSpec as P
from jax.experimental import pallas as pl
from jax.experimental.pallas import tpu as pltpu

HEAD_DIM = 128


epsilon = 1e-06
negative = -1e30


def frame_slots(frames, tile_pos, frame_count, shard_rows, owners, capacity):
    row_count = frames.shape[0]
    row_ids = jnp.arange(row_count, dtype=jnp.int32)
    usable = row_ids < frame_count[0]
    owner = jnp.where(usable, tile_pos // shard_rows, owners)
    hits = (owner[:, None] == jnp.arange(owners, dtype=jnp.int32)[None, :]).astype(jnp.int32)
    earlier = (row_ids[:, None] > row_ids[None, :]).astype(jnp.int32)
    before = jnp.dot(earlier, hits, preferred_element_type=jnp.int32)
    rank = jnp.sum(before * hits, axis=1)
    slot_index = owner * capacity + rank
    slot_ids = jnp.arange(owners * capacity, dtype=jnp.int32)
    match = usable[:, None] & (slot_index[:, None] == slot_ids[None, :])
    filled = jnp.any(match, axis=0)
    local = tile_pos - owner * shard_rows
    slot_local = jnp.sum(jnp.where(match, local[:, None], 0), axis=0)
    slot_local = jnp.where(filled, slot_local, -1)
    slot_rows = jnp.dot(
        match.T.astype(frames.dtype), frames, preferred_element_type=jnp.float32
    ).astype(frames.dtype)
    place_col = jnp.broadcast_to(slot_local[:, None], (slot_local.shape[0], 128)).astype(frames.dtype)
    payload = jnp.concatenate([slot_rows, place_col], axis=1)
    return payload.reshape(owners, capacity, payload.shape[1])


def place_frames(text, incoming, incoming_place, width):
    lookup = incoming_place[None] == jnp.arange(text.shape[0], dtype=jnp.int32)[:, None, None]
    covered = jnp.any(lookup, axis=(1, 2))
    placed = lax.dot_general(
        lookup.astype(incoming.dtype), incoming, (((1, 2), (0, 1)), ((), ())),
        preferred_element_type=jnp.float32,
    )[:, :width].astype(text.dtype)
    return jnp.where(covered[:, None], placed, text)


def exchange_kernel(payload_ref, out_ref, send_a, recv_a, send_b, recv_b, local_sem):
    seq_count = lax.axis_size("seq")
    vis_count = lax.axis_size("vis")
    ring = vis_count // 2
    me_seq = lax.axis_index("seq")
    me_vis = lax.axis_index("vis")
    ring_pos = lax.rem(me_vis, ring)
    ring_id = me_vis // ring

    def vis_of(ring_index, position):
        return ring_index * ring + lax.rem(position + ring, ring)

    right = vis_of(ring_id, ring_pos + 1)
    left = vis_of(ring_id, ring_pos - 1)
    partner = vis_of(1 - ring_id, ring_pos)
    barrier = pltpu.get_barrier_semaphore()
    for k in range(1, seq_count):
        pl.semaphore_signal(
            barrier, inc=1, device_id=(lax.rem(me_seq + k, seq_count), me_vis),
            device_id_type=pl.DeviceIdType.MESH,
        )
    for peer in (left, right, partner):
        pl.semaphore_signal(
            barrier, inc=1, device_id=(me_seq, peer), device_id_type=pl.DeviceIdType.MESH
        )
    pl.semaphore_wait(barrier, seq_count + 2)
    base = me_vis * seq_count
    local = pltpu.make_async_copy(payload_ref.at[me_seq], out_ref.at[base + me_seq], local_sem.at[0])
    local.start()
    first = []
    for k in range(1, seq_count):
        target = lax.rem(me_seq + k, seq_count)
        copy = pltpu.make_async_remote_copy(
            src_ref=payload_ref.at[target],
            dst_ref=out_ref.at[base + me_seq],
            send_sem=send_a.at[k],
            recv_sem=recv_a.at[k],
            device_id=(target, me_vis),
            device_id_type=pl.DeviceIdType.MESH,
        )
        copy.start()
        first.append(copy)
    local.wait()
    for k in range(1, seq_count):
        source = lax.rem(me_seq + seq_count - k, seq_count)
        incoming = pltpu.make_async_remote_copy(
            src_ref=payload_ref.at[source],
            dst_ref=out_ref.at[base + source],
            send_sem=send_a.at[k],
            recv_sem=recv_a.at[k],
            device_id=(source, me_vis),
            device_id_type=pl.DeviceIdType.MESH,
        )
        incoming.wait_recv()
    for copy in first:
        copy.wait_send()

    half = seq_count // 2

    def region(owner, part):
        if part == 0:
            return out_ref.at[pl.ds(owner * seq_count, seq_count)]
        start = owner * seq_count + (part - 1) * half
        return out_ref.at[pl.ds(start, half)]

    def link(owner, part, peer, index):
        piece = region(owner, part)
        return pltpu.make_async_remote_copy(
            src_ref=piece,
            dst_ref=piece,
            send_sem=send_b.at[index],
            recv_sem=recv_b.at[index],
            device_id=(me_seq, peer),
            device_id_type=pl.DeviceIdType.MESH,
        )

    far = vis_of(ring_id, ring_pos + 2)
    left_partner = vis_of(1 - ring_id, ring_pos - 1)
    right_partner = vis_of(1 - ring_id, ring_pos + 1)
    far_partner = vis_of(1 - ring_id, ring_pos + 2)
    sent = []

    def send(owner, part, peer, index):
        copy = link(owner, part, peer, index)
        copy.start()
        sent.append(copy)

    send(me_vis, 0, right, 1)
    send(me_vis, 0, left, 2)
    send(me_vis, 0, partner, 3)
    link(partner, 0, partner, 3).wait_recv()
    send(partner, 0, right, 4)
    send(partner, 0, left, 5)
    link(left, 0, left, 1).wait_recv()
    send(left, 1, right, 6)
    link(right, 0, right, 2).wait_recv()
    send(right, 2, left, 7)
    link(left_partner, 0, left, 4).wait_recv()
    send(left_partner, 1, right, 8)
    link(right_partner, 0, right, 5).wait_recv()
    send(right_partner, 2, left, 9)
    link(far, 1, left, 6).wait_recv()
    link(far, 2, right, 7).wait_recv()
    link(far_partner, 1, left, 8).wait_recv()
    link(far_partner, 2, right, 9).wait_recv()
    for copy in sent:
        copy.wait_send()


def exchange_frames(payload, vis_count):
    owners, capacity, width = payload.shape
    return pl.pallas_call(
        exchange_kernel,
        out_shape=jax.ShapeDtypeStruct((vis_count * owners, capacity, width), payload.dtype),
        in_specs=[pl.BlockSpec(memory_space=pl.ANY)],
        out_specs=pl.BlockSpec(memory_space=pl.ANY),
        scratch_shapes=[
            pltpu.SemaphoreType.DMA((owners,)),
            pltpu.SemaphoreType.DMA((owners,)),
            pltpu.SemaphoreType.DMA((10,)),
            pltpu.SemaphoreType.DMA((10,)),
            pltpu.SemaphoreType.DMA((1,)),
        ],
        compiler_params=pltpu.CompilerParams(collective_id=1, has_side_effects=True),
    )(payload)


def on_device(
    text, frames, tile_pos, frame_count, doc_ids, norm_gain, w_query, q_bias, w_key, w_value, v_bias
):
    seq_count = lax.axis_size("seq")
    vis_count = lax.axis_size("vis")
    shard_index = lax.axis_index("seq")
    shard_rows = text.shape[0]
    capacity = shard_rows // (seq_count * vis_count)
    first_row = shard_index * shard_rows
    payload = frame_slots(frames, tile_pos, frame_count, shard_rows, seq_count, capacity)
    gathered = exchange_frames(payload, vis_count)
    width = text.shape[1]
    incoming_place = gathered[:, :, width].astype(jnp.int32)
    merged = place_frames(text, gathered, incoming_place, width)
    widened = merged.astype(jnp.float32)
    mean_square = jnp.mean(widened * widened, axis=1, keepdims=True)
    normed = (widened * lax.rsqrt(mean_square + epsilon) * norm_gain).astype(jnp.bfloat16)
    queries = (jnp.dot(normed, w_query, preferred_element_type=jnp.float32) + q_bias).astype(
        jnp.bfloat16
    )
    key_rows = jnp.dot(normed, w_key, preferred_element_type=jnp.float32).astype(jnp.bfloat16)
    value_rows = (jnp.dot(normed, w_value, preferred_element_type=jnp.float32) + v_bias).astype(
        jnp.bfloat16
    )
    keyval = jnp.concatenate([key_rows, value_rows], axis=1)
    kv_heads = w_key.shape[1] // HEAD_DIM
    per_group = w_query.shape[1] // HEAD_DIM // kv_heads
    own_docs = lax.dynamic_slice_in_dim(doc_ids, first_row, shard_rows)
    incoming_keys = lax.all_gather(keyval, "seq", axis=0, tiled=True)
    doc_start = jnp.sum((doc_ids < own_docs[0]).astype(jnp.int32))
    last_row = first_row + shard_rows - 1
    block_range = jnp.stack([doc_start // KEY_BLOCK, last_row // KEY_BLOCK, first_row]).astype(jnp.int32)
    return flash_attention(block_range, queries, incoming_keys, own_docs, doc_ids, kv_heads)


KEY_BLOCK = 256


def flash_kernel(
    range_ref, q_ref, k_ref, v_ref, qdoc_ref, kdoc_ref, out_ref, peak_ref, total_ref, acc_ref
):
    step = pl.program_id(0)
    block = range_ref[0] + step
    rows = q_ref.shape[0]
    heads = q_ref.shape[1] // HEAD_DIM

    @pl.when(step == 0)
    def _():
        peak_ref[...] = jnp.full(peak_ref.shape, negative, jnp.float32)
        total_ref[...] = jnp.zeros(total_ref.shape, jnp.float32)
        acc_ref[...] = jnp.zeros(acc_ref.shape, jnp.float32)

    @pl.when(block <= range_ref[1])
    def _():
        key_place = block * KEY_BLOCK + lax.broadcasted_iota(jnp.int32, (1, KEY_BLOCK), 1)
        query_place = range_ref[2] + lax.broadcasted_iota(jnp.int32, (rows, 1), 0)
        allowed = (key_place <= query_place) & (kdoc_ref[...] == qdoc_ref[...])
        keys = k_ref[...]
        vals = v_ref[...]
        for h in range(heads):
            cols = slice(h * HEAD_DIM, (h + 1) * HEAD_DIM)
            scores = lax.dot_general(
                q_ref[:, cols], keys, (((1,), (1,)), ((), ())),
                preferred_element_type=jnp.float32,
            ) * HEAD_DIM ** (-0.5)
            scores = jnp.where(allowed, scores, negative)
            old_peak = peak_ref[h]
            new_peak = jnp.maximum(old_peak, jnp.max(scores, axis=1, keepdims=True))
            raised = jnp.where(allowed, jnp.exp(scores - new_peak[:, :1]), 0.0)
            factor = jnp.exp(old_peak - new_peak)
            total_ref[h] = total_ref[h] * factor + jnp.sum(raised, axis=1, keepdims=True)
            peak_ref[h] = new_peak
            product = jnp.dot(raised.astype(jnp.bfloat16), vals, preferred_element_type=jnp.float32)
            acc_ref[:, cols] = acc_ref[:, cols] * factor[:, :1] + product

    @pl.when(step == pl.num_programs(0) - 1)
    def _():
        for h in range(heads):
            cols = slice(h * HEAD_DIM, (h + 1) * HEAD_DIM)
            out_ref[:, cols] = (acc_ref[:, cols] / total_ref[h][:, :1]).astype(out_ref.dtype)


def flash_attention(block_range, queries, keyval, own_docs, doc_ids, kv_heads):
    rows, width = queries.shape
    key_rows = keyval.shape[0]
    steps = key_rows // KEY_BLOCK
    heads = width // HEAD_DIM

    def key_block(j, r):
        return (jnp.minimum(r[0] + j, r[1]), 0)

    def value_block(j, r):
        return (jnp.minimum(r[0] + j, r[1]), 1)

    def doc_block(j, r):
        return (0, jnp.minimum(r[0] + j, r[1]))

    grid_spec = pltpu.PrefetchScalarGridSpec(
        num_scalar_prefetch=1,
        grid=(steps,),
        in_specs=[
            pl.BlockSpec((rows, width), lambda j, r: (0, 0)),
            pl.BlockSpec((KEY_BLOCK, HEAD_DIM), key_block),
            pl.BlockSpec((KEY_BLOCK, HEAD_DIM), value_block),
            pl.BlockSpec((rows, 1), lambda j, r: (0, 0)),
            pl.BlockSpec((1, KEY_BLOCK), doc_block),
        ],
        out_specs=pl.BlockSpec((rows, width), lambda j, r: (0, 0)),
        scratch_shapes=[
            pltpu.VMEM((heads, rows, 1), jnp.float32),
            pltpu.VMEM((heads, rows, 1), jnp.float32),
            pltpu.VMEM((rows, width), jnp.float32),
        ],
    )
    flops = 4 * rows * width * key_rows // 2
    return pl.pallas_call(
        flash_kernel,
        out_shape=jax.ShapeDtypeStruct((rows, width), jnp.bfloat16),
        grid_spec=grid_spec,
        compiler_params=pltpu.CompilerParams(dimension_semantics=("arbitrary",)),
        cost_estimate=pl.CostEstimate(
            flops=flops, transcendentals=rows * heads * key_rows // 2,
            bytes_accessed=2 * (2 * rows * width + key_rows * 2 * HEAD_DIM),
        ),
    )(block_range, queries, keyval, keyval, own_docs.reshape(rows, 1), doc_ids.reshape(1, -1))


def solution(mesh):
    in_specs = (
        P("seq", None),
        P(("seq", "vis"), None),
        P(("seq", "vis")),
        P(("seq", "vis")),
        P(),
        P(),
        P(None, "vis"),
        P("vis"),
        P(None, "vis"),
        P(None, "vis"),
        P("vis"),
    )
    out_specs = P("seq", "vis")
    return jax.shard_map(
        on_device, mesh=mesh, in_specs=in_specs, out_specs=out_specs, check_vma=False
    )
```

```python
import jax
import jax.numpy as jnp
from jax import lax
from jax.sharding import PartitionSpec as P
from jax.experimental import pallas as pl
from jax.experimental.pallas import tpu as pltpu

HEAD_DIM = 128


epsilon = 1e-06
negative = -1e30


def frame_slots(frames, tile_pos, frame_count, shard_rows, owners, capacity):
    row_count = frames.shape[0]
    row_ids = jnp.arange(row_count, dtype=jnp.int32)
    usable = row_ids < frame_count[0]
    owner = jnp.where(usable, tile_pos // shard_rows, owners)
    hits = (owner[:, None] == jnp.arange(owners, dtype=jnp.int32)[None, :]).astype(jnp.int32)
    earlier = (row_ids[:, None] > row_ids[None, :]).astype(jnp.int32)
    before = jnp.dot(earlier, hits, preferred_element_type=jnp.int32)
    rank = jnp.sum(before * hits, axis=1)
    slot_index = owner * capacity + rank
    slot_ids = jnp.arange(owners * capacity, dtype=jnp.int32)
    match = usable[:, None] & (slot_index[:, None] == slot_ids[None, :])
    filled = jnp.any(match, axis=0)
    local = tile_pos - owner * shard_rows
    slot_local = jnp.sum(jnp.where(match, local[:, None], 0), axis=0)
    slot_local = jnp.where(filled, slot_local, -1)
    slot_rows = jnp.dot(
        match.T.astype(frames.dtype), frames, preferred_element_type=jnp.float32
    ).astype(frames.dtype)
    place_col = jnp.broadcast_to(slot_local[:, None], (slot_local.shape[0], 128)).astype(frames.dtype)
    payload = jnp.concatenate([slot_rows, place_col], axis=1)
    return payload.reshape(owners, capacity, payload.shape[1])


def place_frames(text, incoming, incoming_place, width):
    lookup = incoming_place[None] == jnp.arange(text.shape[0], dtype=jnp.int32)[:, None, None]
    covered = jnp.any(lookup, axis=(1, 2))
    placed = lax.dot_general(
        lookup.astype(incoming.dtype), incoming, (((1, 2), (0, 1)), ((), ())),
        preferred_element_type=jnp.float32,
    )[:, :width].astype(text.dtype)
    return jnp.where(covered[:, None], placed, text)


def exchange_kernel(payload_ref, out_ref, send_a, recv_a, send_b, recv_b, local_sem):
    seq_count = lax.axis_size("seq")
    vis_count = lax.axis_size("vis")
    ring = vis_count // 2
    me_seq = lax.axis_index("seq")
    me_vis = lax.axis_index("vis")
    ring_pos = lax.rem(me_vis, ring)
    ring_id = me_vis // ring

    def vis_of(ring_index, position):
        return ring_index * ring + lax.rem(position + ring, ring)

    right = vis_of(ring_id, ring_pos + 1)
    left = vis_of(ring_id, ring_pos - 1)
    partner = vis_of(1 - ring_id, ring_pos)
    barrier = pltpu.get_barrier_semaphore()
    for k in range(1, seq_count):
        pl.semaphore_signal(
            barrier, inc=1, device_id=(lax.rem(me_seq + k, seq_count), me_vis),
            device_id_type=pl.DeviceIdType.MESH,
        )
    for peer in (left, right, partner):
        pl.semaphore_signal(
            barrier, inc=1, device_id=(me_seq, peer), device_id_type=pl.DeviceIdType.MESH
        )
    pl.semaphore_wait(barrier, seq_count + 2)
    base = me_vis * seq_count
    local = pltpu.make_async_copy(payload_ref.at[me_seq], out_ref.at[base + me_seq], local_sem.at[0])
    local.start()
    first = []
    for k in range(1, seq_count):
        target = lax.rem(me_seq + k, seq_count)
        copy = pltpu.make_async_remote_copy(
            src_ref=payload_ref.at[target],
            dst_ref=out_ref.at[base + me_seq],
            send_sem=send_a.at[k],
            recv_sem=recv_a.at[k],
            device_id=(target, me_vis),
            device_id_type=pl.DeviceIdType.MESH,
        )
        copy.start()
        first.append(copy)
    local.wait()
    for k in range(1, seq_count):
        source = lax.rem(me_seq + seq_count - k, seq_count)
        incoming = pltpu.make_async_remote_copy(
            src_ref=payload_ref.at[source],
            dst_ref=out_ref.at[base + source],
            send_sem=send_a.at[k],
            recv_sem=recv_a.at[k],
            device_id=(source, me_vis),
            device_id_type=pl.DeviceIdType.MESH,
        )
        incoming.wait_recv()
    for copy in first:
        copy.wait_send()

    half = seq_count // 2

    def region(owner, part):
        if part == 0:
            return out_ref.at[pl.ds(owner * seq_count, seq_count)]
        start = owner * seq_count + (part - 1) * half
        return out_ref.at[pl.ds(start, half)]

    def link(owner, part, peer, index):
        piece = region(owner, part)
        return pltpu.make_async_remote_copy(
            src_ref=piece,
            dst_ref=piece,
            send_sem=send_b.at[index],
            recv_sem=recv_b.at[index],
            device_id=(me_seq, peer),
            device_id_type=pl.DeviceIdType.MESH,
        )

    far = vis_of(ring_id, ring_pos + 2)
    left_partner = vis_of(1 - ring_id, ring_pos - 1)
    right_partner = vis_of(1 - ring_id, ring_pos + 1)
    far_partner = vis_of(1 - ring_id, ring_pos + 2)
    sent = []

    def send(owner, part, peer, index):
        copy = link(owner, part, peer, index)
        copy.start()
        sent.append(copy)

    send(me_vis, 0, right, 1)
    send(me_vis, 0, left, 2)
    send(me_vis, 0, partner, 3)
    link(partner, 0, partner, 3).wait_recv()
    send(partner, 0, right, 4)
    send(partner, 0, left, 5)
    link(left, 0, left, 1).wait_recv()
    send(left, 1, right, 6)
    link(right, 0, right, 2).wait_recv()
    send(right, 2, left, 7)
    link(left_partner, 0, left, 4).wait_recv()
    send(left_partner, 1, right, 8)
    link(right_partner, 0, right, 5).wait_recv()
    send(right_partner, 2, left, 9)
    link(far, 1, left, 6).wait_recv()
    link(far, 2, right, 7).wait_recv()
    link(far_partner, 1, left, 8).wait_recv()
    link(far_partner, 2, right, 9).wait_recv()
    for copy in sent:
        copy.wait_send()


def exchange_frames(payload, vis_count):
    owners, capacity, width = payload.shape
    return pl.pallas_call(
        exchange_kernel,
        out_shape=jax.ShapeDtypeStruct((vis_count * owners, capacity, width), payload.dtype),
        in_specs=[pl.BlockSpec(memory_space=pl.ANY)],
        out_specs=pl.BlockSpec(memory_space=pl.ANY),
        scratch_shapes=[
            pltpu.SemaphoreType.DMA((owners,)),
            pltpu.SemaphoreType.DMA((owners,)),
            pltpu.SemaphoreType.DMA((10,)),
            pltpu.SemaphoreType.DMA((10,)),
            pltpu.SemaphoreType.DMA((1,)),
        ],
        compiler_params=pltpu.CompilerParams(collective_id=1, has_side_effects=True),
    )(payload)


def on_device(
    text, frames, tile_pos, frame_count, doc_ids, norm_gain, w_query, q_bias, w_key, w_value, v_bias
):
    seq_count = lax.axis_size("seq")
    vis_count = lax.axis_size("vis")
    shard_index = lax.axis_index("seq")
    shard_rows = text.shape[0]
    capacity = shard_rows // (seq_count * vis_count)
    first_row = shard_index * shard_rows
    payload = frame_slots(frames, tile_pos, frame_count, shard_rows, seq_count, capacity)
    gathered = exchange_frames(payload, vis_count)
    width = text.shape[1]
    incoming_place = gathered[:, :, width].astype(jnp.int32)
    merged = place_frames(text, gathered, incoming_place, width)
    widened = merged.astype(jnp.float32)
    mean_square = jnp.mean(widened * widened, axis=1, keepdims=True)
    normed = (widened * lax.rsqrt(mean_square + epsilon) * norm_gain).astype(jnp.bfloat16)
    queries = (jnp.dot(normed, w_query, preferred_element_type=jnp.float32) + q_bias).astype(
        jnp.bfloat16
    )
    key_rows = jnp.dot(normed, w_key, preferred_element_type=jnp.float32).astype(jnp.bfloat16)
    value_rows = (jnp.dot(normed, w_value, preferred_element_type=jnp.float32) + v_bias).astype(
        jnp.bfloat16
    )
    keyval = jnp.concatenate([key_rows, value_rows], axis=1)
    kv_heads = w_key.shape[1] // HEAD_DIM
    per_group = w_query.shape[1] // HEAD_DIM // kv_heads
    own_docs = lax.dynamic_slice_in_dim(doc_ids, first_row, shard_rows)
    incoming_keys = lax.all_gather(keyval, "seq", axis=0, tiled=True)
    doc_start = jnp.sum((doc_ids < own_docs[0]).astype(jnp.int32))
    last_row = first_row + shard_rows - 1
    block_range = jnp.stack([doc_start // KEY_BLOCK, last_row // KEY_BLOCK, first_row]).astype(jnp.int32)
    return flash_attention(block_range, queries, incoming_keys, own_docs, doc_ids, kv_heads)


KEY_BLOCK = 512


CHUNK = 32


def flash_kernel(
    range_ref, q_ref, k_ref, v_ref, qdoc_ref, kdoc_ref, out_ref,
    peak_ref, total_ref, acc_ref, score_ref, weight_ref,
):
    step = pl.program_id(0)
    block = range_ref[0] + step
    rows = q_ref.shape[0]
    heads = q_ref.shape[1] // HEAD_DIM

    @pl.when(step == 0)
    def _():
        peak_ref[...] = jnp.full(peak_ref.shape, negative, jnp.float32)
        total_ref[...] = jnp.zeros(total_ref.shape, jnp.float32)
        acc_ref[...] = jnp.zeros(acc_ref.shape, jnp.float32)

    @pl.when(block <= range_ref[1])
    def _():
        key_place = block * KEY_BLOCK + lax.broadcasted_iota(jnp.int32, (1, KEY_BLOCK), 1)
        key_docs = kdoc_ref[...]
        keys = k_ref[...]
        vals = v_ref[...]
        for h in range(heads):
            cols = slice(h * HEAD_DIM, (h + 1) * HEAD_DIM)
            score_ref[...] = lax.dot_general(
                q_ref[:, cols], keys, (((1,), (1,)), ((), ())),
                preferred_element_type=jnp.float32,
            ) * HEAD_DIM ** (-0.5)

            def chunk(c, carry, h=h, cols=cols):
                r = pl.ds(pl.multiple_of(c * CHUNK, CHUNK), CHUNK)
                query_place = (
                    range_ref[2] + c * CHUNK
                    + lax.broadcasted_iota(jnp.int32, (CHUNK, 1), 0)
                )
                allowed = (key_place <= query_place) & (key_docs == qdoc_ref[r, :])
                scores = jnp.where(allowed, score_ref[r, :], negative)
                old_peak = peak_ref[h, r, :]
                new_peak = jnp.maximum(old_peak, jnp.max(scores, axis=1, keepdims=True))
                raised = jnp.where(allowed, jnp.exp(scores - new_peak), 0.0)
                factor = jnp.exp(old_peak - new_peak)
                total_ref[h, r, :] = total_ref[h, r, :] * factor + jnp.sum(
                    raised, axis=1, keepdims=True
                )
                peak_ref[h, r, :] = new_peak
                weight_ref[r, :] = raised.astype(jnp.bfloat16)
                acc_ref[r, cols] = acc_ref[r, cols] * factor
                return carry

            lax.fori_loop(0, rows // CHUNK, chunk, 0)
            acc_ref[:, cols] = acc_ref[:, cols] + jnp.dot(
                weight_ref[...], vals, preferred_element_type=jnp.float32
            )

    @pl.when(step == pl.num_programs(0) - 1)
    def _():
        for h in range(heads):
            cols = slice(h * HEAD_DIM, (h + 1) * HEAD_DIM)
            out_ref[:, cols] = (acc_ref[:, cols] / total_ref[h]).astype(out_ref.dtype)


def flash_attention(block_range, queries, keyval, own_docs, doc_ids, kv_heads):
    rows, width = queries.shape
    key_rows = keyval.shape[0]
    steps = key_rows // KEY_BLOCK
    heads = width // HEAD_DIM

    def key_block(j, r):
        return (jnp.minimum(r[0] + j, r[1]), 0)

    def value_block(j, r):
        return (jnp.minimum(r[0] + j, r[1]), 1)

    def doc_block(j, r):
        return (0, jnp.minimum(r[0] + j, r[1]))

    grid_spec = pltpu.PrefetchScalarGridSpec(
        num_scalar_prefetch=1,
        grid=(steps,),
        in_specs=[
            pl.BlockSpec((rows, width), lambda j, r: (0, 0)),
            pl.BlockSpec((KEY_BLOCK, HEAD_DIM), key_block),
            pl.BlockSpec((KEY_BLOCK, HEAD_DIM), value_block),
            pl.BlockSpec((rows, 1), lambda j, r: (0, 0)),
            pl.BlockSpec((1, KEY_BLOCK), doc_block),
        ],
        out_specs=pl.BlockSpec((rows, width), lambda j, r: (0, 0)),
        scratch_shapes=[
            pltpu.VMEM((heads, rows, 1), jnp.float32),
            pltpu.VMEM((heads, rows, 1), jnp.float32),
            pltpu.VMEM((rows, width), jnp.float32),
            pltpu.VMEM((rows, KEY_BLOCK), jnp.float32),
            pltpu.VMEM((rows, KEY_BLOCK), jnp.bfloat16),
        ],
    )
    flops = 4 * rows * width * key_rows // 2
    return pl.pallas_call(
        flash_kernel,
        out_shape=jax.ShapeDtypeStruct((rows, width), jnp.bfloat16),
        grid_spec=grid_spec,
        compiler_params=pltpu.CompilerParams(dimension_semantics=("arbitrary",)),
        cost_estimate=pl.CostEstimate(
            flops=flops, transcendentals=rows * heads * key_rows // 2,
            bytes_accessed=2 * (2 * rows * width + key_rows * 2 * HEAD_DIM),
        ),
    )(block_range, queries, keyval, keyval, own_docs.reshape(rows, 1), doc_ids.reshape(1, -1))


def solution(mesh):
    in_specs = (
        P("seq", None),
        P(("seq", "vis"), None),
        P(("seq", "vis")),
        P(("seq", "vis")),
        P(),
        P(),
        P(None, "vis"),
        P("vis"),
        P(None, "vis"),
        P(None, "vis"),
        P("vis"),
    )
    out_specs = P("seq", "vis")
    return jax.shard_map(
        on_device, mesh=mesh, in_specs=in_specs, out_specs=out_specs, check_vma=False
    )
```

```python
import jax
import jax.numpy as jnp
from jax import lax
from jax.sharding import PartitionSpec as P
from jax.experimental import pallas as pl
from jax.experimental.pallas import tpu as pltpu

HEAD_DIM = 128


epsilon = 1e-06
negative = -1e30


def frame_slots(frames, tile_pos, frame_count, shard_rows, owners, capacity):
    row_count = frames.shape[0]
    row_ids = jnp.arange(row_count, dtype=jnp.int32)
    usable = row_ids < frame_count[0]
    owner = jnp.where(usable, tile_pos // shard_rows, owners)
    hits = (owner[:, None] == jnp.arange(owners, dtype=jnp.int32)[None, :]).astype(jnp.int32)
    earlier = (row_ids[:, None] > row_ids[None, :]).astype(jnp.int32)
    before = jnp.dot(earlier, hits, preferred_element_type=jnp.int32)
    rank = jnp.sum(before * hits, axis=1)
    slot_index = owner * capacity + rank
    slot_ids = jnp.arange(owners * capacity, dtype=jnp.int32)
    match = usable[:, None] & (slot_index[:, None] == slot_ids[None, :])
    filled = jnp.any(match, axis=0)
    local = tile_pos - owner * shard_rows
    slot_local = jnp.sum(jnp.where(match, local[:, None], 0), axis=0)
    slot_local = jnp.where(filled, slot_local, -1)
    slot_rows = jnp.dot(
        match.T.astype(frames.dtype), frames, preferred_element_type=jnp.float32
    ).astype(frames.dtype)
    place_col = jnp.broadcast_to(slot_local[:, None], (slot_local.shape[0], 128)).astype(frames.dtype)
    payload = jnp.concatenate([slot_rows, place_col], axis=1)
    return payload.reshape(owners, capacity, payload.shape[1])


def place_frames(text, incoming, incoming_place, width):
    lookup = incoming_place[None] == jnp.arange(text.shape[0], dtype=jnp.int32)[:, None, None]
    covered = jnp.any(lookup, axis=(1, 2))
    placed = lax.dot_general(
        lookup.astype(incoming.dtype), incoming, (((1, 2), (0, 1)), ((), ())),
        preferred_element_type=jnp.float32,
    )[:, :width].astype(text.dtype)
    return jnp.where(covered[:, None], placed, text)


def exchange_kernel(payload_ref, out_ref, send_a, recv_a, send_b, recv_b, local_sem):
    seq_count = lax.axis_size("seq")
    vis_count = lax.axis_size("vis")
    ring = vis_count // 2
    me_seq = lax.axis_index("seq")
    me_vis = lax.axis_index("vis")
    ring_pos = lax.rem(me_vis, ring)
    ring_id = me_vis // ring

    def vis_of(ring_index, position):
        return ring_index * ring + lax.rem(position + ring, ring)

    right = vis_of(ring_id, ring_pos + 1)
    left = vis_of(ring_id, ring_pos - 1)
    partner = vis_of(1 - ring_id, ring_pos)
    barrier = pltpu.get_barrier_semaphore()
    for k in range(1, seq_count):
        pl.semaphore_signal(
            barrier, inc=1, device_id=(lax.rem(me_seq + k, seq_count), me_vis),
            device_id_type=pl.DeviceIdType.MESH,
        )
    for peer in (left, right, partner):
        pl.semaphore_signal(
            barrier, inc=1, device_id=(me_seq, peer), device_id_type=pl.DeviceIdType.MESH
        )
    pl.semaphore_wait(barrier, seq_count + 2)
    base = me_vis * seq_count
    local = pltpu.make_async_copy(payload_ref.at[me_seq], out_ref.at[base + me_seq], local_sem.at[0])
    local.start()
    first = []
    for k in range(1, seq_count):
        target = lax.rem(me_seq + k, seq_count)
        copy = pltpu.make_async_remote_copy(
            src_ref=payload_ref.at[target],
            dst_ref=out_ref.at[base + me_seq],
            send_sem=send_a.at[k],
            recv_sem=recv_a.at[k],
            device_id=(target, me_vis),
            device_id_type=pl.DeviceIdType.MESH,
        )
        copy.start()
        first.append(copy)
    local.wait()
    for k in range(1, seq_count):
        source = lax.rem(me_seq + seq_count - k, seq_count)
        incoming = pltpu.make_async_remote_copy(
            src_ref=payload_ref.at[source],
            dst_ref=out_ref.at[base + source],
            send_sem=send_a.at[k],
            recv_sem=recv_a.at[k],
            device_id=(source, me_vis),
            device_id_type=pl.DeviceIdType.MESH,
        )
        incoming.wait_recv()
    for copy in first:
        copy.wait_send()

    half = seq_count // 2

    def region(owner, part):
        if part == 0:
            return out_ref.at[pl.ds(owner * seq_count, seq_count)]
        start = owner * seq_count + (part - 1) * half
        return out_ref.at[pl.ds(start, half)]

    def link(owner, part, peer, index):
        piece = region(owner, part)
        return pltpu.make_async_remote_copy(
            src_ref=piece,
            dst_ref=piece,
            send_sem=send_b.at[index],
            recv_sem=recv_b.at[index],
            device_id=(me_seq, peer),
            device_id_type=pl.DeviceIdType.MESH,
        )

    far = vis_of(ring_id, ring_pos + 2)
    left_partner = vis_of(1 - ring_id, ring_pos - 1)
    right_partner = vis_of(1 - ring_id, ring_pos + 1)
    far_partner = vis_of(1 - ring_id, ring_pos + 2)
    sent = []

    def send(owner, part, peer, index):
        copy = link(owner, part, peer, index)
        copy.start()
        sent.append(copy)

    send(me_vis, 0, right, 1)
    send(me_vis, 0, left, 2)
    send(me_vis, 0, partner, 3)
    link(partner, 0, partner, 3).wait_recv()
    send(partner, 0, right, 4)
    send(partner, 0, left, 5)
    link(left, 0, left, 1).wait_recv()
    send(left, 1, right, 6)
    link(right, 0, right, 2).wait_recv()
    send(right, 2, left, 7)
    link(left_partner, 0, left, 4).wait_recv()
    send(left_partner, 1, right, 8)
    link(right_partner, 0, right, 5).wait_recv()
    send(right_partner, 2, left, 9)
    link(far, 1, left, 6).wait_recv()
    link(far, 2, right, 7).wait_recv()
    link(far_partner, 1, left, 8).wait_recv()
    link(far_partner, 2, right, 9).wait_recv()
    for copy in sent:
        copy.wait_send()


def exchange_frames(payload, vis_count):
    owners, capacity, width = payload.shape
    return pl.pallas_call(
        exchange_kernel,
        out_shape=jax.ShapeDtypeStruct((vis_count * owners, capacity, width), payload.dtype),
        in_specs=[pl.BlockSpec(memory_space=pl.ANY)],
        out_specs=pl.BlockSpec(memory_space=pl.ANY),
        scratch_shapes=[
            pltpu.SemaphoreType.DMA((owners,)),
            pltpu.SemaphoreType.DMA((owners,)),
            pltpu.SemaphoreType.DMA((10,)),
            pltpu.SemaphoreType.DMA((10,)),
            pltpu.SemaphoreType.DMA((1,)),
        ],
        compiler_params=pltpu.CompilerParams(collective_id=1, has_side_effects=True),
    )(payload)


def on_device(
    text, frames, tile_pos, frame_count, doc_ids, norm_gain, w_query, q_bias, w_key, w_value, v_bias
):
    seq_count = lax.axis_size("seq")
    vis_count = lax.axis_size("vis")
    shard_index = lax.axis_index("seq")
    shard_rows = text.shape[0]
    capacity = shard_rows // (seq_count * vis_count)
    first_row = shard_index * shard_rows
    payload = frame_slots(frames, tile_pos, frame_count, shard_rows, seq_count, capacity)
    gathered = exchange_frames(payload, vis_count)
    width = text.shape[1]
    incoming_place = gathered[:, :, width].astype(jnp.int32)
    merged = place_frames(text, gathered, incoming_place, width)
    widened = merged.astype(jnp.float32)
    mean_square = jnp.mean(widened * widened, axis=1, keepdims=True)
    normed = (widened * lax.rsqrt(mean_square + epsilon) * norm_gain).astype(jnp.bfloat16)
    queries = (jnp.dot(normed, w_query, preferred_element_type=jnp.float32) + q_bias).astype(
        jnp.bfloat16
    )
    key_rows = jnp.dot(normed, w_key, preferred_element_type=jnp.float32).astype(jnp.bfloat16)
    value_rows = (jnp.dot(normed, w_value, preferred_element_type=jnp.float32) + v_bias).astype(
        jnp.bfloat16
    )
    keyval = jnp.concatenate([key_rows, value_rows], axis=1)
    kv_heads = w_key.shape[1] // HEAD_DIM
    per_group = w_query.shape[1] // HEAD_DIM // kv_heads
    own_docs = lax.dynamic_slice_in_dim(doc_ids, first_row, shard_rows)
    incoming_keys = lax.all_gather(keyval, "seq", axis=0, tiled=True)
    doc_start = jnp.sum((doc_ids < own_docs[0]).astype(jnp.int32))
    last_row = first_row + shard_rows - 1
    block_range = jnp.stack([doc_start // KEY_BLOCK, last_row // KEY_BLOCK, first_row]).astype(jnp.int32)
    return flash_attention(block_range, queries, incoming_keys, own_docs, doc_ids, kv_heads)


KEY_BLOCK = 1024


def flash_kernel(
    range_ref, q_ref, k_ref, v_ref, qdoc_ref, kdoc_ref, out_ref, peak_ref, total_ref, acc_ref
):
    step = pl.program_id(0)
    block = range_ref[0] + step
    rows = q_ref.shape[0]
    heads = q_ref.shape[1] // HEAD_DIM

    @pl.when(step == 0)
    def _():
        peak_ref[...] = jnp.full(peak_ref.shape, negative, jnp.float32)
        total_ref[...] = jnp.zeros(total_ref.shape, jnp.float32)
        acc_ref[...] = jnp.zeros(acc_ref.shape, jnp.float32)

    @pl.when(block <= range_ref[1])
    def _():
        key_place = block * KEY_BLOCK + lax.broadcasted_iota(jnp.int32, (1, KEY_BLOCK), 1)
        query_place = range_ref[2] + lax.broadcasted_iota(jnp.int32, (rows, 1), 0)
        allowed = (key_place <= query_place) & (kdoc_ref[...] == qdoc_ref[...])
        keys = k_ref[...]
        vals = v_ref[...]
        for h in range(heads):
            cols = slice(h * HEAD_DIM, (h + 1) * HEAD_DIM)
            scores = lax.dot_general(
                q_ref[:, cols], keys, (((1,), (1,)), ((), ())),
                preferred_element_type=jnp.float32,
            ) * HEAD_DIM ** (-0.5)
            scores = jnp.where(allowed, scores, negative)
            old_peak = peak_ref[h]
            new_peak = jnp.maximum(old_peak, jnp.max(scores, axis=1, keepdims=True))
            raised = jnp.where(allowed, jnp.exp(scores - new_peak[:, :1]), 0.0)
            factor = jnp.exp(old_peak - new_peak)
            total_ref[h] = total_ref[h] * factor + jnp.sum(raised, axis=1, keepdims=True)
            peak_ref[h] = new_peak
            product = jnp.dot(raised.astype(jnp.bfloat16), vals, preferred_element_type=jnp.float32)
            acc_ref[:, cols] = acc_ref[:, cols] * factor[:, :1] + product

    @pl.when(step == pl.num_programs(0) - 1)
    def _():
        for h in range(heads):
            cols = slice(h * HEAD_DIM, (h + 1) * HEAD_DIM)
            out_ref[:, cols] = (acc_ref[:, cols] / total_ref[h][:, :1]).astype(out_ref.dtype)


def flash_attention(block_range, queries, keyval, own_docs, doc_ids, kv_heads):
    rows, width = queries.shape
    key_rows = keyval.shape[0]
    steps = key_rows // KEY_BLOCK
    heads = width // HEAD_DIM

    def key_block(j, r):
        return (jnp.minimum(r[0] + j, r[1]), 0)

    def value_block(j, r):
        return (jnp.minimum(r[0] + j, r[1]), 1)

    def doc_block(j, r):
        return (0, jnp.minimum(r[0] + j, r[1]))

    grid_spec = pltpu.PrefetchScalarGridSpec(
        num_scalar_prefetch=1,
        grid=(steps,),
        in_specs=[
            pl.BlockSpec((rows, width), lambda j, r: (0, 0)),
            pl.BlockSpec((KEY_BLOCK, HEAD_DIM), key_block),
            pl.BlockSpec((KEY_BLOCK, HEAD_DIM), value_block),
            pl.BlockSpec((rows, 1), lambda j, r: (0, 0)),
            pl.BlockSpec((1, KEY_BLOCK), doc_block),
        ],
        out_specs=pl.BlockSpec((rows, width), lambda j, r: (0, 0)),
        scratch_shapes=[
            pltpu.VMEM((heads, rows, 1), jnp.float32),
            pltpu.VMEM((heads, rows, 1), jnp.float32),
            pltpu.VMEM((rows, width), jnp.float32),
        ],
    )
    flops = 4 * rows * width * key_rows // 2
    return pl.pallas_call(
        flash_kernel,
        out_shape=jax.ShapeDtypeStruct((rows, width), jnp.bfloat16),
        grid_spec=grid_spec,
        compiler_params=pltpu.CompilerParams(dimension_semantics=("arbitrary",)),
        cost_estimate=pl.CostEstimate(
            flops=flops, transcendentals=rows * heads * key_rows // 2,
            bytes_accessed=2 * (2 * rows * width + key_rows * 2 * HEAD_DIM),
        ),
    )(block_range, queries, keyval, keyval, own_docs.reshape(rows, 1), doc_ids.reshape(1, -1))


def solution(mesh):
    in_specs = (
        P("seq", None),
        P(("seq", "vis"), None),
        P(("seq", "vis")),
        P(("seq", "vis")),
        P(),
        P(),
        P(None, "vis"),
        P("vis"),
        P(None, "vis"),
        P(None, "vis"),
        P("vis"),
    )
    out_specs = P("seq", "vis")
    return jax.shard_map(
        on_device, mesh=mesh, in_specs=in_specs, out_specs=out_specs, check_vma=False
    )
```

```python
import jax
import jax.numpy as jnp
from jax import lax
from jax.sharding import PartitionSpec as P
from jax.experimental import pallas as pl
from jax.experimental.pallas import tpu as pltpu

HEAD_DIM = 128


epsilon = 1e-06
negative = -1e30


def frame_slots(frames, tile_pos, frame_count, shard_rows, owners, capacity):
    row_count = frames.shape[0]
    row_ids = jnp.arange(row_count, dtype=jnp.int32)
    usable = row_ids < frame_count[0]
    owner = jnp.where(usable, tile_pos // shard_rows, owners)
    hits = (owner[:, None] == jnp.arange(owners, dtype=jnp.int32)[None, :]).astype(jnp.int32)
    earlier = (row_ids[:, None] > row_ids[None, :]).astype(jnp.int32)
    before = jnp.dot(earlier, hits, preferred_element_type=jnp.int32)
    rank = jnp.sum(before * hits, axis=1)
    slot_index = owner * capacity + rank
    slot_ids = jnp.arange(owners * capacity, dtype=jnp.int32)
    match = usable[:, None] & (slot_index[:, None] == slot_ids[None, :])
    filled = jnp.any(match, axis=0)
    local = tile_pos - owner * shard_rows
    slot_local = jnp.sum(jnp.where(match, local[:, None], 0), axis=0)
    slot_local = jnp.where(filled, slot_local, -1)
    slot_rows = jnp.dot(
        match.T.astype(frames.dtype), frames, preferred_element_type=jnp.float32
    ).astype(frames.dtype)
    place_col = jnp.broadcast_to(slot_local[:, None], (slot_local.shape[0], 128)).astype(frames.dtype)
    payload = jnp.concatenate([slot_rows, place_col], axis=1)
    return payload.reshape(owners, capacity, payload.shape[1])


def place_frames(text, incoming, incoming_place, width):
    lookup = incoming_place[None] == jnp.arange(text.shape[0], dtype=jnp.int32)[:, None, None]
    covered = jnp.any(lookup, axis=(1, 2))
    placed = lax.dot_general(
        lookup.astype(incoming.dtype), incoming, (((1, 2), (0, 1)), ((), ())),
        preferred_element_type=jnp.float32,
    )[:, :width].astype(text.dtype)
    return jnp.where(covered[:, None], placed, text)


def exchange_kernel(payload_ref, out_ref, send_a, recv_a, send_b, recv_b, local_sem):
    seq_count = lax.axis_size("seq")
    vis_count = lax.axis_size("vis")
    ring = vis_count // 2
    me_seq = lax.axis_index("seq")
    me_vis = lax.axis_index("vis")
    ring_pos = lax.rem(me_vis, ring)
    ring_id = me_vis // ring

    def vis_of(ring_index, position):
        return ring_index * ring + lax.rem(position + ring, ring)

    right = vis_of(ring_id, ring_pos + 1)
    left = vis_of(ring_id, ring_pos - 1)
    partner = vis_of(1 - ring_id, ring_pos)
    barrier = pltpu.get_barrier_semaphore()
    for k in range(1, seq_count):
        pl.semaphore_signal(
            barrier, inc=1, device_id=(lax.rem(me_seq + k, seq_count), me_vis),
            device_id_type=pl.DeviceIdType.MESH,
        )
    for peer in (left, right, partner):
        pl.semaphore_signal(
            barrier, inc=1, device_id=(me_seq, peer), device_id_type=pl.DeviceIdType.MESH
        )
    pl.semaphore_wait(barrier, seq_count + 2)
    base = me_vis * seq_count
    local = pltpu.make_async_copy(payload_ref.at[me_seq], out_ref.at[base + me_seq], local_sem.at[0])
    local.start()
    first = []
    for k in range(1, seq_count):
        target = lax.rem(me_seq + k, seq_count)
        copy = pltpu.make_async_remote_copy(
            src_ref=payload_ref.at[target],
            dst_ref=out_ref.at[base + me_seq],
            send_sem=send_a.at[k],
            recv_sem=recv_a.at[k],
            device_id=(target, me_vis),
            device_id_type=pl.DeviceIdType.MESH,
        )
        copy.start()
        first.append(copy)
    local.wait()
    for k in range(1, seq_count):
        source = lax.rem(me_seq + seq_count - k, seq_count)
        incoming = pltpu.make_async_remote_copy(
            src_ref=payload_ref.at[source],
            dst_ref=out_ref.at[base + source],
            send_sem=send_a.at[k],
            recv_sem=recv_a.at[k],
            device_id=(source, me_vis),
            device_id_type=pl.DeviceIdType.MESH,
        )
        incoming.wait_recv()
    for copy in first:
        copy.wait_send()

    half = seq_count // 2

    def region(owner, part):
        if part == 0:
            return out_ref.at[pl.ds(owner * seq_count, seq_count)]
        start = owner * seq_count + (part - 1) * half
        return out_ref.at[pl.ds(start, half)]

    def link(owner, part, peer, index):
        piece = region(owner, part)
        return pltpu.make_async_remote_copy(
            src_ref=piece,
            dst_ref=piece,
            send_sem=send_b.at[index],
            recv_sem=recv_b.at[index],
            device_id=(me_seq, peer),
            device_id_type=pl.DeviceIdType.MESH,
        )

    far = vis_of(ring_id, ring_pos + 2)
    left_partner = vis_of(1 - ring_id, ring_pos - 1)
    right_partner = vis_of(1 - ring_id, ring_pos + 1)
    far_partner = vis_of(1 - ring_id, ring_pos + 2)
    sent = []

    def send(owner, part, peer, index):
        copy = link(owner, part, peer, index)
        copy.start()
        sent.append(copy)

    send(me_vis, 0, right, 1)
    send(me_vis, 0, left, 2)
    send(me_vis, 0, partner, 3)
    link(partner, 0, partner, 3).wait_recv()
    send(partner, 0, right, 4)
    send(partner, 0, left, 5)
    link(left, 0, left, 1).wait_recv()
    send(left, 1, right, 6)
    link(right, 0, right, 2).wait_recv()
    send(right, 2, left, 7)
    link(left_partner, 0, left, 4).wait_recv()
    send(left_partner, 1, right, 8)
    link(right_partner, 0, right, 5).wait_recv()
    send(right_partner, 2, left, 9)
    link(far, 1, left, 6).wait_recv()
    link(far, 2, right, 7).wait_recv()
    link(far_partner, 1, left, 8).wait_recv()
    link(far_partner, 2, right, 9).wait_recv()
    for copy in sent:
        copy.wait_send()


def exchange_frames(payload, vis_count):
    owners, capacity, width = payload.shape
    return pl.pallas_call(
        exchange_kernel,
        out_shape=jax.ShapeDtypeStruct((vis_count * owners, capacity, width), payload.dtype),
        in_specs=[pl.BlockSpec(memory_space=pl.ANY)],
        out_specs=pl.BlockSpec(memory_space=pl.ANY),
        scratch_shapes=[
            pltpu.SemaphoreType.DMA((owners,)),
            pltpu.SemaphoreType.DMA((owners,)),
            pltpu.SemaphoreType.DMA((10,)),
            pltpu.SemaphoreType.DMA((10,)),
            pltpu.SemaphoreType.DMA((1,)),
        ],
        compiler_params=pltpu.CompilerParams(collective_id=1, has_side_effects=True),
    )(payload)


def on_device(
    text, frames, tile_pos, frame_count, doc_ids, norm_gain, w_query, q_bias, w_key, w_value, v_bias
):
    seq_count = lax.axis_size("seq")
    vis_count = lax.axis_size("vis")
    shard_index = lax.axis_index("seq")
    shard_rows = text.shape[0]
    capacity = shard_rows // (seq_count * vis_count)
    first_row = shard_index * shard_rows
    payload = frame_slots(frames, tile_pos, frame_count, shard_rows, seq_count, capacity)
    gathered = exchange_frames(payload, vis_count)
    width = text.shape[1]
    incoming_place = gathered[:, :, width].astype(jnp.int32)
    merged = place_frames(text, gathered, incoming_place, width)
    widened = merged.astype(jnp.float32)
    mean_square = jnp.mean(widened * widened, axis=1, keepdims=True)
    normed = (widened * lax.rsqrt(mean_square + epsilon) * norm_gain).astype(jnp.bfloat16)
    queries = (jnp.dot(normed, w_query, preferred_element_type=jnp.float32) + q_bias).astype(
        jnp.bfloat16
    )
    key_rows = jnp.dot(normed, w_key, preferred_element_type=jnp.float32).astype(jnp.bfloat16)
    value_rows = (jnp.dot(normed, w_value, preferred_element_type=jnp.float32) + v_bias).astype(
        jnp.bfloat16
    )
    keyval = jnp.concatenate([key_rows, value_rows], axis=1)
    kv_heads = w_key.shape[1] // HEAD_DIM
    per_group = w_query.shape[1] // HEAD_DIM // kv_heads
    incoming_keys = lax.all_gather(keyval, "seq", axis=0, tiled=True)
    queries, doc_ids = lax.optimization_barrier((queries, doc_ids))
    own_docs = lax.dynamic_slice_in_dim(doc_ids, first_row, shard_rows)
    doc_start = jnp.sum((doc_ids < own_docs[0]).astype(jnp.int32))
    last_row = first_row + shard_rows - 1
    block_range = jnp.stack([doc_start // KEY_BLOCK, last_row // KEY_BLOCK, first_row]).astype(jnp.int32)
    return flash_attention(block_range, queries, incoming_keys, own_docs, doc_ids, kv_heads)


KEY_BLOCK = 512
DOC_SPAN = 2048


def flash_kernel(
    range_ref, q_ref, k_ref, v_ref, qdoc_ref, kdoc_ref, out_ref, peak_ref, total_ref, acc_ref
):
    step = pl.program_id(0)
    block = range_ref[0] + step
    rows = q_ref.shape[0]
    heads = q_ref.shape[1] // HEAD_DIM

    @pl.when(step == 0)
    def _():
        peak_ref[...] = jnp.full(peak_ref.shape, negative, jnp.float32)
        total_ref[...] = jnp.zeros(total_ref.shape, jnp.float32)
        acc_ref[...] = jnp.zeros(acc_ref.shape, jnp.float32)

    @pl.when(block <= range_ref[1])
    def _():
        key_place = block * KEY_BLOCK + lax.broadcasted_iota(jnp.int32, (1, KEY_BLOCK), 1)
        query_place = range_ref[2] + lax.broadcasted_iota(jnp.int32, (rows, 1), 0)
        allowed = (key_place <= query_place) & (kdoc_ref[...] == qdoc_ref[...])
        keys = k_ref[...]
        vals = v_ref[...]
        for h in range(heads):
            cols = slice(h * HEAD_DIM, (h + 1) * HEAD_DIM)
            scores = lax.dot_general(
                q_ref[:, cols], keys, (((1,), (1,)), ((), ())),
                preferred_element_type=jnp.float32,
            ) * HEAD_DIM ** (-0.5)
            scores = jnp.where(allowed, scores, negative)
            old_peak = peak_ref[h]
            new_peak = jnp.maximum(old_peak, jnp.max(scores, axis=1, keepdims=True))
            raised = jnp.where(allowed, jnp.exp(scores - new_peak[:, :1]), 0.0)
            factor = jnp.exp(old_peak - new_peak)
            total_ref[h] = total_ref[h] * factor + jnp.sum(raised, axis=1, keepdims=True)
            peak_ref[h] = new_peak
            product = jnp.dot(raised.astype(jnp.bfloat16), vals, preferred_element_type=jnp.float32)
            acc_ref[:, cols] = acc_ref[:, cols] * factor[:, :1] + product

    @pl.when(step == pl.num_programs(0) - 1)
    def _():
        for h in range(heads):
            cols = slice(h * HEAD_DIM, (h + 1) * HEAD_DIM)
            out_ref[:, cols] = (acc_ref[:, cols] / total_ref[h][:, :1]).astype(out_ref.dtype)


def flash_attention(block_range, queries, keyval, own_docs, doc_ids, kv_heads):
    rows, width = queries.shape
    key_rows = keyval.shape[0]
    steps = min(key_rows // KEY_BLOCK, (DOC_SPAN + rows - 2) // KEY_BLOCK + 2)
    heads = width // HEAD_DIM

    def key_block(j, r):
        return (jnp.minimum(r[0] + j, r[1]), 0)

    def value_block(j, r):
        return (jnp.minimum(r[0] + j, r[1]), 1)

    def doc_block(j, r):
        return (0, jnp.minimum(r[0] + j, r[1]))

    grid_spec = pltpu.PrefetchScalarGridSpec(
        num_scalar_prefetch=1,
        grid=(steps,),
        in_specs=[
            pl.BlockSpec((rows, width), lambda j, r: (0, 0)),
            pl.BlockSpec((KEY_BLOCK, HEAD_DIM), key_block),
            pl.BlockSpec((KEY_BLOCK, HEAD_DIM), value_block),
            pl.BlockSpec((rows, 1), lambda j, r: (0, 0)),
            pl.BlockSpec((1, KEY_BLOCK), doc_block),
        ],
        out_specs=pl.BlockSpec((rows, width), lambda j, r: (0, 0)),
        scratch_shapes=[
            pltpu.VMEM((heads, rows, 1), jnp.float32),
            pltpu.VMEM((heads, rows, 1), jnp.float32),
            pltpu.VMEM((rows, width), jnp.float32),
        ],
    )
    flops = 4 * rows * width * key_rows // 2
    return pl.pallas_call(
        flash_kernel,
        out_shape=jax.ShapeDtypeStruct((rows, width), jnp.bfloat16),
        grid_spec=grid_spec,
        compiler_params=pltpu.CompilerParams(dimension_semantics=("arbitrary",)),
        cost_estimate=pl.CostEstimate(
            flops=flops, transcendentals=rows * heads * key_rows // 2,
            bytes_accessed=2 * (2 * rows * width + key_rows * 2 * HEAD_DIM),
        ),
    )(block_range, queries, keyval, keyval, own_docs.reshape(rows, 1), doc_ids.reshape(1, -1))


def solution(mesh):
    in_specs = (
        P("seq", None),
        P(("seq", "vis"), None),
        P(("seq", "vis")),
        P(("seq", "vis")),
        P(),
        P(),
        P(None, "vis"),
        P("vis"),
        P(None, "vis"),
        P(None, "vis"),
        P("vis"),
    )
    out_specs = P("seq", "vis")
    return jax.shard_map(
        on_device, mesh=mesh, in_specs=in_specs, out_specs=out_specs, check_vma=False
    )
```

```python
import jax
import jax.numpy as jnp
from jax import lax
from jax.sharding import PartitionSpec as P
from jax.experimental import pallas as pl
from jax.experimental.pallas import tpu as pltpu

HEAD_DIM = 128


epsilon = 1e-06
negative = -1e30


def frame_slots(frames, tile_pos, frame_count, shard_rows, owners, capacity):
    row_count = frames.shape[0]
    row_ids = jnp.arange(row_count, dtype=jnp.int32)
    usable = row_ids < frame_count[0]
    owner = jnp.where(usable, tile_pos // shard_rows, owners)
    hits = (owner[:, None] == jnp.arange(owners, dtype=jnp.int32)[None, :]).astype(jnp.int32)
    earlier = (row_ids[:, None] > row_ids[None, :]).astype(jnp.int32)
    before = jnp.dot(earlier, hits, preferred_element_type=jnp.int32)
    rank = jnp.sum(before * hits, axis=1)
    slot_index = owner * capacity + rank
    slot_ids = jnp.arange(owners * capacity, dtype=jnp.int32)
    match = usable[:, None] & (slot_index[:, None] == slot_ids[None, :])
    filled = jnp.any(match, axis=0)
    local = tile_pos - owner * shard_rows
    slot_local = jnp.sum(jnp.where(match, local[:, None], 0), axis=0)
    slot_local = jnp.where(filled, slot_local, -1)
    slot_rows = jnp.dot(
        match.T.astype(frames.dtype), frames, preferred_element_type=jnp.float32
    ).astype(frames.dtype)
    place_col = jnp.broadcast_to(slot_local[:, None], (slot_local.shape[0], 128)).astype(frames.dtype)
    payload = jnp.concatenate([slot_rows, place_col], axis=1)
    return payload.reshape(owners, capacity, payload.shape[1])


def place_frames(text, incoming, incoming_place, width):
    lookup = incoming_place[None] == jnp.arange(text.shape[0], dtype=jnp.int32)[:, None, None]
    covered = jnp.any(lookup, axis=(1, 2))
    placed = lax.dot_general(
        lookup.astype(incoming.dtype), incoming, (((1, 2), (0, 1)), ((), ())),
        preferred_element_type=jnp.float32,
    )[:, :width].astype(text.dtype)
    return jnp.where(covered[:, None], placed, text)


def exchange_kernel(payload_ref, out_ref, send_a, recv_a, send_b, recv_b, local_sem):
    seq_count = lax.axis_size("seq")
    vis_count = lax.axis_size("vis")
    ring = vis_count // 2
    me_seq = lax.axis_index("seq")
    me_vis = lax.axis_index("vis")
    ring_pos = lax.rem(me_vis, ring)
    ring_id = me_vis // ring

    def vis_of(ring_index, position):
        return ring_index * ring + lax.rem(position + ring, ring)

    right = vis_of(ring_id, ring_pos + 1)
    left = vis_of(ring_id, ring_pos - 1)
    partner = vis_of(1 - ring_id, ring_pos)
    barrier = pltpu.get_barrier_semaphore()
    for k in range(1, seq_count):
        pl.semaphore_signal(
            barrier, inc=1, device_id=(lax.rem(me_seq + k, seq_count), me_vis),
            device_id_type=pl.DeviceIdType.MESH,
        )
    for peer in (left, right, partner):
        pl.semaphore_signal(
            barrier, inc=1, device_id=(me_seq, peer), device_id_type=pl.DeviceIdType.MESH
        )
    pl.semaphore_wait(barrier, seq_count + 2)
    base = me_vis * seq_count
    local = pltpu.make_async_copy(payload_ref.at[me_seq], out_ref.at[base + me_seq], local_sem.at[0])
    local.start()
    first = []
    for k in range(1, seq_count):
        target = lax.rem(me_seq + k, seq_count)
        copy = pltpu.make_async_remote_copy(
            src_ref=payload_ref.at[target],
            dst_ref=out_ref.at[base + me_seq],
            send_sem=send_a.at[k],
            recv_sem=recv_a.at[k],
            device_id=(target, me_vis),
            device_id_type=pl.DeviceIdType.MESH,
        )
        copy.start()
        first.append(copy)
    local.wait()
    for k in range(1, seq_count):
        source = lax.rem(me_seq + seq_count - k, seq_count)
        incoming = pltpu.make_async_remote_copy(
            src_ref=payload_ref.at[source],
            dst_ref=out_ref.at[base + source],
            send_sem=send_a.at[k],
            recv_sem=recv_a.at[k],
            device_id=(source, me_vis),
            device_id_type=pl.DeviceIdType.MESH,
        )
        incoming.wait_recv()
    for copy in first:
        copy.wait_send()

    half = seq_count // 2

    def region(owner, part):
        if part == 0:
            return out_ref.at[pl.ds(owner * seq_count, seq_count)]
        start = owner * seq_count + (part - 1) * half
        return out_ref.at[pl.ds(start, half)]

    def link(owner, part, peer, index):
        piece = region(owner, part)
        return pltpu.make_async_remote_copy(
            src_ref=piece,
            dst_ref=piece,
            send_sem=send_b.at[index],
            recv_sem=recv_b.at[index],
            device_id=(me_seq, peer),
            device_id_type=pl.DeviceIdType.MESH,
        )

    far = vis_of(ring_id, ring_pos + 2)
    left_partner = vis_of(1 - ring_id, ring_pos - 1)
    right_partner = vis_of(1 - ring_id, ring_pos + 1)
    far_partner = vis_of(1 - ring_id, ring_pos + 2)
    sent = []

    def send(owner, part, peer, index):
        copy = link(owner, part, peer, index)
        copy.start()
        sent.append(copy)

    send(me_vis, 0, right, 1)
    send(me_vis, 0, left, 2)
    send(me_vis, 0, partner, 3)
    link(partner, 0, partner, 3).wait_recv()
    send(partner, 0, right, 4)
    send(partner, 0, left, 5)
    link(left, 0, left, 1).wait_recv()
    send(left, 1, right, 6)
    link(right, 0, right, 2).wait_recv()
    send(right, 2, left, 7)
    link(left_partner, 0, left, 4).wait_recv()
    send(left_partner, 1, right, 8)
    link(right_partner, 0, right, 5).wait_recv()
    send(right_partner, 2, left, 9)
    link(far, 1, left, 6).wait_recv()
    link(far, 2, right, 7).wait_recv()
    link(far_partner, 1, left, 8).wait_recv()
    link(far_partner, 2, right, 9).wait_recv()
    for copy in sent:
        copy.wait_send()


def exchange_frames(payload, vis_count):
    owners, capacity, width = payload.shape
    return pl.pallas_call(
        exchange_kernel,
        out_shape=jax.ShapeDtypeStruct((vis_count * owners, capacity, width), payload.dtype),
        in_specs=[pl.BlockSpec(memory_space=pl.ANY)],
        out_specs=pl.BlockSpec(memory_space=pl.ANY),
        scratch_shapes=[
            pltpu.SemaphoreType.DMA((owners,)),
            pltpu.SemaphoreType.DMA((owners,)),
            pltpu.SemaphoreType.DMA((10,)),
            pltpu.SemaphoreType.DMA((10,)),
            pltpu.SemaphoreType.DMA((1,)),
        ],
        compiler_params=pltpu.CompilerParams(collective_id=1, has_side_effects=True),
    )(payload)


def gather_kernel(block_ref, out_ref, send_sem, recv_sem, local_sem):
    rows = block_ref.shape[0]
    me_seq = lax.axis_index("seq")
    me_vis = lax.axis_index("vis")
    column = me_seq // 4
    layer = lax.rem(me_seq // 2, 2)
    core = lax.rem(me_seq, 2)
    ring = lax.axis_size("seq") // 4

    def seq_of(y, z, c):
        return (lax.rem(y + ring, ring) * 2 + z) * 2 + c

    mate = seq_of(column, layer, 1 - core)
    across = seq_of(column, 1 - layer, core)
    diagonal = seq_of(column, 1 - layer, 1 - core)
    up = seq_of(column + 1, layer, core)
    down = seq_of(column - 1, layer, core)
    barrier = pltpu.get_barrier_semaphore()
    for peer in (mate, across, diagonal, up, down):
        pl.semaphore_signal(
            barrier, inc=1, device_id=(peer, me_vis), device_id_type=pl.DeviceIdType.MESH
        )
    pl.semaphore_wait(barrier, 5)

    def rows_of(start, count):
        return out_ref.at[pl.ds(pl.multiple_of(start, rows), count)]

    def link(src, dst, peer, index):
        return pltpu.make_async_remote_copy(
            src_ref=src, dst_ref=dst, send_sem=send_sem.at[index], recv_sem=recv_sem.at[index],
            device_id=(peer, me_vis), device_id_type=pl.DeviceIdType.MESH,
        )

    sent = []

    def send(src, dst, peer, index):
        copy = link(src, dst, peer, index)
        copy.start()
        sent.append(copy)

    own = rows_of(me_seq * rows, rows)
    local = pltpu.make_async_copy(block_ref, own, local_sem.at[0])
    local.start()
    send(block_ref, own, mate, 0)
    send(block_ref, own, across, 1)
    send(block_ref, own, diagonal, 2)
    local.wait()
    link(block_ref, rows_of(mate * rows, rows), mate, 0).wait_recv()
    link(block_ref, rows_of(across * rows, rows), across, 1).wait_recv()
    link(block_ref, rows_of(diagonal * rows, rows), diagonal, 2).wait_recv()

    def half(y, h):
        return rows_of((lax.rem(y + ring, ring) * 4 + h * 2) * rows, 2 * rows)

    def quarter(y, h, q):
        return rows_of((lax.rem(y + ring, ring) * 4 + h * 2 + q) * rows, rows)

    mine = half(column, core)
    send(mine, mine, up, 3)
    send(mine, mine, down, 4)
    below = half(column - 1, core)
    link(below, below, down, 3).wait_recv()
    send(below, below, mate, 7)
    piece = quarter(column - 1, core, 0)
    send(piece, piece, up, 5)
    above = half(column + 1, core)
    link(above, above, up, 4).wait_recv()
    send(above, above, mate, 9)
    piece = quarter(column + 1, core, 1)
    send(piece, piece, down, 6)
    far_low = quarter(column + 2, core, 0)
    far_high = quarter(column + 2, core, 1)
    link(far_low, far_low, down, 5).wait_recv()
    link(far_high, far_high, up, 6).wait_recv()
    far = half(column + 2, core)
    send(far, far, mate, 8)
    for offset, index in ((-1, 7), (2, 8), (1, 9)):
        theirs = half(column + offset, 1 - core)
        link(theirs, theirs, mate, index).wait_recv()
    for copy in sent:
        copy.wait_send()


def gather_keys(block, seq_count):
    rows, width = block.shape
    return pl.pallas_call(
        gather_kernel,
        out_shape=jax.ShapeDtypeStruct((seq_count * rows, width), block.dtype),
        in_specs=[pl.BlockSpec(memory_space=pl.ANY)],
        out_specs=pl.BlockSpec(memory_space=pl.ANY),
        scratch_shapes=[
            pltpu.SemaphoreType.DMA((10,)),
            pltpu.SemaphoreType.DMA((10,)),
            pltpu.SemaphoreType.DMA((1,)),
        ],
        compiler_params=pltpu.CompilerParams(collective_id=2, has_side_effects=True),
    )(block)


def on_device(
    text, frames, tile_pos, frame_count, doc_ids, norm_gain, w_query, q_bias, w_key, w_value, v_bias
):
    seq_count = lax.axis_size("seq")
    vis_count = lax.axis_size("vis")
    shard_index = lax.axis_index("seq")
    shard_rows = text.shape[0]
    capacity = shard_rows // (seq_count * vis_count)
    first_row = shard_index * shard_rows
    payload = frame_slots(frames, tile_pos, frame_count, shard_rows, seq_count, capacity)
    gathered = exchange_frames(payload, vis_count)
    width = text.shape[1]
    incoming_place = gathered[:, :, width].astype(jnp.int32)
    merged = place_frames(text, gathered, incoming_place, width)
    widened = merged.astype(jnp.float32)
    mean_square = jnp.mean(widened * widened, axis=1, keepdims=True)
    normed = (widened * lax.rsqrt(mean_square + epsilon) * norm_gain).astype(jnp.bfloat16)
    queries = (jnp.dot(normed, w_query, preferred_element_type=jnp.float32) + q_bias).astype(
        jnp.bfloat16
    )
    key_rows = jnp.dot(normed, w_key, preferred_element_type=jnp.float32).astype(jnp.bfloat16)
    value_rows = (jnp.dot(normed, w_value, preferred_element_type=jnp.float32) + v_bias).astype(
        jnp.bfloat16
    )
    keyval = jnp.concatenate([key_rows, value_rows], axis=1)
    kv_heads = w_key.shape[1] // HEAD_DIM
    per_group = w_query.shape[1] // HEAD_DIM // kv_heads
    incoming_keys = gather_keys(keyval, seq_count)
    queries, doc_ids = lax.optimization_barrier((queries, doc_ids))
    own_docs = lax.dynamic_slice_in_dim(doc_ids, first_row, shard_rows)
    doc_start = jnp.sum((doc_ids < own_docs[0]).astype(jnp.int32))
    last_row = first_row + shard_rows - 1
    block_range = jnp.stack([doc_start // KEY_BLOCK, last_row // KEY_BLOCK, first_row]).astype(jnp.int32)
    return flash_attention(block_range, queries, incoming_keys, own_docs, doc_ids, kv_heads)


KEY_BLOCK = 512
DOC_SPAN = 2048


def flash_kernel(
    range_ref, q_ref, k_ref, v_ref, qdoc_ref, kdoc_ref, out_ref, peak_ref, total_ref, acc_ref
):
    step = pl.program_id(0)
    block = range_ref[0] + step
    rows = q_ref.shape[0]
    heads = q_ref.shape[1] // HEAD_DIM

    @pl.when(step == 0)
    def _():
        peak_ref[...] = jnp.full(peak_ref.shape, negative, jnp.float32)
        total_ref[...] = jnp.zeros(total_ref.shape, jnp.float32)
        acc_ref[...] = jnp.zeros(acc_ref.shape, jnp.float32)

    @pl.when(block <= range_ref[1])
    def _():
        key_place = block * KEY_BLOCK + lax.broadcasted_iota(jnp.int32, (1, KEY_BLOCK), 1)
        query_place = range_ref[2] + lax.broadcasted_iota(jnp.int32, (rows, 1), 0)
        allowed = (key_place <= query_place) & (kdoc_ref[...] == qdoc_ref[...])
        keys = k_ref[...]
        vals = v_ref[...]
        for h in range(heads):
            cols = slice(h * HEAD_DIM, (h + 1) * HEAD_DIM)
            scores = lax.dot_general(
                q_ref[:, cols], keys, (((1,), (1,)), ((), ())),
                preferred_element_type=jnp.float32,
            ) * HEAD_DIM ** (-0.5)
            scores = jnp.where(allowed, scores, negative)
            old_peak = peak_ref[h]
            new_peak = jnp.maximum(old_peak, jnp.max(scores, axis=1, keepdims=True))
            raised = jnp.where(allowed, jnp.exp(scores - new_peak[:, :1]), 0.0)
            factor = jnp.exp(old_peak - new_peak)
            total_ref[h] = total_ref[h] * factor + jnp.sum(raised, axis=1, keepdims=True)
            peak_ref[h] = new_peak
            product = jnp.dot(raised.astype(jnp.bfloat16), vals, preferred_element_type=jnp.float32)
            acc_ref[:, cols] = acc_ref[:, cols] * factor[:, :1] + product

    @pl.when(step == pl.num_programs(0) - 1)
    def _():
        for h in range(heads):
            cols = slice(h * HEAD_DIM, (h + 1) * HEAD_DIM)
            out_ref[:, cols] = (acc_ref[:, cols] / total_ref[h][:, :1]).astype(out_ref.dtype)


def flash_attention(block_range, queries, keyval, own_docs, doc_ids, kv_heads):
    rows, width = queries.shape
    key_rows = keyval.shape[0]
    steps = min(key_rows // KEY_BLOCK, (DOC_SPAN + rows - 2) // KEY_BLOCK + 2)
    heads = width // HEAD_DIM

    def key_block(j, r):
        return (jnp.minimum(r[0] + j, r[1]), 0)

    def value_block(j, r):
        return (jnp.minimum(r[0] + j, r[1]), 1)

    def doc_block(j, r):
        return (0, jnp.minimum(r[0] + j, r[1]))

    grid_spec = pltpu.PrefetchScalarGridSpec(
        num_scalar_prefetch=1,
        grid=(steps,),
        in_specs=[
            pl.BlockSpec((rows, width), lambda j, r: (0, 0)),
            pl.BlockSpec((KEY_BLOCK, HEAD_DIM), key_block),
            pl.BlockSpec((KEY_BLOCK, HEAD_DIM), value_block),
            pl.BlockSpec((rows, 1), lambda j, r: (0, 0)),
            pl.BlockSpec((1, KEY_BLOCK), doc_block),
        ],
        out_specs=pl.BlockSpec((rows, width), lambda j, r: (0, 0)),
        scratch_shapes=[
            pltpu.VMEM((heads, rows, 1), jnp.float32),
            pltpu.VMEM((heads, rows, 1), jnp.float32),
            pltpu.VMEM((rows, width), jnp.float32),
        ],
    )
    flops = 4 * rows * width * key_rows // 2
    return pl.pallas_call(
        flash_kernel,
        out_shape=jax.ShapeDtypeStruct((rows, width), jnp.bfloat16),
        grid_spec=grid_spec,
        compiler_params=pltpu.CompilerParams(dimension_semantics=("arbitrary",)),
        cost_estimate=pl.CostEstimate(
            flops=flops, transcendentals=rows * heads * key_rows // 2,
            bytes_accessed=2 * (2 * rows * width + key_rows * 2 * HEAD_DIM),
        ),
    )(block_range, queries, keyval, keyval, own_docs.reshape(rows, 1), doc_ids.reshape(1, -1))


def solution(mesh):
    in_specs = (
        P("seq", None),
        P(("seq", "vis"), None),
        P(("seq", "vis")),
        P(("seq", "vis")),
        P(),
        P(),
        P(None, "vis"),
        P("vis"),
        P(None, "vis"),
        P(None, "vis"),
        P("vis"),
    )
    out_specs = P("seq", "vis")
    return jax.shard_map(
        on_device, mesh=mesh, in_specs=in_specs, out_specs=out_specs, check_vma=False
    )
```

```python
import jax
import jax.numpy as jnp
from jax import lax
from jax.sharding import PartitionSpec as P
from jax.experimental import pallas as pl
from jax.experimental.pallas import tpu as pltpu

HEAD_DIM = 128


epsilon = 1e-06
negative = -1e30


def frame_slots(frames, tile_pos, frame_count, shard_rows, owners, capacity):
    row_count = frames.shape[0]
    row_ids = jnp.arange(row_count, dtype=jnp.int32)
    usable = row_ids < frame_count[0]
    owner = jnp.where(usable, tile_pos // shard_rows, owners)
    hits = (owner[:, None] == jnp.arange(owners, dtype=jnp.int32)[None, :]).astype(jnp.int32)
    earlier = (row_ids[:, None] > row_ids[None, :]).astype(jnp.int32)
    before = jnp.dot(earlier, hits, preferred_element_type=jnp.int32)
    rank = jnp.sum(before * hits, axis=1)
    slot_index = owner * capacity + rank
    slot_ids = jnp.arange(owners * capacity, dtype=jnp.int32)
    match = usable[:, None] & (slot_index[:, None] == slot_ids[None, :])
    filled = jnp.any(match, axis=0)
    local = tile_pos - owner * shard_rows
    slot_local = jnp.sum(jnp.where(match, local[:, None], 0), axis=0)
    slot_local = jnp.where(filled, slot_local, -1)
    slot_rows = jnp.dot(
        match.T.astype(frames.dtype), frames, preferred_element_type=jnp.float32
    ).astype(frames.dtype)
    place_col = jnp.broadcast_to(slot_local[:, None], (slot_local.shape[0], 128)).astype(frames.dtype)
    payload = jnp.concatenate([slot_rows, place_col], axis=1)
    return payload.reshape(owners, capacity, payload.shape[1])


def place_frames(text, incoming, incoming_place, width):
    lookup = incoming_place[None] == jnp.arange(text.shape[0], dtype=jnp.int32)[:, None, None]
    covered = jnp.any(lookup, axis=(1, 2))
    placed = lax.dot_general(
        lookup.astype(incoming.dtype), incoming, (((1, 2), (0, 1)), ((), ())),
        preferred_element_type=jnp.float32,
    )[:, :width].astype(text.dtype)
    return jnp.where(covered[:, None], placed, text)


def exchange_kernel(payload_ref, out_ref, send_a, recv_a, send_b, recv_b, local_sem):
    seq_count = lax.axis_size("seq")
    vis_count = lax.axis_size("vis")
    ring = vis_count // 2
    me_seq = lax.axis_index("seq")
    me_vis = lax.axis_index("vis")
    ring_pos = lax.rem(me_vis, ring)
    ring_id = me_vis // ring

    def vis_of(ring_index, position):
        return ring_index * ring + lax.rem(position + ring, ring)

    right = vis_of(ring_id, ring_pos + 1)
    left = vis_of(ring_id, ring_pos - 1)
    partner = vis_of(1 - ring_id, ring_pos)
    barrier = pltpu.get_barrier_semaphore()
    for k in range(1, seq_count):
        pl.semaphore_signal(
            barrier, inc=1, device_id=(lax.rem(me_seq + k, seq_count), me_vis),
            device_id_type=pl.DeviceIdType.MESH,
        )
    for peer in (left, right, partner):
        pl.semaphore_signal(
            barrier, inc=1, device_id=(me_seq, peer), device_id_type=pl.DeviceIdType.MESH
        )
    pl.semaphore_wait(barrier, seq_count + 2)
    base = me_vis * seq_count
    local = pltpu.make_async_copy(payload_ref.at[me_seq], out_ref.at[base + me_seq], local_sem.at[0])
    local.start()
    first = []
    for k in range(1, seq_count):
        target = lax.rem(me_seq + k, seq_count)
        copy = pltpu.make_async_remote_copy(
            src_ref=payload_ref.at[target],
            dst_ref=out_ref.at[base + me_seq],
            send_sem=send_a.at[k],
            recv_sem=recv_a.at[k],
            device_id=(target, me_vis),
            device_id_type=pl.DeviceIdType.MESH,
        )
        copy.start()
        first.append(copy)
    local.wait()
    for k in range(1, seq_count):
        source = lax.rem(me_seq + seq_count - k, seq_count)
        incoming = pltpu.make_async_remote_copy(
            src_ref=payload_ref.at[source],
            dst_ref=out_ref.at[base + source],
            send_sem=send_a.at[k],
            recv_sem=recv_a.at[k],
            device_id=(source, me_vis),
            device_id_type=pl.DeviceIdType.MESH,
        )
        incoming.wait_recv()
    for copy in first:
        copy.wait_send()

    half = seq_count // 2

    def region(owner, part):
        if part == 0:
            return out_ref.at[pl.ds(owner * seq_count, seq_count)]
        start = owner * seq_count + (part - 1) * half
        return out_ref.at[pl.ds(start, half)]

    def link(owner, part, peer, index):
        piece = region(owner, part)
        return pltpu.make_async_remote_copy(
            src_ref=piece,
            dst_ref=piece,
            send_sem=send_b.at[index],
            recv_sem=recv_b.at[index],
            device_id=(me_seq, peer),
            device_id_type=pl.DeviceIdType.MESH,
        )

    far = vis_of(ring_id, ring_pos + 2)
    left_partner = vis_of(1 - ring_id, ring_pos - 1)
    right_partner = vis_of(1 - ring_id, ring_pos + 1)
    far_partner = vis_of(1 - ring_id, ring_pos + 2)
    sent = []

    def send(owner, part, peer, index):
        copy = link(owner, part, peer, index)
        copy.start()
        sent.append(copy)

    send(me_vis, 0, right, 1)
    send(me_vis, 0, left, 2)
    send(me_vis, 0, partner, 3)
    link(partner, 0, partner, 3).wait_recv()
    send(partner, 0, right, 4)
    send(partner, 0, left, 5)
    link(left, 0, left, 1).wait_recv()
    send(left, 1, right, 6)
    link(right, 0, right, 2).wait_recv()
    send(right, 2, left, 7)
    link(left_partner, 0, left, 4).wait_recv()
    send(left_partner, 1, right, 8)
    link(right_partner, 0, right, 5).wait_recv()
    send(right_partner, 2, left, 9)
    link(far, 1, left, 6).wait_recv()
    link(far, 2, right, 7).wait_recv()
    link(far_partner, 1, left, 8).wait_recv()
    link(far_partner, 2, right, 9).wait_recv()
    for copy in sent:
        copy.wait_send()


def exchange_frames(payload, vis_count):
    owners, capacity, width = payload.shape
    return pl.pallas_call(
        exchange_kernel,
        out_shape=jax.ShapeDtypeStruct((vis_count * owners, capacity, width), payload.dtype),
        in_specs=[pl.BlockSpec(memory_space=pl.ANY)],
        out_specs=pl.BlockSpec(memory_space=pl.ANY),
        scratch_shapes=[
            pltpu.SemaphoreType.DMA((owners,)),
            pltpu.SemaphoreType.DMA((owners,)),
            pltpu.SemaphoreType.DMA((10,)),
            pltpu.SemaphoreType.DMA((10,)),
            pltpu.SemaphoreType.DMA((1,)),
        ],
        compiler_params=pltpu.CompilerParams(collective_id=1, has_side_effects=True),
    )(payload)


def gather_kernel(
    block_ref, normed_ref, w_ref, bias_ref, out_ref, q_ref, send_sem, recv_sem, local_sem, acc_ref
):
    rows = block_ref.shape[0]
    me_seq = lax.axis_index("seq")
    me_vis = lax.axis_index("vis")
    column = me_seq // 4
    layer = lax.rem(me_seq // 2, 2)
    core = lax.rem(me_seq, 2)
    ring = lax.axis_size("seq") // 4

    def seq_of(y, z, c):
        return (lax.rem(y + ring, ring) * 2 + z) * 2 + c

    mate = seq_of(column, layer, 1 - core)
    across = seq_of(column, 1 - layer, core)
    diagonal = seq_of(column, 1 - layer, 1 - core)
    up = seq_of(column + 1, layer, core)
    down = seq_of(column - 1, layer, core)
    barrier = pltpu.get_barrier_semaphore()
    for peer in (mate, across, diagonal, up, down):
        pl.semaphore_signal(
            barrier, inc=1, device_id=(peer, me_vis), device_id_type=pl.DeviceIdType.MESH
        )
    pl.semaphore_wait(barrier, 5)

    def rows_of(start, count):
        return out_ref.at[pl.ds(pl.multiple_of(start, rows), count)]

    def link(src, dst, peer, index):
        return pltpu.make_async_remote_copy(
            src_ref=src, dst_ref=dst, send_sem=send_sem.at[index], recv_sem=recv_sem.at[index],
            device_id=(peer, me_vis), device_id_type=pl.DeviceIdType.MESH,
        )

    sent = []

    def send(src, dst, peer, index):
        copy = link(src, dst, peer, index)
        copy.start()
        sent.append(copy)

    own = rows_of(me_seq * rows, rows)
    local = pltpu.make_async_copy(block_ref, own, local_sem.at[0])
    local.start()
    send(block_ref, own, mate, 0)
    send(block_ref, own, across, 1)
    send(block_ref, own, diagonal, 2)
    local.wait()
    link(block_ref, rows_of(mate * rows, rows), mate, 0).wait_recv()
    link(block_ref, rows_of(across * rows, rows), across, 1).wait_recv()
    link(block_ref, rows_of(diagonal * rows, rows), diagonal, 2).wait_recv()

    def half(y, h):
        return rows_of((lax.rem(y + ring, ring) * 4 + h * 2) * rows, 2 * rows)

    def quarter(y, h, q):
        return rows_of((lax.rem(y + ring, ring) * 4 + h * 2 + q) * rows, rows)

    depth = normed_ref.shape[1] // 2

    def project(part):
        def body(n_blk, w_blk):
            acc_ref[...] += jnp.dot(n_blk[...], w_blk[...], preferred_element_type=jnp.float32)

        pltpu.emit_pipeline(
            body,
            grid=(depth // PROJ_TILE,),
            in_specs=[
                pl.BlockSpec((normed_ref.shape[0], PROJ_TILE), lambda k: (0, k)),
                pl.BlockSpec((PROJ_TILE, w_ref.shape[1]), lambda k: (k, 0)),
            ],
        )(normed_ref.at[:, pl.ds(part * depth, depth)], w_ref.at[pl.ds(part * depth, depth)])

    acc_ref[...] = jnp.zeros(acc_ref.shape, jnp.float32)
    mine = half(column, core)
    send(mine, mine, up, 3)
    send(mine, mine, down, 4)
    project(0)
    below = half(column - 1, core)
    link(below, below, down, 3).wait_recv()
    send(below, below, mate, 7)
    piece = quarter(column - 1, core, 0)
    send(piece, piece, up, 5)
    above = half(column + 1, core)
    link(above, above, up, 4).wait_recv()
    send(above, above, mate, 9)
    piece = quarter(column + 1, core, 1)
    send(piece, piece, down, 6)
    project(1)
    q_ref[...] = (acc_ref[...] + bias_ref[...]).astype(q_ref.dtype)
    far_low = quarter(column + 2, core, 0)
    far_high = quarter(column + 2, core, 1)
    link(far_low, far_low, down, 5).wait_recv()
    link(far_high, far_high, up, 6).wait_recv()
    far = half(column + 2, core)
    send(far, far, mate, 8)
    for offset, index in ((-1, 7), (2, 8), (1, 9)):
        theirs = half(column + offset, 1 - core)
        link(theirs, theirs, mate, index).wait_recv()
    for copy in sent:
        copy.wait_send()


PROJ_TILE = 512


def gather_keys(block, normed, w_query, q_bias, seq_count):
    rows, width = block.shape
    return pl.pallas_call(
        gather_kernel,
        out_shape=(
            jax.ShapeDtypeStruct((seq_count * rows, width), block.dtype),
            jax.ShapeDtypeStruct((normed.shape[0], w_query.shape[1]), jnp.bfloat16),
        ),
        in_specs=[
            pl.BlockSpec(memory_space=pl.ANY),
            pl.BlockSpec(memory_space=pl.ANY),
            pl.BlockSpec(memory_space=pl.ANY),
            pl.BlockSpec(memory_space=pltpu.VMEM),
        ],
        out_specs=(pl.BlockSpec(memory_space=pl.ANY), pl.BlockSpec(memory_space=pltpu.VMEM)),
        scratch_shapes=[
            pltpu.SemaphoreType.DMA((10,)),
            pltpu.SemaphoreType.DMA((10,)),
            pltpu.SemaphoreType.DMA((1,)),
            pltpu.VMEM((normed.shape[0], w_query.shape[1]), jnp.float32),
        ],
        compiler_params=pltpu.CompilerParams(collective_id=2, has_side_effects=True),
    )(block, normed, w_query, q_bias.reshape(1, -1))


def on_device(
    text, frames, tile_pos, frame_count, doc_ids, norm_gain, w_query, q_bias, w_key, w_value, v_bias
):
    seq_count = lax.axis_size("seq")
    vis_count = lax.axis_size("vis")
    shard_index = lax.axis_index("seq")
    shard_rows = text.shape[0]
    capacity = shard_rows // (seq_count * vis_count)
    first_row = shard_index * shard_rows
    payload = frame_slots(frames, tile_pos, frame_count, shard_rows, seq_count, capacity)
    gathered = exchange_frames(payload, vis_count)
    width = text.shape[1]
    incoming_place = gathered[:, :, width].astype(jnp.int32)
    merged = place_frames(text, gathered, incoming_place, width)
    widened = merged.astype(jnp.float32)
    mean_square = jnp.mean(widened * widened, axis=1, keepdims=True)
    normed = (widened * lax.rsqrt(mean_square + epsilon) * norm_gain).astype(jnp.bfloat16)
    key_rows = jnp.dot(normed, w_key, preferred_element_type=jnp.float32).astype(jnp.bfloat16)
    value_rows = (jnp.dot(normed, w_value, preferred_element_type=jnp.float32) + v_bias).astype(
        jnp.bfloat16
    )
    keyval = jnp.concatenate([key_rows, value_rows], axis=1)
    kv_heads = w_key.shape[1] // HEAD_DIM
    per_group = w_query.shape[1] // HEAD_DIM // kv_heads
    incoming_keys, queries = gather_keys(keyval, normed, w_query, q_bias, seq_count)
    queries, doc_ids = lax.optimization_barrier((queries, doc_ids))
    own_docs = lax.dynamic_slice_in_dim(doc_ids, first_row, shard_rows)
    doc_start = jnp.sum((doc_ids < own_docs[0]).astype(jnp.int32))
    last_row = first_row + shard_rows - 1
    block_range = jnp.stack([doc_start // KEY_BLOCK, last_row // KEY_BLOCK, first_row]).astype(jnp.int32)
    return flash_attention(block_range, queries, incoming_keys, own_docs, doc_ids, kv_heads)


KEY_BLOCK = 512
DOC_SPAN = 2048


def flash_kernel(
    range_ref, q_ref, k_ref, v_ref, qdoc_ref, kdoc_ref, out_ref, peak_ref, total_ref, acc_ref
):
    step = pl.program_id(0)
    block = range_ref[0] + step
    rows = q_ref.shape[0]
    heads = q_ref.shape[1] // HEAD_DIM

    @pl.when(step == 0)
    def _():
        peak_ref[...] = jnp.full(peak_ref.shape, negative, jnp.float32)
        total_ref[...] = jnp.zeros(total_ref.shape, jnp.float32)
        acc_ref[...] = jnp.zeros(acc_ref.shape, jnp.float32)

    @pl.when(block <= range_ref[1])
    def _():
        key_place = block * KEY_BLOCK + lax.broadcasted_iota(jnp.int32, (1, KEY_BLOCK), 1)
        query_place = range_ref[2] + lax.broadcasted_iota(jnp.int32, (rows, 1), 0)
        allowed = (key_place <= query_place) & (kdoc_ref[...] == qdoc_ref[...])
        keys = k_ref[...]
        vals = v_ref[...]
        for h in range(heads):
            cols = slice(h * HEAD_DIM, (h + 1) * HEAD_DIM)
            scores = lax.dot_general(
                q_ref[:, cols], keys, (((1,), (1,)), ((), ())),
                preferred_element_type=jnp.float32,
            ) * HEAD_DIM ** (-0.5)
            scores = jnp.where(allowed, scores, negative)
            old_peak = peak_ref[h]
            new_peak = jnp.maximum(old_peak, jnp.max(scores, axis=1, keepdims=True))
            raised = jnp.where(allowed, jnp.exp(scores - new_peak[:, :1]), 0.0)
            factor = jnp.exp(old_peak - new_peak)
            total_ref[h] = total_ref[h] * factor + jnp.sum(raised, axis=1, keepdims=True)
            peak_ref[h] = new_peak
            product = jnp.dot(raised.astype(jnp.bfloat16), vals, preferred_element_type=jnp.float32)
            acc_ref[:, cols] = acc_ref[:, cols] * factor[:, :1] + product

    @pl.when(step == pl.num_programs(0) - 1)
    def _():
        for h in range(heads):
            cols = slice(h * HEAD_DIM, (h + 1) * HEAD_DIM)
            out_ref[:, cols] = (acc_ref[:, cols] / total_ref[h][:, :1]).astype(out_ref.dtype)


def flash_attention(block_range, queries, keyval, own_docs, doc_ids, kv_heads):
    rows, width = queries.shape
    key_rows = keyval.shape[0]
    steps = min(key_rows // KEY_BLOCK, (DOC_SPAN + rows - 2) // KEY_BLOCK + 2)
    heads = width // HEAD_DIM

    def key_block(j, r):
        return (jnp.minimum(r[0] + j, r[1]), 0)

    def value_block(j, r):
        return (jnp.minimum(r[0] + j, r[1]), 1)

    def doc_block(j, r):
        return (0, jnp.minimum(r[0] + j, r[1]))

    grid_spec = pltpu.PrefetchScalarGridSpec(
        num_scalar_prefetch=1,
        grid=(steps,),
        in_specs=[
            pl.BlockSpec((rows, width), lambda j, r: (0, 0)),
            pl.BlockSpec((KEY_BLOCK, HEAD_DIM), key_block),
            pl.BlockSpec((KEY_BLOCK, HEAD_DIM), value_block),
            pl.BlockSpec((rows, 1), lambda j, r: (0, 0)),
            pl.BlockSpec((1, KEY_BLOCK), doc_block),
        ],
        out_specs=pl.BlockSpec((rows, width), lambda j, r: (0, 0)),
        scratch_shapes=[
            pltpu.VMEM((heads, rows, 1), jnp.float32),
            pltpu.VMEM((heads, rows, 1), jnp.float32),
            pltpu.VMEM((rows, width), jnp.float32),
        ],
    )
    flops = 4 * rows * width * key_rows // 2
    return pl.pallas_call(
        flash_kernel,
        out_shape=jax.ShapeDtypeStruct((rows, width), jnp.bfloat16),
        grid_spec=grid_spec,
        compiler_params=pltpu.CompilerParams(dimension_semantics=("arbitrary",)),
        cost_estimate=pl.CostEstimate(
            flops=flops, transcendentals=rows * heads * key_rows // 2,
            bytes_accessed=2 * (2 * rows * width + key_rows * 2 * HEAD_DIM),
        ),
    )(block_range, queries, keyval, keyval, own_docs.reshape(rows, 1), doc_ids.reshape(1, -1))


def solution(mesh):
    in_specs = (
        P("seq", None),
        P(("seq", "vis"), None),
        P(("seq", "vis")),
        P(("seq", "vis")),
        P(),
        P(),
        P(None, "vis"),
        P("vis"),
        P(None, "vis"),
        P(None, "vis"),
        P("vis"),
    )
    out_specs = P("seq", "vis")
    return jax.shard_map(
        on_device, mesh=mesh, in_specs=in_specs, out_specs=out_specs, check_vma=False
    )
```

```python
import jax
import jax.numpy as jnp
from jax import lax
from jax.sharding import PartitionSpec as P
from jax.experimental import pallas as pl
from jax.experimental.pallas import tpu as pltpu

HEAD_DIM = 128


epsilon = 1e-06
negative = -1e30


def frame_slots(frames, tile_pos, frame_count, shard_rows, owners, capacity):
    row_count = frames.shape[0]
    row_ids = jnp.arange(row_count, dtype=jnp.int32)
    usable = row_ids < frame_count[0]
    owner = jnp.where(usable, tile_pos // shard_rows, owners)
    hits = (owner[:, None] == jnp.arange(owners, dtype=jnp.int32)[None, :]).astype(jnp.int32)
    earlier = (row_ids[:, None] > row_ids[None, :]).astype(jnp.int32)
    before = jnp.dot(earlier, hits, preferred_element_type=jnp.int32)
    rank = jnp.sum(before * hits, axis=1)
    slot_index = owner * capacity + rank
    slot_ids = jnp.arange(owners * capacity, dtype=jnp.int32)
    match = usable[:, None] & (slot_index[:, None] == slot_ids[None, :])
    filled = jnp.any(match, axis=0)
    local = tile_pos - owner * shard_rows
    slot_local = jnp.sum(jnp.where(match, local[:, None], 0), axis=0)
    slot_local = jnp.where(filled, slot_local, -1)
    slot_rows = jnp.dot(
        match.T.astype(frames.dtype), frames, preferred_element_type=jnp.float32
    ).astype(frames.dtype)
    place_col = jnp.broadcast_to(slot_local[:, None], (slot_local.shape[0], 128)).astype(frames.dtype)
    payload = jnp.concatenate([slot_rows, place_col], axis=1)
    return payload.reshape(owners, capacity, payload.shape[1])


def place_frames(text, incoming, incoming_place, width):
    lookup = incoming_place[None] == jnp.arange(text.shape[0], dtype=jnp.int32)[:, None, None]
    covered = jnp.any(lookup, axis=(1, 2))
    placed = lax.dot_general(
        lookup.astype(incoming.dtype), incoming, (((1, 2), (0, 1)), ((), ())),
        preferred_element_type=jnp.float32,
    )[:, :width].astype(text.dtype)
    return jnp.where(covered[:, None], placed, text)


def exchange_kernel(payload_ref, out_ref, send_a, recv_a, send_b, recv_b, local_sem):
    seq_count = lax.axis_size("seq")
    vis_count = lax.axis_size("vis")
    ring = vis_count // 2
    me_seq = lax.axis_index("seq")
    me_vis = lax.axis_index("vis")
    ring_pos = lax.rem(me_vis, ring)
    ring_id = me_vis // ring

    def vis_of(ring_index, position):
        return ring_index * ring + lax.rem(position + ring, ring)

    right = vis_of(ring_id, ring_pos + 1)
    left = vis_of(ring_id, ring_pos - 1)
    partner = vis_of(1 - ring_id, ring_pos)
    barrier = pltpu.get_barrier_semaphore()
    for k in range(1, seq_count):
        pl.semaphore_signal(
            barrier, inc=1, device_id=(lax.rem(me_seq + k, seq_count), me_vis),
            device_id_type=pl.DeviceIdType.MESH,
        )
    for peer in (left, right, partner):
        pl.semaphore_signal(
            barrier, inc=1, device_id=(me_seq, peer), device_id_type=pl.DeviceIdType.MESH
        )
    pl.semaphore_wait(barrier, seq_count + 2)
    base = me_vis * seq_count
    local = pltpu.make_async_copy(payload_ref.at[me_seq], out_ref.at[base + me_seq], local_sem.at[0])
    local.start()
    first = []
    for k in range(1, seq_count):
        target = lax.rem(me_seq + k, seq_count)
        copy = pltpu.make_async_remote_copy(
            src_ref=payload_ref.at[target],
            dst_ref=out_ref.at[base + me_seq],
            send_sem=send_a.at[k],
            recv_sem=recv_a.at[k],
            device_id=(target, me_vis),
            device_id_type=pl.DeviceIdType.MESH,
        )
        copy.start()
        first.append(copy)
    local.wait()
    for k in range(1, seq_count):
        source = lax.rem(me_seq + seq_count - k, seq_count)
        incoming = pltpu.make_async_remote_copy(
            src_ref=payload_ref.at[source],
            dst_ref=out_ref.at[base + source],
            send_sem=send_a.at[k],
            recv_sem=recv_a.at[k],
            device_id=(source, me_vis),
            device_id_type=pl.DeviceIdType.MESH,
        )
        incoming.wait_recv()
    for copy in first:
        copy.wait_send()

    half = seq_count // 2

    def region(owner, part):
        if part == 0:
            return out_ref.at[pl.ds(owner * seq_count, seq_count)]
        start = owner * seq_count + (part - 1) * half
        return out_ref.at[pl.ds(start, half)]

    def link(owner, part, peer, index):
        piece = region(owner, part)
        return pltpu.make_async_remote_copy(
            src_ref=piece,
            dst_ref=piece,
            send_sem=send_b.at[index],
            recv_sem=recv_b.at[index],
            device_id=(me_seq, peer),
            device_id_type=pl.DeviceIdType.MESH,
        )

    far = vis_of(ring_id, ring_pos + 2)
    left_partner = vis_of(1 - ring_id, ring_pos - 1)
    right_partner = vis_of(1 - ring_id, ring_pos + 1)
    far_partner = vis_of(1 - ring_id, ring_pos + 2)
    sent = []

    def send(owner, part, peer, index):
        copy = link(owner, part, peer, index)
        copy.start()
        sent.append(copy)

    send(me_vis, 0, right, 1)
    send(me_vis, 0, left, 2)
    send(me_vis, 0, partner, 3)
    link(partner, 0, partner, 3).wait_recv()
    send(partner, 0, right, 4)
    send(partner, 0, left, 5)
    link(left, 0, left, 1).wait_recv()
    send(left, 1, right, 6)
    link(right, 0, right, 2).wait_recv()
    send(right, 2, left, 7)
    link(left_partner, 0, left, 4).wait_recv()
    send(left_partner, 1, right, 8)
    link(right_partner, 0, right, 5).wait_recv()
    send(right_partner, 2, left, 9)
    link(far, 1, left, 6).wait_recv()
    link(far, 2, right, 7).wait_recv()
    link(far_partner, 1, left, 8).wait_recv()
    link(far_partner, 2, right, 9).wait_recv()
    for copy in sent:
        copy.wait_send()


def exchange_frames(payload, vis_count):
    owners, capacity, width = payload.shape
    return pl.pallas_call(
        exchange_kernel,
        out_shape=jax.ShapeDtypeStruct((vis_count * owners, capacity, width), payload.dtype),
        in_specs=[pl.BlockSpec(memory_space=pl.ANY)],
        out_specs=pl.BlockSpec(memory_space=pl.ANY),
        scratch_shapes=[
            pltpu.SemaphoreType.DMA((owners,)),
            pltpu.SemaphoreType.DMA((owners,)),
            pltpu.SemaphoreType.DMA((10,)),
            pltpu.SemaphoreType.DMA((10,)),
            pltpu.SemaphoreType.DMA((1,)),
        ],
        compiler_params=pltpu.CompilerParams(collective_id=1, has_side_effects=True),
    )(payload)


def gather_kernel(
    block_ref, normed_ref, w_ref, bias_ref, out_ref, q_ref, send_sem, recv_sem, local_sem, acc_ref
):
    rows = block_ref.shape[0]
    me_seq = lax.axis_index("seq")
    me_vis = lax.axis_index("vis")
    column = me_seq // 4
    layer = lax.rem(me_seq // 2, 2)
    core = lax.rem(me_seq, 2)
    ring = lax.axis_size("seq") // 4

    def seq_of(y, z, c):
        return (lax.rem(y + ring, ring) * 2 + z) * 2 + c

    mate = seq_of(column, layer, 1 - core)
    across = seq_of(column, 1 - layer, core)
    diagonal = seq_of(column, 1 - layer, 1 - core)
    up = seq_of(column + 1, layer, core)
    down = seq_of(column - 1, layer, core)
    barrier = pltpu.get_barrier_semaphore()
    for peer in (mate, across, diagonal, up, down):
        pl.semaphore_signal(
            barrier, inc=1, device_id=(peer, me_vis), device_id_type=pl.DeviceIdType.MESH
        )
    pl.semaphore_wait(barrier, 5)

    def rows_of(start, count):
        return out_ref.at[pl.ds(pl.multiple_of(start, rows), count)]

    def link(src, dst, peer, index):
        return pltpu.make_async_remote_copy(
            src_ref=src, dst_ref=dst, send_sem=send_sem.at[index], recv_sem=recv_sem.at[index],
            device_id=(peer, me_vis), device_id_type=pl.DeviceIdType.MESH,
        )

    sent = []

    def send(src, dst, peer, index):
        copy = link(src, dst, peer, index)
        copy.start()
        sent.append(copy)

    own = rows_of(me_seq * rows, rows)
    local = pltpu.make_async_copy(block_ref, own, local_sem.at[0])
    local.start()
    send(block_ref, own, mate, 0)
    send(block_ref, own, across, 1)
    send(block_ref, own, diagonal, 2)
    local.wait()
    link(block_ref, rows_of(mate * rows, rows), mate, 0).wait_recv()
    link(block_ref, rows_of(across * rows, rows), across, 1).wait_recv()
    link(block_ref, rows_of(diagonal * rows, rows), diagonal, 2).wait_recv()

    def half(y, h):
        return rows_of((lax.rem(y + ring, ring) * 4 + h * 2) * rows, 2 * rows)

    def quarter(y, h, q):
        return rows_of((lax.rem(y + ring, ring) * 4 + h * 2 + q) * rows, rows)

    depth = normed_ref.shape[1] // 2

    def project(part):
        def body(n_blk, w_blk):
            acc_ref[...] += jnp.dot(n_blk[...], w_blk[...], preferred_element_type=jnp.float32)

        pltpu.emit_pipeline(
            body,
            grid=(depth // PROJ_TILE,),
            in_specs=[
                pl.BlockSpec((normed_ref.shape[0], PROJ_TILE), lambda k: (0, k)),
                pl.BlockSpec((PROJ_TILE, w_ref.shape[1]), lambda k: (k, 0)),
            ],
        )(normed_ref.at[:, pl.ds(part * depth, depth)], w_ref.at[pl.ds(part * depth, depth)])

    acc_ref[...] = jnp.zeros(acc_ref.shape, jnp.float32)
    mine = half(column, core)
    send(mine, mine, up, 3)
    send(mine, mine, down, 4)
    project(0)
    below = half(column - 1, core)
    link(below, below, down, 3).wait_recv()
    send(below, below, mate, 7)
    piece = quarter(column - 1, core, 0)
    send(piece, piece, up, 5)
    above = half(column + 1, core)
    link(above, above, up, 4).wait_recv()
    send(above, above, mate, 9)
    piece = quarter(column + 1, core, 1)
    send(piece, piece, down, 6)
    project(1)
    q_ref[...] = (acc_ref[...] + bias_ref[...]).astype(q_ref.dtype)
    far_low = quarter(column + 2, core, 0)
    far_high = quarter(column + 2, core, 1)
    link(far_low, far_low, down, 5).wait_recv()
    link(far_high, far_high, up, 6).wait_recv()
    far = half(column + 2, core)
    send(far, far, mate, 8)
    for offset, index in ((-1, 7), (2, 8), (1, 9)):
        theirs = half(column + offset, 1 - core)
        link(theirs, theirs, mate, index).wait_recv()
    for copy in sent:
        copy.wait_send()


PROJ_TILE = 512


def gather_keys(block, normed, w_query, q_bias, seq_count):
    rows, width = block.shape
    return pl.pallas_call(
        gather_kernel,
        out_shape=(
            jax.ShapeDtypeStruct((seq_count * rows, width), block.dtype),
            jax.ShapeDtypeStruct((normed.shape[0], w_query.shape[1]), jnp.bfloat16),
        ),
        in_specs=[
            pl.BlockSpec(memory_space=pl.ANY),
            pl.BlockSpec(memory_space=pl.ANY),
            pl.BlockSpec(memory_space=pl.ANY),
            pl.BlockSpec(memory_space=pltpu.VMEM),
        ],
        out_specs=(pl.BlockSpec(memory_space=pl.ANY), pl.BlockSpec(memory_space=pltpu.VMEM)),
        scratch_shapes=[
            pltpu.SemaphoreType.DMA((10,)),
            pltpu.SemaphoreType.DMA((10,)),
            pltpu.SemaphoreType.DMA((1,)),
            pltpu.VMEM((normed.shape[0], w_query.shape[1]), jnp.float32),
        ],
        compiler_params=pltpu.CompilerParams(collective_id=2, has_side_effects=True),
    )(block, normed, w_query, q_bias.reshape(1, -1))


def on_device(
    text, frames, tile_pos, frame_count, doc_ids, norm_gain, w_query, q_bias, w_key, w_value, v_bias
):
    seq_count = lax.axis_size("seq")
    vis_count = lax.axis_size("vis")
    shard_index = lax.axis_index("seq")
    shard_rows = text.shape[0]
    capacity = shard_rows // (seq_count * vis_count)
    first_row = shard_index * shard_rows
    payload = frame_slots(frames, tile_pos, frame_count, shard_rows, seq_count, capacity)
    gathered = exchange_frames(payload, vis_count)
    width = text.shape[1]
    incoming_place = gathered[:, :, width].astype(jnp.int32)
    merged = place_frames(text, gathered, incoming_place, width)
    widened = merged.astype(jnp.float32)
    mean_square = jnp.mean(widened * widened, axis=1, keepdims=True)
    normed = (widened * lax.rsqrt(mean_square + epsilon) * norm_gain).astype(jnp.bfloat16)
    key_rows = jnp.dot(normed, w_key, preferred_element_type=jnp.float32).astype(jnp.bfloat16)
    value_rows = (jnp.dot(normed, w_value, preferred_element_type=jnp.float32) + v_bias).astype(
        jnp.bfloat16
    )
    keyval = jnp.concatenate([key_rows, value_rows], axis=1)
    kv_heads = w_key.shape[1] // HEAD_DIM
    per_group = w_query.shape[1] // HEAD_DIM // kv_heads
    incoming_keys, queries = gather_keys(keyval, normed, w_query, q_bias, seq_count)
    return flash_attention(doc_ids, queries, incoming_keys)


KEY_BLOCK = 512
DOC_SPAN = 2048


def block_bounds(doc_ref, rows, key_rows):
    first = lax.axis_index("seq") * rows
    first_doc = doc_ref[first]
    low = 0
    for b in range(key_rows // KEY_BLOCK):
        low = low + (doc_ref[(b + 1) * KEY_BLOCK - 1] < first_doc).astype(jnp.int32)
    return low, (first + rows - 1) // KEY_BLOCK, first


def flash_kernel(doc_ref, q_ref, k_ref, v_ref, qdoc_ref, kdoc_ref, out_ref, peak_ref, total_ref, acc_ref, qcol_ref):
    step = pl.program_id(0)
    rows = q_ref.shape[0]
    heads = q_ref.shape[1] // HEAD_DIM
    low, high, first = block_bounds(doc_ref, rows, doc_ref.shape[0])
    block = low + step

    @pl.when(step == 0)
    def _():
        peak_ref[...] = jnp.full(peak_ref.shape, negative, jnp.float32)
        total_ref[...] = jnp.zeros(total_ref.shape, jnp.float32)
        acc_ref[...] = jnp.zeros(acc_ref.shape, jnp.float32)
        spread = jnp.broadcast_to(qdoc_ref[...], (rows, rows))
        diagonal = lax.broadcasted_iota(jnp.int32, (rows, rows), 0) == lax.broadcasted_iota(
            jnp.int32, (rows, rows), 1
        )
        qcol_ref[...] = jnp.sum(jnp.where(diagonal, spread, 0), axis=1, keepdims=True)

    @pl.when(block <= high)
    def _():
        key_place = block * KEY_BLOCK + lax.broadcasted_iota(jnp.int32, (1, KEY_BLOCK), 1)
        query_place = first + lax.broadcasted_iota(jnp.int32, (rows, 1), 0)
        allowed = (key_place <= query_place) & (kdoc_ref[...] == qcol_ref[...])
        keys = k_ref[...]
        vals = v_ref[...]
        for h in range(heads):
            cols = slice(h * HEAD_DIM, (h + 1) * HEAD_DIM)
            scores = lax.dot_general(
                q_ref[:, cols], keys, (((1,), (1,)), ((), ())),
                preferred_element_type=jnp.float32,
            ) * HEAD_DIM ** (-0.5)
            scores = jnp.where(allowed, scores, negative)
            old_peak = peak_ref[h]
            new_peak = jnp.maximum(old_peak, jnp.max(scores, axis=1, keepdims=True))
            raised = jnp.where(allowed, jnp.exp(scores - new_peak[:, :1]), 0.0)
            factor = jnp.exp(old_peak - new_peak)
            total_ref[h] = total_ref[h] * factor + jnp.sum(raised, axis=1, keepdims=True)
            peak_ref[h] = new_peak
            product = jnp.dot(raised.astype(jnp.bfloat16), vals, preferred_element_type=jnp.float32)
            acc_ref[:, cols] = acc_ref[:, cols] * factor[:, :1] + product

    @pl.when(step == pl.num_programs(0) - 1)
    def _():
        for h in range(heads):
            cols = slice(h * HEAD_DIM, (h + 1) * HEAD_DIM)
            out_ref[:, cols] = (acc_ref[:, cols] / total_ref[h][:, :1]).astype(out_ref.dtype)


def flash_attention(doc_ids, queries, keyval):
    rows, width = queries.shape
    key_rows = keyval.shape[0]
    steps = min(key_rows // KEY_BLOCK, (DOC_SPAN + rows - 2) // KEY_BLOCK + 2)
    heads = width // HEAD_DIM

    def clamp(j, d):
        low, high, _ = block_bounds(d, rows, key_rows)
        return jnp.minimum(low + j, high)

    grid_spec = pltpu.PrefetchScalarGridSpec(
        num_scalar_prefetch=1,
        grid=(steps,),
        in_specs=[
            pl.BlockSpec((rows, width), lambda j, d: (0, 0)),
            pl.BlockSpec((KEY_BLOCK, HEAD_DIM), lambda j, d: (clamp(j, d), 0)),
            pl.BlockSpec((KEY_BLOCK, HEAD_DIM), lambda j, d: (clamp(j, d), 1)),
            pl.BlockSpec((1, rows), lambda j, d: (0, lax.axis_index("seq"))),
            pl.BlockSpec((1, KEY_BLOCK), lambda j, d: (0, clamp(j, d))),
        ],
        out_specs=pl.BlockSpec((rows, width), lambda j, d: (0, 0)),
        scratch_shapes=[
            pltpu.VMEM((heads, rows, 1), jnp.float32),
            pltpu.VMEM((heads, rows, 1), jnp.float32),
            pltpu.VMEM((rows, width), jnp.float32),
            pltpu.VMEM((rows, 1), jnp.int32),
        ],
    )
    flops = 4 * rows * width * key_rows // 2
    doc_row = doc_ids.reshape(1, -1)
    return pl.pallas_call(
        flash_kernel,
        out_shape=jax.ShapeDtypeStruct((rows, width), jnp.bfloat16),
        grid_spec=grid_spec,
        compiler_params=pltpu.CompilerParams(dimension_semantics=("arbitrary",)),
        cost_estimate=pl.CostEstimate(
            flops=flops, transcendentals=rows * heads * key_rows // 2,
            bytes_accessed=2 * (2 * rows * width + key_rows * 2 * HEAD_DIM),
        ),
    )(doc_ids, queries, keyval, keyval, doc_row, doc_row)


def solution(mesh):
    in_specs = (
        P("seq", None),
        P(("seq", "vis"), None),
        P(("seq", "vis")),
        P(("seq", "vis")),
        P(),
        P(),
        P(None, "vis"),
        P("vis"),
        P(None, "vis"),
        P(None, "vis"),
        P("vis"),
    )
    out_specs = P("seq", "vis")
    return jax.shard_map(
        on_device, mesh=mesh, in_specs=in_specs, out_specs=out_specs, check_vma=False
    )
```

```python
import jax
import jax.numpy as jnp
from jax import lax
from jax.sharding import PartitionSpec as P
from jax.experimental import pallas as pl
from jax.experimental.pallas import tpu as pltpu

HEAD_DIM = 128


epsilon = 1e-06
negative = -1e30


def frame_slots(frames, tile_pos, frame_count, shard_rows, owners, capacity):
    row_count = frames.shape[0]
    row_ids = jnp.arange(row_count, dtype=jnp.int32)
    usable = row_ids < frame_count[0]
    owner = jnp.where(usable, tile_pos // shard_rows, owners)
    hits = (owner[:, None] == jnp.arange(owners, dtype=jnp.int32)[None, :]).astype(jnp.int32)
    earlier = (row_ids[:, None] > row_ids[None, :]).astype(jnp.int32)
    before = jnp.dot(earlier, hits, preferred_element_type=jnp.int32)
    rank = jnp.sum(before * hits, axis=1)
    slot_index = owner * capacity + rank
    slot_ids = jnp.arange(owners * capacity, dtype=jnp.int32)
    match = usable[:, None] & (slot_index[:, None] == slot_ids[None, :])
    filled = jnp.any(match, axis=0)
    local = tile_pos - owner * shard_rows
    slot_local = jnp.sum(jnp.where(match, local[:, None], 0), axis=0)
    slot_local = jnp.where(filled, slot_local, -1)
    slot_rows = jnp.dot(
        match.T.astype(frames.dtype), frames, preferred_element_type=jnp.float32
    ).astype(frames.dtype)
    place_col = jnp.broadcast_to(slot_local[:, None], (slot_local.shape[0], 128)).astype(frames.dtype)
    payload = jnp.concatenate([slot_rows, place_col], axis=1)
    return payload.reshape(owners, capacity, payload.shape[1])


def place_frames(text, incoming, incoming_place, width):
    lookup = incoming_place[None] == jnp.arange(text.shape[0], dtype=jnp.int32)[:, None, None]
    covered = jnp.any(lookup, axis=(1, 2))
    placed = lax.dot_general(
        lookup.astype(incoming.dtype), incoming, (((1, 2), (0, 1)), ((), ())),
        preferred_element_type=jnp.float32,
    )[:, :width].astype(text.dtype)
    return jnp.where(covered[:, None], placed, text)


def exchange_kernel(payload_ref, out_ref, send_a, recv_a, send_b, recv_b, local_sem):
    seq_count = lax.axis_size("seq")
    vis_count = lax.axis_size("vis")
    ring = vis_count // 2
    me_seq = lax.axis_index("seq")
    me_vis = lax.axis_index("vis")
    ring_pos = lax.rem(me_vis, ring)
    ring_id = me_vis // ring

    def vis_of(ring_index, position):
        return ring_index * ring + lax.rem(position + ring, ring)

    right = vis_of(ring_id, ring_pos + 1)
    left = vis_of(ring_id, ring_pos - 1)
    partner = vis_of(1 - ring_id, ring_pos)
    barrier = pltpu.get_barrier_semaphore()
    for k in range(1, seq_count):
        pl.semaphore_signal(
            barrier, inc=1, device_id=(lax.rem(me_seq + k, seq_count), me_vis),
            device_id_type=pl.DeviceIdType.MESH,
        )
    for peer in (left, right, partner):
        pl.semaphore_signal(
            barrier, inc=1, device_id=(me_seq, peer), device_id_type=pl.DeviceIdType.MESH
        )
    pl.semaphore_wait(barrier, seq_count + 2)
    base = me_vis * seq_count
    local = pltpu.make_async_copy(payload_ref.at[me_seq], out_ref.at[base + me_seq], local_sem.at[0])
    local.start()
    first = []
    for k in range(1, seq_count):
        target = lax.rem(me_seq + k, seq_count)
        copy = pltpu.make_async_remote_copy(
            src_ref=payload_ref.at[target],
            dst_ref=out_ref.at[base + me_seq],
            send_sem=send_a.at[k],
            recv_sem=recv_a.at[k],
            device_id=(target, me_vis),
            device_id_type=pl.DeviceIdType.MESH,
        )
        copy.start()
        first.append(copy)
    local.wait()
    for k in range(1, seq_count):
        source = lax.rem(me_seq + seq_count - k, seq_count)
        incoming = pltpu.make_async_remote_copy(
            src_ref=payload_ref.at[source],
            dst_ref=out_ref.at[base + source],
            send_sem=send_a.at[k],
            recv_sem=recv_a.at[k],
            device_id=(source, me_vis),
            device_id_type=pl.DeviceIdType.MESH,
        )
        incoming.wait_recv()
    for copy in first:
        copy.wait_send()

    half = seq_count // 2

    def region(owner, part):
        if part == 0:
            return out_ref.at[pl.ds(owner * seq_count, seq_count)]
        start = owner * seq_count + (part - 1) * half
        return out_ref.at[pl.ds(start, half)]

    def link(owner, part, peer, index):
        piece = region(owner, part)
        return pltpu.make_async_remote_copy(
            src_ref=piece,
            dst_ref=piece,
            send_sem=send_b.at[index],
            recv_sem=recv_b.at[index],
            device_id=(me_seq, peer),
            device_id_type=pl.DeviceIdType.MESH,
        )

    far = vis_of(ring_id, ring_pos + 2)
    left_partner = vis_of(1 - ring_id, ring_pos - 1)
    right_partner = vis_of(1 - ring_id, ring_pos + 1)
    far_partner = vis_of(1 - ring_id, ring_pos + 2)
    sent = []

    def send(owner, part, peer, index):
        copy = link(owner, part, peer, index)
        copy.start()
        sent.append(copy)

    send(me_vis, 0, right, 1)
    send(me_vis, 0, left, 2)
    send(me_vis, 0, partner, 3)
    link(partner, 0, partner, 3).wait_recv()
    send(partner, 0, right, 4)
    send(partner, 0, left, 5)
    link(left, 0, left, 1).wait_recv()
    send(left, 1, right, 6)
    link(right, 0, right, 2).wait_recv()
    send(right, 2, left, 7)
    link(left_partner, 0, left, 4).wait_recv()
    send(left_partner, 1, right, 8)
    link(right_partner, 0, right, 5).wait_recv()
    send(right_partner, 2, left, 9)
    link(far, 1, left, 6).wait_recv()
    link(far, 2, right, 7).wait_recv()
    link(far_partner, 1, left, 8).wait_recv()
    link(far_partner, 2, right, 9).wait_recv()
    for copy in sent:
        copy.wait_send()


def exchange_frames(payload, vis_count):
    owners, capacity, width = payload.shape
    return pl.pallas_call(
        exchange_kernel,
        out_shape=jax.ShapeDtypeStruct((vis_count * owners, capacity, width), payload.dtype),
        in_specs=[pl.BlockSpec(memory_space=pl.ANY)],
        out_specs=pl.BlockSpec(memory_space=pl.ANY),
        scratch_shapes=[
            pltpu.SemaphoreType.DMA((owners,)),
            pltpu.SemaphoreType.DMA((owners,)),
            pltpu.SemaphoreType.DMA((10,)),
            pltpu.SemaphoreType.DMA((10,)),
            pltpu.SemaphoreType.DMA((1,)),
        ],
        compiler_params=pltpu.CompilerParams(collective_id=1, has_side_effects=True),
    )(payload)


def gather_kernel(
    block_ref, normed_ref, w_ref, bias_ref, out_ref, q_ref, send_sem, recv_sem, local_sem, acc_ref
):
    rows = block_ref.shape[0]
    me_seq = lax.axis_index("seq")
    me_vis = lax.axis_index("vis")
    column = me_seq // 4
    layer = lax.rem(me_seq // 2, 2)
    core = lax.rem(me_seq, 2)
    ring = lax.axis_size("seq") // 4

    def seq_of(y, z, c):
        return (lax.rem(y + ring, ring) * 2 + z) * 2 + c

    mate = seq_of(column, layer, 1 - core)
    across = seq_of(column, 1 - layer, core)
    diagonal = seq_of(column, 1 - layer, 1 - core)
    up = seq_of(column + 1, layer, core)
    down = seq_of(column - 1, layer, core)
    barrier = pltpu.get_barrier_semaphore()
    for peer in (mate, across, diagonal, up, down):
        pl.semaphore_signal(
            barrier, inc=1, device_id=(peer, me_vis), device_id_type=pl.DeviceIdType.MESH
        )
    pl.semaphore_wait(barrier, 5)

    def rows_of(start, count):
        return out_ref.at[pl.ds(pl.multiple_of(start, rows), count)]

    def link(src, dst, peer, index):
        return pltpu.make_async_remote_copy(
            src_ref=src, dst_ref=dst, send_sem=send_sem.at[index], recv_sem=recv_sem.at[index],
            device_id=(peer, me_vis), device_id_type=pl.DeviceIdType.MESH,
        )

    sent = []

    def send(src, dst, peer, index):
        copy = link(src, dst, peer, index)
        copy.start()
        sent.append(copy)

    own = rows_of(me_seq * rows, rows)
    local = pltpu.make_async_copy(block_ref, own, local_sem.at[0])
    local.start()
    send(block_ref, own, mate, 0)
    send(block_ref, own, across, 1)
    send(block_ref, own, diagonal, 2)
    depth = normed_ref.shape[1] // 2

    def project(part):
        def body(n_blk, w_blk):
            acc_ref[...] += jnp.dot(n_blk[...], w_blk[...], preferred_element_type=jnp.float32)

        pltpu.emit_pipeline(
            body,
            grid=(depth // PROJ_TILE,),
            in_specs=[
                pl.BlockSpec((normed_ref.shape[0], PROJ_TILE), lambda k: (0, k)),
                pl.BlockSpec((PROJ_TILE, w_ref.shape[1]), lambda k: (k, 0)),
            ],
        )(normed_ref.at[:, pl.ds(part * depth, depth)], w_ref.at[pl.ds(part * depth, depth)])

    acc_ref[...] = jnp.zeros(acc_ref.shape, jnp.float32)
    project(0)
    local.wait()
    link(block_ref, rows_of(mate * rows, rows), mate, 0).wait_recv()
    link(block_ref, rows_of(across * rows, rows), across, 1).wait_recv()
    link(block_ref, rows_of(diagonal * rows, rows), diagonal, 2).wait_recv()

    def half(y, h):
        return rows_of((lax.rem(y + ring, ring) * 4 + h * 2) * rows, 2 * rows)

    def quarter(y, h, q):
        return rows_of((lax.rem(y + ring, ring) * 4 + h * 2 + q) * rows, rows)

    mine = half(column, core)
    send(mine, mine, up, 3)
    send(mine, mine, down, 4)
    project(1)
    below = half(column - 1, core)
    link(below, below, down, 3).wait_recv()
    send(below, below, mate, 7)
    piece = quarter(column - 1, core, 0)
    send(piece, piece, up, 5)
    above = half(column + 1, core)
    link(above, above, up, 4).wait_recv()
    send(above, above, mate, 9)
    piece = quarter(column + 1, core, 1)
    send(piece, piece, down, 6)
    q_ref[...] = (acc_ref[...] + bias_ref[...]).astype(q_ref.dtype)
    far_low = quarter(column + 2, core, 0)
    far_high = quarter(column + 2, core, 1)
    link(far_low, far_low, down, 5).wait_recv()
    link(far_high, far_high, up, 6).wait_recv()
    far = half(column + 2, core)
    send(far, far, mate, 8)
    for offset, index in ((-1, 7), (2, 8), (1, 9)):
        theirs = half(column + offset, 1 - core)
        link(theirs, theirs, mate, index).wait_recv()
    for copy in sent:
        copy.wait_send()


PROJ_TILE = 512


def gather_keys(block, normed, w_query, q_bias, seq_count):
    rows, width = block.shape
    return pl.pallas_call(
        gather_kernel,
        out_shape=(
            jax.ShapeDtypeStruct((seq_count * rows, width), block.dtype),
            jax.ShapeDtypeStruct((normed.shape[0], w_query.shape[1]), jnp.bfloat16),
        ),
        in_specs=[
            pl.BlockSpec(memory_space=pl.ANY),
            pl.BlockSpec(memory_space=pl.ANY),
            pl.BlockSpec(memory_space=pl.ANY),
            pl.BlockSpec(memory_space=pltpu.VMEM),
        ],
        out_specs=(pl.BlockSpec(memory_space=pl.ANY), pl.BlockSpec(memory_space=pltpu.VMEM)),
        scratch_shapes=[
            pltpu.SemaphoreType.DMA((10,)),
            pltpu.SemaphoreType.DMA((10,)),
            pltpu.SemaphoreType.DMA((1,)),
            pltpu.VMEM((normed.shape[0], w_query.shape[1]), jnp.float32),
        ],
        compiler_params=pltpu.CompilerParams(collective_id=2, has_side_effects=True),
    )(block, normed, w_query, q_bias.reshape(1, -1))


def on_device(
    text, frames, tile_pos, frame_count, doc_ids, norm_gain, w_query, q_bias, w_key, w_value, v_bias
):
    seq_count = lax.axis_size("seq")
    vis_count = lax.axis_size("vis")
    shard_index = lax.axis_index("seq")
    shard_rows = text.shape[0]
    capacity = shard_rows // (seq_count * vis_count)
    first_row = shard_index * shard_rows
    payload = frame_slots(frames, tile_pos, frame_count, shard_rows, seq_count, capacity)
    gathered = exchange_frames(payload, vis_count)
    width = text.shape[1]
    incoming_place = gathered[:, :, width].astype(jnp.int32)
    merged = place_frames(text, gathered, incoming_place, width)
    widened = merged.astype(jnp.float32)
    mean_square = jnp.mean(widened * widened, axis=1, keepdims=True)
    normed = (widened * lax.rsqrt(mean_square + epsilon) * norm_gain).astype(jnp.bfloat16)
    key_rows = jnp.dot(normed, w_key, preferred_element_type=jnp.float32).astype(jnp.bfloat16)
    value_rows = (jnp.dot(normed, w_value, preferred_element_type=jnp.float32) + v_bias).astype(
        jnp.bfloat16
    )
    keyval = jnp.concatenate([key_rows, value_rows], axis=1)
    kv_heads = w_key.shape[1] // HEAD_DIM
    per_group = w_query.shape[1] // HEAD_DIM // kv_heads
    incoming_keys, queries = gather_keys(keyval, normed, w_query, q_bias, seq_count)
    return flash_attention(doc_ids, queries, incoming_keys)


KEY_BLOCK = 512
DOC_SPAN = 2048


def block_bounds(doc_ref, rows, key_rows):
    first = lax.axis_index("seq") * rows
    first_doc = doc_ref[first]
    low = 0
    for b in range(key_rows // KEY_BLOCK):
        low = low + (doc_ref[(b + 1) * KEY_BLOCK - 1] < first_doc).astype(jnp.int32)
    return low, (first + rows - 1) // KEY_BLOCK, first


def flash_kernel(doc_ref, q_ref, k_ref, v_ref, qdoc_ref, kdoc_ref, out_ref, peak_ref, total_ref, acc_ref, qcol_ref):
    step = pl.program_id(0)
    rows = q_ref.shape[0]
    heads = q_ref.shape[1] // HEAD_DIM
    low, high, first = block_bounds(doc_ref, rows, doc_ref.shape[0])
    block = low + step

    @pl.when(step == 0)
    def _():
        peak_ref[...] = jnp.full(peak_ref.shape, negative, jnp.float32)
        total_ref[...] = jnp.zeros(total_ref.shape, jnp.float32)
        acc_ref[...] = jnp.zeros(acc_ref.shape, jnp.float32)
        spread = jnp.broadcast_to(qdoc_ref[...], (rows, rows))
        diagonal = lax.broadcasted_iota(jnp.int32, (rows, rows), 0) == lax.broadcasted_iota(
            jnp.int32, (rows, rows), 1
        )
        qcol_ref[...] = jnp.sum(jnp.where(diagonal, spread, 0), axis=1, keepdims=True)

    @pl.when(block <= high)
    def _():
        key_place = block * KEY_BLOCK + lax.broadcasted_iota(jnp.int32, (1, KEY_BLOCK), 1)
        query_place = first + lax.broadcasted_iota(jnp.int32, (rows, 1), 0)
        allowed = (key_place <= query_place) & (kdoc_ref[...] == qcol_ref[...])
        keys = k_ref[...]
        vals = v_ref[...]
        for h in range(heads):
            cols = slice(h * HEAD_DIM, (h + 1) * HEAD_DIM)
            scores = lax.dot_general(
                q_ref[:, cols], keys, (((1,), (1,)), ((), ())),
                preferred_element_type=jnp.float32,
            ) * HEAD_DIM ** (-0.5)
            scores = jnp.where(allowed, scores, negative)
            old_peak = peak_ref[h]
            new_peak = jnp.maximum(old_peak, jnp.max(scores, axis=1, keepdims=True))
            raised = jnp.where(allowed, jnp.exp(scores - new_peak[:, :1]), 0.0)
            factor = jnp.exp(old_peak - new_peak)
            total_ref[h] = total_ref[h] * factor + jnp.sum(raised, axis=1, keepdims=True)
            peak_ref[h] = new_peak
            product = jnp.dot(raised.astype(jnp.bfloat16), vals, preferred_element_type=jnp.float32)
            acc_ref[:, cols] = acc_ref[:, cols] * factor[:, :1] + product

    @pl.when(step == pl.num_programs(0) - 1)
    def _():
        for h in range(heads):
            cols = slice(h * HEAD_DIM, (h + 1) * HEAD_DIM)
            out_ref[:, cols] = (acc_ref[:, cols] / total_ref[h][:, :1]).astype(out_ref.dtype)


def flash_attention(doc_ids, queries, keyval):
    rows, width = queries.shape
    key_rows = keyval.shape[0]
    steps = min(key_rows // KEY_BLOCK, (DOC_SPAN + rows - 2) // KEY_BLOCK + 2)
    heads = width // HEAD_DIM

    def clamp(j, d):
        low, high, _ = block_bounds(d, rows, key_rows)
        return jnp.minimum(low + j, high)

    grid_spec = pltpu.PrefetchScalarGridSpec(
        num_scalar_prefetch=1,
        grid=(steps,),
        in_specs=[
            pl.BlockSpec((rows, width), lambda j, d: (0, 0)),
            pl.BlockSpec((KEY_BLOCK, HEAD_DIM), lambda j, d: (clamp(j, d), 0)),
            pl.BlockSpec((KEY_BLOCK, HEAD_DIM), lambda j, d: (clamp(j, d), 1)),
            pl.BlockSpec((1, rows), lambda j, d: (0, lax.axis_index("seq"))),
            pl.BlockSpec((1, KEY_BLOCK), lambda j, d: (0, clamp(j, d))),
        ],
        out_specs=pl.BlockSpec((rows, width), lambda j, d: (0, 0)),
        scratch_shapes=[
            pltpu.VMEM((heads, rows, 1), jnp.float32),
            pltpu.VMEM((heads, rows, 1), jnp.float32),
            pltpu.VMEM((rows, width), jnp.float32),
            pltpu.VMEM((rows, 1), jnp.int32),
        ],
    )
    flops = 4 * rows * width * key_rows // 2
    doc_row = doc_ids.reshape(1, -1)
    return pl.pallas_call(
        flash_kernel,
        out_shape=jax.ShapeDtypeStruct((rows, width), jnp.bfloat16),
        grid_spec=grid_spec,
        compiler_params=pltpu.CompilerParams(dimension_semantics=("arbitrary",)),
        cost_estimate=pl.CostEstimate(
            flops=flops, transcendentals=rows * heads * key_rows // 2,
            bytes_accessed=2 * (2 * rows * width + key_rows * 2 * HEAD_DIM),
        ),
    )(doc_ids, queries, keyval, keyval, doc_row, doc_row)


def solution(mesh):
    in_specs = (
        P("seq", None),
        P(("seq", "vis"), None),
        P(("seq", "vis")),
        P(("seq", "vis")),
        P(),
        P(),
        P(None, "vis"),
        P("vis"),
        P(None, "vis"),
        P(None, "vis"),
        P("vis"),
    )
    out_specs = P("seq", "vis")
    return jax.shard_map(
        on_device, mesh=mesh, in_specs=in_specs, out_specs=out_specs, check_vma=False
    )
```

```python
import jax
import jax.numpy as jnp
from jax import lax
from jax.sharding import PartitionSpec as P
from jax.experimental import pallas as pl
from jax.experimental.pallas import tpu as pltpu

HEAD_DIM = 128


epsilon = 1e-06
negative = -1e30


def frame_slots(frames, tile_pos, frame_count, shard_rows, owners, capacity):
    row_count = frames.shape[0]
    row_ids = jnp.arange(row_count, dtype=jnp.int32)
    usable = row_ids < frame_count[0]
    owner = jnp.where(usable, tile_pos // shard_rows, owners)
    hits = (owner[:, None] == jnp.arange(owners, dtype=jnp.int32)[None, :]).astype(jnp.int32)
    earlier = (row_ids[:, None] > row_ids[None, :]).astype(jnp.int32)
    before = jnp.dot(earlier, hits, preferred_element_type=jnp.int32)
    rank = jnp.sum(before * hits, axis=1)
    slot_index = owner * capacity + rank
    slot_ids = jnp.arange(owners * capacity, dtype=jnp.int32)
    match = usable[:, None] & (slot_index[:, None] == slot_ids[None, :])
    filled = jnp.any(match, axis=0)
    local = tile_pos - owner * shard_rows
    slot_local = jnp.sum(jnp.where(match, local[:, None], 0), axis=0)
    slot_local = jnp.where(filled, slot_local, -1)
    slot_rows = jnp.dot(
        match.T.astype(frames.dtype), frames, preferred_element_type=jnp.float32
    ).astype(frames.dtype)
    place_col = jnp.broadcast_to(slot_local[:, None], (slot_local.shape[0], 128)).astype(frames.dtype)
    payload = jnp.concatenate([slot_rows, place_col], axis=1)
    return payload.reshape(owners, capacity, payload.shape[1])


def place_frames(text, incoming, incoming_place, width):
    lookup = incoming_place[None] == jnp.arange(text.shape[0], dtype=jnp.int32)[:, None, None]
    covered = jnp.any(lookup, axis=(1, 2))
    placed = lax.dot_general(
        lookup.astype(incoming.dtype), incoming, (((1, 2), (0, 1)), ((), ())),
        preferred_element_type=jnp.float32,
    )[:, :width].astype(text.dtype)
    return jnp.where(covered[:, None], placed, text)


def exchange_kernel(payload_ref, out_ref, send_a, recv_a, send_b, recv_b, local_sem):
    seq_count = lax.axis_size("seq")
    vis_count = lax.axis_size("vis")
    ring = vis_count // 2
    me_seq = lax.axis_index("seq")
    me_vis = lax.axis_index("vis")
    ring_pos = lax.rem(me_vis, ring)
    ring_id = me_vis // ring

    def vis_of(ring_index, position):
        return ring_index * ring + lax.rem(position + ring, ring)

    right = vis_of(ring_id, ring_pos + 1)
    left = vis_of(ring_id, ring_pos - 1)
    partner = vis_of(1 - ring_id, ring_pos)
    barrier = pltpu.get_barrier_semaphore()
    for k in range(1, seq_count):
        pl.semaphore_signal(
            barrier, inc=1, device_id=(lax.rem(me_seq + k, seq_count), me_vis),
            device_id_type=pl.DeviceIdType.MESH,
        )
    for peer in (left, right, partner):
        pl.semaphore_signal(
            barrier, inc=1, device_id=(me_seq, peer), device_id_type=pl.DeviceIdType.MESH
        )
    pl.semaphore_wait(barrier, seq_count + 2)
    base = me_vis * seq_count
    local = pltpu.make_async_copy(payload_ref.at[me_seq], out_ref.at[base + me_seq], local_sem.at[0])
    local.start()
    first = []
    for k in range(1, seq_count):
        target = lax.rem(me_seq + k, seq_count)
        copy = pltpu.make_async_remote_copy(
            src_ref=payload_ref.at[target],
            dst_ref=out_ref.at[base + me_seq],
            send_sem=send_a.at[k],
            recv_sem=recv_a.at[k],
            device_id=(target, me_vis),
            device_id_type=pl.DeviceIdType.MESH,
        )
        copy.start()
        first.append(copy)
    local.wait()
    for k in range(1, seq_count):
        source = lax.rem(me_seq + seq_count - k, seq_count)
        incoming = pltpu.make_async_remote_copy(
            src_ref=payload_ref.at[source],
            dst_ref=out_ref.at[base + source],
            send_sem=send_a.at[k],
            recv_sem=recv_a.at[k],
            device_id=(source, me_vis),
            device_id_type=pl.DeviceIdType.MESH,
        )
        incoming.wait_recv()
    for copy in first:
        copy.wait_send()

    half = seq_count // 2

    def region(owner, part):
        if part == 0:
            return out_ref.at[pl.ds(owner * seq_count, seq_count)]
        start = owner * seq_count + (part - 1) * half
        return out_ref.at[pl.ds(start, half)]

    def link(owner, part, peer, index):
        piece = region(owner, part)
        return pltpu.make_async_remote_copy(
            src_ref=piece,
            dst_ref=piece,
            send_sem=send_b.at[index],
            recv_sem=recv_b.at[index],
            device_id=(me_seq, peer),
            device_id_type=pl.DeviceIdType.MESH,
        )

    far = vis_of(ring_id, ring_pos + 2)
    left_partner = vis_of(1 - ring_id, ring_pos - 1)
    right_partner = vis_of(1 - ring_id, ring_pos + 1)
    far_partner = vis_of(1 - ring_id, ring_pos + 2)
    sent = []

    def send(owner, part, peer, index):
        copy = link(owner, part, peer, index)
        copy.start()
        sent.append(copy)

    send(me_vis, 0, right, 1)
    send(me_vis, 0, left, 2)
    send(me_vis, 0, partner, 3)
    link(left, 0, left, 1).wait_recv()
    send(left, 1, right, 6)
    link(right, 0, right, 2).wait_recv()
    send(right, 2, left, 7)
    link(partner, 0, partner, 3).wait_recv()
    send(partner, 0, right, 4)
    send(partner, 0, left, 5)
    link(left_partner, 0, left, 4).wait_recv()
    send(left_partner, 1, right, 8)
    link(right_partner, 0, right, 5).wait_recv()
    send(right_partner, 2, left, 9)
    link(far, 1, left, 6).wait_recv()
    link(far, 2, right, 7).wait_recv()
    link(far_partner, 1, left, 8).wait_recv()
    link(far_partner, 2, right, 9).wait_recv()
    for copy in sent:
        copy.wait_send()


def exchange_frames(payload, vis_count):
    owners, capacity, width = payload.shape
    return pl.pallas_call(
        exchange_kernel,
        out_shape=jax.ShapeDtypeStruct((vis_count * owners, capacity, width), payload.dtype),
        in_specs=[pl.BlockSpec(memory_space=pl.ANY)],
        out_specs=pl.BlockSpec(memory_space=pl.ANY),
        scratch_shapes=[
            pltpu.SemaphoreType.DMA((owners,)),
            pltpu.SemaphoreType.DMA((owners,)),
            pltpu.SemaphoreType.DMA((10,)),
            pltpu.SemaphoreType.DMA((10,)),
            pltpu.SemaphoreType.DMA((1,)),
        ],
        compiler_params=pltpu.CompilerParams(collective_id=1, has_side_effects=True),
    )(payload)


def gather_kernel(
    block_ref, normed_ref, w_ref, bias_ref, out_ref, q_ref, send_sem, recv_sem, local_sem, acc_ref
):
    rows = block_ref.shape[0]
    me_seq = lax.axis_index("seq")
    me_vis = lax.axis_index("vis")
    column = me_seq // 4
    layer = lax.rem(me_seq // 2, 2)
    core = lax.rem(me_seq, 2)
    ring = lax.axis_size("seq") // 4

    def seq_of(y, z, c):
        return (lax.rem(y + ring, ring) * 2 + z) * 2 + c

    mate = seq_of(column, layer, 1 - core)
    across = seq_of(column, 1 - layer, core)
    diagonal = seq_of(column, 1 - layer, 1 - core)
    up = seq_of(column + 1, layer, core)
    down = seq_of(column - 1, layer, core)
    barrier = pltpu.get_barrier_semaphore()
    for peer in (mate, across, diagonal, up, down):
        pl.semaphore_signal(
            barrier, inc=1, device_id=(peer, me_vis), device_id_type=pl.DeviceIdType.MESH
        )
    pl.semaphore_wait(barrier, 5)

    def rows_of(start, count):
        return out_ref.at[pl.ds(pl.multiple_of(start, rows), count)]

    def link(src, dst, peer, index):
        return pltpu.make_async_remote_copy(
            src_ref=src, dst_ref=dst, send_sem=send_sem.at[index], recv_sem=recv_sem.at[index],
            device_id=(peer, me_vis), device_id_type=pl.DeviceIdType.MESH,
        )

    sent = []

    def send(src, dst, peer, index):
        copy = link(src, dst, peer, index)
        copy.start()
        sent.append(copy)

    own = rows_of(me_seq * rows, rows)
    local = pltpu.make_async_copy(block_ref, own, local_sem.at[0])
    local.start()
    send(block_ref, own, mate, 0)
    send(block_ref, own, across, 1)
    send(block_ref, own, diagonal, 2)
    depth = normed_ref.shape[1] // 2

    def project(part):
        def body(n_blk, w_blk):
            acc_ref[...] += jnp.dot(n_blk[...], w_blk[...], preferred_element_type=jnp.float32)

        pltpu.emit_pipeline(
            body,
            grid=(depth // PROJ_TILE,),
            in_specs=[
                pl.BlockSpec((normed_ref.shape[0], PROJ_TILE), lambda k: (0, k)),
                pl.BlockSpec((PROJ_TILE, w_ref.shape[1]), lambda k: (k, 0)),
            ],
        )(normed_ref.at[:, pl.ds(part * depth, depth)], w_ref.at[pl.ds(part * depth, depth)])

    acc_ref[...] = jnp.zeros(acc_ref.shape, jnp.float32)
    project(0)
    local.wait()
    link(block_ref, rows_of(mate * rows, rows), mate, 0).wait_recv()
    link(block_ref, rows_of(across * rows, rows), across, 1).wait_recv()
    link(block_ref, rows_of(diagonal * rows, rows), diagonal, 2).wait_recv()

    def half(y, h):
        return rows_of((lax.rem(y + ring, ring) * 4 + h * 2) * rows, 2 * rows)

    def quarter(y, h, q):
        return rows_of((lax.rem(y + ring, ring) * 4 + h * 2 + q) * rows, rows)

    mine = half(column, core)
    send(mine, mine, up, 3)
    send(mine, mine, down, 4)
    project(1)
    below = half(column - 1, core)
    link(below, below, down, 3).wait_recv()
    send(below, below, mate, 7)
    piece = quarter(column - 1, core, 0)
    send(piece, piece, up, 5)
    above = half(column + 1, core)
    link(above, above, up, 4).wait_recv()
    send(above, above, mate, 9)
    piece = quarter(column + 1, core, 1)
    send(piece, piece, down, 6)
    q_ref[...] = (acc_ref[...] + bias_ref[...]).astype(q_ref.dtype)
    far_low = quarter(column + 2, core, 0)
    far_high = quarter(column + 2, core, 1)
    link(far_low, far_low, down, 5).wait_recv()
    link(far_high, far_high, up, 6).wait_recv()
    far = half(column + 2, core)
    send(far, far, mate, 8)
    for offset, index in ((-1, 7), (2, 8), (1, 9)):
        theirs = half(column + offset, 1 - core)
        link(theirs, theirs, mate, index).wait_recv()
    for copy in sent:
        copy.wait_send()


PROJ_TILE = 512


def gather_keys(block, normed, w_query, q_bias, seq_count):
    rows, width = block.shape
    return pl.pallas_call(
        gather_kernel,
        out_shape=(
            jax.ShapeDtypeStruct((seq_count * rows, width), block.dtype),
            jax.ShapeDtypeStruct((normed.shape[0], w_query.shape[1]), jnp.bfloat16),
        ),
        in_specs=[
            pl.BlockSpec(memory_space=pl.ANY),
            pl.BlockSpec(memory_space=pl.ANY),
            pl.BlockSpec(memory_space=pl.ANY),
            pl.BlockSpec(memory_space=pltpu.VMEM),
        ],
        out_specs=(pl.BlockSpec(memory_space=pl.ANY), pl.BlockSpec(memory_space=pltpu.VMEM)),
        scratch_shapes=[
            pltpu.SemaphoreType.DMA((10,)),
            pltpu.SemaphoreType.DMA((10,)),
            pltpu.SemaphoreType.DMA((1,)),
            pltpu.VMEM((normed.shape[0], w_query.shape[1]), jnp.float32),
        ],
        compiler_params=pltpu.CompilerParams(collective_id=2, has_side_effects=True),
    )(block, normed, w_query, q_bias.reshape(1, -1))


def on_device(
    text, frames, tile_pos, frame_count, doc_ids, norm_gain, w_query, q_bias, w_key, w_value, v_bias
):
    seq_count = lax.axis_size("seq")
    vis_count = lax.axis_size("vis")
    shard_index = lax.axis_index("seq")
    shard_rows = text.shape[0]
    capacity = shard_rows // (seq_count * vis_count)
    first_row = shard_index * shard_rows
    payload = frame_slots(frames, tile_pos, frame_count, shard_rows, seq_count, capacity)
    gathered = exchange_frames(payload, vis_count)
    width = text.shape[1]
    incoming_place = gathered[:, :, width].astype(jnp.int32)
    merged = place_frames(text, gathered, incoming_place, width)
    widened = merged.astype(jnp.float32)
    mean_square = jnp.mean(widened * widened, axis=1, keepdims=True)
    normed = (widened * lax.rsqrt(mean_square + epsilon) * norm_gain).astype(jnp.bfloat16)
    key_rows = jnp.dot(normed, w_key, preferred_element_type=jnp.float32).astype(jnp.bfloat16)
    value_rows = (jnp.dot(normed, w_value, preferred_element_type=jnp.float32) + v_bias).astype(
        jnp.bfloat16
    )
    keyval = jnp.concatenate([key_rows, value_rows], axis=1)
    kv_heads = w_key.shape[1] // HEAD_DIM
    per_group = w_query.shape[1] // HEAD_DIM // kv_heads
    incoming_keys, queries = gather_keys(keyval, normed, w_query, q_bias, seq_count)
    return flash_attention(doc_ids, queries, incoming_keys)


KEY_BLOCK = 512
DOC_SPAN = 2048


def block_bounds(doc_ref, rows, key_rows):
    first = lax.axis_index("seq") * rows
    first_doc = doc_ref[first]
    low = 0
    for b in range(key_rows // KEY_BLOCK):
        low = low + (doc_ref[(b + 1) * KEY_BLOCK - 1] < first_doc).astype(jnp.int32)
    return low, (first + rows - 1) // KEY_BLOCK, first


def flash_kernel(doc_ref, q_ref, k_ref, v_ref, qdoc_ref, kdoc_ref, out_ref, peak_ref, total_ref, acc_ref, qcol_ref):
    step = pl.program_id(0)
    rows = q_ref.shape[0]
    heads = q_ref.shape[1] // HEAD_DIM
    low, high, first = block_bounds(doc_ref, rows, doc_ref.shape[0])
    block = low + step

    @pl.when(step == 0)
    def _():
        peak_ref[...] = jnp.full(peak_ref.shape, negative, jnp.float32)
        total_ref[...] = jnp.zeros(total_ref.shape, jnp.float32)
        acc_ref[...] = jnp.zeros(acc_ref.shape, jnp.float32)
        spread = jnp.broadcast_to(qdoc_ref[...], (rows, rows))
        diagonal = lax.broadcasted_iota(jnp.int32, (rows, rows), 0) == lax.broadcasted_iota(
            jnp.int32, (rows, rows), 1
        )
        qcol_ref[...] = jnp.sum(jnp.where(diagonal, spread, 0), axis=1, keepdims=True)

    @pl.when(block <= high)
    def _():
        key_place = block * KEY_BLOCK + lax.broadcasted_iota(jnp.int32, (1, KEY_BLOCK), 1)
        query_place = first + lax.broadcasted_iota(jnp.int32, (rows, 1), 0)
        allowed = (key_place <= query_place) & (kdoc_ref[...] == qcol_ref[...])
        keys = k_ref[...]
        vals = v_ref[...]
        for h in range(heads):
            cols = slice(h * HEAD_DIM, (h + 1) * HEAD_DIM)
            scores = lax.dot_general(
                q_ref[:, cols], keys, (((1,), (1,)), ((), ())),
                preferred_element_type=jnp.float32,
            ) * HEAD_DIM ** (-0.5)
            scores = jnp.where(allowed, scores, negative)
            old_peak = peak_ref[h]
            new_peak = jnp.maximum(old_peak, jnp.max(scores, axis=1, keepdims=True))
            raised = jnp.where(allowed, jnp.exp(scores - new_peak[:, :1]), 0.0)
            factor = jnp.exp(old_peak - new_peak)
            total_ref[h] = total_ref[h] * factor + jnp.sum(raised, axis=1, keepdims=True)
            peak_ref[h] = new_peak
            product = jnp.dot(raised.astype(jnp.bfloat16), vals, preferred_element_type=jnp.float32)
            acc_ref[:, cols] = acc_ref[:, cols] * factor[:, :1] + product

    @pl.when(step == pl.num_programs(0) - 1)
    def _():
        for h in range(heads):
            cols = slice(h * HEAD_DIM, (h + 1) * HEAD_DIM)
            out_ref[:, cols] = (acc_ref[:, cols] / total_ref[h][:, :1]).astype(out_ref.dtype)


def flash_attention(doc_ids, queries, keyval):
    rows, width = queries.shape
    key_rows = keyval.shape[0]
    steps = min(key_rows // KEY_BLOCK, (DOC_SPAN + rows - 2) // KEY_BLOCK + 2)
    heads = width // HEAD_DIM

    def clamp(j, d):
        low, high, _ = block_bounds(d, rows, key_rows)
        return jnp.minimum(low + j, high)

    grid_spec = pltpu.PrefetchScalarGridSpec(
        num_scalar_prefetch=1,
        grid=(steps,),
        in_specs=[
            pl.BlockSpec((rows, width), lambda j, d: (0, 0)),
            pl.BlockSpec((KEY_BLOCK, HEAD_DIM), lambda j, d: (clamp(j, d), 0)),
            pl.BlockSpec((KEY_BLOCK, HEAD_DIM), lambda j, d: (clamp(j, d), 1)),
            pl.BlockSpec((1, rows), lambda j, d: (0, lax.axis_index("seq"))),
            pl.BlockSpec((1, KEY_BLOCK), lambda j, d: (0, clamp(j, d))),
        ],
        out_specs=pl.BlockSpec((rows, width), lambda j, d: (0, 0)),
        scratch_shapes=[
            pltpu.VMEM((heads, rows, 1), jnp.float32),
            pltpu.VMEM((heads, rows, 1), jnp.float32),
            pltpu.VMEM((rows, width), jnp.float32),
            pltpu.VMEM((rows, 1), jnp.int32),
        ],
    )
    flops = 4 * rows * width * key_rows // 2
    doc_row = doc_ids.reshape(1, -1)
    return pl.pallas_call(
        flash_kernel,
        out_shape=jax.ShapeDtypeStruct((rows, width), jnp.bfloat16),
        grid_spec=grid_spec,
        compiler_params=pltpu.CompilerParams(dimension_semantics=("arbitrary",)),
        cost_estimate=pl.CostEstimate(
            flops=flops, transcendentals=rows * heads * key_rows // 2,
            bytes_accessed=2 * (2 * rows * width + key_rows * 2 * HEAD_DIM),
        ),
    )(doc_ids, queries, keyval, keyval, doc_row, doc_row)


def solution(mesh):
    in_specs = (
        P("seq", None),
        P(("seq", "vis"), None),
        P(("seq", "vis")),
        P(("seq", "vis")),
        P(),
        P(),
        P(None, "vis"),
        P("vis"),
        P(None, "vis"),
        P(None, "vis"),
        P("vis"),
    )
    out_specs = P("seq", "vis")
    return jax.shard_map(
        on_device, mesh=mesh, in_specs=in_specs, out_specs=out_specs, check_vma=False
    )
```

```python
import jax
import jax.numpy as jnp
from jax import lax
from jax.sharding import PartitionSpec as P
from jax.experimental import pallas as pl
from jax.experimental.pallas import tpu as pltpu

HEAD_DIM = 128


epsilon = 1e-06
negative = -1e30


def frame_slots(frames, tile_pos, frame_count, shard_rows, owners, capacity):
    row_count = frames.shape[0]
    row_ids = jnp.arange(row_count, dtype=jnp.int32)
    usable = row_ids < frame_count[0]
    owner = jnp.where(usable, tile_pos // shard_rows, owners)
    hits = (owner[:, None] == jnp.arange(owners, dtype=jnp.int32)[None, :]).astype(jnp.int32)
    earlier = (row_ids[:, None] > row_ids[None, :]).astype(jnp.int32)
    before = jnp.dot(earlier, hits, preferred_element_type=jnp.int32)
    rank = jnp.sum(before * hits, axis=1)
    slot_index = owner * capacity + rank
    slot_ids = jnp.arange(owners * capacity, dtype=jnp.int32)
    match = usable[:, None] & (slot_index[:, None] == slot_ids[None, :])
    filled = jnp.any(match, axis=0)
    local = tile_pos - owner * shard_rows
    slot_local = jnp.sum(jnp.where(match, local[:, None], 0), axis=0)
    slot_local = jnp.where(filled, slot_local, -1)
    slot_rows = jnp.dot(
        match.T.astype(frames.dtype), frames, preferred_element_type=jnp.float32
    ).astype(frames.dtype)
    place_col = jnp.broadcast_to(slot_local[:, None], (slot_local.shape[0], 128)).astype(frames.dtype)
    payload = jnp.concatenate([slot_rows, place_col], axis=1)
    return payload.reshape(owners, capacity, payload.shape[1])


def place_frames(text, incoming, incoming_place, width):
    lookup = incoming_place[None] == jnp.arange(text.shape[0], dtype=jnp.int32)[:, None, None]
    covered = jnp.any(lookup, axis=(1, 2))
    placed = lax.dot_general(
        lookup.astype(incoming.dtype), incoming, (((1, 2), (0, 1)), ((), ())),
        preferred_element_type=jnp.float32,
    )[:, :width].astype(text.dtype)
    return jnp.where(covered[:, None], placed, text)


def exchange_kernel(payload_ref, out_ref, send_a, recv_a, send_b, recv_b, local_sem, relay):
    seq_count = lax.axis_size("seq")
    vis_count = lax.axis_size("vis")
    ring = vis_count // 2
    me_seq = lax.axis_index("seq")
    me_vis = lax.axis_index("vis")
    ring_pos = lax.rem(me_vis, ring)
    ring_id = me_vis // ring

    def vis_of(ring_index, position):
        return ring_index * ring + lax.rem(position + ring, ring)

    right = vis_of(ring_id, ring_pos + 1)
    left = vis_of(ring_id, ring_pos - 1)
    partner = vis_of(1 - ring_id, ring_pos)
    level = lax.rem(me_seq // 2, 2)
    flip = me_seq + 2 - 4 * level
    lower = (flip, jnp.where(level == 1, me_vis, partner))
    upper = (flip, jnp.where(level == 0, me_vis, partner))
    barrier = pltpu.get_barrier_semaphore()
    for k in range(1, seq_count):
        pl.semaphore_signal(
            barrier, inc=1, device_id=(lax.rem(me_seq + k, seq_count), me_vis),
            device_id_type=pl.DeviceIdType.MESH,
        )
    for peer in (left, right, partner):
        pl.semaphore_signal(
            barrier, inc=1, device_id=(me_seq, peer), device_id_type=pl.DeviceIdType.MESH
        )
    for device in (lower, upper):
        pl.semaphore_signal(barrier, inc=1, device_id=device, device_id_type=pl.DeviceIdType.MESH)
    pl.semaphore_wait(barrier, seq_count + 4)
    base = me_vis * seq_count
    local = pltpu.make_async_copy(payload_ref.at[me_seq], out_ref.at[base + me_seq], local_sem.at[0])
    local.start()
    first = []
    for k in range(1, seq_count):
        target = lax.rem(me_seq + k, seq_count)
        copy = pltpu.make_async_remote_copy(
            src_ref=payload_ref.at[target],
            dst_ref=out_ref.at[base + me_seq],
            send_sem=send_a.at[k],
            recv_sem=recv_a.at[k],
            device_id=(target, me_vis),
            device_id_type=pl.DeviceIdType.MESH,
        )
        copy.start()
        first.append(copy)
    local.wait()
    for k in range(1, seq_count):
        source = lax.rem(me_seq + seq_count - k, seq_count)
        incoming = pltpu.make_async_remote_copy(
            src_ref=payload_ref.at[source],
            dst_ref=out_ref.at[base + source],
            send_sem=send_a.at[k],
            recv_sem=recv_a.at[k],
            device_id=(source, me_vis),
            device_id_type=pl.DeviceIdType.MESH,
        )
        incoming.wait_recv()
    for copy in first:
        copy.wait_send()

    half = seq_count // 2

    def region(owner, part):
        if part == 0:
            return out_ref.at[pl.ds(owner * seq_count, seq_count)]
        start = owner * seq_count + (part - 1) * half
        return out_ref.at[pl.ds(start, half)]

    def link(owner, part, peer, index):
        piece = region(owner, part)
        return pltpu.make_async_remote_copy(
            src_ref=piece,
            dst_ref=piece,
            send_sem=send_b.at[index],
            recv_sem=recv_b.at[index],
            device_id=(me_seq, peer),
            device_id_type=pl.DeviceIdType.MESH,
        )

    far = vis_of(ring_id, ring_pos + 2)
    left_partner = vis_of(1 - ring_id, ring_pos - 1)
    right_partner = vis_of(1 - ring_id, ring_pos + 1)
    far_partner = vis_of(1 - ring_id, ring_pos + 2)
    sent = []

    def send(owner, part, peer, index):
        copy = link(owner, part, peer, index)
        copy.start()
        sent.append(copy)

    def hop(src, dst, device, index):
        return pltpu.make_async_remote_copy(
            src_ref=src, dst_ref=dst, send_sem=send_b.at[index], recv_sem=recv_b.at[index],
            device_id=device, device_id_type=pl.DeviceIdType.MESH,
        )

    def push(src, dst, device, index):
        copy = hop(src, dst, device, index)
        copy.start()
        sent.append(copy)

    send(me_vis, 0, right, 1)
    send(me_vis, 0, left, 2)
    push(region(me_vis, 1), relay.at[0], upper, 10)
    push(region(me_vis, 2), relay.at[1], lower, 11)
    hop(region(me_vis, 1), relay.at[0], lower, 10).wait_recv()
    lower_vis = lower[1]
    upper_vis = upper[1]
    push(relay.at[0], region(lower_vis, 1), upper, 12)
    hop(region(me_vis, 2), relay.at[1], upper, 11).wait_recv()
    push(relay.at[1], region(upper_vis, 2), lower, 13)
    hop(relay.at[0], region(partner, 1), lower, 12).wait_recv()
    hop(relay.at[1], region(partner, 2), upper, 13).wait_recv()
    send(partner, 0, right, 4)
    send(partner, 0, left, 5)
    link(left, 0, left, 1).wait_recv()
    send(left, 1, right, 6)
    link(right, 0, right, 2).wait_recv()
    send(right, 2, left, 7)
    link(left_partner, 0, left, 4).wait_recv()
    send(left_partner, 1, right, 8)
    link(right_partner, 0, right, 5).wait_recv()
    send(right_partner, 2, left, 9)
    link(far, 1, left, 6).wait_recv()
    link(far, 2, right, 7).wait_recv()
    link(far_partner, 1, left, 8).wait_recv()
    link(far_partner, 2, right, 9).wait_recv()
    for copy in sent:
        copy.wait_send()


def exchange_frames(payload, vis_count):
    owners, capacity, width = payload.shape
    return pl.pallas_call(
        exchange_kernel,
        out_shape=jax.ShapeDtypeStruct((vis_count * owners, capacity, width), payload.dtype),
        in_specs=[pl.BlockSpec(memory_space=pl.ANY)],
        out_specs=pl.BlockSpec(memory_space=pl.ANY),
        scratch_shapes=[
            pltpu.SemaphoreType.DMA((owners,)),
            pltpu.SemaphoreType.DMA((owners,)),
            pltpu.SemaphoreType.DMA((14,)),
            pltpu.SemaphoreType.DMA((14,)),
            pltpu.SemaphoreType.DMA((1,)),
            pltpu.VMEM((2, owners // 2, capacity, width), payload.dtype),
        ],
        compiler_params=pltpu.CompilerParams(collective_id=1, has_side_effects=True),
    )(payload)


def gather_kernel(
    block_ref, normed_ref, w_ref, bias_ref, out_ref, q_ref, send_sem, recv_sem, local_sem, acc_ref
):
    rows = block_ref.shape[0]
    me_seq = lax.axis_index("seq")
    me_vis = lax.axis_index("vis")
    column = me_seq // 4
    layer = lax.rem(me_seq // 2, 2)
    core = lax.rem(me_seq, 2)
    ring = lax.axis_size("seq") // 4

    def seq_of(y, z, c):
        return (lax.rem(y + ring, ring) * 2 + z) * 2 + c

    mate = seq_of(column, layer, 1 - core)
    across = seq_of(column, 1 - layer, core)
    diagonal = seq_of(column, 1 - layer, 1 - core)
    up = seq_of(column + 1, layer, core)
    down = seq_of(column - 1, layer, core)
    barrier = pltpu.get_barrier_semaphore()
    for peer in (mate, across, diagonal, up, down):
        pl.semaphore_signal(
            barrier, inc=1, device_id=(peer, me_vis), device_id_type=pl.DeviceIdType.MESH
        )
    pl.semaphore_wait(barrier, 5)

    def rows_of(start, count):
        return out_ref.at[pl.ds(pl.multiple_of(start, rows), count)]

    def link(src, dst, peer, index):
        return pltpu.make_async_remote_copy(
            src_ref=src, dst_ref=dst, send_sem=send_sem.at[index], recv_sem=recv_sem.at[index],
            device_id=(peer, me_vis), device_id_type=pl.DeviceIdType.MESH,
        )

    sent = []

    def send(src, dst, peer, index):
        copy = link(src, dst, peer, index)
        copy.start()
        sent.append(copy)

    own = rows_of(me_seq * rows, rows)
    local = pltpu.make_async_copy(block_ref, own, local_sem.at[0])
    local.start()
    send(block_ref, own, mate, 0)
    send(block_ref, own, across, 1)
    send(block_ref, own, diagonal, 2)
    depth = normed_ref.shape[1] // 2

    def project(part):
        def body(n_blk, w_blk):
            acc_ref[...] += jnp.dot(n_blk[...], w_blk[...], preferred_element_type=jnp.float32)

        pltpu.emit_pipeline(
            body,
            grid=(depth // PROJ_TILE,),
            in_specs=[
                pl.BlockSpec((normed_ref.shape[0], PROJ_TILE), lambda k: (0, k)),
                pl.BlockSpec((PROJ_TILE, w_ref.shape[1]), lambda k: (k, 0)),
            ],
        )(normed_ref.at[:, pl.ds(part * depth, depth)], w_ref.at[pl.ds(part * depth, depth)])

    acc_ref[...] = jnp.zeros(acc_ref.shape, jnp.float32)
    project(0)
    local.wait()
    link(block_ref, rows_of(mate * rows, rows), mate, 0).wait_recv()
    link(block_ref, rows_of(across * rows, rows), across, 1).wait_recv()
    link(block_ref, rows_of(diagonal * rows, rows), diagonal, 2).wait_recv()

    def half(y, h):
        return rows_of((lax.rem(y + ring, ring) * 4 + h * 2) * rows, 2 * rows)

    def quarter(y, h, q):
        return rows_of((lax.rem(y + ring, ring) * 4 + h * 2 + q) * rows, rows)

    mine = half(column, core)
    send(mine, mine, up, 3)
    send(mine, mine, down, 4)
    project(1)
    below = half(column - 1, core)
    link(below, below, down, 3).wait_recv()
    send(below, below, mate, 7)
    piece = quarter(column - 1, core, 0)
    send(piece, piece, up, 5)
    above = half(column + 1, core)
    link(above, above, up, 4).wait_recv()
    send(above, above, mate, 9)
    piece = quarter(column + 1, core, 1)
    send(piece, piece, down, 6)
    q_ref[...] = (acc_ref[...] + bias_ref[...]).astype(q_ref.dtype)
    far_low = quarter(column + 2, core, 0)
    far_high = quarter(column + 2, core, 1)
    link(far_low, far_low, down, 5).wait_recv()
    link(far_high, far_high, up, 6).wait_recv()
    far = half(column + 2, core)
    send(far, far, mate, 8)
    for offset, index in ((-1, 7), (2, 8), (1, 9)):
        theirs = half(column + offset, 1 - core)
        link(theirs, theirs, mate, index).wait_recv()
    for copy in sent:
        copy.wait_send()


PROJ_TILE = 512


def gather_keys(block, normed, w_query, q_bias, seq_count):
    rows, width = block.shape
    return pl.pallas_call(
        gather_kernel,
        out_shape=(
            jax.ShapeDtypeStruct((seq_count * rows, width), block.dtype),
            jax.ShapeDtypeStruct((normed.shape[0], w_query.shape[1]), jnp.bfloat16),
        ),
        in_specs=[
            pl.BlockSpec(memory_space=pl.ANY),
            pl.BlockSpec(memory_space=pl.ANY),
            pl.BlockSpec(memory_space=pl.ANY),
            pl.BlockSpec(memory_space=pltpu.VMEM),
        ],
        out_specs=(pl.BlockSpec(memory_space=pl.ANY), pl.BlockSpec(memory_space=pltpu.VMEM)),
        scratch_shapes=[
            pltpu.SemaphoreType.DMA((10,)),
            pltpu.SemaphoreType.DMA((10,)),
            pltpu.SemaphoreType.DMA((1,)),
            pltpu.VMEM((normed.shape[0], w_query.shape[1]), jnp.float32),
        ],
        compiler_params=pltpu.CompilerParams(collective_id=2, has_side_effects=True),
    )(block, normed, w_query, q_bias.reshape(1, -1))


def on_device(
    text, frames, tile_pos, frame_count, doc_ids, norm_gain, w_query, q_bias, w_key, w_value, v_bias
):
    seq_count = lax.axis_size("seq")
    vis_count = lax.axis_size("vis")
    shard_index = lax.axis_index("seq")
    shard_rows = text.shape[0]
    capacity = shard_rows // (seq_count * vis_count)
    first_row = shard_index * shard_rows
    payload = frame_slots(frames, tile_pos, frame_count, shard_rows, seq_count, capacity)
    gathered = exchange_frames(payload, vis_count)
    width = text.shape[1]
    incoming_place = gathered[:, :, width].astype(jnp.int32)
    merged = place_frames(text, gathered, incoming_place, width)
    widened = merged.astype(jnp.float32)
    mean_square = jnp.mean(widened * widened, axis=1, keepdims=True)
    normed = (widened * lax.rsqrt(mean_square + epsilon) * norm_gain).astype(jnp.bfloat16)
    key_rows = jnp.dot(normed, w_key, preferred_element_type=jnp.float32).astype(jnp.bfloat16)
    value_rows = (jnp.dot(normed, w_value, preferred_element_type=jnp.float32) + v_bias).astype(
        jnp.bfloat16
    )
    keyval = jnp.concatenate([key_rows, value_rows], axis=1)
    kv_heads = w_key.shape[1] // HEAD_DIM
    per_group = w_query.shape[1] // HEAD_DIM // kv_heads
    incoming_keys, queries = gather_keys(keyval, normed, w_query, q_bias, seq_count)
    return flash_attention(doc_ids, queries, incoming_keys)


KEY_BLOCK = 512
DOC_SPAN = 2048


def block_bounds(doc_ref, rows, key_rows):
    first = lax.axis_index("seq") * rows
    first_doc = doc_ref[first]
    low = 0
    for b in range(key_rows // KEY_BLOCK):
        low = low + (doc_ref[(b + 1) * KEY_BLOCK - 1] < first_doc).astype(jnp.int32)
    return low, (first + rows - 1) // KEY_BLOCK, first


def flash_kernel(doc_ref, q_ref, k_ref, v_ref, qdoc_ref, kdoc_ref, out_ref, peak_ref, total_ref, acc_ref, qcol_ref):
    step = pl.program_id(0)
    rows = q_ref.shape[0]
    heads = q_ref.shape[1] // HEAD_DIM
    low, high, first = block_bounds(doc_ref, rows, doc_ref.shape[0])
    block = low + step

    @pl.when(step == 0)
    def _():
        peak_ref[...] = jnp.full(peak_ref.shape, negative, jnp.float32)
        total_ref[...] = jnp.zeros(total_ref.shape, jnp.float32)
        acc_ref[...] = jnp.zeros(acc_ref.shape, jnp.float32)
        spread = jnp.broadcast_to(qdoc_ref[...], (rows, rows))
        diagonal = lax.broadcasted_iota(jnp.int32, (rows, rows), 0) == lax.broadcasted_iota(
            jnp.int32, (rows, rows), 1
        )
        qcol_ref[...] = jnp.sum(jnp.where(diagonal, spread, 0), axis=1, keepdims=True)

    @pl.when(block <= high)
    def _():
        key_place = block * KEY_BLOCK + lax.broadcasted_iota(jnp.int32, (1, KEY_BLOCK), 1)
        query_place = first + lax.broadcasted_iota(jnp.int32, (rows, 1), 0)
        allowed = (key_place <= query_place) & (kdoc_ref[...] == qcol_ref[...])
        keys = k_ref[...]
        vals = v_ref[...]
        for h in range(heads):
            cols = slice(h * HEAD_DIM, (h + 1) * HEAD_DIM)
            scores = lax.dot_general(
                q_ref[:, cols], keys, (((1,), (1,)), ((), ())),
                preferred_element_type=jnp.float32,
            ) * HEAD_DIM ** (-0.5)
            scores = jnp.where(allowed, scores, negative)
            old_peak = peak_ref[h]
            new_peak = jnp.maximum(old_peak, jnp.max(scores, axis=1, keepdims=True))
            raised = jnp.where(allowed, jnp.exp(scores - new_peak[:, :1]), 0.0)
            factor = jnp.exp(old_peak - new_peak)
            total_ref[h] = total_ref[h] * factor + jnp.sum(raised, axis=1, keepdims=True)
            peak_ref[h] = new_peak
            product = jnp.dot(raised.astype(jnp.bfloat16), vals, preferred_element_type=jnp.float32)
            acc_ref[:, cols] = acc_ref[:, cols] * factor[:, :1] + product

    @pl.when(step == pl.num_programs(0) - 1)
    def _():
        for h in range(heads):
            cols = slice(h * HEAD_DIM, (h + 1) * HEAD_DIM)
            out_ref[:, cols] = (acc_ref[:, cols] / total_ref[h][:, :1]).astype(out_ref.dtype)


def flash_attention(doc_ids, queries, keyval):
    rows, width = queries.shape
    key_rows = keyval.shape[0]
    steps = min(key_rows // KEY_BLOCK, (DOC_SPAN + rows - 2) // KEY_BLOCK + 2)
    heads = width // HEAD_DIM

    def clamp(j, d):
        low, high, _ = block_bounds(d, rows, key_rows)
        return jnp.minimum(low + j, high)

    grid_spec = pltpu.PrefetchScalarGridSpec(
        num_scalar_prefetch=1,
        grid=(steps,),
        in_specs=[
            pl.BlockSpec((rows, width), lambda j, d: (0, 0)),
            pl.BlockSpec((KEY_BLOCK, HEAD_DIM), lambda j, d: (clamp(j, d), 0)),
            pl.BlockSpec((KEY_BLOCK, HEAD_DIM), lambda j, d: (clamp(j, d), 1)),
            pl.BlockSpec((1, rows), lambda j, d: (0, lax.axis_index("seq"))),
            pl.BlockSpec((1, KEY_BLOCK), lambda j, d: (0, clamp(j, d))),
        ],
        out_specs=pl.BlockSpec((rows, width), lambda j, d: (0, 0)),
        scratch_shapes=[
            pltpu.VMEM((heads, rows, 1), jnp.float32),
            pltpu.VMEM((heads, rows, 1), jnp.float32),
            pltpu.VMEM((rows, width), jnp.float32),
            pltpu.VMEM((rows, 1), jnp.int32),
        ],
    )
    flops = 4 * rows * width * key_rows // 2
    doc_row = doc_ids.reshape(1, -1)
    return pl.pallas_call(
        flash_kernel,
        out_shape=jax.ShapeDtypeStruct((rows, width), jnp.bfloat16),
        grid_spec=grid_spec,
        compiler_params=pltpu.CompilerParams(dimension_semantics=("arbitrary",)),
        cost_estimate=pl.CostEstimate(
            flops=flops, transcendentals=rows * heads * key_rows // 2,
            bytes_accessed=2 * (2 * rows * width + key_rows * 2 * HEAD_DIM),
        ),
    )(doc_ids, queries, keyval, keyval, doc_row, doc_row)


def solution(mesh):
    in_specs = (
        P("seq", None),
        P(("seq", "vis"), None),
        P(("seq", "vis")),
        P(("seq", "vis")),
        P(),
        P(),
        P(None, "vis"),
        P("vis"),
        P(None, "vis"),
        P(None, "vis"),
        P("vis"),
    )
    out_specs = P("seq", "vis")
    return jax.shard_map(
        on_device, mesh=mesh, in_specs=in_specs, out_specs=out_specs, check_vma=False
    )
```

```python
import jax
import jax.numpy as jnp
from jax import lax
from jax.sharding import PartitionSpec as P
from jax.experimental import pallas as pl
from jax.experimental.pallas import tpu as pltpu

HEAD_DIM = 128


epsilon = 1e-06
negative = -1e30


def frame_slots(frames, tile_pos, frame_count, shard_rows, owners, capacity):
    row_count = frames.shape[0]
    row_ids = jnp.arange(row_count, dtype=jnp.int32)
    usable = row_ids < frame_count[0]
    owner = jnp.where(usable, tile_pos // shard_rows, owners)
    hits = (owner[:, None] == jnp.arange(owners, dtype=jnp.int32)[None, :]).astype(jnp.int32)
    earlier = (row_ids[:, None] > row_ids[None, :]).astype(jnp.int32)
    before = jnp.dot(earlier, hits, preferred_element_type=jnp.int32)
    rank = jnp.sum(before * hits, axis=1)
    slot_index = owner * capacity + rank
    slot_ids = jnp.arange(owners * capacity, dtype=jnp.int32)
    match = usable[:, None] & (slot_index[:, None] == slot_ids[None, :])
    filled = jnp.any(match, axis=0)
    local = tile_pos - owner * shard_rows
    slot_local = jnp.sum(jnp.where(match, local[:, None], 0), axis=0)
    slot_local = jnp.where(filled, slot_local, -1)
    slot_rows = jnp.dot(
        match.T.astype(frames.dtype), frames, preferred_element_type=jnp.float32
    ).astype(frames.dtype)
    place_col = jnp.broadcast_to(slot_local[:, None], (slot_local.shape[0], 128)).astype(frames.dtype)
    payload = jnp.concatenate([slot_rows, place_col], axis=1)
    return payload.reshape(owners, capacity, payload.shape[1])


def place_frames(text, incoming, incoming_place, width):
    lookup = incoming_place[None] == jnp.arange(text.shape[0], dtype=jnp.int32)[:, None, None]
    covered = jnp.any(lookup, axis=(1, 2))
    placed = lax.dot_general(
        lookup.astype(incoming.dtype), incoming, (((1, 2), (0, 1)), ((), ())),
        preferred_element_type=jnp.float32,
    )[:, :width].astype(text.dtype)
    return jnp.where(covered[:, None], placed, text)


def exchange_kernel(payload_ref, out_ref, send_a, recv_a, send_b, recv_b, local_sem):
    seq_count = lax.axis_size("seq")
    vis_count = lax.axis_size("vis")
    ring = vis_count // 2
    me_seq = lax.axis_index("seq")
    me_vis = lax.axis_index("vis")
    ring_pos = lax.rem(me_vis, ring)
    ring_id = me_vis // ring

    def vis_of(ring_index, position):
        return ring_index * ring + lax.rem(position + ring, ring)

    right = vis_of(ring_id, ring_pos + 1)
    left = vis_of(ring_id, ring_pos - 1)
    partner = vis_of(1 - ring_id, ring_pos)
    barrier = pltpu.get_barrier_semaphore()
    for k in range(1, seq_count):
        pl.semaphore_signal(
            barrier, inc=1, device_id=(lax.rem(me_seq + k, seq_count), me_vis),
            device_id_type=pl.DeviceIdType.MESH,
        )
    for peer in (left, right, partner):
        pl.semaphore_signal(
            barrier, inc=1, device_id=(me_seq, peer), device_id_type=pl.DeviceIdType.MESH
        )
    pl.semaphore_wait(barrier, seq_count + 2)
    base = me_vis * seq_count
    local = pltpu.make_async_copy(payload_ref.at[me_seq], out_ref.at[base], local_sem.at[0])
    local.start()
    first = []
    for k in range(1, seq_count):
        target = lax.rem(me_seq + k, seq_count)
        copy = pltpu.make_async_remote_copy(
            src_ref=payload_ref.at[target],
            dst_ref=out_ref.at[base + k],
            send_sem=send_a.at[k],
            recv_sem=recv_a.at[k],
            device_id=(target, me_vis),
            device_id_type=pl.DeviceIdType.MESH,
        )
        copy.start()
        first.append(copy)
    local.wait()

    def arrivals(ks):
        for k in ks:
            source = lax.rem(me_seq + seq_count - k, seq_count)
            incoming = pltpu.make_async_remote_copy(
                src_ref=payload_ref.at[source],
                dst_ref=out_ref.at[base + k],
                send_sem=send_a.at[k],
                recv_sem=recv_a.at[k],
                device_id=(source, me_vis),
                device_id_type=pl.DeviceIdType.MESH,
            )
            incoming.wait_recv()

    arrivals(range(1, seq_count // 2))

    half = seq_count // 2

    def region(owner, part):
        if part == 0:
            return out_ref.at[pl.ds(owner * seq_count, seq_count)]
        start = owner * seq_count + (part - 1) * half
        return out_ref.at[pl.ds(start, half)]

    def link(owner, part, peer, index):
        piece = region(owner, part)
        return pltpu.make_async_remote_copy(
            src_ref=piece,
            dst_ref=piece,
            send_sem=send_b.at[index],
            recv_sem=recv_b.at[index],
            device_id=(me_seq, peer),
            device_id_type=pl.DeviceIdType.MESH,
        )

    far = vis_of(ring_id, ring_pos + 2)
    left_partner = vis_of(1 - ring_id, ring_pos - 1)
    right_partner = vis_of(1 - ring_id, ring_pos + 1)
    far_partner = vis_of(1 - ring_id, ring_pos + 2)
    sent = []

    def send(owner, part, peer, index):
        copy = link(owner, part, peer, index)
        copy.start()
        sent.append(copy)

    send(me_vis, 1, right, 1)
    send(me_vis, 1, left, 2)
    send(me_vis, 1, partner, 3)
    arrivals(range(seq_count // 2, seq_count))
    for copy in first:
        copy.wait_send()
    send(me_vis, 2, right, 10)
    send(me_vis, 2, left, 11)
    send(me_vis, 2, partner, 12)
    link(partner, 1, partner, 3).wait_recv()
    link(partner, 2, partner, 12).wait_recv()
    send(partner, 0, right, 4)
    send(partner, 0, left, 5)
    link(left, 1, left, 1).wait_recv()
    link(left, 2, left, 10).wait_recv()
    send(left, 1, right, 6)
    link(right, 1, right, 2).wait_recv()
    link(right, 2, right, 11).wait_recv()
    send(right, 2, left, 7)
    link(left_partner, 0, left, 4).wait_recv()
    send(left_partner, 1, right, 8)
    link(right_partner, 0, right, 5).wait_recv()
    send(right_partner, 2, left, 9)
    link(far, 1, left, 6).wait_recv()
    link(far, 2, right, 7).wait_recv()
    link(far_partner, 1, left, 8).wait_recv()
    link(far_partner, 2, right, 9).wait_recv()
    for copy in sent:
        copy.wait_send()


def exchange_frames(payload, vis_count):
    owners, capacity, width = payload.shape
    return pl.pallas_call(
        exchange_kernel,
        out_shape=jax.ShapeDtypeStruct((vis_count * owners, capacity, width), payload.dtype),
        in_specs=[pl.BlockSpec(memory_space=pl.ANY)],
        out_specs=pl.BlockSpec(memory_space=pl.ANY),
        scratch_shapes=[
            pltpu.SemaphoreType.DMA((owners,)),
            pltpu.SemaphoreType.DMA((owners,)),
            pltpu.SemaphoreType.DMA((13,)),
            pltpu.SemaphoreType.DMA((13,)),
            pltpu.SemaphoreType.DMA((1,)),
        ],
        compiler_params=pltpu.CompilerParams(collective_id=1, has_side_effects=True),
    )(payload)


def gather_kernel(
    block_ref, normed_ref, w_ref, bias_ref, out_ref, q_ref, send_sem, recv_sem, local_sem, acc_ref
):
    rows = block_ref.shape[0]
    me_seq = lax.axis_index("seq")
    me_vis = lax.axis_index("vis")
    column = me_seq // 4
    layer = lax.rem(me_seq // 2, 2)
    core = lax.rem(me_seq, 2)
    ring = lax.axis_size("seq") // 4

    def seq_of(y, z, c):
        return (lax.rem(y + ring, ring) * 2 + z) * 2 + c

    mate = seq_of(column, layer, 1 - core)
    across = seq_of(column, 1 - layer, core)
    diagonal = seq_of(column, 1 - layer, 1 - core)
    up = seq_of(column + 1, layer, core)
    down = seq_of(column - 1, layer, core)
    barrier = pltpu.get_barrier_semaphore()
    for peer in (mate, across, diagonal, up, down):
        pl.semaphore_signal(
            barrier, inc=1, device_id=(peer, me_vis), device_id_type=pl.DeviceIdType.MESH
        )
    pl.semaphore_wait(barrier, 5)

    def rows_of(start, count):
        return out_ref.at[pl.ds(pl.multiple_of(start, rows), count)]

    def link(src, dst, peer, index):
        return pltpu.make_async_remote_copy(
            src_ref=src, dst_ref=dst, send_sem=send_sem.at[index], recv_sem=recv_sem.at[index],
            device_id=(peer, me_vis), device_id_type=pl.DeviceIdType.MESH,
        )

    sent = []

    def send(src, dst, peer, index):
        copy = link(src, dst, peer, index)
        copy.start()
        sent.append(copy)

    own = rows_of(me_seq * rows, rows)
    local = pltpu.make_async_copy(block_ref, own, local_sem.at[0])
    local.start()
    send(block_ref, own, mate, 0)
    send(block_ref, own, across, 1)
    send(block_ref, own, diagonal, 2)
    depth = normed_ref.shape[1] // 2

    def project(part):
        def body(n_blk, w_blk):
            acc_ref[...] += jnp.dot(n_blk[...], w_blk[...], preferred_element_type=jnp.float32)

        pltpu.emit_pipeline(
            body,
            grid=(depth // PROJ_TILE,),
            in_specs=[
                pl.BlockSpec((normed_ref.shape[0], PROJ_TILE), lambda k: (0, k)),
                pl.BlockSpec((PROJ_TILE, w_ref.shape[1]), lambda k: (k, 0)),
            ],
        )(normed_ref.at[:, pl.ds(part * depth, depth)], w_ref.at[pl.ds(part * depth, depth)])

    acc_ref[...] = jnp.zeros(acc_ref.shape, jnp.float32)
    project(0)
    local.wait()
    link(block_ref, rows_of(mate * rows, rows), mate, 0).wait_recv()
    link(block_ref, rows_of(across * rows, rows), across, 1).wait_recv()
    link(block_ref, rows_of(diagonal * rows, rows), diagonal, 2).wait_recv()

    def half(y, h):
        return rows_of((lax.rem(y + ring, ring) * 4 + h * 2) * rows, 2 * rows)

    def quarter(y, h, q):
        return rows_of((lax.rem(y + ring, ring) * 4 + h * 2 + q) * rows, rows)

    mine = half(column, core)
    send(mine, mine, up, 3)
    send(mine, mine, down, 4)
    project(1)
    below = half(column - 1, core)
    link(below, below, down, 3).wait_recv()
    send(below, below, mate, 7)
    piece = quarter(column - 1, core, 0)
    send(piece, piece, up, 5)
    above = half(column + 1, core)
    link(above, above, up, 4).wait_recv()
    send(above, above, mate, 9)
    piece = quarter(column + 1, core, 1)
    send(piece, piece, down, 6)
    q_ref[...] = (acc_ref[...] + bias_ref[...]).astype(q_ref.dtype)
    far_low = quarter(column + 2, core, 0)
    far_high = quarter(column + 2, core, 1)
    link(far_low, far_low, down, 5).wait_recv()
    link(far_high, far_high, up, 6).wait_recv()
    far = half(column + 2, core)
    send(far, far, mate, 8)
    for offset, index in ((-1, 7), (2, 8), (1, 9)):
        theirs = half(column + offset, 1 - core)
        link(theirs, theirs, mate, index).wait_recv()
    for copy in sent:
        copy.wait_send()


PROJ_TILE = 512


def gather_keys(block, normed, w_query, q_bias, seq_count):
    rows, width = block.shape
    return pl.pallas_call(
        gather_kernel,
        out_shape=(
            jax.ShapeDtypeStruct((seq_count * rows, width), block.dtype),
            jax.ShapeDtypeStruct((normed.shape[0], w_query.shape[1]), jnp.bfloat16),
        ),
        in_specs=[
            pl.BlockSpec(memory_space=pl.ANY),
            pl.BlockSpec(memory_space=pl.ANY),
            pl.BlockSpec(memory_space=pl.ANY),
            pl.BlockSpec(memory_space=pltpu.VMEM),
        ],
        out_specs=(pl.BlockSpec(memory_space=pl.ANY), pl.BlockSpec(memory_space=pltpu.VMEM)),
        scratch_shapes=[
            pltpu.SemaphoreType.DMA((10,)),
            pltpu.SemaphoreType.DMA((10,)),
            pltpu.SemaphoreType.DMA((1,)),
            pltpu.VMEM((normed.shape[0], w_query.shape[1]), jnp.float32),
        ],
        compiler_params=pltpu.CompilerParams(collective_id=2, has_side_effects=True),
    )(block, normed, w_query, q_bias.reshape(1, -1))


def on_device(
    text, frames, tile_pos, frame_count, doc_ids, norm_gain, w_query, q_bias, w_key, w_value, v_bias
):
    seq_count = lax.axis_size("seq")
    vis_count = lax.axis_size("vis")
    shard_index = lax.axis_index("seq")
    shard_rows = text.shape[0]
    capacity = shard_rows // (seq_count * vis_count)
    first_row = shard_index * shard_rows
    payload = frame_slots(frames, tile_pos, frame_count, shard_rows, seq_count, capacity)
    gathered = exchange_frames(payload, vis_count)
    width = text.shape[1]
    incoming_place = gathered[:, :, width].astype(jnp.int32)
    merged = place_frames(text, gathered, incoming_place, width)
    widened = merged.astype(jnp.float32)
    mean_square = jnp.mean(widened * widened, axis=1, keepdims=True)
    normed = (widened * lax.rsqrt(mean_square + epsilon) * norm_gain).astype(jnp.bfloat16)
    key_rows = jnp.dot(normed, w_key, preferred_element_type=jnp.float32).astype(jnp.bfloat16)
    value_rows = (jnp.dot(normed, w_value, preferred_element_type=jnp.float32) + v_bias).astype(
        jnp.bfloat16
    )
    keyval = jnp.concatenate([key_rows, value_rows], axis=1)
    kv_heads = w_key.shape[1] // HEAD_DIM
    per_group = w_query.shape[1] // HEAD_DIM // kv_heads
    incoming_keys, queries = gather_keys(keyval, normed, w_query, q_bias, seq_count)
    return flash_attention(doc_ids, queries, incoming_keys)


KEY_BLOCK = 512
DOC_SPAN = 2048


def block_bounds(doc_ref, rows, key_rows):
    first = lax.axis_index("seq") * rows
    first_doc = doc_ref[first]
    low = 0
    for b in range(key_rows // KEY_BLOCK):
        low = low + (doc_ref[(b + 1) * KEY_BLOCK - 1] < first_doc).astype(jnp.int32)
    return low, (first + rows - 1) // KEY_BLOCK, first


def flash_kernel(doc_ref, q_ref, k_ref, v_ref, qdoc_ref, kdoc_ref, out_ref, peak_ref, total_ref, acc_ref, qcol_ref):
    step = pl.program_id(0)
    rows = q_ref.shape[0]
    heads = q_ref.shape[1] // HEAD_DIM
    low, high, first = block_bounds(doc_ref, rows, doc_ref.shape[0])
    block = low + step

    @pl.when(step == 0)
    def _():
        peak_ref[...] = jnp.full(peak_ref.shape, negative, jnp.float32)
        total_ref[...] = jnp.zeros(total_ref.shape, jnp.float32)
        acc_ref[...] = jnp.zeros(acc_ref.shape, jnp.float32)
        spread = jnp.broadcast_to(qdoc_ref[...], (rows, rows))
        diagonal = lax.broadcasted_iota(jnp.int32, (rows, rows), 0) == lax.broadcasted_iota(
            jnp.int32, (rows, rows), 1
        )
        qcol_ref[...] = jnp.sum(jnp.where(diagonal, spread, 0), axis=1, keepdims=True)

    @pl.when(block <= high)
    def _():
        key_place = block * KEY_BLOCK + lax.broadcasted_iota(jnp.int32, (1, KEY_BLOCK), 1)
        query_place = first + lax.broadcasted_iota(jnp.int32, (rows, 1), 0)
        allowed = (key_place <= query_place) & (kdoc_ref[...] == qcol_ref[...])
        keys = k_ref[...]
        vals = v_ref[...]
        for h in range(heads):
            cols = slice(h * HEAD_DIM, (h + 1) * HEAD_DIM)
            scores = lax.dot_general(
                q_ref[:, cols], keys, (((1,), (1,)), ((), ())),
                preferred_element_type=jnp.float32,
            ) * HEAD_DIM ** (-0.5)
            scores = jnp.where(allowed, scores, negative)
            old_peak = peak_ref[h]
            new_peak = jnp.maximum(old_peak, jnp.max(scores, axis=1, keepdims=True))
            raised = jnp.where(allowed, jnp.exp(scores - new_peak[:, :1]), 0.0)
            factor = jnp.exp(old_peak - new_peak)
            total_ref[h] = total_ref[h] * factor + jnp.sum(raised, axis=1, keepdims=True)
            peak_ref[h] = new_peak
            product = jnp.dot(raised.astype(jnp.bfloat16), vals, preferred_element_type=jnp.float32)
            acc_ref[:, cols] = acc_ref[:, cols] * factor[:, :1] + product

    @pl.when(step == pl.num_programs(0) - 1)
    def _():
        for h in range(heads):
            cols = slice(h * HEAD_DIM, (h + 1) * HEAD_DIM)
            out_ref[:, cols] = (acc_ref[:, cols] / total_ref[h][:, :1]).astype(out_ref.dtype)


def flash_attention(doc_ids, queries, keyval):
    rows, width = queries.shape
    key_rows = keyval.shape[0]
    steps = min(key_rows // KEY_BLOCK, (DOC_SPAN + rows - 2) // KEY_BLOCK + 2)
    heads = width // HEAD_DIM

    def clamp(j, d):
        low, high, _ = block_bounds(d, rows, key_rows)
        return jnp.minimum(low + j, high)

    grid_spec = pltpu.PrefetchScalarGridSpec(
        num_scalar_prefetch=1,
        grid=(steps,),
        in_specs=[
            pl.BlockSpec((rows, width), lambda j, d: (0, 0)),
            pl.BlockSpec((KEY_BLOCK, HEAD_DIM), lambda j, d: (clamp(j, d), 0)),
            pl.BlockSpec((KEY_BLOCK, HEAD_DIM), lambda j, d: (clamp(j, d), 1)),
            pl.BlockSpec((1, rows), lambda j, d: (0, lax.axis_index("seq"))),
            pl.BlockSpec((1, KEY_BLOCK), lambda j, d: (0, clamp(j, d))),
        ],
        out_specs=pl.BlockSpec((rows, width), lambda j, d: (0, 0)),
        scratch_shapes=[
            pltpu.VMEM((heads, rows, 1), jnp.float32),
            pltpu.VMEM((heads, rows, 1), jnp.float32),
            pltpu.VMEM((rows, width), jnp.float32),
            pltpu.VMEM((rows, 1), jnp.int32),
        ],
    )
    flops = 4 * rows * width * key_rows // 2
    doc_row = doc_ids.reshape(1, -1)
    return pl.pallas_call(
        flash_kernel,
        out_shape=jax.ShapeDtypeStruct((rows, width), jnp.bfloat16),
        grid_spec=grid_spec,
        compiler_params=pltpu.CompilerParams(dimension_semantics=("arbitrary",)),
        cost_estimate=pl.CostEstimate(
            flops=flops, transcendentals=rows * heads * key_rows // 2,
            bytes_accessed=2 * (2 * rows * width + key_rows * 2 * HEAD_DIM),
        ),
    )(doc_ids, queries, keyval, keyval, doc_row, doc_row)


def solution(mesh):
    in_specs = (
        P("seq", None),
        P(("seq", "vis"), None),
        P(("seq", "vis")),
        P(("seq", "vis")),
        P(),
        P(),
        P(None, "vis"),
        P("vis"),
        P(None, "vis"),
        P(None, "vis"),
        P("vis"),
    )
    out_specs = P("seq", "vis")
    return jax.shard_map(
        on_device, mesh=mesh, in_specs=in_specs, out_specs=out_specs, check_vma=False
    )
```

```python
import jax
import jax.numpy as jnp
from jax import lax
from jax.sharding import PartitionSpec as P
from jax.experimental import pallas as pl
from jax.experimental.pallas import tpu as pltpu

HEAD_DIM = 128


epsilon = 1e-06
negative = -1e30


def frame_slots(frames, tile_pos, frame_count, shard_rows, owners, capacity):
    row_count = frames.shape[0]
    row_ids = jnp.arange(row_count, dtype=jnp.int32)
    usable = row_ids < frame_count[0]
    owner = jnp.where(usable, tile_pos // shard_rows, owners)
    hits = (owner[:, None] == jnp.arange(owners, dtype=jnp.int32)[None, :]).astype(jnp.int32)
    earlier = (row_ids[:, None] > row_ids[None, :]).astype(jnp.int32)
    before = jnp.dot(earlier, hits, preferred_element_type=jnp.int32)
    rank = jnp.sum(before * hits, axis=1)
    slot_index = owner * capacity + rank
    slot_ids = jnp.arange(owners * capacity, dtype=jnp.int32)
    match = usable[:, None] & (slot_index[:, None] == slot_ids[None, :])
    filled = jnp.any(match, axis=0)
    local = tile_pos - owner * shard_rows
    slot_local = jnp.sum(jnp.where(match, local[:, None], 0), axis=0)
    slot_local = jnp.where(filled, slot_local, -1)
    slot_rows = jnp.dot(
        match.T.astype(frames.dtype), frames, preferred_element_type=jnp.float32
    ).astype(frames.dtype)
    place_col = jnp.broadcast_to(slot_local[:, None], (slot_local.shape[0], 128)).astype(frames.dtype)
    payload = jnp.concatenate([slot_rows, place_col], axis=1)
    return payload.reshape(owners, capacity, payload.shape[1])


def place_frames(text, incoming, incoming_place, width):
    lookup = incoming_place[None] == jnp.arange(text.shape[0], dtype=jnp.int32)[:, None, None]
    covered = jnp.any(lookup, axis=(1, 2))
    placed = lax.dot_general(
        lookup.astype(incoming.dtype), incoming, (((1, 2), (0, 1)), ((), ())),
        preferred_element_type=jnp.float32,
    )[:, :width].astype(text.dtype)
    return jnp.where(covered[:, None], placed, text)


def exchange_kernel(payload_ref, out_ref, send_a, recv_a, send_b, recv_b, local_sem):
    seq_count = lax.axis_size("seq")
    vis_count = lax.axis_size("vis")
    ring = vis_count // 2
    me_seq = lax.axis_index("seq")
    me_vis = lax.axis_index("vis")
    ring_pos = lax.rem(me_vis, ring)
    ring_id = me_vis // ring

    def vis_of(ring_index, position):
        return ring_index * ring + lax.rem(position + ring, ring)

    right = vis_of(ring_id, ring_pos + 1)
    left = vis_of(ring_id, ring_pos - 1)
    partner = vis_of(1 - ring_id, ring_pos)
    barrier = pltpu.get_barrier_semaphore()
    for k in range(1, seq_count):
        pl.semaphore_signal(
            barrier, inc=1, device_id=(lax.rem(me_seq + k, seq_count), me_vis),
            device_id_type=pl.DeviceIdType.MESH,
        )
    for peer in (left, right, partner):
        pl.semaphore_signal(
            barrier, inc=1, device_id=(me_seq, peer), device_id_type=pl.DeviceIdType.MESH
        )
    pl.semaphore_wait(barrier, seq_count + 2)
    base = me_vis * seq_count
    local = pltpu.make_async_copy(payload_ref.at[me_seq], out_ref.at[base], local_sem.at[0])
    local.start()
    first = []
    for k in range(1, seq_count):
        target = lax.rem(me_seq + k, seq_count)
        copy = pltpu.make_async_remote_copy(
            src_ref=payload_ref.at[target],
            dst_ref=out_ref.at[base + k],
            send_sem=send_a.at[k],
            recv_sem=recv_a.at[k],
            device_id=(target, me_vis),
            device_id_type=pl.DeviceIdType.MESH,
        )
        copy.start()
        first.append(copy)
    local.wait()

    def arrivals(ks):
        for k in ks:
            source = lax.rem(me_seq + seq_count - k, seq_count)
            incoming = pltpu.make_async_remote_copy(
                src_ref=payload_ref.at[source],
                dst_ref=out_ref.at[base + k],
                send_sem=send_a.at[k],
                recv_sem=recv_a.at[k],
                device_id=(source, me_vis),
                device_id_type=pl.DeviceIdType.MESH,
            )
            incoming.wait_recv()

    arrivals(range(1, seq_count // 2))

    half = seq_count // 2

    def region(owner, part):
        if part == 0:
            return out_ref.at[pl.ds(owner * seq_count, seq_count)]
        start = owner * seq_count + (part - 1) * half
        return out_ref.at[pl.ds(start, half)]

    def link(owner, part, peer, index):
        piece = region(owner, part)
        return pltpu.make_async_remote_copy(
            src_ref=piece,
            dst_ref=piece,
            send_sem=send_b.at[index],
            recv_sem=recv_b.at[index],
            device_id=(me_seq, peer),
            device_id_type=pl.DeviceIdType.MESH,
        )

    far = vis_of(ring_id, ring_pos + 2)
    left_partner = vis_of(1 - ring_id, ring_pos - 1)
    right_partner = vis_of(1 - ring_id, ring_pos + 1)
    far_partner = vis_of(1 - ring_id, ring_pos + 2)
    sent = []

    def send(owner, part, peer, index):
        copy = link(owner, part, peer, index)
        copy.start()
        sent.append(copy)

    send(me_vis, 1, right, 1)
    send(me_vis, 1, left, 2)
    send(me_vis, 1, partner, 3)
    arrivals(range(seq_count // 2, seq_count))
    for copy in first:
        copy.wait_send()
    send(me_vis, 2, right, 10)
    send(me_vis, 2, left, 11)
    send(me_vis, 2, partner, 12)
    link(partner, 1, partner, 3).wait_recv()
    send(partner, 1, right, 4)
    send(partner, 1, left, 5)
    link(left, 1, left, 1).wait_recv()
    send(left, 1, right, 6)
    link(partner, 2, partner, 12).wait_recv()
    send(partner, 2, right, 13)
    send(partner, 2, left, 14)
    link(right, 2, right, 11).wait_recv()
    send(right, 2, left, 7)
    link(left_partner, 1, left, 4).wait_recv()
    send(left_partner, 1, right, 8)
    link(right_partner, 2, right, 14).wait_recv()
    send(right_partner, 2, left, 9)
    link(left, 2, left, 10).wait_recv()
    link(right, 1, right, 2).wait_recv()
    link(left_partner, 2, left, 13).wait_recv()
    link(right_partner, 1, right, 5).wait_recv()
    link(far, 1, left, 6).wait_recv()
    link(far, 2, right, 7).wait_recv()
    link(far_partner, 1, left, 8).wait_recv()
    link(far_partner, 2, right, 9).wait_recv()
    for copy in sent:
        copy.wait_send()


def exchange_frames(payload, vis_count):
    owners, capacity, width = payload.shape
    return pl.pallas_call(
        exchange_kernel,
        out_shape=jax.ShapeDtypeStruct((vis_count * owners, capacity, width), payload.dtype),
        in_specs=[pl.BlockSpec(memory_space=pl.ANY)],
        out_specs=pl.BlockSpec(memory_space=pl.ANY),
        scratch_shapes=[
            pltpu.SemaphoreType.DMA((owners,)),
            pltpu.SemaphoreType.DMA((owners,)),
            pltpu.SemaphoreType.DMA((15,)),
            pltpu.SemaphoreType.DMA((15,)),
            pltpu.SemaphoreType.DMA((1,)),
        ],
        compiler_params=pltpu.CompilerParams(collective_id=1, has_side_effects=True),
    )(payload)


def gather_kernel(
    block_ref, normed_ref, w_ref, bias_ref, out_ref, q_ref, send_sem, recv_sem, local_sem, acc_ref
):
    rows = block_ref.shape[0]
    me_seq = lax.axis_index("seq")
    me_vis = lax.axis_index("vis")
    column = me_seq // 4
    layer = lax.rem(me_seq // 2, 2)
    core = lax.rem(me_seq, 2)
    ring = lax.axis_size("seq") // 4

    def seq_of(y, z, c):
        return (lax.rem(y + ring, ring) * 2 + z) * 2 + c

    mate = seq_of(column, layer, 1 - core)
    across = seq_of(column, 1 - layer, core)
    diagonal = seq_of(column, 1 - layer, 1 - core)
    up = seq_of(column + 1, layer, core)
    down = seq_of(column - 1, layer, core)
    barrier = pltpu.get_barrier_semaphore()
    for peer in (mate, across, diagonal, up, down):
        pl.semaphore_signal(
            barrier, inc=1, device_id=(peer, me_vis), device_id_type=pl.DeviceIdType.MESH
        )
    pl.semaphore_wait(barrier, 5)

    def rows_of(start, count):
        return out_ref.at[pl.ds(pl.multiple_of(start, rows), count)]

    def link(src, dst, peer, index):
        return pltpu.make_async_remote_copy(
            src_ref=src, dst_ref=dst, send_sem=send_sem.at[index], recv_sem=recv_sem.at[index],
            device_id=(peer, me_vis), device_id_type=pl.DeviceIdType.MESH,
        )

    sent = []

    def send(src, dst, peer, index):
        copy = link(src, dst, peer, index)
        copy.start()
        sent.append(copy)

    own = rows_of(me_seq * rows, rows)
    local = pltpu.make_async_copy(block_ref, own, local_sem.at[0])
    local.start()
    send(block_ref, own, mate, 0)
    send(block_ref, own, across, 1)
    send(block_ref, own, diagonal, 2)
    depth = normed_ref.shape[1] // 2

    def project(part):
        def body(n_blk, w_blk):
            acc_ref[...] += jnp.dot(n_blk[...], w_blk[...], preferred_element_type=jnp.float32)

        pltpu.emit_pipeline(
            body,
            grid=(depth // PROJ_TILE,),
            in_specs=[
                pl.BlockSpec((normed_ref.shape[0], PROJ_TILE), lambda k: (0, k)),
                pl.BlockSpec((PROJ_TILE, w_ref.shape[1]), lambda k: (k, 0)),
            ],
        )(normed_ref.at[:, pl.ds(part * depth, depth)], w_ref.at[pl.ds(part * depth, depth)])

    acc_ref[...] = jnp.zeros(acc_ref.shape, jnp.float32)
    project(0)
    local.wait()
    link(block_ref, rows_of(mate * rows, rows), mate, 0).wait_recv()
    link(block_ref, rows_of(across * rows, rows), across, 1).wait_recv()
    link(block_ref, rows_of(diagonal * rows, rows), diagonal, 2).wait_recv()

    def half(y, h):
        return rows_of((lax.rem(y + ring, ring) * 4 + h * 2) * rows, 2 * rows)

    def quarter(y, h, q):
        return rows_of((lax.rem(y + ring, ring) * 4 + h * 2 + q) * rows, rows)

    mine = half(column, core)
    send(mine, mine, up, 3)
    send(mine, mine, down, 4)
    project(1)
    below = half(column - 1, core)
    link(below, below, down, 3).wait_recv()
    send(below, below, mate, 7)
    piece = quarter(column - 1, core, 0)
    send(piece, piece, up, 5)
    above = half(column + 1, core)
    link(above, above, up, 4).wait_recv()
    send(above, above, mate, 9)
    piece = quarter(column + 1, core, 1)
    send(piece, piece, down, 6)
    q_ref[...] = (acc_ref[...] + bias_ref[...]).astype(q_ref.dtype)
    far_low = quarter(column + 2, core, 0)
    far_high = quarter(column + 2, core, 1)
    link(far_low, far_low, down, 5).wait_recv()
    link(far_high, far_high, up, 6).wait_recv()
    far = half(column + 2, core)
    send(far, far, mate, 8)
    for offset, index in ((-1, 7), (2, 8), (1, 9)):
        theirs = half(column + offset, 1 - core)
        link(theirs, theirs, mate, index).wait_recv()
    for copy in sent:
        copy.wait_send()


PROJ_TILE = 512


def gather_keys(block, normed, w_query, q_bias, seq_count):
    rows, width = block.shape
    return pl.pallas_call(
        gather_kernel,
        out_shape=(
            jax.ShapeDtypeStruct((seq_count * rows, width), block.dtype),
            jax.ShapeDtypeStruct((normed.shape[0], w_query.shape[1]), jnp.bfloat16),
        ),
        in_specs=[
            pl.BlockSpec(memory_space=pl.ANY),
            pl.BlockSpec(memory_space=pl.ANY),
            pl.BlockSpec(memory_space=pl.ANY),
            pl.BlockSpec(memory_space=pltpu.VMEM),
        ],
        out_specs=(pl.BlockSpec(memory_space=pl.ANY), pl.BlockSpec(memory_space=pltpu.VMEM)),
        scratch_shapes=[
            pltpu.SemaphoreType.DMA((10,)),
            pltpu.SemaphoreType.DMA((10,)),
            pltpu.SemaphoreType.DMA((1,)),
            pltpu.VMEM((normed.shape[0], w_query.shape[1]), jnp.float32),
        ],
        compiler_params=pltpu.CompilerParams(collective_id=2, has_side_effects=True),
    )(block, normed, w_query, q_bias.reshape(1, -1))


def on_device(
    text, frames, tile_pos, frame_count, doc_ids, norm_gain, w_query, q_bias, w_key, w_value, v_bias
):
    seq_count = lax.axis_size("seq")
    vis_count = lax.axis_size("vis")
    shard_index = lax.axis_index("seq")
    shard_rows = text.shape[0]
    capacity = shard_rows // (seq_count * vis_count)
    first_row = shard_index * shard_rows
    payload = frame_slots(frames, tile_pos, frame_count, shard_rows, seq_count, capacity)
    gathered = exchange_frames(payload, vis_count)
    width = text.shape[1]
    incoming_place = gathered[:, :, width].astype(jnp.int32)
    merged = place_frames(text, gathered, incoming_place, width)
    widened = merged.astype(jnp.float32)
    mean_square = jnp.mean(widened * widened, axis=1, keepdims=True)
    normed = (widened * lax.rsqrt(mean_square + epsilon) * norm_gain).astype(jnp.bfloat16)
    key_rows = jnp.dot(normed, w_key, preferred_element_type=jnp.float32).astype(jnp.bfloat16)
    value_rows = (jnp.dot(normed, w_value, preferred_element_type=jnp.float32) + v_bias).astype(
        jnp.bfloat16
    )
    keyval = jnp.concatenate([key_rows, value_rows], axis=1)
    kv_heads = w_key.shape[1] // HEAD_DIM
    per_group = w_query.shape[1] // HEAD_DIM // kv_heads
    incoming_keys, queries = gather_keys(keyval, normed, w_query, q_bias, seq_count)
    return flash_attention(doc_ids, queries, incoming_keys)


KEY_BLOCK = 512
DOC_SPAN = 2048


def block_bounds(doc_ref, rows, key_rows):
    first = lax.axis_index("seq") * rows
    first_doc = doc_ref[first]
    low = 0
    for b in range(key_rows // KEY_BLOCK):
        low = low + (doc_ref[(b + 1) * KEY_BLOCK - 1] < first_doc).astype(jnp.int32)
    return low, (first + rows - 1) // KEY_BLOCK, first


def flash_kernel(doc_ref, q_ref, k_ref, v_ref, qdoc_ref, kdoc_ref, out_ref, peak_ref, total_ref, acc_ref, qcol_ref):
    step = pl.program_id(0)
    rows = q_ref.shape[0]
    heads = q_ref.shape[1] // HEAD_DIM
    low, high, first = block_bounds(doc_ref, rows, doc_ref.shape[0])
    block = low + step

    @pl.when(step == 0)
    def _():
        peak_ref[...] = jnp.full(peak_ref.shape, negative, jnp.float32)
        total_ref[...] = jnp.zeros(total_ref.shape, jnp.float32)
        acc_ref[...] = jnp.zeros(acc_ref.shape, jnp.float32)
        spread = jnp.broadcast_to(qdoc_ref[...], (rows, rows))
        diagonal = lax.broadcasted_iota(jnp.int32, (rows, rows), 0) == lax.broadcasted_iota(
            jnp.int32, (rows, rows), 1
        )
        qcol_ref[...] = jnp.sum(jnp.where(diagonal, spread, 0), axis=1, keepdims=True)

    @pl.when(block <= high)
    def _():
        key_place = block * KEY_BLOCK + lax.broadcasted_iota(jnp.int32, (1, KEY_BLOCK), 1)
        query_place = first + lax.broadcasted_iota(jnp.int32, (rows, 1), 0)
        allowed = (key_place <= query_place) & (kdoc_ref[...] == qcol_ref[...])
        keys = k_ref[...]
        vals = v_ref[...]
        for h in range(heads):
            cols = slice(h * HEAD_DIM, (h + 1) * HEAD_DIM)
            scores = lax.dot_general(
                q_ref[:, cols], keys, (((1,), (1,)), ((), ())),
                preferred_element_type=jnp.float32,
            ) * HEAD_DIM ** (-0.5)
            scores = jnp.where(allowed, scores, negative)
            old_peak = peak_ref[h]
            new_peak = jnp.maximum(old_peak, jnp.max(scores, axis=1, keepdims=True))
            raised = jnp.where(allowed, jnp.exp(scores - new_peak[:, :1]), 0.0)
            factor = jnp.exp(old_peak - new_peak)
            total_ref[h] = total_ref[h] * factor + jnp.sum(raised, axis=1, keepdims=True)
            peak_ref[h] = new_peak
            product = jnp.dot(raised.astype(jnp.bfloat16), vals, preferred_element_type=jnp.float32)
            acc_ref[:, cols] = acc_ref[:, cols] * factor[:, :1] + product

    @pl.when(step == pl.num_programs(0) - 1)
    def _():
        for h in range(heads):
            cols = slice(h * HEAD_DIM, (h + 1) * HEAD_DIM)
            out_ref[:, cols] = (acc_ref[:, cols] / total_ref[h][:, :1]).astype(out_ref.dtype)


def flash_attention(doc_ids, queries, keyval):
    rows, width = queries.shape
    key_rows = keyval.shape[0]
    steps = min(key_rows // KEY_BLOCK, (DOC_SPAN + rows - 2) // KEY_BLOCK + 2)
    heads = width // HEAD_DIM

    def clamp(j, d):
        low, high, _ = block_bounds(d, rows, key_rows)
        return jnp.minimum(low + j, high)

    grid_spec = pltpu.PrefetchScalarGridSpec(
        num_scalar_prefetch=1,
        grid=(steps,),
        in_specs=[
            pl.BlockSpec((rows, width), lambda j, d: (0, 0)),
            pl.BlockSpec((KEY_BLOCK, HEAD_DIM), lambda j, d: (clamp(j, d), 0)),
            pl.BlockSpec((KEY_BLOCK, HEAD_DIM), lambda j, d: (clamp(j, d), 1)),
            pl.BlockSpec((1, rows), lambda j, d: (0, lax.axis_index("seq"))),
            pl.BlockSpec((1, KEY_BLOCK), lambda j, d: (0, clamp(j, d))),
        ],
        out_specs=pl.BlockSpec((rows, width), lambda j, d: (0, 0)),
        scratch_shapes=[
            pltpu.VMEM((heads, rows, 1), jnp.float32),
            pltpu.VMEM((heads, rows, 1), jnp.float32),
            pltpu.VMEM((rows, width), jnp.float32),
            pltpu.VMEM((rows, 1), jnp.int32),
        ],
    )
    flops = 4 * rows * width * key_rows // 2
    doc_row = doc_ids.reshape(1, -1)
    return pl.pallas_call(
        flash_kernel,
        out_shape=jax.ShapeDtypeStruct((rows, width), jnp.bfloat16),
        grid_spec=grid_spec,
        compiler_params=pltpu.CompilerParams(dimension_semantics=("arbitrary",)),
        cost_estimate=pl.CostEstimate(
            flops=flops, transcendentals=rows * heads * key_rows // 2,
            bytes_accessed=2 * (2 * rows * width + key_rows * 2 * HEAD_DIM),
        ),
    )(doc_ids, queries, keyval, keyval, doc_row, doc_row)


def solution(mesh):
    in_specs = (
        P("seq", None),
        P(("seq", "vis"), None),
        P(("seq", "vis")),
        P(("seq", "vis")),
        P(),
        P(),
        P(None, "vis"),
        P("vis"),
        P(None, "vis"),
        P(None, "vis"),
        P("vis"),
    )
    out_specs = P("seq", "vis")
    return jax.shard_map(
        on_device, mesh=mesh, in_specs=in_specs, out_specs=out_specs, check_vma=False
    )
```

```python
import jax
import jax.numpy as jnp
from jax import lax
from jax.sharding import PartitionSpec as P
from jax.experimental import pallas as pl
from jax.experimental.pallas import tpu as pltpu

HEAD_DIM = 128


epsilon = 1e-06
negative = -1e30


def frame_slots(frames, tile_pos, frame_count, shard_rows, owners, capacity):
    row_count = frames.shape[0]
    row_ids = jnp.arange(row_count, dtype=jnp.int32)
    usable = row_ids < frame_count[0]
    owner = jnp.where(usable, tile_pos // shard_rows, owners)
    hits = (owner[:, None] == jnp.arange(owners, dtype=jnp.int32)[None, :]).astype(jnp.int32)
    earlier = (row_ids[:, None] > row_ids[None, :]).astype(jnp.int32)
    before = jnp.dot(earlier, hits, preferred_element_type=jnp.int32)
    rank = jnp.sum(before * hits, axis=1)
    slot_index = owner * capacity + rank
    slot_ids = jnp.arange(owners * capacity, dtype=jnp.int32)
    match = usable[:, None] & (slot_index[:, None] == slot_ids[None, :])
    filled = jnp.any(match, axis=0)
    local = tile_pos - owner * shard_rows
    slot_local = jnp.sum(jnp.where(match, local[:, None], 0), axis=0)
    slot_local = jnp.where(filled, slot_local, -1)
    slot_rows = jnp.dot(
        match.T.astype(frames.dtype), frames, preferred_element_type=jnp.float32
    ).astype(frames.dtype)
    place_col = jnp.broadcast_to(slot_local[:, None], (slot_local.shape[0], 128)).astype(frames.dtype)
    payload = jnp.concatenate([slot_rows, place_col], axis=1)
    return payload.reshape(owners, capacity, payload.shape[1])


def place_frames(text, incoming, incoming_place, width):
    lookup = incoming_place[None] == jnp.arange(text.shape[0], dtype=jnp.int32)[:, None, None]
    covered = jnp.any(lookup, axis=(1, 2))
    placed = lax.dot_general(
        lookup.astype(incoming.dtype), incoming, (((1, 2), (0, 1)), ((), ())),
        preferred_element_type=jnp.float32,
    )[:, :width].astype(text.dtype)
    return jnp.where(covered[:, None], placed, text)


def exchange_kernel(payload_ref, out_ref, send_a, recv_a, send_b, recv_b, local_sem):
    seq_count = lax.axis_size("seq")
    vis_count = lax.axis_size("vis")
    ring = vis_count // 2
    me_seq = lax.axis_index("seq")
    me_vis = lax.axis_index("vis")
    ring_pos = lax.rem(me_vis, ring)
    ring_id = me_vis // ring

    def vis_of(ring_index, position):
        return ring_index * ring + lax.rem(position + ring, ring)

    right = vis_of(ring_id, ring_pos + 1)
    left = vis_of(ring_id, ring_pos - 1)
    partner = vis_of(1 - ring_id, ring_pos)
    barrier = pltpu.get_barrier_semaphore()
    for k in range(1, seq_count):
        pl.semaphore_signal(
            barrier, inc=1, device_id=(lax.rem(me_seq + k, seq_count), me_vis),
            device_id_type=pl.DeviceIdType.MESH,
        )
    for peer in (left, right, partner):
        pl.semaphore_signal(
            barrier, inc=1, device_id=(me_seq, peer), device_id_type=pl.DeviceIdType.MESH
        )
    pl.semaphore_wait(barrier, seq_count + 2)
    base = me_vis * seq_count
    local = pltpu.make_async_copy(payload_ref.at[me_seq], out_ref.at[base], local_sem.at[0])
    local.start()
    first = []
    for k in range(1, seq_count):
        target = lax.rem(me_seq + k, seq_count)
        copy = pltpu.make_async_remote_copy(
            src_ref=payload_ref.at[target],
            dst_ref=out_ref.at[base + k],
            send_sem=send_a.at[k],
            recv_sem=recv_a.at[k],
            device_id=(target, me_vis),
            device_id_type=pl.DeviceIdType.MESH,
        )
        copy.start()
        first.append(copy)
    local.wait()

    def arrivals(ks):
        for k in ks:
            source = lax.rem(me_seq + seq_count - k, seq_count)
            incoming = pltpu.make_async_remote_copy(
                src_ref=payload_ref.at[source],
                dst_ref=out_ref.at[base + k],
                send_sem=send_a.at[k],
                recv_sem=recv_a.at[k],
                device_id=(source, me_vis),
                device_id_type=pl.DeviceIdType.MESH,
            )
            incoming.wait_recv()

    waves = WAVES
    size = seq_count // waves
    split = waves // 2
    far = vis_of(ring_id, ring_pos + 2)
    left_partner = vis_of(1 - ring_id, ring_pos - 1)
    right_partner = vis_of(1 - ring_id, ring_pos + 1)
    far_partner = vis_of(1 - ring_id, ring_pos + 2)
    sent = []

    def part(owner, w):
        return out_ref.at[pl.ds(owner * seq_count + w * size, size)]

    def link(owner, w, peer, kind):
        piece = part(owner, w)
        return pltpu.make_async_remote_copy(
            src_ref=piece, dst_ref=piece,
            send_sem=send_b.at[kind * waves + w], recv_sem=recv_b.at[kind * waves + w],
            device_id=(me_seq, peer), device_id_type=pl.DeviceIdType.MESH,
        )

    def send(owner, w, peer, kind):
        copy = link(owner, w, peer, kind)
        copy.start()
        sent.append(copy)

    for w in range(waves):
        arrivals(range(max(1, w * size), (w + 1) * size))
        send(me_vis, w, right, 0)
        send(me_vis, w, left, 1)
        send(me_vis, w, partner, 2)
    for copy in first:
        copy.wait_send()
    for w in range(waves):
        link(partner, w, partner, 2).wait_recv()
        send(partner, w, right, 3)
        send(partner, w, left, 4)
        if w < split:
            link(left, w, left, 0).wait_recv()
            send(left, w, right, 5)
        else:
            link(right, w, right, 1).wait_recv()
            send(right, w, left, 6)
    for w in range(waves):
        if w < split:
            link(left_partner, w, left, 3).wait_recv()
            send(left_partner, w, right, 7)
        else:
            link(right_partner, w, right, 4).wait_recv()
            send(right_partner, w, left, 8)
    for w in range(waves):
        if w < split:
            link(right, w, right, 1).wait_recv()
            link(right_partner, w, right, 4).wait_recv()
            link(far, w, left, 5).wait_recv()
            link(far_partner, w, left, 7).wait_recv()
        else:
            link(left, w, left, 0).wait_recv()
            link(left_partner, w, left, 3).wait_recv()
            link(far, w, right, 6).wait_recv()
            link(far_partner, w, right, 8).wait_recv()
    for copy in sent:
        copy.wait_send()


def exchange_frames(payload, vis_count):
    owners, capacity, width = payload.shape
    return pl.pallas_call(
        exchange_kernel,
        out_shape=jax.ShapeDtypeStruct((vis_count * owners, capacity, width), payload.dtype),
        in_specs=[pl.BlockSpec(memory_space=pl.ANY)],
        out_specs=pl.BlockSpec(memory_space=pl.ANY),
        scratch_shapes=[
            pltpu.SemaphoreType.DMA((owners,)),
            pltpu.SemaphoreType.DMA((owners,)),
            pltpu.SemaphoreType.DMA((9 * WAVES,)),
            pltpu.SemaphoreType.DMA((9 * WAVES,)),
            pltpu.SemaphoreType.DMA((1,)),
        ],
        compiler_params=pltpu.CompilerParams(collective_id=1, has_side_effects=True),
    )(payload)


def gather_kernel(
    block_ref, normed_ref, w_ref, bias_ref, out_ref, q_ref, send_sem, recv_sem, local_sem, acc_ref
):
    rows = block_ref.shape[0]
    me_seq = lax.axis_index("seq")
    me_vis = lax.axis_index("vis")
    column = me_seq // 4
    layer = lax.rem(me_seq // 2, 2)
    core = lax.rem(me_seq, 2)
    ring = lax.axis_size("seq") // 4

    def seq_of(y, z, c):
        return (lax.rem(y + ring, ring) * 2 + z) * 2 + c

    mate = seq_of(column, layer, 1 - core)
    across = seq_of(column, 1 - layer, core)
    diagonal = seq_of(column, 1 - layer, 1 - core)
    up = seq_of(column + 1, layer, core)
    down = seq_of(column - 1, layer, core)
    barrier = pltpu.get_barrier_semaphore()
    for peer in (mate, across, diagonal, up, down):
        pl.semaphore_signal(
            barrier, inc=1, device_id=(peer, me_vis), device_id_type=pl.DeviceIdType.MESH
        )
    pl.semaphore_wait(barrier, 5)

    def rows_of(start, count):
        return out_ref.at[pl.ds(pl.multiple_of(start, rows), count)]

    def link(src, dst, peer, index):
        return pltpu.make_async_remote_copy(
            src_ref=src, dst_ref=dst, send_sem=send_sem.at[index], recv_sem=recv_sem.at[index],
            device_id=(peer, me_vis), device_id_type=pl.DeviceIdType.MESH,
        )

    sent = []

    def send(src, dst, peer, index):
        copy = link(src, dst, peer, index)
        copy.start()
        sent.append(copy)

    own = rows_of(me_seq * rows, rows)
    local = pltpu.make_async_copy(block_ref, own, local_sem.at[0])
    local.start()
    send(block_ref, own, mate, 0)
    send(block_ref, own, across, 1)
    send(block_ref, own, diagonal, 2)
    depth = normed_ref.shape[1] // 2

    def project(part):
        def body(n_blk, w_blk):
            acc_ref[...] += jnp.dot(n_blk[...], w_blk[...], preferred_element_type=jnp.float32)

        pltpu.emit_pipeline(
            body,
            grid=(depth // PROJ_TILE,),
            in_specs=[
                pl.BlockSpec((normed_ref.shape[0], PROJ_TILE), lambda k: (0, k)),
                pl.BlockSpec((PROJ_TILE, w_ref.shape[1]), lambda k: (k, 0)),
            ],
        )(normed_ref.at[:, pl.ds(part * depth, depth)], w_ref.at[pl.ds(part * depth, depth)])

    acc_ref[...] = jnp.zeros(acc_ref.shape, jnp.float32)
    project(0)
    local.wait()
    link(block_ref, rows_of(mate * rows, rows), mate, 0).wait_recv()
    link(block_ref, rows_of(across * rows, rows), across, 1).wait_recv()
    link(block_ref, rows_of(diagonal * rows, rows), diagonal, 2).wait_recv()

    def half(y, h):
        return rows_of((lax.rem(y + ring, ring) * 4 + h * 2) * rows, 2 * rows)

    def quarter(y, h, q):
        return rows_of((lax.rem(y + ring, ring) * 4 + h * 2 + q) * rows, rows)

    mine = half(column, core)
    send(mine, mine, up, 3)
    send(mine, mine, down, 4)
    project(1)
    below = half(column - 1, core)
    link(below, below, down, 3).wait_recv()
    send(below, below, mate, 7)
    piece = quarter(column - 1, core, 0)
    send(piece, piece, up, 5)
    above = half(column + 1, core)
    link(above, above, up, 4).wait_recv()
    send(above, above, mate, 9)
    piece = quarter(column + 1, core, 1)
    send(piece, piece, down, 6)
    q_ref[...] = (acc_ref[...] + bias_ref[...]).astype(q_ref.dtype)
    far_low = quarter(column + 2, core, 0)
    far_high = quarter(column + 2, core, 1)
    link(far_low, far_low, down, 5).wait_recv()
    link(far_high, far_high, up, 6).wait_recv()
    far = half(column + 2, core)
    send(far, far, mate, 8)
    for offset, index in ((-1, 7), (2, 8), (1, 9)):
        theirs = half(column + offset, 1 - core)
        link(theirs, theirs, mate, index).wait_recv()
    for copy in sent:
        copy.wait_send()


PROJ_TILE = 512


def gather_keys(block, normed, w_query, q_bias, seq_count):
    rows, width = block.shape
    return pl.pallas_call(
        gather_kernel,
        out_shape=(
            jax.ShapeDtypeStruct((seq_count * rows, width), block.dtype),
            jax.ShapeDtypeStruct((normed.shape[0], w_query.shape[1]), jnp.bfloat16),
        ),
        in_specs=[
            pl.BlockSpec(memory_space=pl.ANY),
            pl.BlockSpec(memory_space=pl.ANY),
            pl.BlockSpec(memory_space=pl.ANY),
            pl.BlockSpec(memory_space=pltpu.VMEM),
        ],
        out_specs=(pl.BlockSpec(memory_space=pl.ANY), pl.BlockSpec(memory_space=pltpu.VMEM)),
        scratch_shapes=[
            pltpu.SemaphoreType.DMA((10,)),
            pltpu.SemaphoreType.DMA((10,)),
            pltpu.SemaphoreType.DMA((1,)),
            pltpu.VMEM((normed.shape[0], w_query.shape[1]), jnp.float32),
        ],
        compiler_params=pltpu.CompilerParams(collective_id=2, has_side_effects=True),
    )(block, normed, w_query, q_bias.reshape(1, -1))


def on_device(
    text, frames, tile_pos, frame_count, doc_ids, norm_gain, w_query, q_bias, w_key, w_value, v_bias
):
    seq_count = lax.axis_size("seq")
    vis_count = lax.axis_size("vis")
    shard_index = lax.axis_index("seq")
    shard_rows = text.shape[0]
    capacity = shard_rows // (seq_count * vis_count)
    first_row = shard_index * shard_rows
    payload = frame_slots(frames, tile_pos, frame_count, shard_rows, seq_count, capacity)
    gathered = exchange_frames(payload, vis_count)
    width = text.shape[1]
    incoming_place = gathered[:, :, width].astype(jnp.int32)
    merged = place_frames(text, gathered, incoming_place, width)
    widened = merged.astype(jnp.float32)
    mean_square = jnp.mean(widened * widened, axis=1, keepdims=True)
    normed = (widened * lax.rsqrt(mean_square + epsilon) * norm_gain).astype(jnp.bfloat16)
    key_rows = jnp.dot(normed, w_key, preferred_element_type=jnp.float32).astype(jnp.bfloat16)
    value_rows = (jnp.dot(normed, w_value, preferred_element_type=jnp.float32) + v_bias).astype(
        jnp.bfloat16
    )
    keyval = jnp.concatenate([key_rows, value_rows], axis=1)
    kv_heads = w_key.shape[1] // HEAD_DIM
    per_group = w_query.shape[1] // HEAD_DIM // kv_heads
    incoming_keys, queries = gather_keys(keyval, normed, w_query, q_bias, seq_count)
    return flash_attention(doc_ids, queries, incoming_keys)


KEY_BLOCK = 512
WAVES = 4
DOC_SPAN = 2048


def block_bounds(doc_ref, rows, key_rows):
    first = lax.axis_index("seq") * rows
    first_doc = doc_ref[first]
    low = 0
    for b in range(key_rows // KEY_BLOCK):
        low = low + (doc_ref[(b + 1) * KEY_BLOCK - 1] < first_doc).astype(jnp.int32)
    return low, (first + rows - 1) // KEY_BLOCK, first


def flash_kernel(doc_ref, q_ref, k_ref, v_ref, qdoc_ref, kdoc_ref, out_ref, peak_ref, total_ref, acc_ref, qcol_ref):
    step = pl.program_id(0)
    rows = q_ref.shape[0]
    heads = q_ref.shape[1] // HEAD_DIM
    low, high, first = block_bounds(doc_ref, rows, doc_ref.shape[0])
    block = low + step

    @pl.when(step == 0)
    def _():
        peak_ref[...] = jnp.full(peak_ref.shape, negative, jnp.float32)
        total_ref[...] = jnp.zeros(total_ref.shape, jnp.float32)
        acc_ref[...] = jnp.zeros(acc_ref.shape, jnp.float32)
        spread = jnp.broadcast_to(qdoc_ref[...], (rows, rows))
        diagonal = lax.broadcasted_iota(jnp.int32, (rows, rows), 0) == lax.broadcasted_iota(
            jnp.int32, (rows, rows), 1
        )
        qcol_ref[...] = jnp.sum(jnp.where(diagonal, spread, 0), axis=1, keepdims=True)

    @pl.when(block <= high)
    def _():
        key_place = block * KEY_BLOCK + lax.broadcasted_iota(jnp.int32, (1, KEY_BLOCK), 1)
        query_place = first + lax.broadcasted_iota(jnp.int32, (rows, 1), 0)
        allowed = (key_place <= query_place) & (kdoc_ref[...] == qcol_ref[...])
        keys = k_ref[...]
        vals = v_ref[...]
        for h in range(heads):
            cols = slice(h * HEAD_DIM, (h + 1) * HEAD_DIM)
            scores = lax.dot_general(
                q_ref[:, cols], keys, (((1,), (1,)), ((), ())),
                preferred_element_type=jnp.float32,
            ) * HEAD_DIM ** (-0.5)
            scores = jnp.where(allowed, scores, negative)
            old_peak = peak_ref[h]
            new_peak = jnp.maximum(old_peak, jnp.max(scores, axis=1, keepdims=True))
            raised = jnp.where(allowed, jnp.exp(scores - new_peak[:, :1]), 0.0)
            factor = jnp.exp(old_peak - new_peak)
            total_ref[h] = total_ref[h] * factor + jnp.sum(raised, axis=1, keepdims=True)
            peak_ref[h] = new_peak
            product = jnp.dot(raised.astype(jnp.bfloat16), vals, preferred_element_type=jnp.float32)
            acc_ref[:, cols] = acc_ref[:, cols] * factor[:, :1] + product

    @pl.when(step == pl.num_programs(0) - 1)
    def _():
        for h in range(heads):
            cols = slice(h * HEAD_DIM, (h + 1) * HEAD_DIM)
            out_ref[:, cols] = (acc_ref[:, cols] / total_ref[h][:, :1]).astype(out_ref.dtype)


def flash_attention(doc_ids, queries, keyval):
    rows, width = queries.shape
    key_rows = keyval.shape[0]
    steps = min(key_rows // KEY_BLOCK, (DOC_SPAN + rows - 2) // KEY_BLOCK + 2)
    heads = width // HEAD_DIM

    def clamp(j, d):
        low, high, _ = block_bounds(d, rows, key_rows)
        return jnp.minimum(low + j, high)

    grid_spec = pltpu.PrefetchScalarGridSpec(
        num_scalar_prefetch=1,
        grid=(steps,),
        in_specs=[
            pl.BlockSpec((rows, width), lambda j, d: (0, 0)),
            pl.BlockSpec((KEY_BLOCK, HEAD_DIM), lambda j, d: (clamp(j, d), 0)),
            pl.BlockSpec((KEY_BLOCK, HEAD_DIM), lambda j, d: (clamp(j, d), 1)),
            pl.BlockSpec((1, rows), lambda j, d: (0, lax.axis_index("seq"))),
            pl.BlockSpec((1, KEY_BLOCK), lambda j, d: (0, clamp(j, d))),
        ],
        out_specs=pl.BlockSpec((rows, width), lambda j, d: (0, 0)),
        scratch_shapes=[
            pltpu.VMEM((heads, rows, 1), jnp.float32),
            pltpu.VMEM((heads, rows, 1), jnp.float32),
            pltpu.VMEM((rows, width), jnp.float32),
            pltpu.VMEM((rows, 1), jnp.int32),
        ],
    )
    flops = 4 * rows * width * key_rows // 2
    doc_row = doc_ids.reshape(1, -1)
    return pl.pallas_call(
        flash_kernel,
        out_shape=jax.ShapeDtypeStruct((rows, width), jnp.bfloat16),
        grid_spec=grid_spec,
        compiler_params=pltpu.CompilerParams(dimension_semantics=("arbitrary",)),
        cost_estimate=pl.CostEstimate(
            flops=flops, transcendentals=rows * heads * key_rows // 2,
            bytes_accessed=2 * (2 * rows * width + key_rows * 2 * HEAD_DIM),
        ),
    )(doc_ids, queries, keyval, keyval, doc_row, doc_row)


def solution(mesh):
    in_specs = (
        P("seq", None),
        P(("seq", "vis"), None),
        P(("seq", "vis")),
        P(("seq", "vis")),
        P(),
        P(),
        P(None, "vis"),
        P("vis"),
        P(None, "vis"),
        P(None, "vis"),
        P("vis"),
    )
    out_specs = P("seq", "vis")
    return jax.shard_map(
        on_device, mesh=mesh, in_specs=in_specs, out_specs=out_specs, check_vma=False
    )
```

```python
import jax
import jax.numpy as jnp
from jax import lax
from jax.sharding import PartitionSpec as P
from jax.experimental import pallas as pl
from jax.experimental.pallas import tpu as pltpu

HEAD_DIM = 128


epsilon = 1e-06
negative = -1e30


def frame_slots(frames, tile_pos, frame_count, shard_rows, owners, capacity):
    row_count = frames.shape[0]
    row_ids = jnp.arange(row_count, dtype=jnp.int32)
    usable = row_ids < frame_count[0]
    owner = jnp.where(usable, tile_pos // shard_rows, owners)
    hits = (owner[:, None] == jnp.arange(owners, dtype=jnp.int32)[None, :]).astype(jnp.int32)
    earlier = (row_ids[:, None] > row_ids[None, :]).astype(jnp.int32)
    before = jnp.dot(earlier, hits, preferred_element_type=jnp.int32)
    rank = jnp.sum(before * hits, axis=1)
    slot_index = owner * capacity + rank
    slot_ids = jnp.arange(owners * capacity, dtype=jnp.int32)
    match = usable[:, None] & (slot_index[:, None] == slot_ids[None, :])
    filled = jnp.any(match, axis=0)
    local = tile_pos - owner * shard_rows
    slot_local = jnp.sum(jnp.where(match, local[:, None], 0), axis=0)
    slot_local = jnp.where(filled, slot_local, -1)
    slot_rows = jnp.dot(
        match.T.astype(frames.dtype), frames, preferred_element_type=jnp.float32
    ).astype(frames.dtype)
    place_col = jnp.broadcast_to(slot_local[:, None], (slot_local.shape[0], 128)).astype(frames.dtype)
    payload = jnp.concatenate([slot_rows, place_col], axis=1)
    return payload.reshape(owners, capacity, payload.shape[1])


def place_frames(text, incoming, incoming_place, width):
    lookup = incoming_place[None] == jnp.arange(text.shape[0], dtype=jnp.int32)[:, None, None]
    covered = jnp.any(lookup, axis=(1, 2))
    placed = lax.dot_general(
        lookup.astype(incoming.dtype), incoming, (((1, 2), (0, 1)), ((), ())),
        preferred_element_type=jnp.float32,
    )[:, :width].astype(text.dtype)
    return jnp.where(covered[:, None], placed, text)


def exchange_kernel(payload_ref, out_ref, send_a, recv_a, send_b, recv_b, local_sem):
    seq_count = lax.axis_size("seq")
    vis_count = lax.axis_size("vis")
    ring = vis_count // 2
    me_seq = lax.axis_index("seq")
    me_vis = lax.axis_index("vis")
    ring_pos = lax.rem(me_vis, ring)
    ring_id = me_vis // ring

    def vis_of(ring_index, position):
        return ring_index * ring + lax.rem(position + ring, ring)

    right = vis_of(ring_id, ring_pos + 1)
    left = vis_of(ring_id, ring_pos - 1)
    partner = vis_of(1 - ring_id, ring_pos)
    barrier = pltpu.get_barrier_semaphore()
    for k in range(1, seq_count):
        pl.semaphore_signal(
            barrier, inc=1, device_id=(lax.rem(me_seq + k, seq_count), me_vis),
            device_id_type=pl.DeviceIdType.MESH,
        )
    for peer in (left, right, partner):
        pl.semaphore_signal(
            barrier, inc=1, device_id=(me_seq, peer), device_id_type=pl.DeviceIdType.MESH
        )
    pl.semaphore_wait(barrier, seq_count + 2)
    base = me_vis * seq_count
    local = pltpu.make_async_copy(payload_ref.at[me_seq], out_ref.at[base], local_sem.at[0])
    local.start()
    first = []
    for k in range(1, seq_count):
        target = lax.rem(me_seq + k, seq_count)
        copy = pltpu.make_async_remote_copy(
            src_ref=payload_ref.at[target],
            dst_ref=out_ref.at[base + k],
            send_sem=send_a.at[k],
            recv_sem=recv_a.at[k],
            device_id=(target, me_vis),
            device_id_type=pl.DeviceIdType.MESH,
        )
        copy.start()
        first.append(copy)
    local.wait()

    def arrivals(ks):
        for k in ks:
            source = lax.rem(me_seq + seq_count - k, seq_count)
            incoming = pltpu.make_async_remote_copy(
                src_ref=payload_ref.at[source],
                dst_ref=out_ref.at[base + k],
                send_sem=send_a.at[k],
                recv_sem=recv_a.at[k],
                device_id=(source, me_vis),
                device_id_type=pl.DeviceIdType.MESH,
            )
            incoming.wait_recv()

    arrivals(range(1, seq_count // 2))

    half = seq_count // 2

    def region(owner, part):
        if part == 0:
            return out_ref.at[pl.ds(owner * seq_count, seq_count)]
        start = owner * seq_count + (part - 1) * half
        return out_ref.at[pl.ds(start, half)]

    def link(owner, part, peer, index):
        piece = region(owner, part)
        return pltpu.make_async_remote_copy(
            src_ref=piece,
            dst_ref=piece,
            send_sem=send_b.at[index],
            recv_sem=recv_b.at[index],
            device_id=(me_seq, peer),
            device_id_type=pl.DeviceIdType.MESH,
        )

    far = vis_of(ring_id, ring_pos + 2)
    left_partner = vis_of(1 - ring_id, ring_pos - 1)
    right_partner = vis_of(1 - ring_id, ring_pos + 1)
    far_partner = vis_of(1 - ring_id, ring_pos + 2)
    sent = []

    def send(owner, part, peer, index):
        copy = link(owner, part, peer, index)
        copy.start()
        sent.append(copy)

    send(me_vis, 1, right, 1)
    send(me_vis, 1, left, 2)
    send(me_vis, 1, partner, 3)
    arrivals(range(seq_count // 2, seq_count))
    for copy in first:
        copy.wait_send()
    send(me_vis, 2, right, 10)
    send(me_vis, 2, left, 11)
    send(me_vis, 2, partner, 12)
    link(partner, 1, partner, 3).wait_recv()
    send(partner, 1, right, 4)
    send(partner, 1, left, 5)
    link(left, 1, left, 1).wait_recv()
    send(left, 1, right, 6)
    link(partner, 2, partner, 12).wait_recv()
    send(partner, 2, right, 13)
    send(partner, 2, left, 14)
    link(right, 2, right, 11).wait_recv()
    send(right, 2, left, 7)
    link(left_partner, 1, left, 4).wait_recv()
    send(left_partner, 1, right, 8)
    link(right_partner, 2, right, 14).wait_recv()
    send(right_partner, 2, left, 9)
    link(left, 2, left, 10).wait_recv()
    link(right, 1, right, 2).wait_recv()
    link(left_partner, 2, left, 13).wait_recv()
    link(right_partner, 1, right, 5).wait_recv()
    link(far, 1, left, 6).wait_recv()
    link(far, 2, right, 7).wait_recv()
    link(far_partner, 1, left, 8).wait_recv()
    link(far_partner, 2, right, 9).wait_recv()
    for copy in sent:
        copy.wait_send()


def exchange_frames(payload, vis_count):
    owners, capacity, width = payload.shape
    return pl.pallas_call(
        exchange_kernel,
        out_shape=jax.ShapeDtypeStruct((vis_count * owners, capacity, width), payload.dtype),
        in_specs=[pl.BlockSpec(memory_space=pl.ANY)],
        out_specs=pl.BlockSpec(memory_space=pl.ANY),
        scratch_shapes=[
            pltpu.SemaphoreType.DMA((owners,)),
            pltpu.SemaphoreType.DMA((owners,)),
            pltpu.SemaphoreType.DMA((15,)),
            pltpu.SemaphoreType.DMA((15,)),
            pltpu.SemaphoreType.DMA((1,)),
        ],
        compiler_params=pltpu.CompilerParams(collective_id=1, has_side_effects=True),
    )(payload)


def gather_kernel(
    block_ref, normed_ref, w_ref, bias_ref, out_ref, q_ref, send_sem, recv_sem, local_sem, acc_ref
):
    rows = block_ref.shape[0]
    me_seq = lax.axis_index("seq")
    me_vis = lax.axis_index("vis")
    column = me_seq // 4
    layer = lax.rem(me_seq // 2, 2)
    core = lax.rem(me_seq, 2)
    ring = lax.axis_size("seq") // 4

    def seq_of(y, z, c):
        return (lax.rem(y + ring, ring) * 2 + z) * 2 + c

    mate = seq_of(column, layer, 1 - core)
    across = seq_of(column, 1 - layer, core)
    diagonal = seq_of(column, 1 - layer, 1 - core)
    up = seq_of(column + 1, layer, core)
    down = seq_of(column - 1, layer, core)
    barrier = pltpu.get_barrier_semaphore()
    for peer in (mate, across, up, down):
        pl.semaphore_signal(
            barrier, inc=1, device_id=(peer, me_vis), device_id_type=pl.DeviceIdType.MESH
        )
    pl.semaphore_wait(barrier, 4)

    def rows_of(start, count):
        return out_ref.at[pl.ds(pl.multiple_of(start, rows), count)]

    def link(src, dst, peer, index):
        return pltpu.make_async_remote_copy(
            src_ref=src, dst_ref=dst, send_sem=send_sem.at[index], recv_sem=recv_sem.at[index],
            device_id=(peer, me_vis), device_id_type=pl.DeviceIdType.MESH,
        )

    sent = []

    def send(src, dst, peer, index):
        copy = link(src, dst, peer, index)
        copy.start()
        sent.append(copy)

    own = rows_of(me_seq * rows, rows)
    local = pltpu.make_async_copy(block_ref, own, local_sem.at[0])
    local.start()
    send(block_ref, own, mate, 0)
    send(block_ref, own, across, 1)
    depth = normed_ref.shape[1] // 2

    def project(part):
        def body(n_blk, w_blk):
            acc_ref[...] += jnp.dot(n_blk[...], w_blk[...], preferred_element_type=jnp.float32)

        pltpu.emit_pipeline(
            body,
            grid=(depth // PROJ_TILE,),
            in_specs=[
                pl.BlockSpec((normed_ref.shape[0], PROJ_TILE), lambda k: (0, k)),
                pl.BlockSpec((PROJ_TILE, w_ref.shape[1]), lambda k: (k, 0)),
            ],
        )(normed_ref.at[:, pl.ds(part * depth, depth)], w_ref.at[pl.ds(part * depth, depth)])

    acc_ref[...] = jnp.zeros(acc_ref.shape, jnp.float32)
    project(0)
    local.wait()
    link(block_ref, rows_of(mate * rows, rows), mate, 0).wait_recv()
    crossed = rows_of(across * rows, rows)
    link(block_ref, crossed, across, 1).wait_recv()
    send(crossed, crossed, mate, 2)
    landed = rows_of(diagonal * rows, rows)
    link(landed, landed, mate, 2).wait_recv()

    def half(y, h):
        return rows_of((lax.rem(y + ring, ring) * 4 + h * 2) * rows, 2 * rows)

    def quarter(y, h, q):
        return rows_of((lax.rem(y + ring, ring) * 4 + h * 2 + q) * rows, rows)

    mine = half(column, core)
    send(mine, mine, up, 3)
    send(mine, mine, down, 4)
    project(1)
    below = half(column - 1, core)
    link(below, below, down, 3).wait_recv()
    send(below, below, mate, 7)
    piece = quarter(column - 1, core, 0)
    send(piece, piece, up, 5)
    above = half(column + 1, core)
    link(above, above, up, 4).wait_recv()
    send(above, above, mate, 9)
    piece = quarter(column + 1, core, 1)
    send(piece, piece, down, 6)
    q_ref[...] = (acc_ref[...] + bias_ref[...]).astype(q_ref.dtype)
    far_low = quarter(column + 2, core, 0)
    far_high = quarter(column + 2, core, 1)
    link(far_low, far_low, down, 5).wait_recv()
    link(far_high, far_high, up, 6).wait_recv()
    far = half(column + 2, core)
    send(far, far, mate, 8)
    for offset, index in ((-1, 7), (2, 8), (1, 9)):
        theirs = half(column + offset, 1 - core)
        link(theirs, theirs, mate, index).wait_recv()
    for copy in sent:
        copy.wait_send()


PROJ_TILE = 512


def gather_keys(block, normed, w_query, q_bias, seq_count):
    rows, width = block.shape
    return pl.pallas_call(
        gather_kernel,
        out_shape=(
            jax.ShapeDtypeStruct((seq_count * rows, width), block.dtype),
            jax.ShapeDtypeStruct((normed.shape[0], w_query.shape[1]), jnp.bfloat16),
        ),
        in_specs=[
            pl.BlockSpec(memory_space=pl.ANY),
            pl.BlockSpec(memory_space=pl.ANY),
            pl.BlockSpec(memory_space=pl.ANY),
            pl.BlockSpec(memory_space=pltpu.VMEM),
        ],
        out_specs=(pl.BlockSpec(memory_space=pl.ANY), pl.BlockSpec(memory_space=pltpu.VMEM)),
        scratch_shapes=[
            pltpu.SemaphoreType.DMA((10,)),
            pltpu.SemaphoreType.DMA((10,)),
            pltpu.SemaphoreType.DMA((1,)),
            pltpu.VMEM((normed.shape[0], w_query.shape[1]), jnp.float32),
        ],
        compiler_params=pltpu.CompilerParams(collective_id=2, has_side_effects=True),
    )(block, normed, w_query, q_bias.reshape(1, -1))


def on_device(
    text, frames, tile_pos, frame_count, doc_ids, norm_gain, w_query, q_bias, w_key, w_value, v_bias
):
    seq_count = lax.axis_size("seq")
    vis_count = lax.axis_size("vis")
    shard_index = lax.axis_index("seq")
    shard_rows = text.shape[0]
    capacity = shard_rows // (seq_count * vis_count)
    first_row = shard_index * shard_rows
    payload = frame_slots(frames, tile_pos, frame_count, shard_rows, seq_count, capacity)
    gathered = exchange_frames(payload, vis_count)
    width = text.shape[1]
    incoming_place = gathered[:, :, width].astype(jnp.int32)
    merged = place_frames(text, gathered, incoming_place, width)
    widened = merged.astype(jnp.float32)
    mean_square = jnp.mean(widened * widened, axis=1, keepdims=True)
    normed = (widened * lax.rsqrt(mean_square + epsilon) * norm_gain).astype(jnp.bfloat16)
    key_rows = jnp.dot(normed, w_key, preferred_element_type=jnp.float32).astype(jnp.bfloat16)
    value_rows = (jnp.dot(normed, w_value, preferred_element_type=jnp.float32) + v_bias).astype(
        jnp.bfloat16
    )
    keyval = jnp.concatenate([key_rows, value_rows], axis=1)
    kv_heads = w_key.shape[1] // HEAD_DIM
    per_group = w_query.shape[1] // HEAD_DIM // kv_heads
    incoming_keys, queries = gather_keys(keyval, normed, w_query, q_bias, seq_count)
    return flash_attention(doc_ids, queries, incoming_keys)


KEY_BLOCK = 512
DOC_SPAN = 2048


def block_bounds(doc_ref, rows, key_rows):
    first = lax.axis_index("seq") * rows
    first_doc = doc_ref[first]
    low = 0
    for b in range(key_rows // KEY_BLOCK):
        low = low + (doc_ref[(b + 1) * KEY_BLOCK - 1] < first_doc).astype(jnp.int32)
    return low, (first + rows - 1) // KEY_BLOCK, first


def flash_kernel(doc_ref, q_ref, k_ref, v_ref, qdoc_ref, kdoc_ref, out_ref, peak_ref, total_ref, acc_ref, qcol_ref):
    step = pl.program_id(0)
    rows = q_ref.shape[0]
    heads = q_ref.shape[1] // HEAD_DIM
    low, high, first = block_bounds(doc_ref, rows, doc_ref.shape[0])
    block = low + step

    @pl.when(step == 0)
    def _():
        peak_ref[...] = jnp.full(peak_ref.shape, negative, jnp.float32)
        total_ref[...] = jnp.zeros(total_ref.shape, jnp.float32)
        acc_ref[...] = jnp.zeros(acc_ref.shape, jnp.float32)
        spread = jnp.broadcast_to(qdoc_ref[...], (rows, rows))
        diagonal = lax.broadcasted_iota(jnp.int32, (rows, rows), 0) == lax.broadcasted_iota(
            jnp.int32, (rows, rows), 1
        )
        qcol_ref[...] = jnp.sum(jnp.where(diagonal, spread, 0), axis=1, keepdims=True)

    @pl.when(block <= high)
    def _():
        key_place = block * KEY_BLOCK + lax.broadcasted_iota(jnp.int32, (1, KEY_BLOCK), 1)
        query_place = first + lax.broadcasted_iota(jnp.int32, (rows, 1), 0)
        allowed = (key_place <= query_place) & (kdoc_ref[...] == qcol_ref[...])
        keys = k_ref[...]
        vals = v_ref[...]
        for h in range(heads):
            cols = slice(h * HEAD_DIM, (h + 1) * HEAD_DIM)
            scores = lax.dot_general(
                q_ref[:, cols], keys, (((1,), (1,)), ((), ())),
                preferred_element_type=jnp.float32,
            ) * HEAD_DIM ** (-0.5)
            scores = jnp.where(allowed, scores, negative)
            old_peak = peak_ref[h]
            new_peak = jnp.maximum(old_peak, jnp.max(scores, axis=1, keepdims=True))
            raised = jnp.where(allowed, jnp.exp(scores - new_peak[:, :1]), 0.0)
            factor = jnp.exp(old_peak - new_peak)
            total_ref[h] = total_ref[h] * factor + jnp.sum(raised, axis=1, keepdims=True)
            peak_ref[h] = new_peak
            product = jnp.dot(raised.astype(jnp.bfloat16), vals, preferred_element_type=jnp.float32)
            acc_ref[:, cols] = acc_ref[:, cols] * factor[:, :1] + product

    @pl.when(step == pl.num_programs(0) - 1)
    def _():
        for h in range(heads):
            cols = slice(h * HEAD_DIM, (h + 1) * HEAD_DIM)
            out_ref[:, cols] = (acc_ref[:, cols] / total_ref[h][:, :1]).astype(out_ref.dtype)


def flash_attention(doc_ids, queries, keyval):
    rows, width = queries.shape
    key_rows = keyval.shape[0]
    steps = min(key_rows // KEY_BLOCK, (DOC_SPAN + rows - 2) // KEY_BLOCK + 2)
    heads = width // HEAD_DIM

    def clamp(j, d):
        low, high, _ = block_bounds(d, rows, key_rows)
        return jnp.minimum(low + j, high)

    grid_spec = pltpu.PrefetchScalarGridSpec(
        num_scalar_prefetch=1,
        grid=(steps,),
        in_specs=[
            pl.BlockSpec((rows, width), lambda j, d: (0, 0)),
            pl.BlockSpec((KEY_BLOCK, HEAD_DIM), lambda j, d: (clamp(j, d), 0)),
            pl.BlockSpec((KEY_BLOCK, HEAD_DIM), lambda j, d: (clamp(j, d), 1)),
            pl.BlockSpec((1, rows), lambda j, d: (0, lax.axis_index("seq"))),
            pl.BlockSpec((1, KEY_BLOCK), lambda j, d: (0, clamp(j, d))),
        ],
        out_specs=pl.BlockSpec((rows, width), lambda j, d: (0, 0)),
        scratch_shapes=[
            pltpu.VMEM((heads, rows, 1), jnp.float32),
            pltpu.VMEM((heads, rows, 1), jnp.float32),
            pltpu.VMEM((rows, width), jnp.float32),
            pltpu.VMEM((rows, 1), jnp.int32),
        ],
    )
    flops = 4 * rows * width * key_rows // 2
    doc_row = doc_ids.reshape(1, -1)
    return pl.pallas_call(
        flash_kernel,
        out_shape=jax.ShapeDtypeStruct((rows, width), jnp.bfloat16),
        grid_spec=grid_spec,
        compiler_params=pltpu.CompilerParams(dimension_semantics=("arbitrary",)),
        cost_estimate=pl.CostEstimate(
            flops=flops, transcendentals=rows * heads * key_rows // 2,
            bytes_accessed=2 * (2 * rows * width + key_rows * 2 * HEAD_DIM),
        ),
    )(doc_ids, queries, keyval, keyval, doc_row, doc_row)


def solution(mesh):
    in_specs = (
        P("seq", None),
        P(("seq", "vis"), None),
        P(("seq", "vis")),
        P(("seq", "vis")),
        P(),
        P(),
        P(None, "vis"),
        P("vis"),
        P(None, "vis"),
        P(None, "vis"),
        P("vis"),
    )
    out_specs = P("seq", "vis")
    return jax.shard_map(
        on_device, mesh=mesh, in_specs=in_specs, out_specs=out_specs, check_vma=False
    )
```

```python
import jax
import jax.numpy as jnp
from jax import lax
from jax.sharding import PartitionSpec as P
from jax.experimental import pallas as pl
from jax.experimental.pallas import tpu as pltpu

HEAD_DIM = 128


epsilon = 1e-06
negative = -1e30


def frame_slots(frames, tile_pos, frame_count, shard_rows, owners, capacity):
    row_count = frames.shape[0]
    row_ids = jnp.arange(row_count, dtype=jnp.int32)
    usable = row_ids < frame_count[0]
    owner = jnp.where(usable, tile_pos // shard_rows, owners)
    hits = (owner[:, None] == jnp.arange(owners, dtype=jnp.int32)[None, :]).astype(jnp.int32)
    earlier = (row_ids[:, None] > row_ids[None, :]).astype(jnp.int32)
    before = jnp.dot(earlier, hits, preferred_element_type=jnp.int32)
    rank = jnp.sum(before * hits, axis=1)
    slot_index = owner * capacity + rank
    slot_ids = jnp.arange(owners * capacity, dtype=jnp.int32)
    match = usable[:, None] & (slot_index[:, None] == slot_ids[None, :])
    filled = jnp.any(match, axis=0)
    local = tile_pos - owner * shard_rows
    slot_local = jnp.sum(jnp.where(match, local[:, None], 0), axis=0)
    slot_local = jnp.where(filled, slot_local, -1)
    slot_rows = jnp.dot(
        match.T.astype(frames.dtype), frames, preferred_element_type=jnp.float32
    ).astype(frames.dtype)
    place_col = jnp.broadcast_to(slot_local[:, None], (slot_local.shape[0], 128)).astype(frames.dtype)
    payload = jnp.concatenate([slot_rows, place_col], axis=1)
    return payload.reshape(owners, capacity, payload.shape[1])


def place_frames(text, incoming, incoming_place, width):
    lookup = incoming_place[None] == jnp.arange(text.shape[0], dtype=jnp.int32)[:, None, None]
    covered = jnp.any(lookup, axis=(1, 2))
    placed = lax.dot_general(
        lookup.astype(incoming.dtype), incoming, (((1, 2), (0, 1)), ((), ())),
        preferred_element_type=jnp.float32,
    )[:, :width].astype(text.dtype)
    return jnp.where(covered[:, None], placed, text)


def exchange_kernel(payload_ref, out_ref, send_a, recv_a, send_b, recv_b, local_sem):
    seq_count = lax.axis_size("seq")
    vis_count = lax.axis_size("vis")
    ring = vis_count // 2
    me_seq = lax.axis_index("seq")
    me_vis = lax.axis_index("vis")
    ring_pos = lax.rem(me_vis, ring)
    ring_id = me_vis // ring

    def vis_of(ring_index, position):
        return ring_index * ring + lax.rem(position + ring, ring)

    right = vis_of(ring_id, ring_pos + 1)
    left = vis_of(ring_id, ring_pos - 1)
    partner = vis_of(1 - ring_id, ring_pos)
    barrier = pltpu.get_barrier_semaphore()
    for k in range(1, seq_count):
        pl.semaphore_signal(
            barrier, inc=1, device_id=(lax.rem(me_seq + k, seq_count), me_vis),
            device_id_type=pl.DeviceIdType.MESH,
        )
    for peer in (left, right, partner):
        pl.semaphore_signal(
            barrier, inc=1, device_id=(me_seq, peer), device_id_type=pl.DeviceIdType.MESH
        )
    pl.semaphore_wait(barrier, seq_count + 2)
    base = me_vis * seq_count
    local = pltpu.make_async_copy(payload_ref.at[me_seq], out_ref.at[base], local_sem.at[0])
    local.start()
    first = []
    for k in range(1, seq_count):
        target = lax.rem(me_seq + k, seq_count)
        copy = pltpu.make_async_remote_copy(
            src_ref=payload_ref.at[target],
            dst_ref=out_ref.at[base + k],
            send_sem=send_a.at[k],
            recv_sem=recv_a.at[k],
            device_id=(target, me_vis),
            device_id_type=pl.DeviceIdType.MESH,
        )
        copy.start()
        first.append(copy)
    local.wait()

    def arrivals(ks):
        for k in ks:
            source = lax.rem(me_seq + seq_count - k, seq_count)
            incoming = pltpu.make_async_remote_copy(
                src_ref=payload_ref.at[source],
                dst_ref=out_ref.at[base + k],
                send_sem=send_a.at[k],
                recv_sem=recv_a.at[k],
                device_id=(source, me_vis),
                device_id_type=pl.DeviceIdType.MESH,
            )
            incoming.wait_recv()

    arrivals(range(1, seq_count // 2))

    half = seq_count // 2

    def region(owner, part):
        if part == 0:
            return out_ref.at[pl.ds(owner * seq_count, seq_count)]
        start = owner * seq_count + (part - 1) * half
        return out_ref.at[pl.ds(start, half)]

    def link(owner, part, peer, index):
        piece = region(owner, part)
        return pltpu.make_async_remote_copy(
            src_ref=piece,
            dst_ref=piece,
            send_sem=send_b.at[index],
            recv_sem=recv_b.at[index],
            device_id=(me_seq, peer),
            device_id_type=pl.DeviceIdType.MESH,
        )

    far = vis_of(ring_id, ring_pos + 2)
    left_partner = vis_of(1 - ring_id, ring_pos - 1)
    right_partner = vis_of(1 - ring_id, ring_pos + 1)
    far_partner = vis_of(1 - ring_id, ring_pos + 2)
    sent = []

    def send(owner, part, peer, index):
        copy = link(owner, part, peer, index)
        copy.start()
        sent.append(copy)

    send(me_vis, 1, right, 1)
    send(me_vis, 1, left, 2)
    send(me_vis, 1, partner, 3)
    arrivals(range(seq_count // 2, seq_count))
    for copy in first:
        copy.wait_send()
    send(me_vis, 2, right, 10)
    send(me_vis, 2, left, 11)
    send(me_vis, 2, partner, 12)
    link(partner, 1, partner, 3).wait_recv()
    send(partner, 1, right, 4)
    send(partner, 1, left, 5)
    link(left, 1, left, 1).wait_recv()
    send(left, 1, right, 6)
    link(partner, 2, partner, 12).wait_recv()
    send(partner, 2, right, 13)
    send(partner, 2, left, 14)
    link(right, 2, right, 11).wait_recv()
    send(right, 2, left, 7)
    link(left_partner, 1, left, 4).wait_recv()
    send(left_partner, 1, right, 8)
    link(right_partner, 2, right, 14).wait_recv()
    send(right_partner, 2, left, 9)
    link(left, 2, left, 10).wait_recv()
    link(right, 1, right, 2).wait_recv()
    link(left_partner, 2, left, 13).wait_recv()
    link(right_partner, 1, right, 5).wait_recv()
    link(far, 1, left, 6).wait_recv()
    link(far, 2, right, 7).wait_recv()
    link(far_partner, 1, left, 8).wait_recv()
    link(far_partner, 2, right, 9).wait_recv()
    for copy in sent:
        copy.wait_send()


def exchange_frames(payload, vis_count):
    owners, capacity, width = payload.shape
    return pl.pallas_call(
        exchange_kernel,
        out_shape=jax.ShapeDtypeStruct((vis_count * owners, capacity, width), payload.dtype),
        in_specs=[pl.BlockSpec(memory_space=pl.ANY)],
        out_specs=pl.BlockSpec(memory_space=pl.ANY),
        scratch_shapes=[
            pltpu.SemaphoreType.DMA((owners,)),
            pltpu.SemaphoreType.DMA((owners,)),
            pltpu.SemaphoreType.DMA((15,)),
            pltpu.SemaphoreType.DMA((15,)),
            pltpu.SemaphoreType.DMA((1,)),
        ],
        compiler_params=pltpu.CompilerParams(collective_id=1, has_side_effects=True),
    )(payload)


def gather_kernel(
    block_ref, normed_ref, w_ref, bias_ref, out_ref, q_ref, send_sem, recv_sem, local_sem, acc_ref
):
    rows = block_ref.shape[0]
    me_seq = lax.axis_index("seq")
    me_vis = lax.axis_index("vis")
    column = me_seq // 4
    layer = lax.rem(me_seq // 2, 2)
    core = lax.rem(me_seq, 2)
    ring = lax.axis_size("seq") // 4

    def seq_of(y, z, c):
        return (lax.rem(y + ring, ring) * 2 + z) * 2 + c

    mate = seq_of(column, layer, 1 - core)
    across = seq_of(column, 1 - layer, core)
    diagonal = seq_of(column, 1 - layer, 1 - core)
    up = seq_of(column + 1, layer, core)
    down = seq_of(column - 1, layer, core)
    barrier = pltpu.get_barrier_semaphore()
    for peer in (mate, across, diagonal, up, down):
        pl.semaphore_signal(
            barrier, inc=1, device_id=(peer, me_vis), device_id_type=pl.DeviceIdType.MESH
        )
    pl.semaphore_wait(barrier, 5)

    def rows_of(start, count):
        return out_ref.at[pl.ds(pl.multiple_of(start, rows), count)]

    def link(src, dst, peer, index):
        return pltpu.make_async_remote_copy(
            src_ref=src, dst_ref=dst, send_sem=send_sem.at[index], recv_sem=recv_sem.at[index],
            device_id=(peer, me_vis), device_id_type=pl.DeviceIdType.MESH,
        )

    sent = []

    def send(src, dst, peer, index):
        copy = link(src, dst, peer, index)
        copy.start()
        sent.append(copy)

    own = rows_of(me_seq * rows, rows)
    local = pltpu.make_async_copy(block_ref, own, local_sem.at[0])
    local.start()
    send(block_ref, own, mate, 0)
    send(block_ref, own, across, 1)
    send(block_ref, own, diagonal, 2)
    depth = normed_ref.shape[1] // 2

    def project(part):
        def body(n_blk, w_blk):
            acc_ref[...] += jnp.dot(n_blk[...], w_blk[...], preferred_element_type=jnp.float32)

        pltpu.emit_pipeline(
            body,
            grid=(depth // PROJ_TILE,),
            in_specs=[
                pl.BlockSpec((normed_ref.shape[0], PROJ_TILE), lambda k: (0, k)),
                pl.BlockSpec((PROJ_TILE, w_ref.shape[1]), lambda k: (k, 0)),
            ],
        )(normed_ref.at[:, pl.ds(part * depth, depth)], w_ref.at[pl.ds(part * depth, depth)])

    acc_ref[...] = jnp.zeros(acc_ref.shape, jnp.float32)
    project(0)
    local.wait()
    link(block_ref, rows_of(mate * rows, rows), mate, 0).wait_recv()
    link(block_ref, rows_of(across * rows, rows), across, 1).wait_recv()
    link(block_ref, rows_of(diagonal * rows, rows), diagonal, 2).wait_recv()

    def half(y, h):
        return rows_of((lax.rem(y + ring, ring) * 4 + h * 2) * rows, 2 * rows)

    def quarter(y, h, q):
        return rows_of((lax.rem(y + ring, ring) * 4 + h * 2 + q) * rows, rows)

    first_mine = quarter(column, core, 0)
    second_mine = quarter(column, core, 1)
    send(first_mine, first_mine, up, 3)
    send(second_mine, second_mine, down, 4)
    send(second_mine, second_mine, up, 10)
    send(first_mine, first_mine, down, 11)
    project(1)
    piece = quarter(column - 1, core, 0)
    link(piece, piece, down, 3).wait_recv()
    send(piece, piece, up, 5)
    piece = quarter(column + 1, core, 1)
    link(piece, piece, up, 4).wait_recv()
    send(piece, piece, down, 6)
    below = half(column - 1, core)
    rest = quarter(column - 1, core, 1)
    link(rest, rest, down, 10).wait_recv()
    send(below, below, mate, 7)
    above = half(column + 1, core)
    rest = quarter(column + 1, core, 0)
    link(rest, rest, up, 11).wait_recv()
    send(above, above, mate, 9)
    q_ref[...] = (acc_ref[...] + bias_ref[...]).astype(q_ref.dtype)
    far_low = quarter(column + 2, core, 0)
    far_high = quarter(column + 2, core, 1)
    link(far_low, far_low, down, 5).wait_recv()
    link(far_high, far_high, up, 6).wait_recv()
    far = half(column + 2, core)
    send(far, far, mate, 8)
    for offset, index in ((-1, 7), (2, 8), (1, 9)):
        theirs = half(column + offset, 1 - core)
        link(theirs, theirs, mate, index).wait_recv()
    for copy in sent:
        copy.wait_send()


PROJ_TILE = 512


def gather_keys(block, normed, w_query, q_bias, seq_count):
    rows, width = block.shape
    return pl.pallas_call(
        gather_kernel,
        out_shape=(
            jax.ShapeDtypeStruct((seq_count * rows, width), block.dtype),
            jax.ShapeDtypeStruct((normed.shape[0], w_query.shape[1]), jnp.bfloat16),
        ),
        in_specs=[
            pl.BlockSpec(memory_space=pl.ANY),
            pl.BlockSpec(memory_space=pl.ANY),
            pl.BlockSpec(memory_space=pl.ANY),
            pl.BlockSpec(memory_space=pltpu.VMEM),
        ],
        out_specs=(pl.BlockSpec(memory_space=pl.ANY), pl.BlockSpec(memory_space=pltpu.VMEM)),
        scratch_shapes=[
            pltpu.SemaphoreType.DMA((12,)),
            pltpu.SemaphoreType.DMA((12,)),
            pltpu.SemaphoreType.DMA((1,)),
            pltpu.VMEM((normed.shape[0], w_query.shape[1]), jnp.float32),
        ],
        compiler_params=pltpu.CompilerParams(collective_id=2, has_side_effects=True),
    )(block, normed, w_query, q_bias.reshape(1, -1))


def on_device(
    text, frames, tile_pos, frame_count, doc_ids, norm_gain, w_query, q_bias, w_key, w_value, v_bias
):
    seq_count = lax.axis_size("seq")
    vis_count = lax.axis_size("vis")
    shard_index = lax.axis_index("seq")
    shard_rows = text.shape[0]
    capacity = shard_rows // (seq_count * vis_count)
    first_row = shard_index * shard_rows
    payload = frame_slots(frames, tile_pos, frame_count, shard_rows, seq_count, capacity)
    gathered = exchange_frames(payload, vis_count)
    width = text.shape[1]
    incoming_place = gathered[:, :, width].astype(jnp.int32)
    merged = place_frames(text, gathered, incoming_place, width)
    widened = merged.astype(jnp.float32)
    mean_square = jnp.mean(widened * widened, axis=1, keepdims=True)
    normed = (widened * lax.rsqrt(mean_square + epsilon) * norm_gain).astype(jnp.bfloat16)
    key_rows = jnp.dot(normed, w_key, preferred_element_type=jnp.float32).astype(jnp.bfloat16)
    value_rows = (jnp.dot(normed, w_value, preferred_element_type=jnp.float32) + v_bias).astype(
        jnp.bfloat16
    )
    keyval = jnp.concatenate([key_rows, value_rows], axis=1)
    kv_heads = w_key.shape[1] // HEAD_DIM
    per_group = w_query.shape[1] // HEAD_DIM // kv_heads
    incoming_keys, queries = gather_keys(keyval, normed, w_query, q_bias, seq_count)
    return flash_attention(doc_ids, queries, incoming_keys)


KEY_BLOCK = 512
DOC_SPAN = 2048


def block_bounds(doc_ref, rows, key_rows):
    first = lax.axis_index("seq") * rows
    first_doc = doc_ref[first]
    low = 0
    for b in range(key_rows // KEY_BLOCK):
        low = low + (doc_ref[(b + 1) * KEY_BLOCK - 1] < first_doc).astype(jnp.int32)
    return low, (first + rows - 1) // KEY_BLOCK, first


def flash_kernel(doc_ref, q_ref, k_ref, v_ref, qdoc_ref, kdoc_ref, out_ref, peak_ref, total_ref, acc_ref, qcol_ref):
    step = pl.program_id(0)
    rows = q_ref.shape[0]
    heads = q_ref.shape[1] // HEAD_DIM
    low, high, first = block_bounds(doc_ref, rows, doc_ref.shape[0])
    block = low + step

    @pl.when(step == 0)
    def _():
        peak_ref[...] = jnp.full(peak_ref.shape, negative, jnp.float32)
        total_ref[...] = jnp.zeros(total_ref.shape, jnp.float32)
        acc_ref[...] = jnp.zeros(acc_ref.shape, jnp.float32)
        spread = jnp.broadcast_to(qdoc_ref[...], (rows, rows))
        diagonal = lax.broadcasted_iota(jnp.int32, (rows, rows), 0) == lax.broadcasted_iota(
            jnp.int32, (rows, rows), 1
        )
        qcol_ref[...] = jnp.sum(jnp.where(diagonal, spread, 0), axis=1, keepdims=True)

    @pl.when(block <= high)
    def _():
        key_place = block * KEY_BLOCK + lax.broadcasted_iota(jnp.int32, (1, KEY_BLOCK), 1)
        query_place = first + lax.broadcasted_iota(jnp.int32, (rows, 1), 0)
        allowed = (key_place <= query_place) & (kdoc_ref[...] == qcol_ref[...])
        keys = k_ref[...]
        vals = v_ref[...]
        for h in range(heads):
            cols = slice(h * HEAD_DIM, (h + 1) * HEAD_DIM)
            scores = lax.dot_general(
                q_ref[:, cols], keys, (((1,), (1,)), ((), ())),
                preferred_element_type=jnp.float32,
            ) * HEAD_DIM ** (-0.5)
            scores = jnp.where(allowed, scores, negative)
            old_peak = peak_ref[h]
            new_peak = jnp.maximum(old_peak, jnp.max(scores, axis=1, keepdims=True))
            raised = jnp.where(allowed, jnp.exp(scores - new_peak[:, :1]), 0.0)
            factor = jnp.exp(old_peak - new_peak)
            total_ref[h] = total_ref[h] * factor + jnp.sum(raised, axis=1, keepdims=True)
            peak_ref[h] = new_peak
            product = jnp.dot(raised.astype(jnp.bfloat16), vals, preferred_element_type=jnp.float32)
            acc_ref[:, cols] = acc_ref[:, cols] * factor[:, :1] + product

    @pl.when(step == pl.num_programs(0) - 1)
    def _():
        for h in range(heads):
            cols = slice(h * HEAD_DIM, (h + 1) * HEAD_DIM)
            out_ref[:, cols] = (acc_ref[:, cols] / total_ref[h][:, :1]).astype(out_ref.dtype)


def flash_attention(doc_ids, queries, keyval):
    rows, width = queries.shape
    key_rows = keyval.shape[0]
    steps = min(key_rows // KEY_BLOCK, (DOC_SPAN + rows - 2) // KEY_BLOCK + 2)
    heads = width // HEAD_DIM

    def clamp(j, d):
        low, high, _ = block_bounds(d, rows, key_rows)
        return jnp.minimum(low + j, high)

    grid_spec = pltpu.PrefetchScalarGridSpec(
        num_scalar_prefetch=1,
        grid=(steps,),
        in_specs=[
            pl.BlockSpec((rows, width), lambda j, d: (0, 0)),
            pl.BlockSpec((KEY_BLOCK, HEAD_DIM), lambda j, d: (clamp(j, d), 0)),
            pl.BlockSpec((KEY_BLOCK, HEAD_DIM), lambda j, d: (clamp(j, d), 1)),
            pl.BlockSpec((1, rows), lambda j, d: (0, lax.axis_index("seq"))),
            pl.BlockSpec((1, KEY_BLOCK), lambda j, d: (0, clamp(j, d))),
        ],
        out_specs=pl.BlockSpec((rows, width), lambda j, d: (0, 0)),
        scratch_shapes=[
            pltpu.VMEM((heads, rows, 1), jnp.float32),
            pltpu.VMEM((heads, rows, 1), jnp.float32),
            pltpu.VMEM((rows, width), jnp.float32),
            pltpu.VMEM((rows, 1), jnp.int32),
        ],
    )
    flops = 4 * rows * width * key_rows // 2
    doc_row = doc_ids.reshape(1, -1)
    return pl.pallas_call(
        flash_kernel,
        out_shape=jax.ShapeDtypeStruct((rows, width), jnp.bfloat16),
        grid_spec=grid_spec,
        compiler_params=pltpu.CompilerParams(dimension_semantics=("arbitrary",)),
        cost_estimate=pl.CostEstimate(
            flops=flops, transcendentals=rows * heads * key_rows // 2,
            bytes_accessed=2 * (2 * rows * width + key_rows * 2 * HEAD_DIM),
        ),
    )(doc_ids, queries, keyval, keyval, doc_row, doc_row)


def solution(mesh):
    in_specs = (
        P("seq", None),
        P(("seq", "vis"), None),
        P(("seq", "vis")),
        P(("seq", "vis")),
        P(),
        P(),
        P(None, "vis"),
        P("vis"),
        P(None, "vis"),
        P(None, "vis"),
        P("vis"),
    )
    out_specs = P("seq", "vis")
    return jax.shard_map(
        on_device, mesh=mesh, in_specs=in_specs, out_specs=out_specs, check_vma=False
    )
```

```python
import jax
import jax.numpy as jnp
from jax import lax
from jax.sharding import PartitionSpec as P
from jax.experimental import pallas as pl
from jax.experimental.pallas import tpu as pltpu

HEAD_DIM = 128


epsilon = 1e-06
negative = -1e30


def frame_slots(frames, tile_pos, frame_count, shard_rows, owners, capacity):
    row_count = frames.shape[0]
    row_ids = jnp.arange(row_count, dtype=jnp.int32)
    usable = row_ids < frame_count[0]
    owner = jnp.where(usable, tile_pos // shard_rows, owners)
    hits = (owner[:, None] == jnp.arange(owners, dtype=jnp.int32)[None, :]).astype(jnp.int32)
    earlier = (row_ids[:, None] > row_ids[None, :]).astype(jnp.int32)
    before = jnp.dot(earlier, hits, preferred_element_type=jnp.int32)
    rank = jnp.sum(before * hits, axis=1)
    slot_index = owner * capacity + rank
    slot_ids = jnp.arange(owners * capacity, dtype=jnp.int32)
    match = usable[:, None] & (slot_index[:, None] == slot_ids[None, :])
    filled = jnp.any(match, axis=0)
    local = tile_pos - owner * shard_rows
    slot_local = jnp.sum(jnp.where(match, local[:, None], 0), axis=0)
    slot_local = jnp.where(filled, slot_local, -1)
    slot_rows = jnp.dot(
        match.T.astype(frames.dtype), frames, preferred_element_type=jnp.float32
    ).astype(frames.dtype)
    place_col = jnp.broadcast_to(slot_local[:, None], (slot_local.shape[0], 128)).astype(frames.dtype)
    payload = jnp.concatenate([slot_rows, place_col], axis=1)
    return payload.reshape(owners, capacity, payload.shape[1])


def place_frames(text, incoming, incoming_place, width):
    lookup = incoming_place[None] == jnp.arange(text.shape[0], dtype=jnp.int32)[:, None, None]
    covered = jnp.any(lookup, axis=(1, 2))
    placed = lax.dot_general(
        lookup.astype(incoming.dtype), incoming, (((1, 2), (0, 1)), ((), ())),
        preferred_element_type=jnp.float32,
    )[:, :width].astype(text.dtype)
    return jnp.where(covered[:, None], placed, text)


def exchange_kernel(payload_ref, out_ref, send_a, recv_a, send_b, recv_b, local_sem):
    seq_count = lax.axis_size("seq")
    vis_count = lax.axis_size("vis")
    ring = vis_count // 2
    me_seq = lax.axis_index("seq")
    me_vis = lax.axis_index("vis")
    ring_pos = lax.rem(me_vis, ring)
    ring_id = me_vis // ring

    def vis_of(ring_index, position):
        return ring_index * ring + lax.rem(position + ring, ring)

    right = vis_of(ring_id, ring_pos + 1)
    left = vis_of(ring_id, ring_pos - 1)
    partner = vis_of(1 - ring_id, ring_pos)
    barrier = pltpu.get_barrier_semaphore()
    for k in range(1, seq_count):
        pl.semaphore_signal(
            barrier, inc=1, device_id=(lax.rem(me_seq + k, seq_count), me_vis),
            device_id_type=pl.DeviceIdType.MESH,
        )
    for peer in (left, right, partner):
        pl.semaphore_signal(
            barrier, inc=1, device_id=(me_seq, peer), device_id_type=pl.DeviceIdType.MESH
        )
    pl.semaphore_wait(barrier, seq_count + 2)
    base = me_vis * seq_count
    local = pltpu.make_async_copy(payload_ref.at[me_seq], out_ref.at[base], local_sem.at[0])
    local.start()
    first = []
    for k in range(1, seq_count):
        target = lax.rem(me_seq + k, seq_count)
        copy = pltpu.make_async_remote_copy(
            src_ref=payload_ref.at[target],
            dst_ref=out_ref.at[base + k],
            send_sem=send_a.at[k],
            recv_sem=recv_a.at[k],
            device_id=(target, me_vis),
            device_id_type=pl.DeviceIdType.MESH,
        )
        copy.start()
        first.append(copy)
    local.wait()

    def arrivals(ks):
        for k in ks:
            source = lax.rem(me_seq + seq_count - k, seq_count)
            incoming = pltpu.make_async_remote_copy(
                src_ref=payload_ref.at[source],
                dst_ref=out_ref.at[base + k],
                send_sem=send_a.at[k],
                recv_sem=recv_a.at[k],
                device_id=(source, me_vis),
                device_id_type=pl.DeviceIdType.MESH,
            )
            incoming.wait_recv()

    arrivals(range(1, seq_count // 2))

    half = seq_count // 2

    def region(owner, part):
        if part == 0:
            return out_ref.at[pl.ds(owner * seq_count, seq_count)]
        start = owner * seq_count + (part - 1) * half
        return out_ref.at[pl.ds(start, half)]

    def link(owner, part, peer, index):
        piece = region(owner, part)
        return pltpu.make_async_remote_copy(
            src_ref=piece,
            dst_ref=piece,
            send_sem=send_b.at[index],
            recv_sem=recv_b.at[index],
            device_id=(me_seq, peer),
            device_id_type=pl.DeviceIdType.MESH,
        )

    far = vis_of(ring_id, ring_pos + 2)
    left_partner = vis_of(1 - ring_id, ring_pos - 1)
    right_partner = vis_of(1 - ring_id, ring_pos + 1)
    far_partner = vis_of(1 - ring_id, ring_pos + 2)
    sent = []

    def send(owner, part, peer, index):
        copy = link(owner, part, peer, index)
        copy.start()
        sent.append(copy)

    send(me_vis, 1, right, 1)
    send(me_vis, 1, left, 2)
    send(me_vis, 1, partner, 3)
    arrivals(range(seq_count // 2, seq_count))
    for copy in first:
        copy.wait_send()
    send(me_vis, 2, right, 10)
    send(me_vis, 2, left, 11)
    send(me_vis, 2, partner, 12)
    link(partner, 1, partner, 3).wait_recv()
    send(partner, 1, right, 4)
    send(partner, 1, left, 5)
    link(left, 1, left, 1).wait_recv()
    send(left, 1, right, 6)
    link(partner, 2, partner, 12).wait_recv()
    send(partner, 2, right, 13)
    send(partner, 2, left, 14)
    link(right, 2, right, 11).wait_recv()
    send(right, 2, left, 7)
    link(left_partner, 1, left, 4).wait_recv()
    send(left_partner, 1, right, 8)
    link(right_partner, 2, right, 14).wait_recv()
    send(right_partner, 2, left, 9)
    link(left, 2, left, 10).wait_recv()
    link(right, 1, right, 2).wait_recv()
    link(left_partner, 2, left, 13).wait_recv()
    link(right_partner, 1, right, 5).wait_recv()
    link(far, 1, left, 6).wait_recv()
    link(far, 2, right, 7).wait_recv()
    link(far_partner, 1, left, 8).wait_recv()
    link(far_partner, 2, right, 9).wait_recv()
    for copy in sent:
        copy.wait_send()


def exchange_frames(payload, vis_count):
    owners, capacity, width = payload.shape
    return pl.pallas_call(
        exchange_kernel,
        out_shape=jax.ShapeDtypeStruct((vis_count * owners, capacity, width), payload.dtype),
        in_specs=[pl.BlockSpec(memory_space=pl.ANY)],
        out_specs=pl.BlockSpec(memory_space=pl.ANY),
        scratch_shapes=[
            pltpu.SemaphoreType.DMA((owners,)),
            pltpu.SemaphoreType.DMA((owners,)),
            pltpu.SemaphoreType.DMA((15,)),
            pltpu.SemaphoreType.DMA((15,)),
            pltpu.SemaphoreType.DMA((1,)),
        ],
        compiler_params=pltpu.CompilerParams(collective_id=1, has_side_effects=True),
    )(payload)


def gather_kernel(
    block_ref, normed_ref, w_ref, bias_ref, out_ref, q_ref, send_sem, recv_sem, local_sem, acc_ref
):
    rows = block_ref.shape[0]
    me_seq = lax.axis_index("seq")
    me_vis = lax.axis_index("vis")
    column = me_seq // 4
    layer = lax.rem(me_seq // 2, 2)
    core = lax.rem(me_seq, 2)
    ring = lax.axis_size("seq") // 4

    def seq_of(y, z, c):
        return (lax.rem(y + ring, ring) * 2 + z) * 2 + c

    mate = seq_of(column, layer, 1 - core)
    across = seq_of(column, 1 - layer, core)
    diagonal = seq_of(column, 1 - layer, 1 - core)
    up = seq_of(column + 1, layer, core)
    down = seq_of(column - 1, layer, core)
    barrier = pltpu.get_barrier_semaphore()
    for peer in (mate, across, diagonal, up, down):
        pl.semaphore_signal(
            barrier, inc=1, device_id=(peer, me_vis), device_id_type=pl.DeviceIdType.MESH
        )
    pl.semaphore_wait(barrier, 5)

    def rows_of(start, count):
        return out_ref.at[pl.ds(pl.multiple_of(start, rows), count)]

    def link(src, dst, peer, index):
        return pltpu.make_async_remote_copy(
            src_ref=src, dst_ref=dst, send_sem=send_sem.at[index], recv_sem=recv_sem.at[index],
            device_id=(peer, me_vis), device_id_type=pl.DeviceIdType.MESH,
        )

    sent = []

    def send(src, dst, peer, index):
        copy = link(src, dst, peer, index)
        copy.start()
        sent.append(copy)

    own = rows_of(me_seq * rows, rows)
    local = pltpu.make_async_copy(block_ref, own, local_sem.at[0])
    local.start()
    send(block_ref, own, mate, 0)
    send(block_ref, own, across, 1)
    send(block_ref, own, diagonal, 2)
    depth = normed_ref.shape[1] // 2

    def project(part):
        def body(n_blk, w_blk):
            acc_ref[...] += jnp.dot(n_blk[...], w_blk[...], preferred_element_type=jnp.float32)

        pltpu.emit_pipeline(
            body,
            grid=(depth // PROJ_TILE,),
            in_specs=[
                pl.BlockSpec((normed_ref.shape[0], PROJ_TILE), lambda k: (0, k)),
                pl.BlockSpec((PROJ_TILE, w_ref.shape[1]), lambda k: (k, 0)),
            ],
        )(normed_ref.at[:, pl.ds(part * depth, depth)], w_ref.at[pl.ds(part * depth, depth)])

    acc_ref[...] = jnp.zeros(acc_ref.shape, jnp.float32)
    project(0)
    local.wait()
    link(block_ref, rows_of(mate * rows, rows), mate, 0).wait_recv()
    link(block_ref, rows_of(across * rows, rows), across, 1).wait_recv()
    link(block_ref, rows_of(diagonal * rows, rows), diagonal, 2).wait_recv()

    def half(y, h):
        return rows_of((lax.rem(y + ring, ring) * 4 + h * 2) * rows, 2 * rows)

    def quarter(y, h, q):
        return rows_of((lax.rem(y + ring, ring) * 4 + h * 2 + q) * rows, rows)

    mine = half(column, core)
    send(mine, mine, up, 3)
    send(mine, mine, down, 4)
    project(1)
    below = half(column - 1, core)
    link(below, below, down, 3).wait_recv()
    send(below, below, mate, 7)
    piece = quarter(column - 1, core, 0)
    send(piece, piece, up, 5)
    above = half(column + 1, core)
    link(above, above, up, 4).wait_recv()
    send(above, above, mate, 9)
    piece = quarter(column + 1, core, 1)
    send(piece, piece, down, 6)
    q_ref[...] = (acc_ref[...] + bias_ref[...]).astype(q_ref.dtype)
    far_low = quarter(column + 2, core, 0)
    far_high = quarter(column + 2, core, 1)
    link(far_low, far_low, down, 5).wait_recv()
    link(far_high, far_high, up, 6).wait_recv()
    far = half(column + 2, core)
    send(far, far, mate, 8)
    for offset, index in ((-1, 7), (2, 8), (1, 9)):
        theirs = half(column + offset, 1 - core)
        link(theirs, theirs, mate, index).wait_recv()
    for copy in sent:
        copy.wait_send()


PROJ_TILE = 512


def gather_keys(block, normed, w_query, q_bias, seq_count):
    rows, width = block.shape
    return pl.pallas_call(
        gather_kernel,
        out_shape=(
            jax.ShapeDtypeStruct((seq_count * rows, width), block.dtype),
            jax.ShapeDtypeStruct((normed.shape[0], w_query.shape[1]), jnp.bfloat16),
        ),
        in_specs=[
            pl.BlockSpec(memory_space=pl.ANY),
            pl.BlockSpec(memory_space=pl.ANY),
            pl.BlockSpec(memory_space=pl.ANY),
            pl.BlockSpec(memory_space=pltpu.VMEM),
        ],
        out_specs=(pl.BlockSpec(memory_space=pl.ANY), pl.BlockSpec(memory_space=pltpu.VMEM)),
        scratch_shapes=[
            pltpu.SemaphoreType.DMA((10,)),
            pltpu.SemaphoreType.DMA((10,)),
            pltpu.SemaphoreType.DMA((1,)),
            pltpu.VMEM((normed.shape[0], w_query.shape[1]), jnp.float32),
        ],
        compiler_params=pltpu.CompilerParams(collective_id=2, has_side_effects=True),
    )(block, normed, w_query, q_bias.reshape(1, -1))


def on_device(
    text, frames, tile_pos, frame_count, doc_ids, norm_gain, w_query, q_bias, w_key, w_value, v_bias
):
    seq_count = lax.axis_size("seq")
    vis_count = lax.axis_size("vis")
    shard_index = lax.axis_index("seq")
    shard_rows = text.shape[0]
    capacity = shard_rows // (seq_count * vis_count)
    first_row = shard_index * shard_rows
    payload = frame_slots(frames, tile_pos, frame_count, shard_rows, seq_count, capacity)
    gathered = exchange_frames(payload, vis_count)
    width = text.shape[1]
    incoming_place = gathered[:, :, width].astype(jnp.int32)
    merged = place_frames(text, gathered, incoming_place, width)
    widened = merged.astype(jnp.float32)
    mean_square = jnp.mean(widened * widened, axis=1, keepdims=True)
    normed = (widened * lax.rsqrt(mean_square + epsilon) * norm_gain).astype(jnp.bfloat16)
    key_rows = jnp.dot(normed, w_key, preferred_element_type=jnp.float32).astype(jnp.bfloat16)
    value_rows = (jnp.dot(normed, w_value, preferred_element_type=jnp.float32) + v_bias).astype(
        jnp.bfloat16
    )
    keyval = jnp.concatenate([key_rows, value_rows], axis=1)
    kv_heads = w_key.shape[1] // HEAD_DIM
    per_group = w_query.shape[1] // HEAD_DIM // kv_heads
    incoming_keys, queries = gather_keys(keyval, normed, w_query, q_bias, seq_count)
    return flash_attention(doc_ids, queries, incoming_keys)


KEY_BLOCK = 512
DOC_SPAN = 2048


def block_bounds(doc_ref, rows, key_rows):
    first = lax.axis_index("seq") * rows
    first_doc = doc_ref[first]
    low = 0
    for b in range(key_rows // KEY_BLOCK):
        low = low + (doc_ref[(b + 1) * KEY_BLOCK - 1] < first_doc).astype(jnp.int32)
    return low, (first + rows - 1) // KEY_BLOCK, first


def flash_kernel(doc_ref, q_ref, k_ref, v_ref, qdoc_ref, kdoc_ref, out_ref, peak_ref, total_ref, acc_ref, qcol_ref):
    step = pl.program_id(0)
    rows = q_ref.shape[0]
    heads = q_ref.shape[1] // HEAD_DIM
    low, high, first = block_bounds(doc_ref, rows, doc_ref.shape[0])
    block = low + step

    @pl.when(step == 0)
    def _():
        peak_ref[...] = jnp.full(peak_ref.shape, negative, jnp.float32)
        total_ref[...] = jnp.zeros(total_ref.shape, jnp.float32)
        acc_ref[...] = jnp.zeros(acc_ref.shape, jnp.float32)
        spread = jnp.broadcast_to(qdoc_ref[...], (rows, rows))
        diagonal = lax.broadcasted_iota(jnp.int32, (rows, rows), 0) == lax.broadcasted_iota(
            jnp.int32, (rows, rows), 1
        )
        qcol_ref[...] = jnp.sum(jnp.where(diagonal, spread, 0), axis=1, keepdims=True)

    @pl.when(block <= high)
    def _():
        key_place = block * KEY_BLOCK + lax.broadcasted_iota(jnp.int32, (1, KEY_BLOCK), 1)
        query_place = first + lax.broadcasted_iota(jnp.int32, (rows, 1), 0)
        allowed = (key_place <= query_place) & (kdoc_ref[...] == qcol_ref[...])
        keys = k_ref[...]
        vals = v_ref[...]
        for h in range(heads):
            cols = slice(h * HEAD_DIM, (h + 1) * HEAD_DIM)
            scores = lax.dot_general(
                q_ref[:, cols], keys, (((1,), (1,)), ((), ())),
                preferred_element_type=jnp.float32,
            ) * HEAD_DIM ** (-0.5)
            scores = jnp.where(allowed, scores, negative)
            old_peak = peak_ref[h]
            new_peak = jnp.maximum(old_peak, jnp.max(scores, axis=1, keepdims=True))
            raised = jnp.where(allowed, jnp.exp(scores - new_peak[:, :1]), 0.0)
            factor = jnp.exp(old_peak - new_peak)
            total_ref[h] = total_ref[h] * factor + jnp.sum(raised, axis=1, keepdims=True)
            peak_ref[h] = new_peak
            product = jnp.dot(raised.astype(jnp.bfloat16), vals, preferred_element_type=jnp.float32)
            acc_ref[:, cols] = acc_ref[:, cols] * factor[:, :1] + product

    @pl.when(step == pl.num_programs(0) - 1)
    def _():
        for h in range(heads):
            cols = slice(h * HEAD_DIM, (h + 1) * HEAD_DIM)
            out_ref[:, cols] = (acc_ref[:, cols] / total_ref[h][:, :1]).astype(out_ref.dtype)


def flash_attention(doc_ids, queries, keyval):
    rows, width = queries.shape
    key_rows = keyval.shape[0]
    steps = max(
        (first + rows - 1) // KEY_BLOCK - max(0, first - DOC_SPAN + 1) // KEY_BLOCK + 1
        for first in range(0, key_rows, rows)
    )
    heads = width // HEAD_DIM

    def clamp(j, d):
        low, high, _ = block_bounds(d, rows, key_rows)
        return jnp.minimum(low + j, high)

    grid_spec = pltpu.PrefetchScalarGridSpec(
        num_scalar_prefetch=1,
        grid=(steps,),
        in_specs=[
            pl.BlockSpec((rows, width), lambda j, d: (0, 0)),
            pl.BlockSpec((KEY_BLOCK, HEAD_DIM), lambda j, d: (clamp(j, d), 0)),
            pl.BlockSpec((KEY_BLOCK, HEAD_DIM), lambda j, d: (clamp(j, d), 1)),
            pl.BlockSpec((1, rows), lambda j, d: (0, lax.axis_index("seq"))),
            pl.BlockSpec((1, KEY_BLOCK), lambda j, d: (0, clamp(j, d))),
        ],
        out_specs=pl.BlockSpec((rows, width), lambda j, d: (0, 0)),
        scratch_shapes=[
            pltpu.VMEM((heads, rows, 1), jnp.float32),
            pltpu.VMEM((heads, rows, 1), jnp.float32),
            pltpu.VMEM((rows, width), jnp.float32),
            pltpu.VMEM((rows, 1), jnp.int32),
        ],
    )
    flops = 4 * rows * width * key_rows // 2
    doc_row = doc_ids.reshape(1, -1)
    return pl.pallas_call(
        flash_kernel,
        out_shape=jax.ShapeDtypeStruct((rows, width), jnp.bfloat16),
        grid_spec=grid_spec,
        compiler_params=pltpu.CompilerParams(dimension_semantics=("arbitrary",)),
        cost_estimate=pl.CostEstimate(
            flops=flops, transcendentals=rows * heads * key_rows // 2,
            bytes_accessed=2 * (2 * rows * width + key_rows * 2 * HEAD_DIM),
        ),
    )(doc_ids, queries, keyval, keyval, doc_row, doc_row)


def solution(mesh):
    in_specs = (
        P("seq", None),
        P(("seq", "vis"), None),
        P(("seq", "vis")),
        P(("seq", "vis")),
        P(),
        P(),
        P(None, "vis"),
        P("vis"),
        P(None, "vis"),
        P(None, "vis"),
        P("vis"),
    )
    out_specs = P("seq", "vis")
    return jax.shard_map(
        on_device, mesh=mesh, in_specs=in_specs, out_specs=out_specs, check_vma=False
    )
```

```python
import jax
import jax.numpy as jnp
from jax import lax
from jax.sharding import PartitionSpec as P
from jax.experimental import pallas as pl
from jax.experimental.pallas import tpu as pltpu

HEAD_DIM = 128


epsilon = 1e-06
negative = -1e30


def frame_slots(frames, tile_pos, frame_count, shard_rows, owners, capacity):
    row_count = frames.shape[0]
    row_ids = jnp.arange(row_count, dtype=jnp.int32)
    usable = row_ids < frame_count[0]
    owner = jnp.where(usable, tile_pos // shard_rows, owners)
    hits = (owner[:, None] == jnp.arange(owners, dtype=jnp.int32)[None, :]).astype(jnp.int32)
    earlier = (row_ids[:, None] > row_ids[None, :]).astype(jnp.int32)
    before = jnp.dot(earlier, hits, preferred_element_type=jnp.int32)
    rank = jnp.sum(before * hits, axis=1)
    slot_index = owner * capacity + rank
    slot_ids = jnp.arange(owners * capacity, dtype=jnp.int32)
    match = usable[:, None] & (slot_index[:, None] == slot_ids[None, :])
    filled = jnp.any(match, axis=0)
    local = tile_pos - owner * shard_rows
    slot_local = jnp.sum(jnp.where(match, local[:, None], 0), axis=0)
    slot_local = jnp.where(filled, slot_local, -1)
    slot_rows = jnp.dot(
        match.T.astype(frames.dtype), frames, preferred_element_type=jnp.float32
    ).astype(frames.dtype)
    place_col = jnp.broadcast_to(slot_local[:, None], (slot_local.shape[0], 128)).astype(frames.dtype)
    payload = jnp.concatenate([slot_rows, place_col], axis=1)
    return payload.reshape(owners, capacity, payload.shape[1])


def place_frames(text, incoming, incoming_place, width):
    lookup = incoming_place[None] == jnp.arange(text.shape[0], dtype=jnp.int32)[:, None, None]
    covered = jnp.any(lookup, axis=(1, 2))
    placed = lax.dot_general(
        lookup.astype(incoming.dtype), incoming, (((1, 2), (0, 1)), ((), ())),
        preferred_element_type=jnp.float32,
    )[:, :width].astype(text.dtype)
    return jnp.where(covered[:, None], placed, text)


def exchange_kernel(payload_ref, out_ref, send_a, recv_a, send_b, recv_b, local_sem):
    seq_count = lax.axis_size("seq")
    vis_count = lax.axis_size("vis")
    ring = vis_count // 2
    me_seq = lax.axis_index("seq")
    me_vis = lax.axis_index("vis")
    ring_pos = lax.rem(me_vis, ring)
    ring_id = me_vis // ring

    def vis_of(ring_index, position):
        return ring_index * ring + lax.rem(position + ring, ring)

    right = vis_of(ring_id, ring_pos + 1)
    left = vis_of(ring_id, ring_pos - 1)
    partner = vis_of(1 - ring_id, ring_pos)
    barrier = pltpu.get_barrier_semaphore()
    for k in range(1, seq_count):
        pl.semaphore_signal(
            barrier, inc=1, device_id=(lax.rem(me_seq + k, seq_count), me_vis),
            device_id_type=pl.DeviceIdType.MESH,
        )
    for peer in (left, right, partner):
        pl.semaphore_signal(
            barrier, inc=1, device_id=(me_seq, peer), device_id_type=pl.DeviceIdType.MESH
        )
    pl.semaphore_wait(barrier, seq_count + 2)
    base = me_vis * seq_count
    local = pltpu.make_async_copy(payload_ref.at[me_seq], out_ref.at[base], local_sem.at[0])
    local.start()
    first = []
    for k in range(1, seq_count):
        target = lax.rem(me_seq + k, seq_count)
        copy = pltpu.make_async_remote_copy(
            src_ref=payload_ref.at[target],
            dst_ref=out_ref.at[base + k],
            send_sem=send_a.at[k],
            recv_sem=recv_a.at[k],
            device_id=(target, me_vis),
            device_id_type=pl.DeviceIdType.MESH,
        )
        copy.start()
        first.append(copy)
    local.wait()

    def arrivals(ks):
        for k in ks:
            source = lax.rem(me_seq + seq_count - k, seq_count)
            incoming = pltpu.make_async_remote_copy(
                src_ref=payload_ref.at[source],
                dst_ref=out_ref.at[base + k],
                send_sem=send_a.at[k],
                recv_sem=recv_a.at[k],
                device_id=(source, me_vis),
                device_id_type=pl.DeviceIdType.MESH,
            )
            incoming.wait_recv()

    arrivals(range(1, seq_count // 2))

    half = seq_count // 2

    def region(owner, part):
        if part == 0:
            return out_ref.at[pl.ds(owner * seq_count, seq_count)]
        start = owner * seq_count + (part - 1) * half
        return out_ref.at[pl.ds(start, half)]

    def link(owner, part, peer, index):
        piece = region(owner, part)
        return pltpu.make_async_remote_copy(
            src_ref=piece,
            dst_ref=piece,
            send_sem=send_b.at[index],
            recv_sem=recv_b.at[index],
            device_id=(me_seq, peer),
            device_id_type=pl.DeviceIdType.MESH,
        )

    far = vis_of(ring_id, ring_pos + 2)
    left_partner = vis_of(1 - ring_id, ring_pos - 1)
    right_partner = vis_of(1 - ring_id, ring_pos + 1)
    far_partner = vis_of(1 - ring_id, ring_pos + 2)
    sent = []

    def send(owner, part, peer, index):
        copy = link(owner, part, peer, index)
        copy.start()
        sent.append(copy)

    send(me_vis, 1, right, 1)
    send(me_vis, 1, left, 2)
    send(me_vis, 1, partner, 3)
    arrivals(range(seq_count // 2, seq_count))
    for copy in first:
        copy.wait_send()
    send(me_vis, 2, right, 10)
    send(me_vis, 2, left, 11)
    send(me_vis, 2, partner, 12)
    link(partner, 1, partner, 3).wait_recv()
    send(partner, 1, right, 4)
    send(partner, 1, left, 5)
    link(left, 1, left, 1).wait_recv()
    send(left, 1, right, 6)
    link(partner, 2, partner, 12).wait_recv()
    send(partner, 2, right, 13)
    send(partner, 2, left, 14)
    link(right, 2, right, 11).wait_recv()
    send(right, 2, left, 7)
    link(left_partner, 1, left, 4).wait_recv()
    send(left_partner, 1, right, 8)
    link(right_partner, 2, right, 14).wait_recv()
    send(right_partner, 2, left, 9)
    link(left, 2, left, 10).wait_recv()
    link(right, 1, right, 2).wait_recv()
    link(left_partner, 2, left, 13).wait_recv()
    link(right_partner, 1, right, 5).wait_recv()
    link(far, 1, left, 6).wait_recv()
    link(far, 2, right, 7).wait_recv()
    link(far_partner, 1, left, 8).wait_recv()
    link(far_partner, 2, right, 9).wait_recv()
    for copy in sent:
        copy.wait_send()


def exchange_frames(payload, vis_count):
    owners, capacity, width = payload.shape
    return pl.pallas_call(
        exchange_kernel,
        out_shape=jax.ShapeDtypeStruct((vis_count * owners, capacity, width), payload.dtype),
        in_specs=[pl.BlockSpec(memory_space=pl.ANY)],
        out_specs=pl.BlockSpec(memory_space=pl.ANY),
        scratch_shapes=[
            pltpu.SemaphoreType.DMA((owners,)),
            pltpu.SemaphoreType.DMA((owners,)),
            pltpu.SemaphoreType.DMA((15,)),
            pltpu.SemaphoreType.DMA((15,)),
            pltpu.SemaphoreType.DMA((1,)),
        ],
        compiler_params=pltpu.CompilerParams(collective_id=1, has_side_effects=True),
    )(payload)


def gather_kernel(
    key_ref, value_ref, normed_ref, w_ref, bias_ref, out_ref, q_ref, send_sem, recv_sem, local_sem,
    acc_ref,
):
    rows = key_ref.shape[0]
    lane = key_ref.shape[1]
    me_seq = lax.axis_index("seq")
    me_vis = lax.axis_index("vis")
    column = me_seq // 4
    layer = lax.rem(me_seq // 2, 2)
    core = lax.rem(me_seq, 2)
    ring = lax.axis_size("seq") // 4

    def seq_of(y, z, c):
        return (lax.rem(y + ring, ring) * 2 + z) * 2 + c

    mate = seq_of(column, layer, 1 - core)
    across = seq_of(column, 1 - layer, core)
    diagonal = seq_of(column, 1 - layer, 1 - core)
    up = seq_of(column + 1, layer, core)
    down = seq_of(column - 1, layer, core)
    barrier = pltpu.get_barrier_semaphore()
    for peer in (mate, across, diagonal, up, down):
        pl.semaphore_signal(
            barrier, inc=1, device_id=(peer, me_vis), device_id_type=pl.DeviceIdType.MESH
        )
    pl.semaphore_wait(barrier, 5)

    def rows_of(start, count):
        return out_ref.at[pl.ds(pl.multiple_of(start, rows), count)]

    def link(src, dst, peer, index):
        return pltpu.make_async_remote_copy(
            src_ref=src, dst_ref=dst, send_sem=send_sem.at[index], recv_sem=recv_sem.at[index],
            device_id=(peer, me_vis), device_id_type=pl.DeviceIdType.MESH,
        )

    sent = []

    def send(src, dst, peer, index):
        copy = link(src, dst, peer, index)
        copy.start()
        sent.append(copy)

    parts = ((key_ref, 0, 0), (value_ref, lane, 10))

    def slab(start, offset):
        return rows_of(start, rows).at[:, pl.ds(offset, lane)]

    locals_ = []
    for src_ref, offset, extra in parts:
        own = slab(me_seq * rows, offset)
        local = pltpu.make_async_copy(src_ref, own, local_sem.at[extra // 10])
        local.start()
        locals_.append(local)
        send(src_ref, own, mate, 0 + extra)
        send(src_ref, own, across, 1 + extra)
        send(src_ref, own, diagonal, 2 + extra)
    depth = normed_ref.shape[1] // 2

    def project(part):
        def body(n_blk, w_blk):
            acc_ref[...] += jnp.dot(n_blk[...], w_blk[...], preferred_element_type=jnp.float32)

        pltpu.emit_pipeline(
            body,
            grid=(depth // PROJ_TILE,),
            in_specs=[
                pl.BlockSpec((normed_ref.shape[0], PROJ_TILE), lambda k: (0, k)),
                pl.BlockSpec((PROJ_TILE, w_ref.shape[1]), lambda k: (k, 0)),
            ],
        )(normed_ref.at[:, pl.ds(part * depth, depth)], w_ref.at[pl.ds(part * depth, depth)])

    acc_ref[...] = jnp.zeros(acc_ref.shape, jnp.float32)
    project(0)
    for local in locals_:
        local.wait()
    for src_ref, offset, extra in parts:
        link(src_ref, slab(mate * rows, offset), mate, 0 + extra).wait_recv()
        link(src_ref, slab(across * rows, offset), across, 1 + extra).wait_recv()
        link(src_ref, slab(diagonal * rows, offset), diagonal, 2 + extra).wait_recv()

    def half(y, h):
        return rows_of((lax.rem(y + ring, ring) * 4 + h * 2) * rows, 2 * rows)

    def quarter(y, h, q):
        return rows_of((lax.rem(y + ring, ring) * 4 + h * 2 + q) * rows, rows)

    mine = half(column, core)
    send(mine, mine, up, 3)
    send(mine, mine, down, 4)
    project(1)
    below = half(column - 1, core)
    link(below, below, down, 3).wait_recv()
    send(below, below, mate, 7)
    piece = quarter(column - 1, core, 0)
    send(piece, piece, up, 5)
    above = half(column + 1, core)
    link(above, above, up, 4).wait_recv()
    send(above, above, mate, 9)
    piece = quarter(column + 1, core, 1)
    send(piece, piece, down, 6)
    q_ref[...] = (acc_ref[...] + bias_ref[...]).astype(q_ref.dtype)
    far_low = quarter(column + 2, core, 0)
    far_high = quarter(column + 2, core, 1)
    link(far_low, far_low, down, 5).wait_recv()
    link(far_high, far_high, up, 6).wait_recv()
    far = half(column + 2, core)
    send(far, far, mate, 8)
    for offset, index in ((-1, 7), (2, 8), (1, 9)):
        theirs = half(column + offset, 1 - core)
        link(theirs, theirs, mate, index).wait_recv()
    for copy in sent:
        copy.wait_send()


PROJ_TILE = 512


def gather_keys(keys, values, normed, w_query, q_bias, seq_count):
    rows, lane = keys.shape
    width = 2 * lane
    block = keys
    return pl.pallas_call(
        gather_kernel,
        out_shape=(
            jax.ShapeDtypeStruct((seq_count * rows, width), block.dtype),
            jax.ShapeDtypeStruct((normed.shape[0], w_query.shape[1]), jnp.bfloat16),
        ),
        in_specs=[
            pl.BlockSpec(memory_space=pl.ANY),
            pl.BlockSpec(memory_space=pl.ANY),
            pl.BlockSpec(memory_space=pl.ANY),
            pl.BlockSpec(memory_space=pl.ANY),
            pl.BlockSpec(memory_space=pltpu.VMEM),
        ],
        out_specs=(pl.BlockSpec(memory_space=pl.ANY), pl.BlockSpec(memory_space=pltpu.VMEM)),
        scratch_shapes=[
            pltpu.SemaphoreType.DMA((13,)),
            pltpu.SemaphoreType.DMA((13,)),
            pltpu.SemaphoreType.DMA((2,)),
            pltpu.VMEM((normed.shape[0], w_query.shape[1]), jnp.float32),
        ],
        compiler_params=pltpu.CompilerParams(collective_id=2, has_side_effects=True),
    )(keys, values, normed, w_query, q_bias.reshape(1, -1))


def on_device(
    text, frames, tile_pos, frame_count, doc_ids, norm_gain, w_query, q_bias, w_key, w_value, v_bias
):
    seq_count = lax.axis_size("seq")
    vis_count = lax.axis_size("vis")
    shard_index = lax.axis_index("seq")
    shard_rows = text.shape[0]
    capacity = shard_rows // (seq_count * vis_count)
    first_row = shard_index * shard_rows
    payload = frame_slots(frames, tile_pos, frame_count, shard_rows, seq_count, capacity)
    gathered = exchange_frames(payload, vis_count)
    width = text.shape[1]
    incoming_place = gathered[:, :, width].astype(jnp.int32)
    merged = place_frames(text, gathered, incoming_place, width)
    widened = merged.astype(jnp.float32)
    mean_square = jnp.mean(widened * widened, axis=1, keepdims=True)
    normed = (widened * lax.rsqrt(mean_square + epsilon) * norm_gain).astype(jnp.bfloat16)
    key_rows = jnp.dot(normed, w_key, preferred_element_type=jnp.float32).astype(jnp.bfloat16)
    value_rows = (jnp.dot(normed, w_value, preferred_element_type=jnp.float32) + v_bias).astype(
        jnp.bfloat16
    )
    kv_heads = w_key.shape[1] // HEAD_DIM
    per_group = w_query.shape[1] // HEAD_DIM // kv_heads
    incoming_keys, queries = gather_keys(key_rows, value_rows, normed, w_query, q_bias, seq_count)
    return flash_attention(doc_ids, queries, incoming_keys)


KEY_BLOCK = 512
DOC_SPAN = 2048


def block_bounds(doc_ref, rows, key_rows):
    first = lax.axis_index("seq") * rows
    first_doc = doc_ref[first]
    low = 0
    for b in range(key_rows // KEY_BLOCK):
        low = low + (doc_ref[(b + 1) * KEY_BLOCK - 1] < first_doc).astype(jnp.int32)
    return low, (first + rows - 1) // KEY_BLOCK, first


def flash_kernel(doc_ref, q_ref, k_ref, v_ref, qdoc_ref, kdoc_ref, out_ref, peak_ref, total_ref, acc_ref, qcol_ref):
    step = pl.program_id(0)
    rows = q_ref.shape[0]
    heads = q_ref.shape[1] // HEAD_DIM
    low, high, first = block_bounds(doc_ref, rows, doc_ref.shape[0])
    block = low + step

    @pl.when(step == 0)
    def _():
        peak_ref[...] = jnp.full(peak_ref.shape, negative, jnp.float32)
        total_ref[...] = jnp.zeros(total_ref.shape, jnp.float32)
        acc_ref[...] = jnp.zeros(acc_ref.shape, jnp.float32)
        spread = jnp.broadcast_to(qdoc_ref[...], (rows, rows))
        diagonal = lax.broadcasted_iota(jnp.int32, (rows, rows), 0) == lax.broadcasted_iota(
            jnp.int32, (rows, rows), 1
        )
        qcol_ref[...] = jnp.sum(jnp.where(diagonal, spread, 0), axis=1, keepdims=True)

    @pl.when(block <= high)
    def _():
        key_place = block * KEY_BLOCK + lax.broadcasted_iota(jnp.int32, (1, KEY_BLOCK), 1)
        query_place = first + lax.broadcasted_iota(jnp.int32, (rows, 1), 0)
        allowed = (key_place <= query_place) & (kdoc_ref[...] == qcol_ref[...])
        keys = k_ref[...]
        vals = v_ref[...]
        for h in range(heads):
            cols = slice(h * HEAD_DIM, (h + 1) * HEAD_DIM)
            scores = lax.dot_general(
                q_ref[:, cols], keys, (((1,), (1,)), ((), ())),
                preferred_element_type=jnp.float32,
            ) * HEAD_DIM ** (-0.5)
            scores = jnp.where(allowed, scores, negative)
            old_peak = peak_ref[h]
            new_peak = jnp.maximum(old_peak, jnp.max(scores, axis=1, keepdims=True))
            raised = jnp.where(allowed, jnp.exp(scores - new_peak[:, :1]), 0.0)
            factor = jnp.exp(old_peak - new_peak)
            total_ref[h] = total_ref[h] * factor + jnp.sum(raised, axis=1, keepdims=True)
            peak_ref[h] = new_peak
            product = jnp.dot(raised.astype(jnp.bfloat16), vals, preferred_element_type=jnp.float32)
            acc_ref[:, cols] = acc_ref[:, cols] * factor[:, :1] + product

    @pl.when(step == pl.num_programs(0) - 1)
    def _():
        for h in range(heads):
            cols = slice(h * HEAD_DIM, (h + 1) * HEAD_DIM)
            out_ref[:, cols] = (acc_ref[:, cols] / total_ref[h][:, :1]).astype(out_ref.dtype)


def flash_attention(doc_ids, queries, keyval):
    rows, width = queries.shape
    key_rows = keyval.shape[0]
    steps = max(
        (first + rows - 1) // KEY_BLOCK - max(0, first - DOC_SPAN + 1) // KEY_BLOCK + 1
        for first in range(0, key_rows, rows)
    )
    heads = width // HEAD_DIM

    def clamp(j, d):
        low, high, _ = block_bounds(d, rows, key_rows)
        return jnp.minimum(low + j, high)

    grid_spec = pltpu.PrefetchScalarGridSpec(
        num_scalar_prefetch=1,
        grid=(steps,),
        in_specs=[
            pl.BlockSpec((rows, width), lambda j, d: (0, 0)),
            pl.BlockSpec((KEY_BLOCK, HEAD_DIM), lambda j, d: (clamp(j, d), 0)),
            pl.BlockSpec((KEY_BLOCK, HEAD_DIM), lambda j, d: (clamp(j, d), 1)),
            pl.BlockSpec((1, rows), lambda j, d: (0, lax.axis_index("seq"))),
            pl.BlockSpec((1, KEY_BLOCK), lambda j, d: (0, clamp(j, d))),
        ],
        out_specs=pl.BlockSpec((rows, width), lambda j, d: (0, 0)),
        scratch_shapes=[
            pltpu.VMEM((heads, rows, 1), jnp.float32),
            pltpu.VMEM((heads, rows, 1), jnp.float32),
            pltpu.VMEM((rows, width), jnp.float32),
            pltpu.VMEM((rows, 1), jnp.int32),
        ],
    )
    flops = 4 * rows * width * key_rows // 2
    doc_row = doc_ids.reshape(1, -1)
    return pl.pallas_call(
        flash_kernel,
        out_shape=jax.ShapeDtypeStruct((rows, width), jnp.bfloat16),
        grid_spec=grid_spec,
        compiler_params=pltpu.CompilerParams(dimension_semantics=("arbitrary",)),
        cost_estimate=pl.CostEstimate(
            flops=flops, transcendentals=rows * heads * key_rows // 2,
            bytes_accessed=2 * (2 * rows * width + key_rows * 2 * HEAD_DIM),
        ),
    )(doc_ids, queries, keyval, keyval, doc_row, doc_row)


def solution(mesh):
    in_specs = (
        P("seq", None),
        P(("seq", "vis"), None),
        P(("seq", "vis")),
        P(("seq", "vis")),
        P(),
        P(),
        P(None, "vis"),
        P("vis"),
        P(None, "vis"),
        P(None, "vis"),
        P("vis"),
    )
    out_specs = P("seq", "vis")
    return jax.shard_map(
        on_device, mesh=mesh, in_specs=in_specs, out_specs=out_specs, check_vma=False
    )
```

```python
import jax
import jax.numpy as jnp
from jax import lax
from jax.sharding import PartitionSpec as P
from jax.experimental import pallas as pl
from jax.experimental.pallas import tpu as pltpu

HEAD_DIM = 128


epsilon = 1e-06
negative = -1e30


def frame_slots(frames, tile_pos, frame_count, shard_rows, owners, capacity):
    row_count = frames.shape[0]
    row_ids = jnp.arange(row_count, dtype=jnp.int32)
    usable = row_ids < frame_count[0]
    owner = jnp.where(usable, tile_pos // shard_rows, owners)
    hits = (owner[:, None] == jnp.arange(owners, dtype=jnp.int32)[None, :]).astype(jnp.int32)
    earlier = (row_ids[:, None] > row_ids[None, :]).astype(jnp.int32)
    before = jnp.dot(earlier, hits, preferred_element_type=jnp.int32)
    rank = jnp.sum(before * hits, axis=1)
    slot_index = owner * capacity + rank
    slot_ids = jnp.arange(owners * capacity, dtype=jnp.int32)
    match = usable[:, None] & (slot_index[:, None] == slot_ids[None, :])
    filled = jnp.any(match, axis=0)
    local = tile_pos - owner * shard_rows
    slot_local = jnp.sum(jnp.where(match, local[:, None], 0), axis=0)
    slot_local = jnp.where(filled, slot_local, -1)
    slot_rows = jnp.dot(
        match.T.astype(frames.dtype), frames, preferred_element_type=jnp.float32
    ).astype(frames.dtype)
    place_col = jnp.broadcast_to(slot_local[:, None], (slot_local.shape[0], 128)).astype(frames.dtype)
    payload = jnp.concatenate([slot_rows, place_col], axis=1)
    return payload.reshape(owners, capacity, payload.shape[1])


def place_frames(text, incoming, incoming_place, width):
    lookup = incoming_place[None] == jnp.arange(text.shape[0], dtype=jnp.int32).astype(incoming.dtype)[:, None, None]
    covered = jnp.any(lookup, axis=(1, 2))
    placed = lax.dot_general(
        lookup.astype(incoming.dtype), incoming, (((1, 2), (0, 1)), ((), ())),
        preferred_element_type=jnp.float32,
    )[:, :width].astype(text.dtype)
    return jnp.where(covered[:, None], placed, text)


def exchange_kernel(payload_ref, out_ref, send_a, recv_a, send_b, recv_b, local_sem):
    seq_count = lax.axis_size("seq")
    vis_count = lax.axis_size("vis")
    ring = vis_count // 2
    me_seq = lax.axis_index("seq")
    me_vis = lax.axis_index("vis")
    ring_pos = lax.rem(me_vis, ring)
    ring_id = me_vis // ring

    def vis_of(ring_index, position):
        return ring_index * ring + lax.rem(position + ring, ring)

    right = vis_of(ring_id, ring_pos + 1)
    left = vis_of(ring_id, ring_pos - 1)
    partner = vis_of(1 - ring_id, ring_pos)
    barrier = pltpu.get_barrier_semaphore()
    for k in range(1, seq_count):
        pl.semaphore_signal(
            barrier, inc=1, device_id=(lax.rem(me_seq + k, seq_count), me_vis),
            device_id_type=pl.DeviceIdType.MESH,
        )
    for peer in (left, right, partner):
        pl.semaphore_signal(
            barrier, inc=1, device_id=(me_seq, peer), device_id_type=pl.DeviceIdType.MESH
        )
    pl.semaphore_wait(barrier, seq_count + 2)
    base = me_vis * seq_count
    local = pltpu.make_async_copy(payload_ref.at[me_seq], out_ref.at[base], local_sem.at[0])
    local.start()
    first = []
    for k in range(1, seq_count):
        target = lax.rem(me_seq + k, seq_count)
        copy = pltpu.make_async_remote_copy(
            src_ref=payload_ref.at[target],
            dst_ref=out_ref.at[base + k],
            send_sem=send_a.at[k],
            recv_sem=recv_a.at[k],
            device_id=(target, me_vis),
            device_id_type=pl.DeviceIdType.MESH,
        )
        copy.start()
        first.append(copy)
    local.wait()

    def arrivals(ks):
        for k in ks:
            source = lax.rem(me_seq + seq_count - k, seq_count)
            incoming = pltpu.make_async_remote_copy(
                src_ref=payload_ref.at[source],
                dst_ref=out_ref.at[base + k],
                send_sem=send_a.at[k],
                recv_sem=recv_a.at[k],
                device_id=(source, me_vis),
                device_id_type=pl.DeviceIdType.MESH,
            )
            incoming.wait_recv()

    arrivals(range(1, seq_count // 2))

    half = seq_count // 2

    def region(owner, part):
        if part == 0:
            return out_ref.at[pl.ds(owner * seq_count, seq_count)]
        start = owner * seq_count + (part - 1) * half
        return out_ref.at[pl.ds(start, half)]

    def link(owner, part, peer, index):
        piece = region(owner, part)
        return pltpu.make_async_remote_copy(
            src_ref=piece,
            dst_ref=piece,
            send_sem=send_b.at[index],
            recv_sem=recv_b.at[index],
            device_id=(me_seq, peer),
            device_id_type=pl.DeviceIdType.MESH,
        )

    far = vis_of(ring_id, ring_pos + 2)
    left_partner = vis_of(1 - ring_id, ring_pos - 1)
    right_partner = vis_of(1 - ring_id, ring_pos + 1)
    far_partner = vis_of(1 - ring_id, ring_pos + 2)
    sent = []

    def send(owner, part, peer, index):
        copy = link(owner, part, peer, index)
        copy.start()
        sent.append(copy)

    send(me_vis, 1, right, 1)
    send(me_vis, 1, left, 2)
    send(me_vis, 1, partner, 3)
    arrivals(range(seq_count // 2, seq_count))
    for copy in first:
        copy.wait_send()
    send(me_vis, 2, right, 10)
    send(me_vis, 2, left, 11)
    send(me_vis, 2, partner, 12)
    link(partner, 1, partner, 3).wait_recv()
    send(partner, 1, right, 4)
    send(partner, 1, left, 5)
    link(left, 1, left, 1).wait_recv()
    send(left, 1, right, 6)
    link(partner, 2, partner, 12).wait_recv()
    send(partner, 2, right, 13)
    send(partner, 2, left, 14)
    link(right, 2, right, 11).wait_recv()
    send(right, 2, left, 7)
    link(left_partner, 1, left, 4).wait_recv()
    send(left_partner, 1, right, 8)
    link(right_partner, 2, right, 14).wait_recv()
    send(right_partner, 2, left, 9)
    link(left, 2, left, 10).wait_recv()
    link(right, 1, right, 2).wait_recv()
    link(left_partner, 2, left, 13).wait_recv()
    link(right_partner, 1, right, 5).wait_recv()
    link(far, 1, left, 6).wait_recv()
    link(far, 2, right, 7).wait_recv()
    link(far_partner, 1, left, 8).wait_recv()
    link(far_partner, 2, right, 9).wait_recv()
    for copy in sent:
        copy.wait_send()


def exchange_frames(payload, vis_count):
    owners, capacity, width = payload.shape
    return pl.pallas_call(
        exchange_kernel,
        out_shape=jax.ShapeDtypeStruct((vis_count * owners, capacity, width), payload.dtype),
        in_specs=[pl.BlockSpec(memory_space=pl.ANY)],
        out_specs=pl.BlockSpec(memory_space=pl.ANY),
        scratch_shapes=[
            pltpu.SemaphoreType.DMA((owners,)),
            pltpu.SemaphoreType.DMA((owners,)),
            pltpu.SemaphoreType.DMA((15,)),
            pltpu.SemaphoreType.DMA((15,)),
            pltpu.SemaphoreType.DMA((1,)),
        ],
        compiler_params=pltpu.CompilerParams(collective_id=1, has_side_effects=True),
    )(payload)


def gather_kernel(
    key_ref, value_ref, normed_ref, w_ref, bias_ref, out_ref, q_ref, send_sem, recv_sem, local_sem,
    acc_ref,
):
    rows = key_ref.shape[0]
    lane = key_ref.shape[1]
    me_seq = lax.axis_index("seq")
    me_vis = lax.axis_index("vis")
    column = me_seq // 4
    layer = lax.rem(me_seq // 2, 2)
    core = lax.rem(me_seq, 2)
    ring = lax.axis_size("seq") // 4

    def seq_of(y, z, c):
        return (lax.rem(y + ring, ring) * 2 + z) * 2 + c

    mate = seq_of(column, layer, 1 - core)
    across = seq_of(column, 1 - layer, core)
    diagonal = seq_of(column, 1 - layer, 1 - core)
    up = seq_of(column + 1, layer, core)
    down = seq_of(column - 1, layer, core)
    barrier = pltpu.get_barrier_semaphore()
    for peer in (mate, across, diagonal, up, down):
        pl.semaphore_signal(
            barrier, inc=1, device_id=(peer, me_vis), device_id_type=pl.DeviceIdType.MESH
        )
    pl.semaphore_wait(barrier, 5)

    def rows_of(start, count):
        return out_ref.at[pl.ds(pl.multiple_of(start, rows), count)]

    def link(src, dst, peer, index):
        return pltpu.make_async_remote_copy(
            src_ref=src, dst_ref=dst, send_sem=send_sem.at[index], recv_sem=recv_sem.at[index],
            device_id=(peer, me_vis), device_id_type=pl.DeviceIdType.MESH,
        )

    sent = []

    def send(src, dst, peer, index):
        copy = link(src, dst, peer, index)
        copy.start()
        sent.append(copy)

    parts = ((key_ref, 0, 0), (value_ref, lane, 10))

    def slab(start, offset):
        return rows_of(start, rows).at[:, pl.ds(offset, lane)]

    locals_ = []
    for src_ref, offset, extra in parts:
        own = slab(me_seq * rows, offset)
        local = pltpu.make_async_copy(src_ref, own, local_sem.at[extra // 10])
        local.start()
        locals_.append(local)
        send(src_ref, own, mate, 0 + extra)
        send(src_ref, own, across, 1 + extra)
        send(src_ref, own, diagonal, 2 + extra)
    depth = normed_ref.shape[1] // 2

    def project(part):
        def body(n_blk, w_blk):
            acc_ref[...] += jnp.dot(n_blk[...], w_blk[...], preferred_element_type=jnp.float32)

        pltpu.emit_pipeline(
            body,
            grid=(depth // PROJ_TILE,),
            in_specs=[
                pl.BlockSpec((normed_ref.shape[0], PROJ_TILE), lambda k: (0, k)),
                pl.BlockSpec((PROJ_TILE, w_ref.shape[1]), lambda k: (k, 0)),
            ],
        )(normed_ref.at[:, pl.ds(part * depth, depth)], w_ref.at[pl.ds(part * depth, depth)])

    acc_ref[...] = jnp.zeros(acc_ref.shape, jnp.float32)
    project(0)
    for local in locals_:
        local.wait()
    for src_ref, offset, extra in parts:
        link(src_ref, slab(mate * rows, offset), mate, 0 + extra).wait_recv()
        link(src_ref, slab(across * rows, offset), across, 1 + extra).wait_recv()
        link(src_ref, slab(diagonal * rows, offset), diagonal, 2 + extra).wait_recv()

    def half(y, h):
        return rows_of((lax.rem(y + ring, ring) * 4 + h * 2) * rows, 2 * rows)

    def quarter(y, h, q):
        return rows_of((lax.rem(y + ring, ring) * 4 + h * 2 + q) * rows, rows)

    mine = half(column, core)
    send(mine, mine, up, 3)
    send(mine, mine, down, 4)
    project(1)
    below = half(column - 1, core)
    link(below, below, down, 3).wait_recv()
    send(below, below, mate, 7)
    piece = quarter(column - 1, core, 0)
    send(piece, piece, up, 5)
    above = half(column + 1, core)
    link(above, above, up, 4).wait_recv()
    send(above, above, mate, 9)
    piece = quarter(column + 1, core, 1)
    send(piece, piece, down, 6)
    q_ref[...] = (acc_ref[...] + bias_ref[...]).astype(q_ref.dtype)
    far_low = quarter(column + 2, core, 0)
    far_high = quarter(column + 2, core, 1)
    link(far_low, far_low, down, 5).wait_recv()
    link(far_high, far_high, up, 6).wait_recv()
    far = half(column + 2, core)
    send(far, far, mate, 8)
    for offset, index in ((-1, 7), (2, 8), (1, 9)):
        theirs = half(column + offset, 1 - core)
        link(theirs, theirs, mate, index).wait_recv()
    for copy in sent:
        copy.wait_send()


PROJ_TILE = 512


def gather_keys(keys, values, normed, w_query, q_bias, seq_count):
    rows, lane = keys.shape
    width = 2 * lane
    block = keys
    return pl.pallas_call(
        gather_kernel,
        out_shape=(
            jax.ShapeDtypeStruct((seq_count * rows, width), block.dtype),
            jax.ShapeDtypeStruct((normed.shape[0], w_query.shape[1]), jnp.bfloat16),
        ),
        in_specs=[
            pl.BlockSpec(memory_space=pl.ANY),
            pl.BlockSpec(memory_space=pl.ANY),
            pl.BlockSpec(memory_space=pl.ANY),
            pl.BlockSpec(memory_space=pl.ANY),
            pl.BlockSpec(memory_space=pltpu.VMEM),
        ],
        out_specs=(pl.BlockSpec(memory_space=pl.ANY), pl.BlockSpec(memory_space=pltpu.VMEM)),
        scratch_shapes=[
            pltpu.SemaphoreType.DMA((13,)),
            pltpu.SemaphoreType.DMA((13,)),
            pltpu.SemaphoreType.DMA((2,)),
            pltpu.VMEM((normed.shape[0], w_query.shape[1]), jnp.float32),
        ],
        compiler_params=pltpu.CompilerParams(collective_id=2, has_side_effects=True),
    )(keys, values, normed, w_query, q_bias.reshape(1, -1))


def on_device(
    text, frames, tile_pos, frame_count, doc_ids, norm_gain, w_query, q_bias, w_key, w_value, v_bias
):
    seq_count = lax.axis_size("seq")
    vis_count = lax.axis_size("vis")
    shard_index = lax.axis_index("seq")
    shard_rows = text.shape[0]
    capacity = shard_rows // (seq_count * vis_count)
    first_row = shard_index * shard_rows
    payload = frame_slots(frames, tile_pos, frame_count, shard_rows, seq_count, capacity)
    gathered = exchange_frames(payload, vis_count)
    width = text.shape[1]
    incoming_place = gathered[:, :, width]
    merged = place_frames(text, gathered, incoming_place, width)
    widened = merged.astype(jnp.float32)
    mean_square = jnp.mean(widened * widened, axis=1, keepdims=True)
    normed = (widened * lax.rsqrt(mean_square + epsilon) * norm_gain).astype(jnp.bfloat16)
    key_rows = jnp.dot(normed, w_key, preferred_element_type=jnp.float32).astype(jnp.bfloat16)
    value_rows = (jnp.dot(normed, w_value, preferred_element_type=jnp.float32) + v_bias).astype(
        jnp.bfloat16
    )
    kv_heads = w_key.shape[1] // HEAD_DIM
    per_group = w_query.shape[1] // HEAD_DIM // kv_heads
    incoming_keys, queries = gather_keys(key_rows, value_rows, normed, w_query, q_bias, seq_count)
    return flash_attention(doc_ids, queries, incoming_keys)


KEY_BLOCK = 512
DOC_SPAN = 2048


def block_bounds(doc_ref, rows, key_rows):
    first = lax.axis_index("seq") * rows
    first_doc = doc_ref[first]
    low = 0
    for b in range(key_rows // KEY_BLOCK):
        low = low + (doc_ref[(b + 1) * KEY_BLOCK - 1] < first_doc).astype(jnp.int32)
    return low, (first + rows - 1) // KEY_BLOCK, first


def flash_kernel(doc_ref, q_ref, k_ref, v_ref, qdoc_ref, kdoc_ref, out_ref, peak_ref, total_ref, acc_ref, qcol_ref):
    step = pl.program_id(0)
    rows = q_ref.shape[0]
    heads = q_ref.shape[1] // HEAD_DIM
    low, high, first = block_bounds(doc_ref, rows, doc_ref.shape[0])
    block = low + step

    @pl.when(step == 0)
    def _():
        peak_ref[...] = jnp.full(peak_ref.shape, negative, jnp.float32)
        total_ref[...] = jnp.zeros(total_ref.shape, jnp.float32)
        acc_ref[...] = jnp.zeros(acc_ref.shape, jnp.float32)
        spread = jnp.broadcast_to(qdoc_ref[...], (rows, rows))
        diagonal = lax.broadcasted_iota(jnp.int32, (rows, rows), 0) == lax.broadcasted_iota(
            jnp.int32, (rows, rows), 1
        )
        qcol_ref[...] = jnp.sum(jnp.where(diagonal, spread, 0), axis=1, keepdims=True)

    @pl.when(block <= high)
    def _():
        key_place = block * KEY_BLOCK + lax.broadcasted_iota(jnp.int32, (1, KEY_BLOCK), 1)
        query_place = first + lax.broadcasted_iota(jnp.int32, (rows, 1), 0)
        allowed = (key_place <= query_place) & (kdoc_ref[...] == qcol_ref[...])
        keys = k_ref[...]
        vals = v_ref[...]
        for h in range(heads):
            cols = slice(h * HEAD_DIM, (h + 1) * HEAD_DIM)
            scores = lax.dot_general(
                q_ref[:, cols], keys, (((1,), (1,)), ((), ())),
                preferred_element_type=jnp.float32,
            ) * HEAD_DIM ** (-0.5)
            scores = jnp.where(allowed, scores, negative)
            old_peak = peak_ref[h]
            new_peak = jnp.maximum(old_peak, jnp.max(scores, axis=1, keepdims=True))
            raised = jnp.where(allowed, jnp.exp(scores - new_peak[:, :1]), 0.0)
            factor = jnp.exp(old_peak - new_peak)
            total_ref[h] = total_ref[h] * factor + jnp.sum(raised, axis=1, keepdims=True)
            peak_ref[h] = new_peak
            product = jnp.dot(raised.astype(jnp.bfloat16), vals, preferred_element_type=jnp.float32)
            acc_ref[:, cols] = acc_ref[:, cols] * factor[:, :1] + product

    @pl.when(step == pl.num_programs(0) - 1)
    def _():
        for h in range(heads):
            cols = slice(h * HEAD_DIM, (h + 1) * HEAD_DIM)
            out_ref[:, cols] = (acc_ref[:, cols] / total_ref[h][:, :1]).astype(out_ref.dtype)


def flash_attention(doc_ids, queries, keyval):
    rows, width = queries.shape
    key_rows = keyval.shape[0]
    steps = max(
        (first + rows - 1) // KEY_BLOCK - max(0, first - DOC_SPAN + 1) // KEY_BLOCK + 1
        for first in range(0, key_rows, rows)
    )
    heads = width // HEAD_DIM

    def clamp(j, d):
        low, high, _ = block_bounds(d, rows, key_rows)
        return jnp.minimum(low + j, high)

    grid_spec = pltpu.PrefetchScalarGridSpec(
        num_scalar_prefetch=1,
        grid=(steps,),
        in_specs=[
            pl.BlockSpec((rows, width), lambda j, d: (0, 0)),
            pl.BlockSpec((KEY_BLOCK, HEAD_DIM), lambda j, d: (clamp(j, d), 0)),
            pl.BlockSpec((KEY_BLOCK, HEAD_DIM), lambda j, d: (clamp(j, d), 1)),
            pl.BlockSpec((1, rows), lambda j, d: (0, lax.axis_index("seq"))),
            pl.BlockSpec((1, KEY_BLOCK), lambda j, d: (0, clamp(j, d))),
        ],
        out_specs=pl.BlockSpec((rows, width), lambda j, d: (0, 0)),
        scratch_shapes=[
            pltpu.VMEM((heads, rows, 1), jnp.float32),
            pltpu.VMEM((heads, rows, 1), jnp.float32),
            pltpu.VMEM((rows, width), jnp.float32),
            pltpu.VMEM((rows, 1), jnp.int32),
        ],
    )
    flops = 4 * rows * width * key_rows // 2
    doc_row = doc_ids.reshape(1, -1)
    return pl.pallas_call(
        flash_kernel,
        out_shape=jax.ShapeDtypeStruct((rows, width), jnp.bfloat16),
        grid_spec=grid_spec,
        compiler_params=pltpu.CompilerParams(dimension_semantics=("arbitrary",)),
        cost_estimate=pl.CostEstimate(
            flops=flops, transcendentals=rows * heads * key_rows // 2,
            bytes_accessed=2 * (2 * rows * width + key_rows * 2 * HEAD_DIM),
        ),
    )(doc_ids, queries, keyval, keyval, doc_row, doc_row)


def solution(mesh):
    in_specs = (
        P("seq", None),
        P(("seq", "vis"), None),
        P(("seq", "vis")),
        P(("seq", "vis")),
        P(),
        P(),
        P(None, "vis"),
        P("vis"),
        P(None, "vis"),
        P(None, "vis"),
        P("vis"),
    )
    out_specs = P("seq", "vis")
    return jax.shard_map(
        on_device, mesh=mesh, in_specs=in_specs, out_specs=out_specs, check_vma=False
    )
```

```python
import jax
import jax.numpy as jnp
from jax import lax
from jax.sharding import PartitionSpec as P
from jax.experimental import pallas as pl
from jax.experimental.pallas import tpu as pltpu

HEAD_DIM = 128


epsilon = 1e-06
negative = -1e30


def frame_slots(frames, tile_pos, frame_count, shard_rows, owners, capacity):
    row_count = frames.shape[0]
    row_ids = jnp.arange(row_count, dtype=jnp.int32)
    usable = row_ids < frame_count[0]
    owner = jnp.where(usable, tile_pos // shard_rows, owners)
    hits = (owner[:, None] == jnp.arange(owners, dtype=jnp.int32)[None, :]).astype(jnp.int32)
    earlier = (row_ids[:, None] > row_ids[None, :]).astype(jnp.int32)
    before = jnp.dot(earlier, hits, preferred_element_type=jnp.int32)
    rank = jnp.sum(before * hits, axis=1)
    slot_index = owner * capacity + rank
    slot_ids = jnp.arange(owners * capacity, dtype=jnp.int32)
    match = usable[:, None] & (slot_index[:, None] == slot_ids[None, :])
    filled = jnp.any(match, axis=0)
    local = tile_pos - owner * shard_rows
    slot_local = jnp.sum(jnp.where(match, local[:, None], 0), axis=0)
    slot_local = jnp.where(filled, slot_local, -1)
    slot_rows = jnp.dot(
        match.T.astype(frames.dtype), frames, preferred_element_type=jnp.float32
    ).astype(frames.dtype)
    place_col = jnp.broadcast_to(slot_local[:, None], (slot_local.shape[0], 128)).astype(frames.dtype)
    payload = jnp.concatenate([slot_rows, place_col], axis=1)
    return payload.reshape(owners, capacity, payload.shape[1])


def place_frames(text, incoming, incoming_place, width):
    lookup = incoming_place[None] == jnp.arange(text.shape[0], dtype=jnp.int32)[:, None, None]
    covered = jnp.any(lookup, axis=(1, 2))
    placed = lax.dot_general(
        lookup.astype(incoming.dtype), incoming, (((1, 2), (0, 1)), ((), ())),
        preferred_element_type=jnp.float32,
    )[:, :width].astype(text.dtype)
    return jnp.where(covered[:, None], placed, text)


def exchange_kernel(payload_ref, out_ref, send_a, recv_a, send_b, recv_b, local_sem):
    seq_count = lax.axis_size("seq")
    vis_count = lax.axis_size("vis")
    ring = vis_count // 2
    me_seq = lax.axis_index("seq")
    me_vis = lax.axis_index("vis")
    ring_pos = lax.rem(me_vis, ring)
    ring_id = me_vis // ring

    def vis_of(ring_index, position):
        return ring_index * ring + lax.rem(position + ring, ring)

    right = vis_of(ring_id, ring_pos + 1)
    left = vis_of(ring_id, ring_pos - 1)
    partner = vis_of(1 - ring_id, ring_pos)
    barrier = pltpu.get_barrier_semaphore()
    for k in range(1, seq_count):
        pl.semaphore_signal(
            barrier, inc=1, device_id=(lax.rem(me_seq + k, seq_count), me_vis),
            device_id_type=pl.DeviceIdType.MESH,
        )
    for peer in (left, right, partner):
        pl.semaphore_signal(
            barrier, inc=1, device_id=(me_seq, peer), device_id_type=pl.DeviceIdType.MESH
        )
    pl.semaphore_wait(barrier, seq_count + 2)
    base = me_vis * seq_count
    local = pltpu.make_async_copy(payload_ref.at[me_seq], out_ref.at[base], local_sem.at[0])
    local.start()
    first = []
    for k in range(1, seq_count):
        target = lax.rem(me_seq + k, seq_count)
        copy = pltpu.make_async_remote_copy(
            src_ref=payload_ref.at[target],
            dst_ref=out_ref.at[base + k],
            send_sem=send_a.at[k],
            recv_sem=recv_a.at[k],
            device_id=(target, me_vis),
            device_id_type=pl.DeviceIdType.MESH,
        )
        copy.start()
        first.append(copy)
    local.wait()

    def arrivals(ks):
        for k in ks:
            source = lax.rem(me_seq + seq_count - k, seq_count)
            incoming = pltpu.make_async_remote_copy(
                src_ref=payload_ref.at[source],
                dst_ref=out_ref.at[base + k],
                send_sem=send_a.at[k],
                recv_sem=recv_a.at[k],
                device_id=(source, me_vis),
                device_id_type=pl.DeviceIdType.MESH,
            )
            incoming.wait_recv()

    arrivals(range(1, seq_count // 2))

    half = seq_count // 2

    def region(owner, part):
        if part == 0:
            return out_ref.at[pl.ds(owner * seq_count, seq_count)]
        start = owner * seq_count + (part - 1) * half
        return out_ref.at[pl.ds(start, half)]

    def link(owner, part, peer, index):
        piece = region(owner, part)
        return pltpu.make_async_remote_copy(
            src_ref=piece,
            dst_ref=piece,
            send_sem=send_b.at[index],
            recv_sem=recv_b.at[index],
            device_id=(me_seq, peer),
            device_id_type=pl.DeviceIdType.MESH,
        )

    far = vis_of(ring_id, ring_pos + 2)
    left_partner = vis_of(1 - ring_id, ring_pos - 1)
    right_partner = vis_of(1 - ring_id, ring_pos + 1)
    far_partner = vis_of(1 - ring_id, ring_pos + 2)
    sent = []

    def send(owner, part, peer, index):
        copy = link(owner, part, peer, index)
        copy.start()
        sent.append(copy)

    send(me_vis, 1, right, 1)
    send(me_vis, 1, left, 2)
    send(me_vis, 1, partner, 3)
    arrivals(range(seq_count // 2, seq_count))
    for copy in first:
        copy.wait_send()
    send(me_vis, 2, right, 10)
    send(me_vis, 2, left, 11)
    send(me_vis, 2, partner, 12)
    link(partner, 1, partner, 3).wait_recv()
    send(partner, 1, right, 4)
    send(partner, 1, left, 5)
    link(left, 1, left, 1).wait_recv()
    send(left, 1, right, 6)
    link(partner, 2, partner, 12).wait_recv()
    send(partner, 2, right, 13)
    send(partner, 2, left, 14)
    link(right, 2, right, 11).wait_recv()
    send(right, 2, left, 7)
    link(left_partner, 1, left, 4).wait_recv()
    send(left_partner, 1, right, 8)
    link(right_partner, 2, right, 14).wait_recv()
    send(right_partner, 2, left, 9)
    link(left, 2, left, 10).wait_recv()
    link(right, 1, right, 2).wait_recv()
    link(left_partner, 2, left, 13).wait_recv()
    link(right_partner, 1, right, 5).wait_recv()
    link(far, 1, left, 6).wait_recv()
    link(far, 2, right, 7).wait_recv()
    link(far_partner, 1, left, 8).wait_recv()
    link(far_partner, 2, right, 9).wait_recv()
    for copy in sent:
        copy.wait_send()


def exchange_frames(payload, vis_count):
    owners, capacity, width = payload.shape
    return pl.pallas_call(
        exchange_kernel,
        out_shape=jax.ShapeDtypeStruct((vis_count * owners, capacity, width), payload.dtype),
        in_specs=[pl.BlockSpec(memory_space=pl.ANY)],
        out_specs=pl.BlockSpec(memory_space=pl.ANY),
        scratch_shapes=[
            pltpu.SemaphoreType.DMA((owners,)),
            pltpu.SemaphoreType.DMA((owners,)),
            pltpu.SemaphoreType.DMA((15,)),
            pltpu.SemaphoreType.DMA((15,)),
            pltpu.SemaphoreType.DMA((1,)),
        ],
        compiler_params=pltpu.CompilerParams(collective_id=1, has_side_effects=True),
    )(payload)


def gather_kernel(
    key_ref, value_ref, normed_ref, w_ref, bias_ref, out_ref, q_ref, send_sem, recv_sem, local_sem,
    acc_ref,
):
    rows = key_ref.shape[0]
    lane = key_ref.shape[1]
    me_seq = lax.axis_index("seq")
    me_vis = lax.axis_index("vis")
    column = me_seq // 4
    layer = lax.rem(me_seq // 2, 2)
    core = lax.rem(me_seq, 2)
    ring = lax.axis_size("seq") // 4

    def seq_of(y, z, c):
        return (lax.rem(y + ring, ring) * 2 + z) * 2 + c

    mate = seq_of(column, layer, 1 - core)
    across = seq_of(column, 1 - layer, core)
    diagonal = seq_of(column, 1 - layer, 1 - core)
    up = seq_of(column + 1, layer, core)
    down = seq_of(column - 1, layer, core)
    barrier = pltpu.get_barrier_semaphore()
    for peer in (mate, across, diagonal, up, down):
        pl.semaphore_signal(
            barrier, inc=1, device_id=(peer, me_vis), device_id_type=pl.DeviceIdType.MESH
        )
    pl.semaphore_wait(barrier, 5)

    def rows_of(start, count):
        return out_ref.at[pl.ds(pl.multiple_of(start, rows), count)]

    def link(src, dst, peer, index):
        return pltpu.make_async_remote_copy(
            src_ref=src, dst_ref=dst, send_sem=send_sem.at[index], recv_sem=recv_sem.at[index],
            device_id=(peer, me_vis), device_id_type=pl.DeviceIdType.MESH,
        )

    sent = []

    def send(src, dst, peer, index):
        copy = link(src, dst, peer, index)
        copy.start()
        sent.append(copy)

    parts = ((key_ref, 0, 0), (value_ref, lane, 10))

    def slab(start, offset):
        return rows_of(start, rows).at[:, pl.ds(offset, lane)]

    locals_ = []
    for src_ref, offset, extra in parts:
        own = slab(me_seq * rows, offset)
        local = pltpu.make_async_copy(src_ref, own, local_sem.at[extra // 10])
        local.start()
        locals_.append(local)
        send(src_ref, own, mate, 0 + extra)
        send(src_ref, own, across, 1 + extra)
        send(src_ref, own, diagonal, 2 + extra)
    depth = normed_ref.shape[1] // 2

    def project(part):
        def body(n_blk, w_blk):
            acc_ref[...] += jnp.dot(n_blk[...], w_blk[...], preferred_element_type=jnp.float32)

        pltpu.emit_pipeline(
            body,
            grid=(depth // PROJ_TILE,),
            in_specs=[
                pl.BlockSpec((normed_ref.shape[0], PROJ_TILE), lambda k: (0, k)),
                pl.BlockSpec((PROJ_TILE, w_ref.shape[1]), lambda k: (k, 0)),
            ],
        )(normed_ref.at[:, pl.ds(part * depth, depth)], w_ref.at[pl.ds(part * depth, depth)])

    acc_ref[...] = jnp.zeros(acc_ref.shape, jnp.float32)
    project(0)
    for local in locals_:
        local.wait()
    for src_ref, offset, extra in parts:
        link(src_ref, slab(mate * rows, offset), mate, 0 + extra).wait_recv()
        link(src_ref, slab(across * rows, offset), across, 1 + extra).wait_recv()
        link(src_ref, slab(diagonal * rows, offset), diagonal, 2 + extra).wait_recv()

    def half(y, h):
        return rows_of((lax.rem(y + ring, ring) * 4 + h * 2) * rows, 2 * rows)

    def quarter(y, h, q):
        return rows_of((lax.rem(y + ring, ring) * 4 + h * 2 + q) * rows, rows)

    mine = half(column, core)
    send(mine, mine, up, 3)
    send(mine, mine, down, 4)
    project(1)
    below = half(column - 1, core)
    link(below, below, down, 3).wait_recv()
    send(below, below, mate, 7)
    piece = quarter(column - 1, core, 0)
    send(piece, piece, up, 5)
    above = half(column + 1, core)
    link(above, above, up, 4).wait_recv()
    send(above, above, mate, 9)
    piece = quarter(column + 1, core, 1)
    send(piece, piece, down, 6)
    q_ref[...] = (acc_ref[...] + bias_ref[...]).astype(q_ref.dtype)
    far_low = quarter(column + 2, core, 0)
    far_high = quarter(column + 2, core, 1)
    link(far_low, far_low, down, 5).wait_recv()
    link(far_high, far_high, up, 6).wait_recv()
    far = half(column + 2, core)
    send(far, far, mate, 8)
    for offset, index in ((-1, 7), (2, 8), (1, 9)):
        theirs = half(column + offset, 1 - core)
        link(theirs, theirs, mate, index).wait_recv()
    for copy in sent:
        copy.wait_send()


PROJ_TILE = 1024


def gather_keys(keys, values, normed, w_query, q_bias, seq_count):
    rows, lane = keys.shape
    width = 2 * lane
    block = keys
    return pl.pallas_call(
        gather_kernel,
        out_shape=(
            jax.ShapeDtypeStruct((seq_count * rows, width), block.dtype),
            jax.ShapeDtypeStruct((normed.shape[0], w_query.shape[1]), jnp.bfloat16),
        ),
        in_specs=[
            pl.BlockSpec(memory_space=pl.ANY),
            pl.BlockSpec(memory_space=pl.ANY),
            pl.BlockSpec(memory_space=pl.ANY),
            pl.BlockSpec(memory_space=pl.ANY),
            pl.BlockSpec(memory_space=pltpu.VMEM),
        ],
        out_specs=(pl.BlockSpec(memory_space=pl.ANY), pl.BlockSpec(memory_space=pltpu.VMEM)),
        scratch_shapes=[
            pltpu.SemaphoreType.DMA((13,)),
            pltpu.SemaphoreType.DMA((13,)),
            pltpu.SemaphoreType.DMA((2,)),
            pltpu.VMEM((normed.shape[0], w_query.shape[1]), jnp.float32),
        ],
        compiler_params=pltpu.CompilerParams(collective_id=2, has_side_effects=True),
    )(keys, values, normed, w_query, q_bias.reshape(1, -1))


def on_device(
    text, frames, tile_pos, frame_count, doc_ids, norm_gain, w_query, q_bias, w_key, w_value, v_bias
):
    seq_count = lax.axis_size("seq")
    vis_count = lax.axis_size("vis")
    shard_index = lax.axis_index("seq")
    shard_rows = text.shape[0]
    capacity = shard_rows // (seq_count * vis_count)
    first_row = shard_index * shard_rows
    payload = frame_slots(frames, tile_pos, frame_count, shard_rows, seq_count, capacity)
    gathered = exchange_frames(payload, vis_count)
    width = text.shape[1]
    incoming_place = gathered[:, :, width].astype(jnp.int32)
    merged = place_frames(text, gathered, incoming_place, width)
    widened = merged.astype(jnp.float32)
    mean_square = jnp.mean(widened * widened, axis=1, keepdims=True)
    normed = (widened * lax.rsqrt(mean_square + epsilon) * norm_gain).astype(jnp.bfloat16)
    key_rows = jnp.dot(normed, w_key, preferred_element_type=jnp.float32).astype(jnp.bfloat16)
    value_rows = (jnp.dot(normed, w_value, preferred_element_type=jnp.float32) + v_bias).astype(
        jnp.bfloat16
    )
    kv_heads = w_key.shape[1] // HEAD_DIM
    per_group = w_query.shape[1] // HEAD_DIM // kv_heads
    incoming_keys, queries = gather_keys(key_rows, value_rows, normed, w_query, q_bias, seq_count)
    return flash_attention(doc_ids, queries, incoming_keys)


KEY_BLOCK = 512
DOC_SPAN = 2048


def block_bounds(doc_ref, rows, key_rows):
    first = lax.axis_index("seq") * rows
    first_doc = doc_ref[first]
    low = 0
    for b in range(key_rows // KEY_BLOCK):
        low = low + (doc_ref[(b + 1) * KEY_BLOCK - 1] < first_doc).astype(jnp.int32)
    return low, (first + rows - 1) // KEY_BLOCK, first


def flash_kernel(doc_ref, q_ref, k_ref, v_ref, qdoc_ref, kdoc_ref, out_ref, peak_ref, total_ref, acc_ref, qcol_ref):
    step = pl.program_id(0)
    rows = q_ref.shape[0]
    heads = q_ref.shape[1] // HEAD_DIM
    low, high, first = block_bounds(doc_ref, rows, doc_ref.shape[0])
    block = low + step

    @pl.when(step == 0)
    def _():
        peak_ref[...] = jnp.full(peak_ref.shape, negative, jnp.float32)
        total_ref[...] = jnp.zeros(total_ref.shape, jnp.float32)
        acc_ref[...] = jnp.zeros(acc_ref.shape, jnp.float32)
        spread = jnp.broadcast_to(qdoc_ref[...], (rows, rows))
        diagonal = lax.broadcasted_iota(jnp.int32, (rows, rows), 0) == lax.broadcasted_iota(
            jnp.int32, (rows, rows), 1
        )
        qcol_ref[...] = jnp.sum(jnp.where(diagonal, spread, 0), axis=1, keepdims=True)

    @pl.when(block <= high)
    def _():
        key_place = block * KEY_BLOCK + lax.broadcasted_iota(jnp.int32, (1, KEY_BLOCK), 1)
        query_place = first + lax.broadcasted_iota(jnp.int32, (rows, 1), 0)
        allowed = (key_place <= query_place) & (kdoc_ref[...] == qcol_ref[...])
        keys = k_ref[...]
        vals = v_ref[...]
        for h in range(heads):
            cols = slice(h * HEAD_DIM, (h + 1) * HEAD_DIM)
            scores = lax.dot_general(
                q_ref[:, cols], keys, (((1,), (1,)), ((), ())),
                preferred_element_type=jnp.float32,
            ) * HEAD_DIM ** (-0.5)
            scores = jnp.where(allowed, scores, negative)
            old_peak = peak_ref[h]
            new_peak = jnp.maximum(old_peak, jnp.max(scores, axis=1, keepdims=True))
            raised = jnp.where(allowed, jnp.exp(scores - new_peak[:, :1]), 0.0)
            factor = jnp.exp(old_peak - new_peak)
            total_ref[h] = total_ref[h] * factor + jnp.sum(raised, axis=1, keepdims=True)
            peak_ref[h] = new_peak
            product = jnp.dot(raised.astype(jnp.bfloat16), vals, preferred_element_type=jnp.float32)
            acc_ref[:, cols] = acc_ref[:, cols] * factor[:, :1] + product

    @pl.when(step == pl.num_programs(0) - 1)
    def _():
        for h in range(heads):
            cols = slice(h * HEAD_DIM, (h + 1) * HEAD_DIM)
            out_ref[:, cols] = (acc_ref[:, cols] / total_ref[h][:, :1]).astype(out_ref.dtype)


def flash_attention(doc_ids, queries, keyval):
    rows, width = queries.shape
    key_rows = keyval.shape[0]
    steps = max(
        (first + rows - 1) // KEY_BLOCK - max(0, first - DOC_SPAN + 1) // KEY_BLOCK + 1
        for first in range(0, key_rows, rows)
    )
    heads = width // HEAD_DIM

    def clamp(j, d):
        low, high, _ = block_bounds(d, rows, key_rows)
        return jnp.minimum(low + j, high)

    grid_spec = pltpu.PrefetchScalarGridSpec(
        num_scalar_prefetch=1,
        grid=(steps,),
        in_specs=[
            pl.BlockSpec((rows, width), lambda j, d: (0, 0)),
            pl.BlockSpec((KEY_BLOCK, HEAD_DIM), lambda j, d: (clamp(j, d), 0)),
            pl.BlockSpec((KEY_BLOCK, HEAD_DIM), lambda j, d: (clamp(j, d), 1)),
            pl.BlockSpec((1, rows), lambda j, d: (0, lax.axis_index("seq"))),
            pl.BlockSpec((1, KEY_BLOCK), lambda j, d: (0, clamp(j, d))),
        ],
        out_specs=pl.BlockSpec((rows, width), lambda j, d: (0, 0)),
        scratch_shapes=[
            pltpu.VMEM((heads, rows, 1), jnp.float32),
            pltpu.VMEM((heads, rows, 1), jnp.float32),
            pltpu.VMEM((rows, width), jnp.float32),
            pltpu.VMEM((rows, 1), jnp.int32),
        ],
    )
    flops = 4 * rows * width * key_rows // 2
    doc_row = doc_ids.reshape(1, -1)
    return pl.pallas_call(
        flash_kernel,
        out_shape=jax.ShapeDtypeStruct((rows, width), jnp.bfloat16),
        grid_spec=grid_spec,
        compiler_params=pltpu.CompilerParams(dimension_semantics=("arbitrary",)),
        cost_estimate=pl.CostEstimate(
            flops=flops, transcendentals=rows * heads * key_rows // 2,
            bytes_accessed=2 * (2 * rows * width + key_rows * 2 * HEAD_DIM),
        ),
    )(doc_ids, queries, keyval, keyval, doc_row, doc_row)


def solution(mesh):
    in_specs = (
        P("seq", None),
        P(("seq", "vis"), None),
        P(("seq", "vis")),
        P(("seq", "vis")),
        P(),
        P(),
        P(None, "vis"),
        P("vis"),
        P(None, "vis"),
        P(None, "vis"),
        P("vis"),
    )
    out_specs = P("seq", "vis")
    return jax.shard_map(
        on_device, mesh=mesh, in_specs=in_specs, out_specs=out_specs, check_vma=False
    )
```
